32 devices in a mesh: sec: 4 (over x, core), col: 8 (over z, y).
Axes of the slice: x: 2, y: 2, z: 4, core: 2. Of those that a mesh axis runs over, the one named last changes fastest.
Arguments:
- column_state: float32 [2048, 128], P('col'), may hold values from -6 to 6
- mixing_rate: float32 [128], replicated, may hold values from 0.05 to 0.2
- neighbours: int32 [512, 4], P('col'), may hold values from 0 to 511, as said below
- assignment: int32 [2048, 1], P('col'), may hold values from 0 to 23; in each aligned block of 256 rows (0 to 255, 256 to 511, ...) at most 21 rows name the same one
- substeps: int32 [2048], P('col'), may hold values from 1 to 4
- cloud_state: bfloat16 [4, 2, 58, 32, 1344], P('sec', None, None, None, 'col'), may hold values from -6 to 6
- level_map: float32 [58, 64], replicated, may hold values from -0.75 to 0.75
- saturation: float32 [58], replicated, may hold values from -0.5 to 0.5
Outputs:
- new_columns: float32 [2048, 128], P('col')
- new_cloud_state: bfloat16 [4, 2, 58, 32, 1344], P('sec', None, None, None, 'col')
The draws below stay inside these ranges and needn't reach their ends.
Inputs may be any that keep to these rules, and one draw needn't show every extreme that they name: `neighbours`: each neighbour lies within 64 elements of its own element in the order of elements that wraps around, and some lie exactly 64 away. `assignment`: in each aligned block of 256 columns no cloud device is named by more than 21 columns, and in some block one is named by exactly 21.
All inputs are finite; a program needn't handle non-finite values.
Results may differ from the reference program's by a relative error of at most 0.001.
Values sent between devices are 32-bit elements; how exact they have to be, the bound alone decides.
No kernel may reach another device: no remote copies, remote signals or barrier semaphores. Data moves between devices by JAX's collectives and lax.ppermute only.
A program may use at most 64 MiB of HBM per device.

```python
import math
import jax
import jax.numpy as jnp
import numpy as np
from jax import lax

CH = 256
LEV = 64
FIELDS = 2
CZ = 58
CX = 32
MAX_SUB = 4
EH = 64
NELEM = 512
NCOLS = 2048
CAP = 21
N_SEC = 4
N_COL = 8


def draw_neighbours(key, part):
    first_key, second_key = jax.random.split(jax.random.fold_in(key, 71))
    reach = jax.random.randint(first_key, (NELEM, 4), 1, EH + 1)
    orient = jax.random.randint(second_key, (NELEM, 4), 0, 2) * 2 - 1
    offset = reach * orient
    element = jnp.arange(NELEM, dtype=jnp.int32)
    corner = jnp.arange(4, dtype=jnp.int32)
    offset = jnp.where((element[:, None] % 64 == 0) & (corner[None, :] == 0), EH, offset)
    return jnp.mod(element[:, None] + offset, NELEM).astype(jnp.int32)


def set_ends(result, rng, least, high):
    dims = result.shape
    place = [jax.random.randint(jax.random.fold_in(rng, axis), (), 0, dims[axis]) for axis in range(len(dims))]
    result = result.at[tuple(place)].set(least)
    longest = dims.index(max(dims))
    place[longest] = (place[longest] + 1) % dims[longest]
    return result.at[tuple(place)].set(high)


def block_scale(key, shape, pieces, low, largest):
    level, own = 1.0, jax.random.fold_in(key, 6)
    for position, shards_of in pieces:
        heights = jnp.exp(jax.random.uniform(jax.random.fold_in(own, position), (shards_of,), jnp.float32, low / len(pieces), largest / len(pieces)))
        level = level * jnp.repeat(heights, shape[position] // shards_of).reshape([-1 if axis == position else 1 for axis in range(len(shape))])
    return level


def routed_block(own_key, own, number, rows, number_of, top, limit, lean):
    order = jax.random.permutation(own_key, number_of)
    heavy_load, usual = load_shares(number_of, rows * top, limit, lean, True), load_shares(number_of, rows * top, limit, lean, False)
    places = jnp.arange(number_of)

    def named(tallies, turn):
        used = int((tallies > 0).sum())
        fixed = max(1, used // 4)
        moved = fixed + (places - fixed + turn * (used - fixed)) % max(1, number_of - fixed)
        return jnp.zeros((number_of,), jnp.int32).at[order[jnp.where(places < fixed, places, moved)]].set(jnp.asarray(tallies, jnp.int32))

    tallies = jnp.where(number % 4 == 0, named(heavy_load, number // 4), named(usual, number - number // 4 - 1))
    mixed = jax.random.permutation(jax.random.fold_in(own, 3), number_of)
    donor, taker = mixed[0:number_of // 2 * 2:2], mixed[1:number_of // 2 * 2:2]
    slack = jnp.minimum(tallies[donor] - 1, limit - tallies[taker]) // 2
    slack = jnp.where((donor == order[0]) | (taker == order[0]) | (tallies[taker] == 0), 0, jnp.maximum(slack, 0))
    moved = jax.random.randint(jax.random.fold_in(own, 4), (number_of // 2,), 0, 1 << 20) % (slack + 1)
    tallies = tallies.at[donor].add(-moved).at[taker].add(moved)
    members = jnp.searchsorted(jnp.cumsum(tallies), jnp.arange(rows * top), side="right").astype(jnp.int32)
    listing = members.reshape(top, rows).T
    listing = listing[jax.random.permutation(jax.random.fold_in(own, 1), rows)]
    turn = jax.random.randint(jax.random.fold_in(own, 2), (rows, 1), 0, top)
    return jnp.take_along_axis(listing, (jnp.arange(top)[None, :] + turn) % top, axis=1)


def load_shares(amount, total, most, lean, full):
    loads = [(1 << 20) // math.isqrt(standing ** lean) + 1 for standing in range(1, amount + 1)]
    largest = most if full else min(most, max(-(-total // amount), total * loads[0] // sum(loads)))
    least = 1 if total - largest >= amount - 1 else 0
    given, spare = [largest] + [least] * (amount - 1), total - largest - least * (amount - 1)
    while spare > 0:
        candidates = [i for i in range(1, amount) if given[i] < largest] or [i for i in range(1, amount) if given[i] < most]
        mass, left = sum([loads[i] for i in candidates]), spare
        for i in candidates:
            extra = min(most - given[i], max(1, left * loads[i] // mass), spare)
            given[i] = given[i] + extra
            spare = spare - extra
    return np.array(given)


def gaussian(key, dims, deviation, most, shards=(), kind=jnp.bfloat16):
    factor_of = block_scale(key, dims, shards, -0.22, 0.18) if shards else 1.0
    result = jax.random.normal(key, dims, jnp.float32) * deviation * factor_of
    return jnp.minimum(jnp.maximum(result, -most), most).astype(kind)


def setup_inputs(seed: int = 0) -> dict:
    seeds = jax.random.split(jax.random.key(seed), 9)
    column_state = gaussian(seeds[0], (NCOLS, FIELDS * LEV), 1.0, 6.0, ((0, 8),), jnp.float32)
    mixing_rate = jnp.clip(jnp.exp(jax.random.uniform(seeds[1], (FIELDS * LEV,), jnp.float32, math.log(0.05), math.log(0.2))), 0.05, 0.2)
    neighbours = draw_neighbours(jax.random.fold_in(seeds[8], 71), 0)
    assignment_keys = jax.random.split(jax.random.fold_in(seeds[3], 1), NCOLS // CH)
    assignment_turns = jax.random.permutation(jax.random.fold_in(seeds[3], 3), NCOLS // CH)
    assignment = jax.vmap(lambda own, number: routed_block(jax.random.fold_in(seeds[3], 2), own, number, CH, (N_SEC - 1) * N_COL, 1, CAP, 2))(assignment_keys, assignment_turns).reshape((NCOLS, 1))
    substeps = set_ends(jax.random.randint(seeds[4], (NCOLS,), 1, 5), jax.random.fold_in(seeds[4], 1), 1, 4).astype(jnp.int32)
    cloud_state = gaussian(seeds[5], (N_SEC, FIELDS, CZ, CX, N_COL * N_COL * CAP), 1.0, 6.0, ((0, 4), (4, 8)))
    level_map = gaussian(seeds[6], (CZ, LEV), LEV ** -0.5, 0.75, (), jnp.float32)
    saturation = jnp.clip(jax.random.uniform(seeds[7], (CZ,), jnp.float32, -0.5, 0.5), -0.5, 0.5)
    return dict(column_state=column_state, mixing_rate=mixing_rate, neighbours=neighbours, assignment=assignment, substeps=substeps, cloud_state=cloud_state, level_map=level_map, saturation=saturation)


RELAX = 0.25
HORIZ = 0.12
VERTIC = 0.1
LATENT = 2.5
VMIX = 0.2
HIGH = lax.Precision.HIGHEST


def vertical_term(values, levels):
    shaped = values.reshape(values.shape[0], -1, levels)
    upper = jnp.concatenate([shaped[:, :, 1:], shaped[:, :, -1:]], axis=2)
    lower = jnp.concatenate([shaped[:, :, :1], shaped[:, :, :-1]], axis=2)
    return (upper + lower - 2.0 * shaped).reshape(values.shape)


def advance(columns, mixing_rate, element_means, near_ids, own_means, levels):
    spread = jnp.sum(element_means[near_ids], axis=1) - 4.0 * own_means
    return columns + mixing_rate[None, :] * jnp.repeat(spread, 4, axis=0) + VMIX * vertical_term(columns, levels)


def slot_ranks(targets, destinations):
    onehot = (targets[:, None] == jnp.arange(destinations, dtype=jnp.int32)[None, :]).astype(jnp.int32)
    running = jnp.cumsum(onehot, axis=0) - 1
    return jnp.sum(running * onehot, axis=1).astype(jnp.int32)


def cloud_substep(fields, target, saturation):
    mean_now = jnp.mean(fields, axis=2)
    fields = fields + RELAX * (target - mean_now)[:, :, None, :]
    across = jnp.roll(fields, 1, axis=2) + jnp.roll(fields, -1, axis=2) - 2.0 * fields
    upper = jnp.concatenate([fields[:, 1:], fields[:, -1:]], axis=1)
    lower = jnp.concatenate([fields[:, :1], fields[:, :-1]], axis=1)
    fields = fields + HORIZ * across + VERTIC * (upper + lower - 2.0 * fields)
    condensed = 0.5 * jnp.maximum(fields[1] - saturation[:, None, None], 0.0)
    return jnp.stack([fields[0] + LATENT * condensed, fields[1] - condensed])


def run_cloud(block, columns, counts, level_map, saturation, levels):
    shaped = columns.reshape(columns.shape[0], -1, levels)
    target = jnp.einsum("zl,sfl->fzs", level_map, shaped, precision=HIGH)
    start = block.astype(jnp.float32)
    fields = start
    for substep_index in range(MAX_SUB):
        stepped = cloud_substep(fields, target, saturation)
        fields = jnp.where((counts > substep_index)[None, None, None, :], stepped, fields)
    change = jnp.mean(fields, axis=2) - jnp.mean(start, axis=2)
    tendency = jnp.einsum("zl,fzs->sfl", level_map, change, precision=HIGH).reshape(columns.shape[0], -1)
    return fields.astype(jnp.bfloat16), tendency


def reference(column_state, mixing_rate, neighbours, assignment, substeps, cloud_state, level_map, saturation):
    levels = level_map.shape[1]
    width = column_state.shape[1]
    element_means = jnp.mean(column_state.reshape(-1, 4, width), axis=1)
    advanced = advance(column_state, mixing_rate, element_means, neighbours, element_means, levels)
    clouds = (N_SEC - 1) * N_COL
    per_device = N_COL * CAP
    targets = assignment[:, 0].astype(jnp.int32)
    ranks = jax.vmap(slot_ranks, in_axes=(0, None))(targets.reshape(N_COL, CH), clouds).reshape(-1)
    host_ids = jnp.arange(N_COL * CH, dtype=jnp.int32) // CH
    flat = (targets * per_device + host_ids * CAP + ranks).astype(jnp.int32)
    slot_columns = jnp.zeros((clouds * per_device, width), jnp.float32).at[flat].set(advanced)
    slot_counts = jnp.zeros((clouds * per_device,), jnp.int32).at[flat].set(substeps)
    zero_index = jnp.zeros((), jnp.int32)

    def one_block(index):
        sec_index = (index // N_COL + 1).astype(jnp.int32)
        col_index = (index % N_COL).astype(jnp.int32)
        block = lax.dynamic_slice(cloud_state, (sec_index, zero_index, zero_index, zero_index, (col_index * per_device).astype(jnp.int32)), (1,) + cloud_state.shape[1:4] + (per_device,))[0]
        block_columns = lax.dynamic_slice_in_dim(slot_columns, (index * per_device).astype(jnp.int32), per_device, 0)
        block_counts = lax.dynamic_slice_in_dim(slot_counts, (index * per_device).astype(jnp.int32), per_device, 0)
        return run_cloud(block, block_columns, block_counts, level_map, saturation, levels)

    new_blocks, tendencies = lax.map(one_block, jnp.arange(clouds, dtype=jnp.int32))
    shape_inner = cloud_state.shape[1:4]
    new_blocks = new_blocks.reshape((N_SEC - 1, N_COL) + shape_inner + (per_device,))
    new_blocks = jnp.transpose(new_blocks, (0, 2, 3, 4, 1, 5)).reshape((N_SEC - 1,) + shape_inner + (N_COL * per_device,))
    new_cloud_state = jnp.concatenate([cloud_state[:1], new_blocks], axis=0)
    summed = advanced + tendencies.reshape(-1, width)[flat]
    is_water = (jnp.arange(width) // levels == 1)[None, :]
    new_columns = jnp.where(is_water, jnp.maximum(summed, 0.0), summed)
    return new_columns, new_cloud_state
```

```python
import functools

import jax
import jax.numpy as jnp
from jax import lax
from jax.experimental import pallas as pl
from jax.experimental.pallas import tpu as pltpu
from jax.sharding import PartitionSpec as P

MAX_SUB = 4
RELAX = 0.25
HORIZ = 0.12
VERTIC = 0.1
LATENT = 2.5
VMIX = 0.2
HIGH = lax.Precision.HIGHEST
LANES = 128
F32 = jnp.float32
I32 = jnp.int32


def iota(shape, dim):
    return lax.broadcasted_iota(I32, shape, dim)


def mm(a, b, contract, precision=HIGH):
    return lax.dot_general(
        a, b, (contract, ((), ())), precision=precision, preferred_element_type=F32
    )


NN = ((1,), (0,))
NT = ((1,), (1,))
TN = ((0,), (0,))


def divided(value, by):
    return jnp.floor((value.astype(F32) + 0.5) * (1.0 / by)).astype(I32)


def vertical_mix(values, levels):
    upper = jnp.concatenate([values[1:levels], values[levels - 1 : levels]], axis=0)
    lower = jnp.concatenate([values[0:1], values[0 : levels - 1]], axis=0)
    inner = values[0:levels]
    return inner + VERTIC * (upper + lower - 2.0 * inner)


def means_kernel(columns_ref, means_ref):
    elements = means_ref.shape[0]
    total = columns_ref[pl.ds(0, elements, stride=4), :]
    for k in range(1, 4):
        total = total + columns_ref[pl.ds(k, elements, stride=4), :]
    means_ref[...] = 0.25 * total


def host_kernel(
    where_ref,
    columns_ref,
    means_ref,
    mixing_ref,
    neighbours_ref,
    targets_ref,
    substeps_ref,
    map_ref,
    base_ref,
    sides_ref,
    pack_ref,
    counts_ref,
    slots_ref,
    fold_ref,
    unfold_ref,
    *,
    col_count,
    capacity,
    padded,
    clouds,
):
    section = where_ref[0]
    position = where_ref[1]
    rows, width = columns_ref.shape
    levels = map_ref.shape[1]
    cloud_levels = map_ref.shape[0]
    elements = rows // 4
    block = col_count * padded
    near = neighbours_ref[...] - (position - 1) * elements
    near = jnp.where(near < 0, near + elements * col_count, near)
    near = jnp.where(near >= elements * col_count, near - elements * col_count, near)
    window = iota((3 * elements, elements), 0)
    picks = jnp.where(window == iota((3 * elements, elements), 1) + elements, -4.0, 0.0)
    for k in range(near.shape[0]):
        picks = picks + jnp.where(window == near[k : k + 1, :], 1.0, 0.0)
    row_element = divided(iota((rows, elements), 0), 4)
    spread_rows = jnp.where(row_element == iota((rows, elements), 1), 1.0, 0.0)
    weights = mm(spread_rows, picks, NT)
    sides_ref[:, :elements] = weights[:, :elements]
    sides_ref[:, elements:] = weights[:, 2 * elements :]
    own = mm(weights[:, elements : 2 * elements], means_ref[...], NN)
    values = columns_ref[...]
    lane = iota((rows, width), 1)
    level = lane - levels * divided(lane, levels)
    upper = jnp.where(level == levels - 1, values, pltpu.roll(values, width - 1, 1))
    lower = jnp.where(level == 0, values, pltpu.roll(values, 1, 1))
    base_ref[...] = values + mixing_ref[...] * own + VMIX * (upper + lower - 2.0 * values)
    targets = targets_ref[...]
    onehot = jnp.where(iota((clouds, rows), 0) == targets, 1.0, 0.0)
    before = jnp.where(iota((rows, rows), 0) < iota((rows, rows), 1), 1.0, 0.0)
    running = mm(onehot, before, NN)
    ranks = jnp.sum(running * onehot, axis=0, keepdims=True).astype(I32)
    owner = divided(targets, col_count)
    slot = (targets - owner * col_count) * padded + ranks
    mine = jnp.where(owner + 1 == section, slot, -1)
    pack = jnp.where(iota((block, rows), 0) == mine, 1.0, 0.0)
    pack_ref[...] = pack
    count_rows = jnp.where(
        iota((width, rows), 0) == levels - 1, substeps_ref[...].astype(F32), 0.0
    )
    counts_ref[...] = mm(pack, count_rows, NT)
    everywhere = (owner * block + slot).astype(F32)
    identity = jnp.where(iota((rows, rows), 0) == iota((rows, rows), 1), 1.0, 0.0)
    slots_ref[...] = mm(identity, jnp.broadcast_to(everywhere, (LANES, rows)), NT)
    plain = map_ref[...]
    folded = RELAX * vertical_mix(plain, cloud_levels)
    for ref, value in ((fold_ref, folded), (unfold_ref, plain)):
        ref[...] = jnp.zeros_like(ref)
        for f in range(width // levels):
            ref[f * levels : f * levels + cloud_levels, f * levels : (f + 1) * levels] = value


def pack_kernel(
    base_ref, sides_ref, left_ref, right_ref, mixing_ref, pack_ref, counts_ref, fold_ref,
    advanced_ref, out_ref,
):
    halo = jnp.concatenate([left_ref[...], right_ref[...]], axis=0)
    spread = mm(sides_ref[...], halo, NN)
    advanced = base_ref[...] + mixing_ref[...] * spread
    advanced_ref[...] = advanced
    packed = mm(pack_ref[...], advanced, NN)
    out_ref[...] = mm(packed, fold_ref[...], NT) + counts_ref[...]


def linear(below, here, above):
    east = [pltpu.roll(here[3], 1, 0), here[0], here[1], here[2]]
    west = [here[1], here[2], here[3], pltpu.roll(here[0], 7, 0)]
    keep = 1.0 - 2.0 * HORIZ - 2.0 * VERTIC
    return [
        keep * here[j] + HORIZ * (east[j] + west[j]) + VERTIC * (below[j] + above[j])
        for j in range(4)
    ]


def groups(ref, index):
    return [ref[index + (pl.ds(8 * j, 8),)] for j in range(4)]


def prepare_kernel(state_ref, moved_ref, means_ref, natural_ref, sums_ref):
    fields, levels, columns, slots = state_ref.shape
    tiles = moved_ref.shape[0]
    for tile in range(tiles):
        width = min(LANES, slots - tile * LANES)
        for f in range(fields):

            def widen(z, carry):
                value = state_ref[f, z, :, tile * LANES : tile * LANES + width].astype(F32)
                natural_ref[z, :, :width] = value
                return carry

            lax.fori_loop(0, levels, widen, 0, unroll=2)

            def strided(z):
                return [natural_ref[z, pl.ds(j, 8, stride=4), :] for j in range(4)]

            def level(z, carry):
                below, here = carry
                above = strided(jnp.minimum(z + 1, levels - 1))
                out = linear(below, here, above)
                for j in range(4):
                    moved_ref[tile, f, z, pl.ds(8 * j, 8), :] = out[j]
                sums_ref[pl.ds(pl.multiple_of(z * 8, 8), 8), :] = (here[0] + here[1]) + (here[2] + here[3])
                return here, above

            first = strided(0)
            lax.fori_loop(0, levels, level, (first, first), unroll=2)
            means_ref[tile, f] = folded_sums(sums_ref, columns)


def folded_sums(sums_ref, columns):
    rows = sums_ref.shape[0] // 8
    total = sums_ref[pl.ds(0, rows, stride=8), :]
    for k in range(1, 8):
        total = total + sums_ref[pl.ds(k, rows, stride=8), :]
    return total * (1.0 / columns)


def slot_map(block, slots, capacity, padded):
    slot = iota((block, slots), 1)
    row = slot + (padded - capacity) * divided(slot, capacity)
    return jnp.where(iota((block, slots), 0) == row, 1.0, 0.0)


def water_kernel(
    received_ref,
    moved_ref,
    means_ref,
    saturation_ref,
    unfold_ref,
    water_ref,
    excess_ref,
    offsets_ref,
    counts_ref,
    back_ref,
    target_ref,
    sums_ref,
    change_ref,
    *,
    capacity,
    padded,
    slots,
    stride,
):
    tiles, _, levels, columns, _ = moved_ref.shape
    block = received_ref.shape[0]
    places = slot_map(block, slots, capacity, padded)
    arrived = mm(received_ref[...], places, TN)
    change_ref[...] = jnp.zeros_like(change_ref)
    for tile in range(tiles):
        width = min(LANES, slots - tile * LANES)
        target_ref[...] = jnp.zeros_like(target_ref)
        target_ref[:, :width] = arrived[:, tile * LANES : tile * LANES + width]
        count = target_ref[stride - 1 : stride, :]
        counts_ref[tile] = jnp.broadcast_to(count, (8, LANES))
        goal = [target_ref[f * stride : f * stride + levels, :] for f in range(2)]
        start = [means_ref[tile, f, :levels, :] for f in range(2)]
        mean = list(start)
        for n in range(MAX_SUB):
            mixed = [vertical_mix(mean[f], levels) for f in range(2)]
            offset = [goal[f] - RELAX * mixed[f] for f in range(2)]
            for f in range(2):
                offsets_ref[n, tile, f, :levels, :] = offset[f]
            active = jnp.broadcast_to(count, (8, LANES)) > float(n)

            def finish(z, lin, old):
                shift = jnp.broadcast_to(offsets_ref[n, tile, 1, pl.ds(z, 1), :], (8, LANES))
                limit = jnp.broadcast_to(saturation_ref[pl.ds(z, 1), :], (8, LANES))
                total = None
                for j in range(4):
                    v = lin[j] + shift
                    h = jnp.maximum(v - limit, 0.0)
                    u = v - 0.5 * h
                    if old is not None:
                        u = jnp.where(active, u, old[j])
                    excess_ref[n, tile, z, pl.ds(8 * j, 8), :] = h
                    water_ref[tile, z, pl.ds(8 * j, 8), :] = u
                    total = h if total is None else total + h
                sums_ref[pl.ds(pl.multiple_of(z * 8, 8), 8), :] = total

            if n == 0:

                def level(z, carry):
                    finish(z, groups(moved_ref, (tile, 1, z)), None)
                    return carry

                lax.fori_loop(0, levels, level, 0, unroll=2)
            else:

                def level(z, carry):
                    below, here = carry
                    above = groups(water_ref, (tile, jnp.minimum(z + 1, levels - 1)))
                    finish(z, linear(below, here, above), here)
                    return here, above

                first = groups(water_ref, (tile, 0))
                lax.fori_loop(0, levels, level, (first, first), unroll=2)
            spilled = folded_sums(sums_ref, columns)[:levels]
            step = [
                mixed[0] + offset[0] + (0.5 * LATENT) * spilled,
                mixed[1] + offset[1] - 0.5 * spilled,
            ]
            keep = count > float(n)
            mean = [jnp.where(keep, step[f], mean[f]) for f in range(2)]
        for f in range(2):
            change_ref[f * stride : f * stride + levels, tile * LANES : tile * LANES + width] = (
                mean[f] - start[f]
            )[:, :width]
    spread = mm(places, change_ref[...], NT)
    back_ref[...] = mm(spread, unfold_ref[...], NN)


def energy_kernel(
    state_ref, moved_ref, water_ref, excess_ref, offsets_ref, counts_ref, out_ref, energy_ref,
    natural_ref,
):
    tiles, _, levels, columns, _ = moved_ref.shape
    slots = state_ref.shape[3]
    for tile in range(tiles):
        width = min(LANES, slots - tile * LANES)
        count = counts_ref[tile]
        for n in range(MAX_SUB):
            active = count > float(n)

            def finish(z, lin, old):
                shift = jnp.broadcast_to(offsets_ref[n, tile, 0, pl.ds(z, 1), :], (8, LANES))
                h = groups(excess_ref, (n, tile, z))
                for j in range(4):
                    u = lin[j] + shift + (0.5 * LATENT) * h[j]
                    if old is not None:
                        u = jnp.where(active, u, old[j])
                    energy_ref[z, pl.ds(8 * j, 8), :] = u

            if n == 0:

                def level(z, carry):
                    finish(z, groups(moved_ref, (tile, 0, z)), None)
                    return carry

                lax.fori_loop(0, levels, level, 0, unroll=2)
            else:

                def level(z, carry):
                    below, here = carry
                    above = groups(energy_ref, (jnp.minimum(z + 1, levels - 1),))
                    finish(z, linear(below, here, above), here)
                    return here, above

                first = groups(energy_ref, (0,))
                lax.fori_loop(0, levels, level, (first, first), unroll=2)
        for f in range(2):

            def permute(z, carry):
                source = groups(energy_ref, (z,)) if f == 0 else groups(water_ref, (tile, z))
                for j in range(4):
                    natural_ref[z, pl.ds(j, 8, stride=4), :] = source[j]
                return carry

            lax.fori_loop(0, levels, permute, 0, unroll=2)
            held = jnp.broadcast_to(count[0:1, :width], (columns, width)) > 0.0

            def narrow(z, carry):
                at = slice(tile * LANES, tile * LANES + width)
                old = state_ref[f, z, :, at].astype(F32)
                value = jnp.where(held, natural_ref[z, :, :width], old)
                out_ref[f, z, :, at] = value.astype(jnp.bfloat16)
                return carry

            lax.fori_loop(0, levels, narrow, 0, unroll=2)


def final_kernel(advanced_ref, slots_ref, gathered_ref, out_ref, *, levels):
    rows, width = advanced_ref.shape
    sections, block, _ = gathered_ref.shape
    summed = advanced_ref[...]
    place = slots_ref[:, :1].astype(I32)
    for s in range(1, sections):
        picks = jnp.where(iota((rows, block), 1) + (s - 1) * block == place, 1.0, 0.0)
        summed = summed + mm(picks, gathered_ref[s], NN)
    water = divided(iota((rows, width), 1), levels) == 1
    out_ref[...] = jnp.where(water, jnp.maximum(summed, 0.0), summed)


def shape(*dims, dtype=F32):
    return jax.ShapeDtypeStruct(dims, dtype)


VMEM = pl.BlockSpec(memory_space=pltpu.VMEM)
SMEM = pl.BlockSpec(memory_space=pltpu.SMEM)
PARAMS = pltpu.CompilerParams(vmem_limit_bytes=60 << 20)


def call(kernel, inputs, out_shape, name, scratch=(), first=VMEM):
    many = isinstance(out_shape, (list, tuple))
    return pl.pallas_call(
        kernel,
        out_shape=out_shape,
        in_specs=[first] + [VMEM] * (len(inputs) - 1),
        out_specs=[VMEM] * len(out_shape) if many else VMEM,
        scratch_shapes=list(scratch),
        compiler_params=PARAMS,
        name=name,
    )(*inputs)


def body(
    column_state, mixing_rate, neighbours, assignment, substeps, cloud_state, level_map, saturation
):
    col_count = lax.axis_size("col")
    sec_count = lax.axis_size("sec")
    section = lax.axis_index("sec")
    position = lax.axis_index("col")
    rows, width = column_state.shape
    cloud_levels, levels = level_map.shape
    _, fields, _, columns, slots = cloud_state.shape
    elements = rows // 4
    capacity = slots // col_count
    padded = -(-capacity // 8) * 8
    block = col_count * padded
    clouds = (sec_count - 1) * col_count
    tiles = -(-slots // LANES)
    level_rows = -(-cloud_levels // 8) * 8
    mixing = mixing_rate.reshape(1, width)
    state = cloud_state[0]

    means = call(means_kernel, (column_state,), shape(elements, width), "means")
    ring = [(i, (i + 1) % col_count) for i in range(col_count)]
    left = lax.ppermute(means, "col", ring)
    right = lax.ppermute(means, "col", [(j, i) for i, j in ring])

    where = jnp.stack([section, position]).astype(I32)
    base, sides, pack, counts, places, fold, unfold = call(
        functools.partial(
            host_kernel, col_count=col_count, capacity=capacity, padded=padded, clouds=clouds
        ),
        (
            where,
            column_state,
            means,
            mixing,
            neighbours.T,
            assignment.reshape(1, rows),
            substeps.reshape(1, rows),
            level_map,
        ),
        [
            shape(rows, width),
            shape(rows, 2 * elements),
            shape(block, rows),
            shape(block, width),
            shape(rows, LANES),
            shape(width, width),
            shape(width, width),
        ],
        "host",
        first=SMEM,
    )
    moved, cloud_means = call(
        prepare_kernel,
        (state,),
        [
            shape(tiles, fields, cloud_levels, columns, LANES),
            shape(tiles, fields, level_rows, LANES),
        ],
        "prepare",
        scratch=[
            pltpu.VMEM((cloud_levels, columns, LANES), F32),
            pltpu.VMEM((level_rows * 8, LANES), F32),
        ],
    )
    advanced, outgoing = call(
        pack_kernel,
        (base, sides, left, right, mixing, pack, counts, fold),
        [shape(rows, width), shape(block, width)],
        "pack",
    )
    received = lax.all_to_all(outgoing, "col", split_axis=0, concat_axis=0, tiled=True)
    water, excess, offsets, slot_counts, back = call(
        functools.partial(
            water_kernel, capacity=capacity, padded=padded, slots=slots, stride=levels
        ),
        (
            received,
            moved,
            cloud_means,
            jnp.broadcast_to(saturation[:, None], (cloud_levels, LANES)),
            unfold,
        ),
        [
            shape(tiles, cloud_levels, columns, LANES),
            shape(MAX_SUB, tiles, cloud_levels, columns, LANES),
            shape(MAX_SUB, tiles, fields, level_rows, LANES),
            shape(tiles, 8, LANES),
            shape(block, width),
        ],
        "water",
        scratch=[
            pltpu.VMEM((width, LANES), F32),
            pltpu.VMEM((level_rows * 8, LANES), F32),
            pltpu.VMEM((width, slots), F32),
        ],
    )
    returned = lax.all_to_all(back, "col", split_axis=0, concat_axis=0, tiled=True)
    new_block = call(
        energy_kernel,
        (state, moved, water, excess, offsets, slot_counts),
        shape(fields, cloud_levels, columns, slots, dtype=jnp.bfloat16),
        "energy",
        scratch=[
            pltpu.VMEM((cloud_levels, columns, LANES), F32),
            pltpu.VMEM((cloud_levels, columns, LANES), F32),
        ],
    )
    gathered = lax.all_gather(returned, "sec", axis=0, tiled=False)
    new_columns = call(
        functools.partial(final_kernel, levels=levels),
        (advanced, places, gathered),
        shape(rows, width),
        "final",
    )
    return new_columns, new_block[None]


def solution(mesh):
    in_specs = (
        P("col", None),
        P(),
        P("col", None),
        P("col", None),
        P("col"),
        P("sec", None, None, None, "col"),
        P(),
        P(),
    )
    out_specs = (P("col", None), P("sec", None, None, None, "col"))
    return jax.shard_map(body, mesh=mesh, in_specs=in_specs, out_specs=out_specs, check_vma=False)
```

```python
import functools

import jax
import jax.numpy as jnp
from jax import lax
from jax.experimental import pallas as pl
from jax.experimental.pallas import tpu as pltpu
from jax.sharding import PartitionSpec as P

MAX_SUB = 4
RELAX = 0.25
HORIZ = 0.12
VERTIC = 0.1
LATENT = 2.5
VMIX = 0.2
HIGH = lax.Precision.HIGHEST
LANES = 128
F32 = jnp.float32
BF16 = jnp.bfloat16
STEP = 10
SHRINK = 1.0 / LATENT
I32 = jnp.int32


def iota(shape, dim):
    return lax.broadcasted_iota(I32, shape, dim)


def mm(a, b, contract, precision=HIGH):
    return lax.dot_general(
        a, b, (contract, ((), ())), precision=precision, preferred_element_type=F32
    )


NN = ((1,), (0,))
NT = ((1,), (1,))
TN = ((0,), (0,))


def divided(value, by):
    return jnp.floor((value.astype(F32) + 0.5) * (1.0 / by)).astype(I32)


def split(values):
    high = values.astype(BF16)
    rest = values - high.astype(F32)
    middle = rest.astype(BF16)
    low = (rest - middle.astype(F32)).astype(BF16)
    return low, middle, high


def select(picks, values, contract, swap=False):
    total = None
    for part in split(values):
        a, b = (part, picks) if swap else (picks, part)
        term = lax.dot_general(a, b, (contract, ((), ())), preferred_element_type=F32)
        total = term if total is None else total + term
    return total


def vertical_mix(values, levels):
    upper = jnp.concatenate([values[1:levels], values[levels - 1 : levels]], axis=0)
    lower = jnp.concatenate([values[0:1], values[0 : levels - 1]], axis=0)
    inner = values[0:levels]
    return inner + VERTIC * (upper + lower - 2.0 * inner)


def means_kernel(columns_ref, means_ref):
    elements = means_ref.shape[0]
    total = columns_ref[pl.ds(0, elements, stride=4), :]
    for k in range(1, 4):
        total = total + columns_ref[pl.ds(k, elements, stride=4), :]
    means_ref[...] = 0.25 * total


def host_kernel(
    columns_ref,
    means_ref,
    mixing_ref,
    neighbours_ref,
    targets_ref,
    substeps_ref,
    map_ref,
    base_ref,
    sides_ref,
    wanted_ref,
    constant_ref,
    slots_ref,
    fold_ref,
    unfold_ref,
    *,
    col_count,
    padded,
    clouds,
):
    section = lax.axis_index("sec")
    position = lax.axis_index("col")
    rows, width = columns_ref.shape
    levels = map_ref.shape[1]
    cloud_levels = map_ref.shape[0]
    elements = rows // 4
    block = col_count * padded
    near = neighbours_ref[...] - (position - 1) * elements
    near = jnp.where(near < 0, near + elements * col_count, near)
    near = jnp.where(near >= elements * col_count, near - elements * col_count, near)
    window = iota((3 * elements, elements), 0)
    picks = jnp.where(window == iota((3 * elements, elements), 1) + elements, -4.0, 0.0)
    for k in range(near.shape[0]):
        picks = picks + jnp.where(window == near[k : k + 1, :], 1.0, 0.0)
    row_element = divided(iota((rows, elements), 0), 4)
    spread_rows = jnp.where(row_element == iota((rows, elements), 1), 1.0, 0.0)
    weights = mm(spread_rows.astype(BF16), picks.astype(BF16), NT, None)
    sides = jnp.concatenate([weights[:, :elements], weights[:, 2 * elements :]], axis=1)
    sides = sides.astype(BF16)
    sides_ref[...] = sides
    own = select(weights[:, elements : 2 * elements].astype(BF16), means_ref[...], NN)
    values = columns_ref[...]
    lane = iota((rows, width), 1)
    level = lane - levels * divided(lane, levels)
    upper = jnp.where(level == levels - 1, values, pltpu.roll(values, width - 1, 1))
    lower = jnp.where(level == 0, values, pltpu.roll(values, 1, 1))
    base = values + mixing_ref[...] * own + VMIX * (upper + lower - 2.0 * values)
    base_ref[...] = base
    targets = targets_ref[...]
    onehot = jnp.where(iota((clouds, rows), 0) == targets, 1.0, 0.0)
    before = jnp.where(iota((rows, rows), 0) < iota((rows, rows), 1), 1.0, 0.0)
    running = mm(onehot.astype(BF16), before.astype(BF16), NN, None)
    ranks = jnp.sum(running * onehot, axis=0, keepdims=True).astype(I32)
    owner = divided(targets, col_count)
    slot = (targets - owner * col_count) * padded + ranks
    mine = jnp.where(owner + 1 == section, slot, -1)
    pack = jnp.where(iota((block, rows), 0) == mine, 1.0, 0.0).astype(BF16)
    wanted_ref[...] = mm(pack, sides, NN, None).astype(BF16)
    plain = map_ref[...]
    folded = RELAX * vertical_mix(plain, cloud_levels)
    for ref, value in ((fold_ref, folded), (unfold_ref, plain)):
        ref[...] = jnp.zeros_like(ref)
        for f in range(width // levels):
            ref[f * levels : f * levels + cloud_levels, f * levels : (f + 1) * levels] = value
    count_rows = jnp.where(
        iota((width, rows), 0) == levels - 1, substeps_ref[...].astype(F32), 0.0
    )
    counts = mm(pack, count_rows.astype(BF16), NT, None)
    constant_ref[...] = mm(select(pack, base, NN), fold_ref[...], NT) + counts
    everywhere = jnp.broadcast_to((owner * block + slot).astype(F32), (LANES, rows))
    identity = jnp.where(iota((rows, rows), 0) == iota((rows, rows), 1), 1.0, 0.0)
    slots_ref[...] = select(identity.astype(BF16), everywhere, NT)


def pack_kernel(wanted_ref, left_ref, right_ref, mixing_ref, constant_ref, fold_ref, out_ref):
    halo = jnp.concatenate([left_ref[...], right_ref[...]], axis=0)
    spread = mixing_ref[...] * select(wanted_ref[...], halo, NN)
    out_ref[...] = constant_ref[...] + mm(spread, fold_ref[...], NT)


class Segment:
    def __init__(self, lane0, width, levels, begin):
        self.lane0, self.width, self.begin, self.levels = lane0, width, begin, levels
        self.steps = -(-levels // (LANES // width))
        self.groups = -(-levels // self.steps)
        self.missing = self.groups * self.steps - levels
        self.blocks = -(-self.steps // STEP)
        self.rows = (begin + 1, begin + 1 + self.steps)

    def group_steps(self, g):
        return self.steps - (self.missing if g == self.groups - 1 else 0)


def segments_of(slots, levels):
    segments, begin = [], 0
    for lane0 in range(0, slots, LANES):
        segments.append(Segment(lane0, min(LANES, slots - lane0), levels, begin))
        begin += segments[-1].steps + 2
    rows = max([begin] + [s.begin + 2 + s.blocks * STEP for s in segments])
    return segments, -(-rows // 8) * 8


def fill_spare(segments, load, store):
    def turned(value, shift):
        tall = jnp.broadcast_to(value, (8, LANES)) if value.shape[0] == 1 else value
        return pltpu.roll(tall, shift % LANES, 1)[: value.shape[0]]

    for s in segments:
        if s.missing:
            row = s.rows[1] - s.missing
            value = load(row - 1)
            lane = iota(value.shape, 1)
            store(row, jnp.where(lane >= (s.groups - 1) * s.width, value, load(row)))
        first, last = load(s.rows[0]), load(s.rows[1] - 1)
        before, after = first, last
        if s.groups > 1:
            lane = iota(first.shape, 1)
            before = jnp.where(lane < s.width, first, turned(last, s.width))
            after = jnp.where(lane < (s.groups - 1) * s.width, turned(first, -s.width), last)
        store(s.begin, before)
        store(s.rows[1], after)


def fill_wide(segments, ref):
    def store(row, value):
        ref[row] = value

    fill_spare(segments, lambda row: ref[row], store)


def fill_flat(segments, ref):
    def store(row, value):
        ref[row : row + 1, :] = value

    fill_spare(segments, lambda row: ref[row : row + 1, :], store)


def linear(below, here, above):
    east = [pltpu.roll(here[3], 1, 0), here[0], here[1], here[2]]
    west = [here[1], here[2], here[3], pltpu.roll(here[0], 7, 0)]
    keep = (1.0 - 2.0 * HORIZ - 2.0 * VERTIC) / VERTIC
    return [
        (below[j] + above[j]) + ((HORIZ / VERTIC) * (east[j] + west[j]) + keep * here[j])
        for j in range(4)
    ]


def groups(ref, index):
    return [ref[index + (pl.ds(8 * j, 8),)] for j in range(4)]


def strided(ref, row):
    return [ref[row, pl.ds(j, 8, stride=4), :] for j in range(4)]


def sweep(segment, load, work):
    def block(i, carry):
        row = segment.begin + i * STEP
        held = [load(row), load(row + 1)]
        for k in range(STEP):
            held.append(load(row + k + 2))
            work(row + k + 1, held[k], held[k + 1], held[k + 2])
        return carry

    lax.fori_loop(0, segment.blocks, block, 0)


def folded_sums(sums_ref, columns):
    rows = sums_ref.shape[0] // 8
    total = sums_ref[pl.ds(0, rows, stride=8), :]
    for k in range(1, 8):
        total = total + sums_ref[pl.ds(k, rows, stride=8), :]
    return total * (1.0 / columns)


def slab(row):
    return pl.ds(pl.multiple_of(row * 8, 8), 8)


def spread_row(ref, row):
    return jnp.broadcast_to(ref[pl.ds(row, 1), :], (8, LANES))


def lane_places(segments):
    return [(s, g) for s in segments for g in range(s.groups)]


def prepare_kernel(
    state_ref,
    saturation_ref,
    moved_ref,
    means_ref,
    limits_ref,
    places_ref,
    state_buf,
    moved_buf,
    natural_ref,
    sums_ref,
    in_sems,
    out_sems,
    *,
    segments,
    capacity,
    padded,
):
    fields, levels, columns, slots = state_ref.shape
    order = list(range(fields))[::-1]
    loads = [pltpu.make_async_copy(state_ref.at[f], state_buf.at[f], in_sems.at[f]) for f in range(fields)]
    for f in order:
        loads[f].start()
    for t, (s, g) in enumerate(lane_places(segments)):
        lane = iota((places_ref.shape[0], LANES), 1) - g * s.width
        slot = s.lane0 + lane
        row = slot + (padded - capacity) * divided(jnp.maximum(slot, 0), capacity)
        inside = (lane >= 0) & (lane < s.width)
        hit = jnp.where(inside & (iota(lane.shape, 0) == row), 1.0, 0.0)
        places_ref[:, t * LANES : (t + 1) * LANES] = hit.astype(BF16)
    limits_ref[...] = jnp.zeros_like(limits_ref)
    for s in segments:

        def limit(k, carry):
            lane = iota((1, LANES), 1)
            value = jnp.full((1, LANES), saturation_ref[k])
            for g in range(1, s.groups):
                other = saturation_ref[jnp.minimum(k + g * s.steps, levels - 1)]
                value = jnp.where(lane >= g * s.width, other, value)
            limits_ref[pl.ds(s.begin + 1 + k, 1), :] = 0.5 * value
            return carry

        lax.fori_loop(0, s.steps, limit, 0)
    stores = []
    for f in order:
        scale = SHRINK if f == 0 else 1.0
        loads[f].wait()
        for s in segments:
            at = slice(s.lane0, s.lane0 + s.width)

            def widen(k, carry):
                parts = []
                for g in range(s.groups):
                    level = jnp.minimum(g * s.steps + k, levels - 1)
                    parts.append(state_buf[f, level, :, at].astype(F32))
                spare = LANES - s.groups * s.width
                if spare:
                    parts.append(jnp.zeros((columns, spare), F32))
                value = jnp.concatenate(parts, axis=1) if len(parts) > 1 else parts[0]
                natural_ref[s.begin + 1 + k] = scale * value if scale != 1.0 else value
                return carry

            lax.fori_loop(0, s.steps, widen, 0, unroll=2)
        fill_wide(segments, natural_ref)
        for s in segments:

            def work(row, below, here, above):
                out = linear(below, here, above)
                for j in range(4):
                    moved_buf[f, row, pl.ds(8 * j, 8), :] = out[j]
                sums_ref[slab(row), :] = (here[0] + here[1]) + (here[2] + here[3])

            sweep(s, lambda row: strided(natural_ref, row), work)
        means_ref[f] = folded_sums(sums_ref, columns) * (1.0 / scale)
        stores.append(pltpu.make_async_copy(moved_buf.at[f], moved_ref.at[f], out_sems.at[f]))
        stores[-1].start()
    for copy in stores:
        copy.wait()


def water_kernel(
    received_ref,
    places_ref,
    moved_ref,
    means_ref,
    limits_ref,
    unfold_ref,
    water_ref,
    spill_ref,
    offsets_ref,
    counts_ref,
    back_ref,
    moved_buf,
    even_ref,
    odd_ref,
    spill_buf,
    goal_ref,
    mean_ref,
    shift_ref,
    limit_ref,
    sums_ref,
    change_ref,
    in_sem,
    spill_sems,
    out_sem,
    *,
    segments,
    levels,
    stride,
):
    rows = means_ref.shape[1]
    columns = moved_buf.shape[1]
    load = pltpu.make_async_copy(moved_ref.at[1], moved_buf, in_sem)
    load.start()
    arrived = select(places_ref[...], received_ref[...], TN, swap=True)
    goal_ref[...] = jnp.zeros_like(goal_ref)
    counts_ref[...] = jnp.zeros_like(counts_ref)
    for s in segments:
        count = None
        for t, (owner, g) in enumerate(lane_places(segments)):
            if owner is not s:
                continue
            lanes = slice(t * LANES, (t + 1) * LANES)
            number = s.group_steps(g)
            for f in range(2):
                first = f * stride + g * s.steps
                at = slice(s.rows[0], s.rows[0] + number)
                goal_ref[f, at, :] = goal_ref[f, at, :] + arrived[first : first + number, lanes]
            part = arrived[stride - 1 : stride, lanes]
            count = part if count is None else count + part
        counts_ref[s.rows[0] : s.rows[1], :] = jnp.broadcast_to(count, (s.steps, LANES))
    for f in range(2):
        mean_ref[f] = means_ref[f]
    load.wait()
    spills = []
    source, target = None, even_ref
    for n in range(MAX_SUB):
        scale = 10.0 ** (n + 1)
        expected = []
        for f in range(2):
            fill_flat(segments, mean_ref.at[f])
            mean = mean_ref[f]
            mixed = mean + VERTIC * (
                pltpu.roll(mean, 1, 0) + pltpu.roll(mean, rows - 1, 0) - 2.0 * mean
            )
            offset = goal_ref[f] - RELAX * mixed
            expected.append(mixed + offset)
            if f == 1:
                shift_ref[...] = scale * offset
            else:
                offsets_ref[n] = (scale * SHRINK) * offset
        limit_ref[...] = scale * limits_ref[...]
        for s in segments:
            active = spread_row(counts_ref, s.rows[0]) > float(n)

            def finish(row, lin, old):
                shift = spread_row(shift_ref, row)
                limit = spread_row(limit_ref, row)
                total = None
                for j in range(4):
                    v = lin[j] + shift
                    c = jnp.maximum(0.5 * v - limit, 0.0)
                    u = v - c
                    if old is not None:
                        u = jnp.where(active, u, old[j])
                    spill_buf[n, row, pl.ds(8 * j, 8), :] = c
                    target[row, pl.ds(8 * j, 8), :] = u
                    total = c if total is None else total + c
                sums_ref[slab(row), :] = total

            if n == 0:

                def block(i, carry):
                    for k in range(STEP):
                        row = s.begin + 1 + i * STEP + k
                        finish(row, groups(moved_buf, (row,)), None)
                    return carry

                lax.fori_loop(0, s.blocks, block, 0)
            else:

                def work(row, below, here, above):
                    finish(row, linear(below, here, above), here)

                sweep(s, lambda row: groups(source, (row,)), work)
        spills.append(pltpu.make_async_copy(spill_buf.at[n], spill_ref.at[n], spill_sems.at[n]))
        spills[-1].start()
        spilled = folded_sums(sums_ref, columns) * (1.0 / scale)
        step = [expected[0] + LATENT * spilled, expected[1] - spilled]
        keep = counts_ref[...] > float(n)
        for f in range(2):
            mean_ref[f] = jnp.where(keep, step[f], mean_ref[f])
        if n + 1 < MAX_SUB:
            fill_wide(segments, target)
        source, target = target, (odd_ref if target is even_ref else even_ref)
    leave = pltpu.make_async_copy(source, water_ref, out_sem)
    leave.start()
    change_ref[...] = jnp.zeros_like(change_ref)
    for f in range(2):
        change = mean_ref[f] - means_ref[f]
        for t, (s, g) in enumerate(lane_places(segments)):
            first, number = f * stride + g * s.steps, s.group_steps(g)
            change_ref[first : first + number, t * LANES : (t + 1) * LANES] = change[
                s.rows[0] : s.rows[0] + number
            ]
    spread = select(places_ref[...], change_ref[...], NT)
    back_ref[...] = mm(spread, unfold_ref[...], NN)
    for copy in spills:
        copy.wait()
    leave.wait()


def energy_kernel(
    state_ref,
    moved_ref,
    water_ref,
    spill_ref,
    offsets_ref,
    counts_ref,
    out_ref,
    state_buf,
    moved_buf,
    water_buf,
    spill_buf,
    out_buf,
    even_ref,
    odd_ref,
    natural_ref,
    state_sems,
    moved_sem,
    water_sem,
    spill_sems,
    out_sems,
    *,
    segments,
):
    fields, levels, columns, _ = state_ref.shape
    waters = pltpu.make_async_copy(water_ref, water_buf, water_sem)
    states = [pltpu.make_async_copy(state_ref.at[f], state_buf.at[f], state_sems.at[f]) for f in range(fields)]
    moved = pltpu.make_async_copy(moved_ref.at[0], moved_buf, moved_sem)
    spills = [
        pltpu.make_async_copy(spill_ref.at[n], spill_buf.at[n], spill_sems.at[n])
        for n in range(MAX_SUB)
    ]
    waters.start()
    states[1].start()
    moved.start()
    for n in range(MAX_SUB):
        spills[n].start()
    states[0].start()
    leaves = [pltpu.make_async_copy(out_buf.at[f], out_ref.at[f], out_sems.at[f]) for f in range(fields)]

    def finish_field(f, source):
        for s in segments:
            count = spread_row(counts_ref, s.rows[0])
            back = jnp.zeros((8, LANES), F32)
            for n in range(1, MAX_SUB + 1):
                scale = 10.0**-n * (LATENT if f == 0 else 1.0)
                back = jnp.where(count == float(n), scale, back)

            def permute(row, carry):
                value = groups(source, (row,))
                for j in range(4):
                    natural_ref[row, pl.ds(j, 8, stride=4), :] = value[j] * back
                return carry

            lax.fori_loop(s.rows[0], s.rows[1], permute, 0, unroll=2)
            for g in range(s.groups):
                lanes = slice(g * s.width, (g + 1) * s.width)
                at = slice(s.lane0, s.lane0 + s.width)
                held = jnp.broadcast_to(count[0:1, lanes], (columns, s.width)) > 0.0

                def narrow(k, carry):
                    level = g * s.steps + k
                    old = state_buf[f, level, :, at].astype(F32)
                    value = jnp.where(held, natural_ref[s.begin + 1 + k, :, lanes], old)
                    out_buf[f, level, :, at] = value.astype(BF16)
                    return carry

                lax.fori_loop(0, s.group_steps(g), narrow, 0, unroll=2)
        leaves[f].start()

    waters.wait()
    states[1].wait()
    finish_field(1, water_buf)
    moved.wait()
    source, target = None, even_ref
    for n in range(MAX_SUB):
        spills[n].wait()
        for s in segments:
            active = spread_row(counts_ref, s.rows[0]) > float(n)

            def finish(row, lin, old):
                shift = spread_row(offsets_ref.at[n], row)
                c = groups(spill_buf, (n, row))
                for j in range(4):
                    u = (lin[j] + shift) + c[j]
                    if old is not None:
                        u = jnp.where(active, u, old[j])
                    target[row, pl.ds(8 * j, 8), :] = u

            if n == 0:

                def block(i, carry):
                    for k in range(STEP):
                        row = s.begin + 1 + i * STEP + k
                        finish(row, groups(moved_buf, (row,)), None)
                    return carry

                lax.fori_loop(0, s.blocks, block, 0)
            else:

                def work(row, below, here, above):
                    finish(row, linear(below, here, above), here)

                sweep(s, lambda row: groups(source, (row,)), work)
        if n + 1 < MAX_SUB:
            fill_wide(segments, target)
        source, target = target, (odd_ref if target is even_ref else even_ref)
    states[0].wait()
    finish_field(0, source)
    for f in range(fields):
        leaves[f].wait()


def final_kernel(
    base_ref, sides_ref, left_ref, right_ref, mixing_ref, slots_ref, gathered_ref, out_ref, *, levels
):
    rows, width = base_ref.shape
    sections, block, _ = gathered_ref.shape
    halo = jnp.concatenate([left_ref[...], right_ref[...]], axis=0)
    summed = base_ref[...] + mixing_ref[...] * select(sides_ref[...], halo, NN)
    place = slots_ref[:, :1].astype(I32)
    for s in range(1, sections):
        picks = jnp.where(iota((rows, block), 1) + (s - 1) * block == place, 1.0, 0.0)
        summed = summed + select(picks.astype(BF16), gathered_ref[s], NN)
    water = divided(iota((rows, width), 1), levels) == 1
    out_ref[...] = jnp.where(water, jnp.maximum(summed, 0.0), summed)


SPACES = dict(
    auto=pl.BlockSpec(memory_space=pltpu.VMEM),
    near=pl.BlockSpec(memory_space=pltpu.VMEM),
    far=pl.BlockSpec(memory_space=pl.ANY),
    scalar=pl.BlockSpec(memory_space=pltpu.SMEM),
)


def call(kernel, name, inputs, outputs, scratch=(), limit=8):
    arrays = [
        pltpu.with_memory_space_constraint(x, pltpu.VMEM) if space == "near" else x
        for space, x in inputs
    ]
    shapes = [
        (pltpu.VMEM if space == "near" else jax.ShapeDtypeStruct)(dims, dtype)
        for space, dims, dtype in outputs
    ]
    return pl.pallas_call(
        kernel,
        out_shape=shapes,
        in_specs=[SPACES[space] for space, _ in inputs],
        out_specs=[SPACES[space] for space, _, _ in outputs],
        scratch_shapes=list(scratch),
        compiler_params=pltpu.CompilerParams(vmem_limit_bytes=limit << 20),
        name=name,
    )(*arrays)


def body(
    column_state, mixing_rate, neighbours, assignment, substeps, cloud_state, level_map, saturation
):
    col_count = lax.axis_size("col")
    sec_count = lax.axis_size("sec")
    count, width = column_state.shape
    cloud_levels, levels = level_map.shape
    _, fields, _, columns, slots = cloud_state.shape
    elements = count // 4
    capacity = slots // col_count
    padded = -(-capacity // 8) * 8
    block = col_count * padded
    clouds = (sec_count - 1) * col_count
    segments, rows = segments_of(slots, cloud_levels)
    mapped = LANES * len(lane_places(segments))
    mixing = mixing_rate.reshape(1, width)
    state = cloud_state[0]
    dma = pltpu.SemaphoreType.DMA

    def wide(*lead):
        return pltpu.VMEM((*lead, rows, columns, LANES), F32)

    (means,) = call(
        means_kernel, "means", [("auto", column_state)], [("near", (elements, width), F32)]
    )
    ring = [(i, (i + 1) % col_count) for i in range(col_count)]
    left = lax.ppermute(means, "col", ring)
    right = lax.ppermute(means, "col", [(j, i) for i, j in ring])

    base, sides, wanted, constant, homes, fold, unfold = call(
        functools.partial(host_kernel, col_count=col_count, padded=padded, clouds=clouds),
        "host",
        [
            ("auto", column_state),
            ("near", means),
            ("auto", mixing),
            ("auto", neighbours.T),
            ("auto", assignment.reshape(1, count)),
            ("auto", substeps.reshape(1, count)),
            ("auto", level_map),
        ],
        [
            ("near", (count, width), F32),
            ("near", (count, 2 * elements), BF16),
            ("near", (block, 2 * elements), BF16),
            ("near", (block, width), F32),
            ("near", (count, LANES), F32),
            ("near", (width, width), F32),
            ("near", (width, width), F32),
        ],
    )
    (outgoing,) = call(
        pack_kernel,
        "pack",
        [
            ("near", wanted),
            ("near", left),
            ("near", right),
            ("auto", mixing),
            ("near", constant),
            ("near", fold),
        ],
        [("auto", (block, width), F32)],
    )
    received = lax.all_to_all(outgoing, "col", split_axis=0, concat_axis=0, tiled=True)
    moved, cloud_means, limits, places = call(
        functools.partial(
            prepare_kernel, segments=segments, capacity=capacity, padded=padded
        ),
        "prepare",
        [("far", state), ("scalar", saturation)],
        [
            ("far", (fields, rows, columns, LANES), F32),
            ("near", (fields, rows, LANES), F32),
            ("near", (rows, LANES), F32),
            ("near", (block, mapped), BF16),
        ],
        scratch=[
            pltpu.VMEM(state.shape, BF16),
            wide(fields),
            wide(),
            pltpu.VMEM((rows * 8, LANES), F32),
            dma((fields,)),
            dma((fields,)),
        ],
        limit=16,
    )
    water, spill, offsets, counts, back = call(
        functools.partial(water_kernel, segments=segments, levels=cloud_levels, stride=levels),
        "water",
        [
            ("near", received),
            ("near", places),
            ("far", moved),
            ("near", cloud_means),
            ("near", limits),
            ("near", unfold),
        ],
        [
            ("far", (rows, columns, LANES), F32),
            ("far", (MAX_SUB, rows, columns, LANES), F32),
            ("near", (MAX_SUB, rows, LANES), F32),
            ("near", (rows, LANES), F32),
            ("auto", (block, width), F32),
        ],
        scratch=[
            wide(),
            wide(),
            wide(),
            wide(MAX_SUB),
            pltpu.VMEM((fields, rows, LANES), F32),
            pltpu.VMEM((fields, rows, LANES), F32),
            pltpu.VMEM((rows, LANES), F32),
            pltpu.VMEM((rows, LANES), F32),
            pltpu.VMEM((rows * 8, LANES), F32),
            pltpu.VMEM((width, mapped), F32),
            dma(()),
            dma((MAX_SUB,)),
            dma(()),
        ],
        limit=24,
    )
    returned = lax.all_to_all(back, "col", split_axis=0, concat_axis=0, tiled=True)
    (new_block,) = call(
        functools.partial(energy_kernel, segments=segments),
        "energy",
        [
            ("far", state),
            ("far", moved),
            ("far", water),
            ("far", spill),
            ("near", offsets),
            ("near", counts),
        ],
        [("far", state.shape, BF16)],
        scratch=[
            pltpu.VMEM(state.shape, BF16),
            wide(),
            wide(),
            wide(MAX_SUB),
            pltpu.VMEM(state.shape, BF16),
            wide(),
            wide(),
            wide(),
            dma((fields,)),
            dma(()),
            dma(()),
            dma((MAX_SUB,)),
            dma((fields,)),
        ],
        limit=32,
    )
    gathered = lax.all_gather(returned, "sec", axis=0, tiled=False)
    (new_columns,) = call(
        functools.partial(final_kernel, levels=levels),
        "final",
        [
            ("near", base),
            ("near", sides),
            ("near", left),
            ("near", right),
            ("auto", mixing),
            ("near", homes),
            ("near", gathered),
        ],
        [("auto", (count, width), F32)],
    )
    return new_columns, new_block[None]


def solution(mesh):
    in_specs = (
        P("col", None),
        P(),
        P("col", None),
        P("col", None),
        P("col"),
        P("sec", None, None, None, "col"),
        P(),
        P(),
    )
    out_specs = (P("col", None), P("sec", None, None, None, "col"))
    return jax.shard_map(body, mesh=mesh, in_specs=in_specs, out_specs=out_specs, check_vma=False)
```

```python
import functools

import jax
import jax.numpy as jnp
from jax import lax
from jax.experimental import pallas as pl
from jax.experimental.pallas import tpu as pltpu
from jax.sharding import PartitionSpec as P

MAX_SUB = 4
RELAX = 0.25
HORIZ = 0.12
VERTIC = 0.1
LATENT = 2.5
VMIX = 0.2
HIGH = lax.Precision.HIGHEST
LANES = 128
F32 = jnp.float32
BF16 = jnp.bfloat16
STEP = 10
SHRINK = 1.0 / LATENT
I32 = jnp.int32


def iota(shape, dim):
    return lax.broadcasted_iota(I32, shape, dim)


def mm(a, b, contract, precision=HIGH):
    return lax.dot_general(
        a, b, (contract, ((), ())), precision=precision, preferred_element_type=F32
    )


NN = ((1,), (0,))
NT = ((1,), (1,))
TN = ((0,), (0,))


def divided(value, by):
    return jnp.floor((value.astype(F32) + 0.5) * (1.0 / by)).astype(I32)


def split(values):
    high = values.astype(BF16)
    rest = values - high.astype(F32)
    middle = rest.astype(BF16)
    low = (rest - middle.astype(F32)).astype(BF16)
    return low, middle, high


def select(picks, values, contract, swap=False):
    total = None
    for part in split(values):
        a, b = (part, picks) if swap else (picks, part)
        term = lax.dot_general(a, b, (contract, ((), ())), preferred_element_type=F32)
        total = term if total is None else total + term
    return total


def vertical_mix(values, levels):
    upper = jnp.concatenate([values[1:levels], values[levels - 1 : levels]], axis=0)
    lower = jnp.concatenate([values[0:1], values[0 : levels - 1]], axis=0)
    inner = values[0:levels]
    return inner + VERTIC * (upper + lower - 2.0 * inner)


def means_kernel(columns_ref, means_ref):
    elements = means_ref.shape[0]
    total = columns_ref[pl.ds(0, elements, stride=4), :]
    for k in range(1, 4):
        total = total + columns_ref[pl.ds(k, elements, stride=4), :]
    means_ref[...] = 0.25 * total


def host_kernel(
    columns_ref,
    means_ref,
    mixing_ref,
    neighbours_ref,
    targets_ref,
    substeps_ref,
    map_ref,
    base_ref,
    sides_ref,
    wanted_ref,
    constant_ref,
    slots_ref,
    fold_ref,
    unfold_ref,
    *,
    col_count,
    padded,
    clouds,
):
    section = lax.axis_index("sec")
    position = lax.axis_index("col")
    rows, width = columns_ref.shape
    levels = map_ref.shape[1]
    cloud_levels = map_ref.shape[0]
    elements = rows // 4
    block = col_count * padded
    near = neighbours_ref[...] - (position - 1) * elements
    near = jnp.where(near < 0, near + elements * col_count, near)
    near = jnp.where(near >= elements * col_count, near - elements * col_count, near)
    window = iota((3 * elements, elements), 0)
    picks = jnp.where(window == iota((3 * elements, elements), 1) + elements, -4.0, 0.0)
    for k in range(near.shape[0]):
        picks = picks + jnp.where(window == near[k : k + 1, :], 1.0, 0.0)
    row_element = divided(iota((rows, elements), 0), 4)
    spread_rows = jnp.where(row_element == iota((rows, elements), 1), 1.0, 0.0)
    weights = mm(spread_rows.astype(BF16), picks.astype(BF16), NT, None)
    sides = jnp.concatenate([weights[:, :elements], weights[:, 2 * elements :]], axis=1)
    sides = sides.astype(BF16)
    sides_ref[...] = sides
    own = select(weights[:, elements : 2 * elements].astype(BF16), means_ref[...], NN)
    values = columns_ref[...]
    lane = iota((rows, width), 1)
    level = lane - levels * divided(lane, levels)
    upper = jnp.where(level == levels - 1, values, pltpu.roll(values, width - 1, 1))
    lower = jnp.where(level == 0, values, pltpu.roll(values, 1, 1))
    base = values + mixing_ref[...] * own + VMIX * (upper + lower - 2.0 * values)
    base_ref[...] = base
    targets = targets_ref[...]
    onehot = jnp.where(iota((clouds, rows), 0) == targets, 1.0, 0.0)
    before = jnp.where(iota((rows, rows), 0) < iota((rows, rows), 1), 1.0, 0.0)
    running = mm(onehot.astype(BF16), before.astype(BF16), NN, None)
    ranks = jnp.sum(running * onehot, axis=0, keepdims=True).astype(I32)
    owner = divided(targets, col_count)
    slot = (targets - owner * col_count) * padded + ranks
    mine = jnp.where(owner + 1 == section, slot, -1)
    pack = jnp.where(iota((block, rows), 0) == mine, 1.0, 0.0).astype(BF16)
    wanted_ref[...] = mm(pack, sides, NN, None).astype(BF16)
    plain = map_ref[...]
    folded = RELAX * vertical_mix(plain, cloud_levels)
    for ref, value in ((fold_ref, folded), (unfold_ref, plain)):
        ref[...] = jnp.zeros_like(ref)
        for f in range(width // levels):
            ref[f * levels : f * levels + cloud_levels, f * levels : (f + 1) * levels] = value
    count_rows = jnp.where(
        iota((width, rows), 0) == levels - 1, substeps_ref[...].astype(F32), 0.0
    )
    counts = mm(pack, count_rows.astype(BF16), NT, None)
    constant_ref[...] = mm(select(pack, base, NN), fold_ref[...], NT) + counts
    fold_ref[...] = fold_ref[...] * mixing_ref[...]
    everywhere = jnp.broadcast_to((owner * block + slot).astype(F32), (LANES, rows))
    identity = jnp.where(iota((rows, rows), 0) == iota((rows, rows), 1), 1.0, 0.0)
    slots_ref[...] = select(identity.astype(BF16), everywhere, NT)


def pack_kernel(wanted_ref, left_ref, right_ref, constant_ref, fold_ref, out_ref):
    halo = jnp.concatenate([left_ref[...], right_ref[...]], axis=0)
    spread = select(wanted_ref[...], halo, NN)
    out_ref[...] = constant_ref[...] + mm(spread, fold_ref[...], NT)


class Segment:
    def __init__(self, lane0, width, levels, begin):
        self.lane0, self.width, self.begin, self.levels = lane0, width, begin, levels
        self.steps = -(-levels // (LANES // width))
        self.groups = -(-levels // self.steps)
        self.missing = self.groups * self.steps - levels
        self.blocks = -(-self.steps // STEP)
        self.rows = (begin + 1, begin + 1 + self.steps)

    def group_steps(self, g):
        return self.steps - (self.missing if g == self.groups - 1 else 0)


def segments_of(slots, levels):
    segments, begin = [], 0
    for lane0 in range(0, slots, LANES):
        segments.append(Segment(lane0, min(LANES, slots - lane0), levels, begin))
        begin += segments[-1].steps + 2
    rows = max([begin] + [s.begin + 2 + s.blocks * STEP for s in segments])
    return segments, rows, -(-rows // 8) * 8


def fill_spare(segments, load, store):
    def turned(value, shift):
        tall = jnp.broadcast_to(value, (8, LANES)) if value.shape[0] == 1 else value
        return pltpu.roll(tall, shift % LANES, 1)[: value.shape[0]]

    for s in segments:
        if s.missing:
            row = s.rows[1] - s.missing
            value = load(row - 1)
            lane = iota(value.shape, 1)
            store(row, jnp.where(lane >= (s.groups - 1) * s.width, value, load(row)))
        first, last = load(s.rows[0]), load(s.rows[1] - 1)
        before, after = first, last
        if s.groups > 1:
            lane = iota(first.shape, 1)
            before = jnp.where(lane < s.width, first, turned(last, s.width))
            after = jnp.where(lane < (s.groups - 1) * s.width, turned(first, -s.width), last)
        store(s.begin, before)
        store(s.rows[1], after)


def fill_wide(segments, ref):
    def store(row, value):
        ref[row] = value

    fill_spare(segments, lambda row: ref[row], store)


def fill_flat(segments, ref):
    def store(row, value):
        ref[row : row + 1, :] = value

    fill_spare(segments, lambda row: ref[row : row + 1, :], store)


def linear(below, here, above):
    east = [pltpu.roll(here[3], 1, 0), here[0], here[1], here[2]]
    west = [here[1], here[2], here[3], pltpu.roll(here[0], 7, 0)]
    keep = (1.0 - 2.0 * HORIZ - 2.0 * VERTIC) / VERTIC
    return [
        (below[j] + above[j]) + ((HORIZ / VERTIC) * (east[j] + west[j]) + keep * here[j])
        for j in range(4)
    ]


def groups(ref, index):
    return [ref[index + (pl.ds(8 * j, 8),)] for j in range(4)]


def strided(ref, row):
    return [ref[row, pl.ds(j, 8, stride=4), :] for j in range(4)]


def sweep(segment, load, work):
    def block(i, carry):
        row = segment.begin + i * STEP
        held = [load(row), load(row + 1)]
        for k in range(STEP):
            held.append(load(row + k + 2))
            work(row + k + 1, held[k], held[k + 1], held[k + 2])
        return carry

    lax.fori_loop(0, segment.blocks, block, 0)


def each(count, size, work):
    size = min(size, count)

    def run(first):
        for k in range(size):
            work(first + k)

    if count // size:
        lax.fori_loop(0, count // size, lambda i, c: (run(i * size), c)[1], 0)
    if count % size:
        run(count - size)


def widen(state_ref, natural_ref, segments, scale):
    levels, columns, _ = state_ref.shape
    for s in segments:
        at = slice(s.lane0, s.lane0 + s.width)

        def one(k):
            parts = []
            for g in range(s.groups):
                level = jnp.minimum(g * s.steps + k, levels - 1)
                parts.append(state_ref[level, :, at].astype(F32))
            spare = LANES - s.groups * s.width
            if spare:
                parts.append(jnp.zeros((columns, spare), F32))
            value = jnp.concatenate(parts, axis=1) if len(parts) > 1 else parts[0]
            natural_ref[s.begin + 1 + k] = scale * value if scale != 1.0 else value

        each(s.steps, STEP, one)


def folded_sums(sums_ref, columns):
    rows = sums_ref.shape[0] // 8
    total = sums_ref[pl.ds(0, rows, stride=8), :]
    for k in range(1, 8):
        total = total + sums_ref[pl.ds(k, rows, stride=8), :]
    return total * (1.0 / columns)


def slab(row):
    return pl.ds(pl.multiple_of(row * 8, 8), 8)


def spread_row(ref, row):
    return jnp.broadcast_to(ref[pl.ds(row, 1), :], (8, LANES))


def lane_places(segments):
    return [(s, g) for s in segments for g in range(s.groups)]


def slot_map(segments, block, capacity, padded):
    tiles = []
    for s, g in lane_places(segments):
        lane = iota((8, LANES), 1) - g * s.width
        slot = s.lane0 + lane
        row = slot + (padded - capacity) * divided(jnp.maximum(slot, 0), capacity)
        row = jnp.where((lane >= 0) & (lane < s.width), row, -1)[0:1]
        tiles.append(jnp.where(iota((block, LANES), 0) == row, 1.0, 0.0).astype(BF16))
    return jnp.concatenate(tiles, axis=1)


def prepare_kernel(
    state_ref,
    saturation_ref,
    moved_ref,
    means_ref,
    limits_ref,
    state_buf,
    natural_ref,
    sums_ref,
    flat_ref,
    sems,
    *,
    segments,
):
    fields, levels, columns, _ = state_ref.shape
    loads = [
        pltpu.make_async_copy(state_ref.at[f], state_buf.at[f], sems.at[f]) for f in range(fields)
    ]
    loads[1].start()
    loads[0].start()
    tall = flat_ref.shape[0]
    here = iota((tall, levels), 0) == iota((tall, levels), 1)
    diagonal = jnp.where(here, 0.5 * saturation_ref[...], 0.0)
    flat_ref[...] = select(jnp.ones((levels, LANES), BF16), diagonal, NN, swap=True)
    limits_ref[...] = jnp.zeros_like(limits_ref)
    for s in segments:
        lane = iota((s.steps, LANES), 1)
        value = flat_ref[0 : s.steps, :]
        for g in range(1, s.groups):
            other = flat_ref[g * s.steps : (g + 1) * s.steps, :]
            value = jnp.where(lane >= g * s.width, other, value)
        limits_ref[s.rows[0] : s.rows[1], :] = value
    sums_ref[...] = jnp.zeros_like(sums_ref)
    loads[1].wait()
    widen(state_buf.at[1], natural_ref, segments, 1.0)
    fill_wide(segments, natural_ref)
    for s in segments:

        def work(row, below, here, above):
            out = linear(below, here, above)
            for j in range(4):
                moved_ref[row, pl.ds(8 * j, 8), :] = out[j]
            sums_ref[slab(row), :] = (here[0] + here[1]) + (here[2] + here[3])

        sweep(s, lambda row: strided(natural_ref, row), work)
    means_ref[1] = folded_sums(sums_ref, columns)
    loads[0].wait()
    widen(state_buf.at[0], natural_ref, segments, 1.0)
    for s in segments:

        def total(k):
            value = groups(natural_ref, (s.begin + 1 + k,))
            sums_ref[slab(s.begin + 1 + k), :] = (value[0] + value[1]) + (value[2] + value[3])

        each(s.steps, STEP, total)
    means_ref[0] = folded_sums(sums_ref, columns)


def water_kernel(
    received_ref,
    moved_ref,
    means_ref,
    limits_ref,
    unfold_far,
    water_far,
    spill_far,
    flats_far,
    back_far,
    unfold_ref,
    even_ref,
    odd_ref,
    spill_buf,
    flats_ref,
    goal_ref,
    mean_ref,
    shift_ref,
    limit_ref,
    sums_ref,
    change_ref,
    back_ref,
    in_sem,
    spill_sems,
    water_sem,
    flat_sem,
    back_sems,
    *,
    segments,
    capacity,
    padded,
    stride,
):
    rows = means_ref.shape[1]
    columns = even_ref.shape[1]
    load = pltpu.make_async_copy(unfold_far, unfold_ref, in_sem)
    load.start()
    places = slot_map(segments, received_ref.shape[0], capacity, padded)
    arrived = select(places, received_ref[...], TN, swap=True)
    goal_ref[...] = jnp.zeros_like(goal_ref)
    flats_ref[...] = jnp.zeros_like(flats_ref)
    sums_ref[...] = jnp.zeros_like(sums_ref)
    counts = flats_ref.at[MAX_SUB + 2]
    for s in segments:
        count = None
        for t, (owner, g) in enumerate(lane_places(segments)):
            if owner is not s:
                continue
            lanes = slice(t * LANES, (t + 1) * LANES)
            number = s.group_steps(g)
            for f in range(2):
                first = f * stride + g * s.steps
                at = slice(s.rows[0], s.rows[0] + number)
                goal_ref[f, at, :] = goal_ref[f, at, :] + arrived[first : first + number, lanes]
            part = arrived[stride - 1 : stride, lanes]
            count = part if count is None else count + part
        counts[s.rows[0] : s.rows[1], :] = jnp.broadcast_to(count, (s.steps, LANES))
    for f in range(2):
        mean_ref[f] = means_ref[f]
    copies = []
    source, target = None, even_ref
    for n in range(MAX_SUB):
        scale = 10.0 ** (n + 1)
        last = n + 1 == MAX_SUB
        expected = []
        for f in range(2):
            fill_flat(segments, mean_ref.at[f])
            mean = mean_ref[f]
            mixed = mean + VERTIC * (
                pltpu.roll(mean, 1, 0) + pltpu.roll(mean, rows - 1, 0) - 2.0 * mean
            )
            offset = goal_ref[f] - RELAX * mixed
            expected.append(mixed + offset)
            if f == 1:
                shift_ref[...] = scale * offset
            else:
                flats_ref[n] = (scale * SHRINK) * offset
        limit_ref[...] = scale * limits_ref[...]
        if last:
            flats_ref[MAX_SUB] = shift_ref[...]
            flats_ref[MAX_SUB + 1] = limit_ref[...]
            copies.append(pltpu.make_async_copy(flats_ref, flats_far, flat_sem))
            copies[-1].start()
        for s in segments:
            active = spread_row(counts, s.rows[0]) > float(n)

            def finish(row, lin, old):
                shift = spread_row(shift_ref, row)
                limit = spread_row(limit_ref, row)
                total = None
                for j in range(4):
                    v = lin[j] + shift
                    c = jnp.maximum(0.5 * v - limit, 0.0)
                    total = c if total is None else total + c
                    if last:
                        continue
                    u = v - c
                    if old is not None:
                        u = jnp.where(active, u, old[j])
                    spill_buf[n, row, pl.ds(8 * j, 8), :] = c
                    target[row, pl.ds(8 * j, 8), :] = u
                sums_ref[slab(row), :] = total

            if n == 0:

                def block(i, carry):
                    for k in range(STEP):
                        row = s.begin + 1 + i * STEP + k
                        finish(row, groups(moved_ref, (row,)), None)
                    return carry

                lax.fori_loop(0, s.blocks, block, 0)
            else:

                def work(row, below, here, above):
                    finish(row, linear(below, here, above), here)

                sweep(s, lambda row: groups(source, (row,)), work)
        if not last:
            copies.append(
                pltpu.make_async_copy(spill_buf.at[n], spill_far.at[n], spill_sems.at[n])
            )
            copies[-1].start()
            fill_wide(segments, target)
            source, target = target, (odd_ref if target is even_ref else even_ref)
        if n + 2 == MAX_SUB:
            copies.append(pltpu.make_async_copy(source, water_far, water_sem))
            copies[-1].start()
        spilled = folded_sums(sums_ref, columns) * (1.0 / scale)
        step = [expected[0] + LATENT * spilled, expected[1] - spilled]
        keep = counts[...] > float(n)
        for f in range(2):
            mean_ref[f] = jnp.where(keep, step[f], mean_ref[f])
    change_ref[...] = jnp.zeros_like(change_ref)
    for f in range(2):
        change = mean_ref[f] - means_ref[f]
        for t, (s, g) in enumerate(lane_places(segments)):
            first, number = f * stride + g * s.steps, s.group_steps(g)
            change_ref[first : first + number, t * LANES : (t + 1) * LANES] = change[
                s.rows[0] : s.rows[0] + number
            ]
    spread = select(places, change_ref[...], NT)
    load.wait()
    back = mm(spread, unfold_ref[...], NN)
    for j in range(back_ref.shape[0]):
        back_ref[j] = back[j * padded : j * padded + capacity]
    for i in range(back_far.shape[0]):
        copies.append(pltpu.make_async_copy(back_ref, back_far.at[i], back_sems.at[i]))
        copies[-1].start()
    for copy in copies:
        copy.wait()


def energy_kernel(
    state_ref,
    water_far,
    spill_far,
    flats_far,
    base_ref,
    sides_ref,
    left_ref,
    right_ref,
    mixing_ref,
    homes_ref,
    out_ref,
    advanced_ref,
    places_ref,
    state_buf,
    water_buf,
    spill_buf,
    flats_ref,
    out_buf,
    even_ref,
    odd_ref,
    last_ref,
    natural_ref,
    state_sems,
    water_sem,
    spill_sems,
    flat_sem,
    out_sems,
    *,
    segments,
):
    fields, levels, columns, _ = state_ref.shape
    states = [
        pltpu.make_async_copy(state_ref.at[f], state_buf.at[f], state_sems.at[f])
        for f in range(fields)
    ]
    flats = pltpu.make_async_copy(flats_far, flats_ref, flat_sem)
    waters = pltpu.make_async_copy(water_far, water_buf, water_sem)
    spills = [
        pltpu.make_async_copy(spill_far.at[n], spill_buf.at[n], spill_sems.at[n])
        for n in range(MAX_SUB - 1)
    ]
    leaves = [
        pltpu.make_async_copy(out_buf.at[f], out_ref.at[f], out_sems.at[f]) for f in range(fields)
    ]
    states[0].start()
    flats.start()
    for copy in spills:
        copy.start()
    waters.start()
    states[1].start()
    halo = jnp.concatenate([left_ref[...], right_ref[...]], axis=0)
    advanced_ref[...] = base_ref[...] + mixing_ref[...] * select(sides_ref[...], halo, NN)
    places_ref[...] = homes_ref[...]
    states[0].wait()
    widen(state_buf.at[0], natural_ref, segments, SHRINK)
    fill_wide(segments, natural_ref)
    flats.wait()
    counts = flats_ref.at[MAX_SUB + 2]
    source, target = natural_ref, even_ref
    for n in range(MAX_SUB):
        last = n + 1 == MAX_SUB
        (waters if last else spills[n]).wait()
        for s in segments:
            active = spread_row(counts, s.rows[0]) > float(n)

            def load(row):
                here = strided(source, row) if n == 0 else groups(source, (row,))
                return (here, groups(water_buf, (row,))) if last else (here, None)

            def work(row, below, here, above):
                shift = spread_row(flats_ref.at[n], row)
                lin = linear(below[0], here[0], above[0])
                if last:
                    water = linear(below[1], here[1], above[1])
                    push = spread_row(flats_ref.at[MAX_SUB], row)
                    limit = spread_row(flats_ref.at[MAX_SUB + 1], row)
                else:
                    spill = groups(spill_buf, (n, row))
                for j in range(4):
                    if last:
                        v = water[j] + push
                        c = jnp.maximum(0.5 * v - limit, 0.0)
                        last_ref[row, pl.ds(8 * j, 8), :] = jnp.where(active, v - c, here[1][j])
                    else:
                        c = spill[j]
                    u = (lin[j] + shift) + c
                    if n:
                        u = jnp.where(active, u, here[0][j])
                    target[row, pl.ds(8 * j, 8), :] = u

            sweep(s, load, work)
        if not last:
            fill_wide(segments, target)
        source, target = target, (odd_ref if target is even_ref else even_ref)
    for f in (1, 0):
        states[1].wait() if f == 1 else None
        found = last_ref if f == 1 else source
        for s in segments:
            count = spread_row(counts, s.rows[0])
            back = jnp.zeros((8, LANES), F32)
            for n in range(1, MAX_SUB + 1):
                scale = 10.0**-n * (LATENT if f == 0 else 1.0)
                back = jnp.where(count == float(n), scale, back)

            def permute(k):
                row = s.begin + 1 + k
                value = groups(found, (row,))
                for j in range(4):
                    natural_ref[row, pl.ds(j, 8, stride=4), :] = value[j] * back

            each(s.steps, STEP, permute)
            at = slice(s.lane0, s.lane0 + s.width)
            held = jnp.broadcast_to(count[0:1, : s.width], (columns, s.width)) > 0.0
            for g in range(s.groups):
                lanes = slice(g * s.width, (g + 1) * s.width)

                def narrow(k):
                    level = g * s.steps + k
                    old = state_buf[f, level, :, at].astype(F32)
                    value = jnp.where(held, natural_ref[s.begin + 1 + k, :, lanes], old)
                    out_buf[f, level, :, at] = value.astype(BF16)

                each(s.group_steps(g), STEP, narrow)
        leaves[f].start()
    for f in range(fields):
        leaves[f].wait()


def final_kernel(advanced_ref, places_ref, gathered_ref, out_ref, table_ref, *, levels, idle, padded):
    rows, width = advanced_ref.shape
    sources, capacity, _ = gathered_ref.shape
    if capacity != padded:
        table_ref[...] = jnp.zeros_like(table_ref)
    for j in range(idle, sources):
        first = (j - idle) * padded
        table_ref[first : first + capacity, :] = gathered_ref[j]
    place = places_ref[:, :1].astype(I32)
    picks = jnp.where(iota((rows, table_ref.shape[0]), 1) == place, 1.0, 0.0)
    summed = advanced_ref[...] + select(picks.astype(BF16), table_ref[...], NN)
    water = divided(iota((rows, width), 1), levels) == 1
    out_ref[...] = jnp.where(water, jnp.maximum(summed, 0.0), summed)


SPACES = dict(
    auto=pl.BlockSpec(memory_space=pltpu.VMEM),
    near=pl.BlockSpec(memory_space=pltpu.VMEM),
    far=pl.BlockSpec(memory_space=pl.ANY),
    scalar=pl.BlockSpec(memory_space=pltpu.SMEM),
)


def call(kernel, name, inputs, outputs, scratch=(), limit=8):
    kept = dict(near=pltpu.VMEM, auto=pltpu.HBM, far=pltpu.HBM, scalar=pltpu.HBM)
    arrays = [pltpu.with_memory_space_constraint(x, kept[space]) for space, x in inputs]
    shapes = [kept[space](dims, dtype) for space, dims, dtype in outputs]
    return pl.pallas_call(
        kernel,
        out_shape=shapes,
        in_specs=[SPACES[space] for space, _ in inputs],
        out_specs=[SPACES[space] for space, _, _ in outputs],
        scratch_shapes=list(scratch),
        compiler_params=pltpu.CompilerParams(vmem_limit_bytes=limit << 20),
        name=name,
    )(*arrays)


def body(
    column_state, mixing_rate, neighbours, assignment, substeps, cloud_state, level_map, saturation
):
    col_count = lax.axis_size("col")
    sec_count = lax.axis_size("sec")
    count, width = column_state.shape
    cloud_levels, levels = level_map.shape
    _, fields, _, columns, slots = cloud_state.shape
    elements = count // 4
    capacity = slots // col_count
    padded = -(-capacity // 8) * 8
    block = col_count * padded
    clouds = (sec_count - 1) * col_count
    segments, used, rows = segments_of(slots, cloud_levels)
    mapped = LANES * len(lane_places(segments))
    mixing = mixing_rate.reshape(1, width)
    state = cloud_state[0]
    dma = pltpu.SemaphoreType.DMA

    def wide(*lead):
        return pltpu.VMEM((*lead, rows, columns, LANES), F32)

    (means,) = call(
        means_kernel, "means", [("auto", column_state)], [("near", (elements, width), F32)]
    )
    ring = [(i, (i + 1) % col_count) for i in range(col_count)]
    left = lax.ppermute(means, "col", ring)
    right = lax.ppermute(means, "col", [(j, i) for i, j in ring])

    base, sides, wanted, constant, homes, fold, unfold = call(
        functools.partial(host_kernel, col_count=col_count, padded=padded, clouds=clouds),
        "host",
        [
            ("auto", column_state),
            ("near", means),
            ("auto", mixing),
            ("auto", neighbours.T),
            ("auto", assignment.reshape(1, count)),
            ("auto", substeps.reshape(1, count)),
            ("auto", level_map),
        ],
        [
            ("auto", (count, width), F32),
            ("auto", (count, 2 * elements), BF16),
            ("near", (block, 2 * elements), BF16),
            ("near", (block, width), F32),
            ("auto", (count, LANES), F32),
            ("near", (width, width), F32),
            ("auto", (width, width), F32),
        ],
    )
    (outgoing,) = call(
        pack_kernel,
        "pack",
        [
            ("near", wanted),
            ("near", left),
            ("near", right),
            ("near", constant),
            ("near", fold),
        ],
        [("auto", (block, width), F32)],
    )
    received = lax.all_to_all(outgoing, "col", split_axis=0, concat_axis=0, tiled=True)
    moved, cloud_means, limits = call(
        functools.partial(prepare_kernel, segments=segments),
        "prepare",
        [("far", state), ("auto", saturation.reshape(1, cloud_levels))],
        [
            ("near", (used, columns, LANES), F32),
            ("near", (fields, rows, LANES), F32),
            ("near", (rows, LANES), F32),
        ],
        scratch=[
            pltpu.VMEM(state.shape, BF16),
            wide(),
            pltpu.VMEM((rows * 8, LANES), F32),
            pltpu.VMEM((max(s.groups * s.steps for s in segments), LANES), F32),
            dma((fields,)),
        ],
        limit=16,
    )
    water, spill, flats, back = call(
        functools.partial(
            water_kernel, segments=segments, capacity=capacity, padded=padded, stride=levels
        ),
        "water",
        [
            ("near", received),
            ("near", moved),
            ("near", cloud_means),
            ("near", limits),
            ("far", unfold),
        ],
        [
            ("far", (rows, columns, LANES), F32),
            ("far", (MAX_SUB - 1, rows, columns, LANES), F32),
            ("far", (MAX_SUB + 3, rows, LANES), F32),
            ("far", (sec_count, col_count, capacity, width), F32),
        ],
        scratch=[
            pltpu.VMEM((width, width), F32),
            wide(),
            wide(),
            wide(MAX_SUB - 1),
            pltpu.VMEM((MAX_SUB + 3, rows, LANES), F32),
            pltpu.VMEM((fields, rows, LANES), F32),
            pltpu.VMEM((fields, rows, LANES), F32),
            pltpu.VMEM((rows, LANES), F32),
            pltpu.VMEM((rows, LANES), F32),
            pltpu.VMEM((rows * 8, LANES), F32),
            pltpu.VMEM((width, mapped), F32),
            pltpu.VMEM((col_count, capacity, width), F32),
            dma(()),
            dma((MAX_SUB - 1,)),
            dma(()),
            dma(()),
            dma((sec_count,)),
        ],
        limit=24,
    )
    returned = lax.all_to_all(
        back.reshape(sec_count * col_count, capacity, width),
        ("sec", "col"),
        split_axis=0,
        concat_axis=0,
        tiled=True,
    )
    new_block, advanced, places = call(
        functools.partial(energy_kernel, segments=segments),
        "energy",
        [
            ("far", state),
            ("far", water),
            ("far", spill),
            ("far", flats),
            ("auto", base),
            ("auto", sides),
            ("near", left),
            ("near", right),
            ("auto", mixing),
            ("auto", homes),
        ],
        [
            ("far", state.shape, BF16),
            ("near", (count, width), F32),
            ("near", (count, LANES), F32),
        ],
        scratch=[
            pltpu.VMEM(state.shape, BF16),
            wide(),
            wide(MAX_SUB - 1),
            pltpu.VMEM((MAX_SUB + 3, rows, LANES), F32),
            pltpu.VMEM(state.shape, BF16),
            wide(),
            wide(),
            wide(),
            wide(),
            dma((fields,)),
            dma(()),
            dma((MAX_SUB - 1,)),
            dma(()),
            dma((fields,)),
        ],
        limit=32,
    )
    (new_columns,) = call(
        functools.partial(final_kernel, levels=levels, idle=col_count, padded=padded),
        "final",
        [("near", advanced), ("near", places), ("near", returned)],
        [("auto", (count, width), F32)],
        scratch=[pltpu.VMEM((clouds * padded, width), F32)],
    )
    return new_columns, new_block[None]


def solution(mesh):
    in_specs = (
        P("col", None),
        P(),
        P("col", None),
        P("col", None),
        P("col"),
        P("sec", None, None, None, "col"),
        P(),
        P(),
    )
    out_specs = (P("col", None), P("sec", None, None, None, "col"))
    return jax.shard_map(body, mesh=mesh, in_specs=in_specs, out_specs=out_specs, check_vma=False)
```

```python
import functools

import jax
import jax.numpy as jnp
from jax import lax
from jax.experimental import pallas as pl
from jax.experimental.pallas import tpu as pltpu
from jax.sharding import PartitionSpec as P

MAX_SUB = 4
RELAX = 0.25
HORIZ = 0.12
VERTIC = 0.1
LATENT = 2.5
VMIX = 0.2
HIGH = lax.Precision.HIGHEST
LANES = 128
F32 = jnp.float32
BF16 = jnp.bfloat16
STEP = 10
SHRINK = 1.0 / LATENT
I32 = jnp.int32


def iota(shape, dim):
    return lax.broadcasted_iota(I32, shape, dim)


def mm(a, b, contract, precision=HIGH):
    return lax.dot_general(
        a, b, (contract, ((), ())), precision=precision, preferred_element_type=F32
    )


NN = ((1,), (0,))
NT = ((1,), (1,))
TN = ((0,), (0,))


def divided(value, by):
    return jnp.floor((value.astype(F32) + 0.5) * (1.0 / by)).astype(I32)


def split(values):
    high = values.astype(BF16)
    rest = values - high.astype(F32)
    middle = rest.astype(BF16)
    low = (rest - middle.astype(F32)).astype(BF16)
    return low, middle, high


def select(picks, values, contract, swap=False):
    total = None
    for part in split(values):
        a, b = (part, picks) if swap else (picks, part)
        term = lax.dot_general(a, b, (contract, ((), ())), preferred_element_type=F32)
        total = term if total is None else total + term
    return total


def vertical_mix(values, levels):
    upper = jnp.concatenate([values[1:levels], values[levels - 1 : levels]], axis=0)
    lower = jnp.concatenate([values[0:1], values[0 : levels - 1]], axis=0)
    inner = values[0:levels]
    return inner + VERTIC * (upper + lower - 2.0 * inner)


def element_of_row(rows):
    elements = rows // 4
    hit = divided(iota((rows, elements), 0), 4) == iota((rows, elements), 1)
    return jnp.where(hit, 1.0, 0.0).astype(BF16)


def element_means(columns_ref):
    elements = columns_ref.shape[0] // 4
    total = columns_ref[pl.ds(0, elements, stride=4), :]
    for k in range(1, 4):
        total = total + columns_ref[pl.ds(k, elements, stride=4), :]
    return 0.25 * total


def own_part(values, means, mixing, levels):
    rows, width = values.shape
    lane = iota((rows, width), 1)
    level = lane - levels * divided(lane, levels)
    upper = jnp.where(level == levels - 1, values, pltpu.roll(values, width - 1, 1))
    lower = jnp.where(level == 0, values, pltpu.roll(values, 1, 1))
    mean = select(element_of_row(rows), means, NN)
    return values - (4.0 * mixing) * mean + VMIX * (upper + lower - 2.0 * values)


def slots_of(targets, col_count, padded, clouds):
    rows = targets.shape[1]
    onehot = jnp.where(iota((clouds, rows), 0) == targets, 1.0, 0.0)
    before = jnp.where(iota((rows, rows), 0) < iota((rows, rows), 1), 1.0, 0.0)
    running = mm(onehot.astype(BF16), before.astype(BF16), NN, None)
    ranks = jnp.sum(running * onehot, axis=0, keepdims=True).astype(I32)
    owner = divided(targets, col_count)
    return owner, (targets - owner * col_count) * padded + ranks


def blocked(ref, value, levels):
    ref[...] = jnp.zeros_like(ref)
    for f in range(ref.shape[0] // levels):
        ref[f * levels : f * levels + value.shape[0], f * levels : (f + 1) * levels] = value


def host_kernel(
    columns_ref,
    mixing_ref,
    neighbours_ref,
    targets_ref,
    substeps_ref,
    map_ref,
    out_ref,
    fold_ref,
    *,
    padded,
    clouds,
):
    rows, width = columns_ref.shape
    cloud_levels, levels = map_ref.shape
    col_count = out_ref.shape[0]
    block = col_count * padded
    means = element_means(columns_ref)
    for c in range(col_count):
        out_ref[c, padded:, :] = means
    blocked(fold_ref, RELAX * vertical_mix(map_ref[...], cloud_levels), levels)
    owner, slot = slots_of(targets_ref[...], col_count, padded, clouds)
    mine = jnp.where(owner + 1 == lax.axis_index("sec"), slot, -1)
    pack = jnp.where(iota((block, rows), 0) == mine, 1.0, 0.0).astype(BF16)
    base = own_part(columns_ref[...], means, mixing_ref[...], levels)
    count = neighbours_ref.shape[0]
    ids = select(element_of_row(rows), neighbours_ref[...].astype(F32), NT, swap=True)
    extras = jnp.concatenate(
        [
            jnp.zeros((cloud_levels, rows), F32),
            ids,
            jnp.zeros((levels - 1 - cloud_levels - count, rows), F32),
            substeps_ref[...].astype(F32),
            jnp.zeros((width - levels, rows), F32),
        ],
        axis=0,
    )
    sent = mm(select(pack, base, NN), fold_ref[...], NT) + select(pack, extras, NT)
    for c in range(col_count):
        out_ref[c, :padded, :] = sent[c * padded : (c + 1) * padded]


def aside_kernel(
    columns_ref,
    mixing_ref,
    neighbours_ref,
    targets_ref,
    map_ref,
    base_ref,
    weights_ref,
    homes_ref,
    fold_ref,
    unfold_ref,
    *,
    col_count,
    padded,
    clouds,
):
    rows, width = columns_ref.shape
    cloud_levels, levels = map_ref.shape
    elements = rows // 4
    position = lax.axis_index("col")
    base_ref[...] = own_part(
        columns_ref[...], element_means(columns_ref), mixing_ref[...], levels
    )
    near = neighbours_ref[...] - (position - 1) * elements
    near = jnp.where(near < 0, near + elements * col_count, near)
    near = jnp.where(near >= elements * col_count, near - elements * col_count, near)
    window = iota((3 * elements, elements), 0)
    picks = jnp.zeros((3 * elements, elements), F32)
    for k in range(near.shape[0]):
        picks = picks + jnp.where(window == near[k : k + 1, :], 1.0, 0.0)
    weights_ref[...] = mm(element_of_row(rows), picks.astype(BF16), NT, None).astype(BF16)
    owner, slot = slots_of(targets_ref[...], col_count, padded, clouds)
    everywhere = (owner * (col_count * padded) + slot).astype(F32)
    identity = jnp.where(iota((rows, rows), 0) == iota((rows, rows), 1), 1.0, 0.0)
    homes_ref[...] = select(
        identity.astype(BF16), jnp.broadcast_to(everywhere, (LANES, rows)), NT
    )
    blocked(fold_ref, RELAX * vertical_mix(map_ref[...], cloud_levels), levels)
    fold_ref[...] = fold_ref[...] * mixing_ref[...]
    blocked(unfold_ref, map_ref[...], levels)


class Segment:
    def __init__(self, lane0, width, levels, begin):
        self.lane0, self.width, self.begin, self.levels = lane0, width, begin, levels
        self.steps = -(-levels // (LANES // width))
        self.groups = -(-levels // self.steps)
        self.missing = self.groups * self.steps - levels
        self.blocks = -(-self.steps // STEP)
        self.rows = (begin + 1, begin + 1 + self.steps)

    def group_steps(self, g):
        return self.steps - (self.missing if g == self.groups - 1 else 0)


def segments_of(slots, levels):
    segments, begin = [], 0
    for lane0 in range(0, slots, LANES):
        segments.append(Segment(lane0, min(LANES, slots - lane0), levels, begin))
        begin += segments[-1].steps + 2
    rows = max([begin] + [s.begin + 2 + s.blocks * STEP for s in segments])
    return segments, rows, -(-rows // 8) * 8


def fill_spare(segments, load, store):
    def turned(value, shift):
        tall = jnp.broadcast_to(value, (8, LANES)) if value.shape[0] == 1 else value
        return pltpu.roll(tall, shift % LANES, 1)[: value.shape[0]]

    for s in segments:
        if s.missing:
            row = s.rows[1] - s.missing
            value = load(row - 1)
            lane = iota(value.shape, 1)
            store(row, jnp.where(lane >= (s.groups - 1) * s.width, value, load(row)))
        first, last = load(s.rows[0]), load(s.rows[1] - 1)
        before, after = first, last
        if s.groups > 1:
            lane = iota(first.shape, 1)
            before = jnp.where(lane < s.width, first, turned(last, s.width))
            after = jnp.where(lane < (s.groups - 1) * s.width, turned(first, -s.width), last)
        store(s.begin, before)
        store(s.rows[1], after)


def fill_wide(segments, ref):
    def store(row, value):
        ref[row] = value

    fill_spare(segments, lambda row: ref[row], store)


def fill_flat(segments, ref):
    def store(row, value):
        ref[row : row + 1, :] = value

    fill_spare(segments, lambda row: ref[row : row + 1, :], store)


def linear(below, here, above):
    east = [pltpu.roll(here[3], 1, 0), here[0], here[1], here[2]]
    west = [here[1], here[2], here[3], pltpu.roll(here[0], 7, 0)]
    keep = (1.0 - 2.0 * HORIZ - 2.0 * VERTIC) / VERTIC
    return [
        (below[j] + above[j]) + ((HORIZ / VERTIC) * (east[j] + west[j]) + keep * here[j])
        for j in range(4)
    ]


def groups(ref, index):
    return [ref[index + (pl.ds(8 * j, 8),)] for j in range(4)]


def strided(ref, row):
    return [ref[row, pl.ds(j, 8, stride=4), :] for j in range(4)]


def sweep(segment, load, work):
    def block(i, carry):
        row = segment.begin + i * STEP
        held = [load(row), load(row + 1)]
        for k in range(STEP):
            held.append(load(row + k + 2))
            work(row + k + 1, held[k], held[k + 1], held[k + 2])
        return carry

    lax.fori_loop(0, segment.blocks, block, 0)


def each(count, size, work):
    size = min(size, count)

    def run(first):
        for k in range(size):
            work(first + k)

    if count // size:
        lax.fori_loop(0, count // size, lambda i, c: (run(i * size), c)[1], 0)
    if count % size:
        run(count - size)


def widen(state_ref, natural_ref, segments, scale):
    levels, columns, _ = state_ref.shape
    for s in segments:
        at = slice(s.lane0, s.lane0 + s.width)

        def one(k):
            parts = []
            for g in range(s.groups):
                level = jnp.minimum(g * s.steps + k, levels - 1)
                parts.append(state_ref[level, :, at].astype(F32))
            spare = LANES - s.groups * s.width
            if spare:
                parts.append(jnp.zeros((columns, spare), F32))
            value = jnp.concatenate(parts, axis=1) if len(parts) > 1 else parts[0]
            natural_ref[s.begin + 1 + k] = scale * value if scale != 1.0 else value

        each(s.steps, STEP, one)


def folded_sums(sums_ref, columns):
    rows = sums_ref.shape[0] // 8
    total = sums_ref[pl.ds(0, rows, stride=8), :]
    for k in range(1, 8):
        total = total + sums_ref[pl.ds(k, rows, stride=8), :]
    return total * (1.0 / columns)


def slab(row):
    return pl.ds(pl.multiple_of(row * 8, 8), 8)


def spread_row(ref, row):
    return jnp.broadcast_to(ref[pl.ds(row, 1), :], (8, LANES))


def turn(value, shift):
    if not shift:
        return value
    height = value.shape[0]
    tall = -(-height // 8) * 8
    if tall != height:
        fill = jnp.zeros((tall - height, LANES), F32)
        value = jnp.concatenate([value, fill], axis=0)
    return pltpu.roll(value, shift % LANES, 1)[:height]


def each(count, size, work):
    size = min(size, count)

    def run(first):
        for k in range(size):
            work(first + k)

    if count // size:
        lax.fori_loop(0, count // size, lambda i, c: (run(i * size), c)[1], 0)
    if count % size:
        run(count - size)


def widen(state_ref, natural_ref, segments, scale):
    levels, columns, _ = state_ref.shape
    for s in segments:
        at = slice(s.lane0, s.lane0 + s.width)

        def one(k):
            parts = []
            for g in range(s.groups):
                level = jnp.minimum(g * s.steps + k, levels - 1)
                parts.append(state_ref[level, :, at].astype(F32))
            spare = LANES - s.groups * s.width
            if spare:
                parts.append(jnp.zeros((columns, spare), F32))
            value = jnp.concatenate(parts, axis=1) if len(parts) > 1 else parts[0]
            natural_ref[s.begin + 1 + k] = scale * value if scale != 1.0 else value

        each(s.steps, STEP, one)


def folded_sums(sums_ref, columns):
    rows = sums_ref.shape[0] // 8
    total = sums_ref[pl.ds(0, rows, stride=8), :]
    for k in range(1, 8):
        total = total + sums_ref[pl.ds(k, rows, stride=8), :]
    return total * (1.0 / columns)


def slab(row):
    return pl.ds(pl.multiple_of(row * 8, 8), 8)


def spread_row(ref, row):
    return jnp.broadcast_to(ref[pl.ds(row, 1), :], (8, LANES))


def lane_places(segments):
    return [(s, g) for s in segments for g in range(s.groups)]


def slot_map(segments, block, capacity, padded):
    tiles = []
    for s in segments:
        lane = iota((8, LANES), 1)
        slot = s.lane0 + lane
        row = slot + (padded - capacity) * divided(slot, capacity)
        row = jnp.where(lane < s.width, row, -1)[0:1]
        tiles.append(jnp.where(iota((block, LANES), 0) == row, 1.0, 0.0).astype(BF16))
    return jnp.concatenate(tiles, axis=1)


def prepare_kernel(
    state_ref,
    saturation_ref,
    moved_ref,
    means_ref,
    limits_ref,
    state_buf,
    natural_ref,
    sums_ref,
    flat_ref,
    sems,
    *,
    segments,
):
    fields, levels, columns, _ = state_ref.shape
    loads = [
        pltpu.make_async_copy(state_ref.at[f], state_buf.at[f], sems.at[f]) for f in range(fields)
    ]
    loads[1].start()
    loads[0].start()
    tall = flat_ref.shape[0]
    here = iota((tall, levels), 0) == iota((tall, levels), 1)
    diagonal = jnp.where(here, 0.5 * saturation_ref[...], 0.0)
    flat_ref[...] = select(jnp.ones((levels, LANES), BF16), diagonal, NN, swap=True)
    limits_ref[...] = jnp.zeros_like(limits_ref)
    for s in segments:
        lane = iota((s.steps, LANES), 1)
        value = flat_ref[0 : s.steps, :]
        for g in range(1, s.groups):
            other = flat_ref[g * s.steps : (g + 1) * s.steps, :]
            value = jnp.where(lane >= g * s.width, other, value)
        limits_ref[s.rows[0] : s.rows[1], :] = value
    sums_ref[...] = jnp.zeros_like(sums_ref)
    loads[1].wait()
    widen(state_buf.at[1], natural_ref, segments, 1.0)
    fill_wide(segments, natural_ref)
    for s in segments:

        def work(row, below, here, above):
            out = linear(below, here, above)
            for j in range(4):
                moved_ref[row, pl.ds(8 * j, 8), :] = out[j]
            sums_ref[slab(row), :] = (here[0] + here[1]) + (here[2] + here[3])

        sweep(s, lambda row: strided(natural_ref, row), work)
    means_ref[1] = folded_sums(sums_ref, columns)
    loads[0].wait()
    widen(state_buf.at[0], natural_ref, segments, 1.0)
    for s in segments:

        def total(k):
            value = groups(natural_ref, (s.begin + 1 + k,))
            sums_ref[slab(s.begin + 1 + k), :] = (value[0] + value[1]) + (value[2] + value[3])

        each(s.steps, STEP, total)
    means_ref[0] = folded_sums(sums_ref, columns)


def water_kernel(
    received_ref,
    moved_ref,
    means_ref,
    limits_ref,
    fold_far,
    unfold_far,
    water_far,
    spill_far,
    flats_far,
    back_far,
    fold_ref,
    unfold_ref,
    even_ref,
    odd_ref,
    spill_buf,
    flats_ref,
    goal_ref,
    mean_ref,
    shift_ref,
    limit_ref,
    sums_ref,
    change_ref,
    back_ref,
    in_sems,
    spill_sems,
    water_sem,
    flat_sem,
    back_sems,
    *,
    segments,
    capacity,
    padded,
    stride,
    levels,
    neighbours,
):
    rows = means_ref.shape[1]
    columns = even_ref.shape[1]
    loads = [
        pltpu.make_async_copy(fold_far, fold_ref, in_sems.at[0]),
        pltpu.make_async_copy(unfold_far, unfold_ref, in_sems.at[1]),
    ]
    for load in loads:
        load.start()
    hosts = received_ref.shape[0]
    block = hosts * padded
    places = slot_map(segments, block, capacity, padded)
    sent = jnp.concatenate([received_ref[j, :padded, :] for j in range(hosts)], axis=0)
    arrived = select(places, sent, TN, swap=True)
    means = jnp.concatenate([received_ref[j, padded:, :] for j in range(hosts)], axis=0)
    element = iota((means.shape[0], arrived.shape[1]), 0).astype(F32)
    wanted = jnp.zeros(element.shape, F32)
    taken = arrived[stride - 1 : stride] > 0.0
    for k in range(neighbours):
        ids = jnp.where(taken, arrived[levels + k : levels + k + 1], -1.0)
        wanted = wanted + jnp.where(element == ids, 1.0, 0.0)
    spread = select(wanted.astype(BF16), means, TN, swap=True)
    loads[0].wait()
    arrived = arrived + mm(fold_ref[...], spread, NN)
    goal_ref[...] = jnp.zeros_like(goal_ref)
    flats_ref[...] = jnp.zeros_like(flats_ref)
    sums_ref[...] = jnp.zeros_like(sums_ref)
    counts = flats_ref.at[MAX_SUB + 2]
    for t, s in enumerate(segments):
        lanes = slice(t * LANES, (t + 1) * LANES)
        count = None
        for g in range(s.groups):
            number = s.group_steps(g)
            at = slice(s.rows[0], s.rows[0] + number)
            for f in range(2):
                first = f * stride + g * s.steps
                part = turn(arrived[first : first + number, lanes], g * s.width)
                goal_ref[f, at, :] = goal_ref[f, at, :] + part if g else part
            part = turn(arrived[stride - 1 : stride, lanes], g * s.width)
            count = part if count is None else count + part
        counts[s.rows[0] : s.rows[1], :] = jnp.broadcast_to(count, (s.steps, LANES))
    for f in range(2):
        mean_ref[f] = means_ref[f]
    copies = []
    source, target = None, even_ref
    for n in range(MAX_SUB):
        scale = 10.0 ** (n + 1)
        last = n + 1 == MAX_SUB
        expected = []
        for f in range(2):
            fill_flat(segments, mean_ref.at[f])
            mean = mean_ref[f]
            mixed = mean + VERTIC * (
                pltpu.roll(mean, 1, 0) + pltpu.roll(mean, rows - 1, 0) - 2.0 * mean
            )
            offset = goal_ref[f] - RELAX * mixed
            expected.append(mixed + offset)
            if f == 1:
                shift_ref[...] = scale * offset
            else:
                flats_ref[n] = (scale * SHRINK) * offset
        limit_ref[...] = scale * limits_ref[...]
        if last:
            flats_ref[MAX_SUB] = shift_ref[...]
            flats_ref[MAX_SUB + 1] = limit_ref[...]
            copies.append(pltpu.make_async_copy(flats_ref, flats_far, flat_sem))
            copies[-1].start()
        for s in segments:
            active = spread_row(counts, s.rows[0]) > float(n)

            def finish(row, lin, old):
                shift = spread_row(shift_ref, row)
                limit = spread_row(limit_ref, row)
                total = None
                for j in range(4):
                    v = lin[j] + shift
                    c = jnp.maximum(0.5 * v - limit, 0.0)
                    total = c if total is None else total + c
                    if last:
                        continue
                    u = v - c
                    if old is not None:
                        u = jnp.where(active, u, old[j])
                    spill_buf[n, row, pl.ds(8 * j, 8), :] = c
                    target[row, pl.ds(8 * j, 8), :] = u
                sums_ref[slab(row), :] = total

            if n == 0:

                def block(i, carry):
                    for k in range(STEP):
                        row = s.begin + 1 + i * STEP + k
                        finish(row, groups(moved_ref, (row,)), None)
                    return carry

                lax.fori_loop(0, s.blocks, block, 0)
            else:

                def work(row, below, here, above):
                    finish(row, linear(below, here, above), here)

                sweep(s, lambda row: groups(source, (row,)), work)
        if not last:
            copies.append(
                pltpu.make_async_copy(spill_buf.at[n], spill_far.at[n], spill_sems.at[n])
            )
            copies[-1].start()
            fill_wide(segments, target)
            source, target = target, (odd_ref if target is even_ref else even_ref)
        if n + 2 == MAX_SUB:
            copies.append(pltpu.make_async_copy(source, water_far, water_sem))
            copies[-1].start()
        spilled = folded_sums(sums_ref, columns) * (1.0 / scale)
        step = [expected[0] + LATENT * spilled, expected[1] - spilled]
        keep = counts[...] > float(n)
        for f in range(2):
            mean_ref[f] = jnp.where(keep, step[f], mean_ref[f])
    change_ref[...] = jnp.zeros_like(change_ref)
    for f in range(2):
        change = mean_ref[f] - means_ref[f]
        for t, s in enumerate(segments):
            for g in range(s.groups):
                first, number = f * stride + g * s.steps, s.group_steps(g)
                part = turn(change[s.rows[0] : s.rows[0] + number], -g * s.width)
                change_ref[first : first + number, t * LANES : (t + 1) * LANES] = part
    spread = select(places, change_ref[...], NT)
    loads[1].wait()
    back = mm(spread, unfold_ref[...], NN)
    for j in range(back_ref.shape[0]):
        back_ref[j] = back[j * padded : j * padded + capacity]
    for i in range(back_far.shape[0]):
        copies.append(pltpu.make_async_copy(back_ref, back_far.at[i], back_sems.at[i]))
        copies[-1].start()
    for copy in copies:
        copy.wait()


def energy_kernel(
    state_ref,
    water_far,
    spill_far,
    flats_far,
    base_ref,
    weights_ref,
    received_ref,
    mixing_ref,
    homes_ref,
    out_ref,
    advanced_ref,
    places_ref,
    state_buf,
    water_buf,
    spill_buf,
    flats_ref,
    out_buf,
    even_ref,
    odd_ref,
    last_ref,
    natural_ref,
    state_sems,
    water_sem,
    spill_sems,
    flat_sem,
    out_sems,
    *,
    segments,
    padded,
):
    fields, levels, columns, _ = state_ref.shape
    states = [
        pltpu.make_async_copy(state_ref.at[f], state_buf.at[f], state_sems.at[f])
        for f in range(fields)
    ]
    flats = pltpu.make_async_copy(flats_far, flats_ref, flat_sem)
    waters = pltpu.make_async_copy(water_far, water_buf, water_sem)
    spills = [
        pltpu.make_async_copy(spill_far.at[n], spill_buf.at[n], spill_sems.at[n])
        for n in range(MAX_SUB - 1)
    ]
    leaves = [
        pltpu.make_async_copy(out_buf.at[f], out_ref.at[f], out_sems.at[f]) for f in range(fields)
    ]
    states[0].start()
    flats.start()
    for copy in spills:
        copy.start()
    waters.start()
    states[1].start()
    hosts = received_ref.shape[0]
    position = lax.axis_index("col")
    around = [jnp.where(position == 0, hosts - 1, position - 1), position]
    around.append(jnp.where(position == hosts - 1, 0, position + 1))
    means = jnp.concatenate([received_ref[j, padded:, :] for j in around], axis=0)
    advanced_ref[...] = base_ref[...] + mixing_ref[...] * select(weights_ref[...], means, NN)
    places_ref[...] = homes_ref[...]
    states[0].wait()
    widen(state_buf.at[0], natural_ref, segments, SHRINK)
    fill_wide(segments, natural_ref)
    flats.wait()
    counts = flats_ref.at[MAX_SUB + 2]
    source, target = natural_ref, even_ref
    for n in range(MAX_SUB):
        last = n + 1 == MAX_SUB
        (waters if last else spills[n]).wait()
        for s in segments:
            active = spread_row(counts, s.rows[0]) > float(n)

            def load(row):
                here = strided(source, row) if n == 0 else groups(source, (row,))
                return (here, groups(water_buf, (row,))) if last else (here, None)

            def work(row, below, here, above):
                shift = spread_row(flats_ref.at[n], row)
                lin = linear(below[0], here[0], above[0])
                if last:
                    water = linear(below[1], here[1], above[1])
                    push = spread_row(flats_ref.at[MAX_SUB], row)
                    limit = spread_row(flats_ref.at[MAX_SUB + 1], row)
                else:
                    spill = groups(spill_buf, (n, row))
                for j in range(4):
                    if last:
                        v = water[j] + push
                        c = jnp.maximum(0.5 * v - limit, 0.0)
                        last_ref[row, pl.ds(8 * j, 8), :] = jnp.where(active, v - c, here[1][j])
                    else:
                        c = spill[j]
                    u = (lin[j] + shift) + c
                    if n:
                        u = jnp.where(active, u, here[0][j])
                    target[row, pl.ds(8 * j, 8), :] = u

            sweep(s, load, work)
        if not last:
            fill_wide(segments, target)
        source, target = target, (odd_ref if target is even_ref else even_ref)
    for f in (1, 0):
        states[1].wait() if f == 1 else None
        found = last_ref if f == 1 else source
        for s in segments:
            count = spread_row(counts, s.rows[0])
            back = jnp.zeros((8, LANES), F32)
            for n in range(1, MAX_SUB + 1):
                scale = 10.0**-n * (LATENT if f == 0 else 1.0)
                back = jnp.where(count == float(n), scale, back)

            def permute(k):
                row = s.begin + 1 + k
                value = groups(found, (row,))
                for j in range(4):
                    natural_ref[row, pl.ds(j, 8, stride=4), :] = value[j] * back

            each(s.steps, STEP, permute)
            at = slice(s.lane0, s.lane0 + s.width)
            held = jnp.broadcast_to(count[0:1, : s.width], (columns, s.width)) > 0.0
            for g in range(s.groups):
                lanes = slice(g * s.width, (g + 1) * s.width)

                def narrow(k):
                    level = g * s.steps + k
                    old = state_buf[f, level, :, at].astype(F32)
                    value = jnp.where(held, natural_ref[s.begin + 1 + k, :, lanes], old)
                    out_buf[f, level, :, at] = value.astype(BF16)

                each(s.group_steps(g), STEP, narrow)
        leaves[f].start()
    for f in range(fields):
        leaves[f].wait()


def final_kernel(advanced_ref, places_ref, gathered_ref, out_ref, table_ref, *, levels, idle, padded):
    rows, width = advanced_ref.shape
    sources, capacity, _ = gathered_ref.shape
    if capacity != padded:
        table_ref[...] = jnp.zeros_like(table_ref)
    for j in range(idle, sources):
        first = (j - idle) * padded
        table_ref[first : first + capacity, :] = gathered_ref[j]
    place = places_ref[:, :1].astype(I32)
    picks = jnp.where(iota((rows, table_ref.shape[0]), 1) == place, 1.0, 0.0)
    summed = advanced_ref[...] + select(picks.astype(BF16), table_ref[...], NN)
    water = divided(iota((rows, width), 1), levels) == 1
    out_ref[...] = jnp.where(water, jnp.maximum(summed, 0.0), summed)


SPACES = dict(
    auto=pl.BlockSpec(memory_space=pltpu.VMEM),
    near=pl.BlockSpec(memory_space=pltpu.VMEM),
    far=pl.BlockSpec(memory_space=pl.ANY),
    scalar=pl.BlockSpec(memory_space=pltpu.SMEM),
)


def call(kernel, name, inputs, outputs, scratch=(), limit=8):
    kept = dict(near=pltpu.VMEM, auto=pltpu.HBM, far=pltpu.HBM, scalar=pltpu.HBM)
    arrays = [pltpu.with_memory_space_constraint(x, kept[space]) for space, x in inputs]
    shapes = [kept[space](dims, dtype) for space, dims, dtype in outputs]
    return pl.pallas_call(
        kernel,
        out_shape=shapes,
        in_specs=[SPACES[space] for space, _ in inputs],
        out_specs=[SPACES[space] for space, _, _ in outputs],
        scratch_shapes=list(scratch),
        compiler_params=pltpu.CompilerParams(vmem_limit_bytes=limit << 20),
        name=name,
    )(*arrays)


def body(
    column_state, mixing_rate, neighbours, assignment, substeps, cloud_state, level_map, saturation
):
    col_count = lax.axis_size("col")
    sec_count = lax.axis_size("sec")
    count, width = column_state.shape
    cloud_levels, levels = level_map.shape
    _, fields, _, columns, slots = cloud_state.shape
    elements = count // 4
    capacity = slots // col_count
    padded = -(-capacity // 8) * 8
    block = col_count * padded
    clouds = (sec_count - 1) * col_count
    segments, used, rows = segments_of(slots, cloud_levels)
    mapped = LANES * len(segments)
    mixing = mixing_rate.reshape(1, width)
    state = cloud_state[0]
    dma = pltpu.SemaphoreType.DMA

    def wide(*lead):
        return pltpu.VMEM((*lead, rows, columns, LANES), F32)

    hosts = dict(padded=padded, clouds=clouds)
    places_in = [
        ("auto", column_state),
        ("auto", mixing),
        ("auto", neighbours.T),
        ("auto", assignment.reshape(1, count)),
    ]
    outgoing, _ = call(
        functools.partial(host_kernel, **hosts),
        "host",
        places_in + [("auto", substeps.reshape(1, count)), ("auto", level_map)],
        [("auto", (col_count, padded + elements, width), F32), ("near", (width, width), F32)],
    )
    received = lax.all_to_all(outgoing, "col", split_axis=0, concat_axis=0, tiled=True)
    base, weights, homes, fold, unfold = call(
        functools.partial(aside_kernel, col_count=col_count, **hosts),
        "aside",
        places_in + [("auto", level_map)],
        [
            ("auto", (count, width), F32),
            ("auto", (count, 3 * elements), BF16),
            ("auto", (count, LANES), F32),
            ("auto", (width, width), F32),
            ("auto", (width, width), F32),
        ],
    )
    moved, cloud_means, limits = call(
        functools.partial(prepare_kernel, segments=segments),
        "prepare",
        [("far", state), ("auto", saturation.reshape(1, cloud_levels))],
        [
            ("near", (used, columns, LANES), F32),
            ("near", (fields, rows, LANES), F32),
            ("near", (rows, LANES), F32),
        ],
        scratch=[
            pltpu.VMEM(state.shape, BF16),
            wide(),
            pltpu.VMEM((rows * 8, LANES), F32),
            pltpu.VMEM((max(s.groups * s.steps for s in segments), LANES), F32),
            dma((fields,)),
        ],
        limit=16,
    )
    water, spill, flats, back = call(
        functools.partial(
            water_kernel,
            segments=segments,
            capacity=capacity,
            padded=padded,
            stride=levels,
            levels=cloud_levels,
            neighbours=neighbours.shape[1],
        ),
        "water",
        [
            ("near", received),
            ("near", moved),
            ("near", cloud_means),
            ("near", limits),
            ("far", fold),
            ("far", unfold),
        ],
        [
            ("far", (rows, columns, LANES), F32),
            ("far", (MAX_SUB - 1, rows, columns, LANES), F32),
            ("far", (MAX_SUB + 3, rows, LANES), F32),
            ("far", (sec_count, col_count, capacity, width), F32),
        ],
        scratch=[
            pltpu.VMEM((width, width), F32),
            pltpu.VMEM((width, width), F32),
            wide(),
            wide(),
            wide(MAX_SUB - 1),
            pltpu.VMEM((MAX_SUB + 3, rows, LANES), F32),
            pltpu.VMEM((fields, rows, LANES), F32),
            pltpu.VMEM((fields, rows, LANES), F32),
            pltpu.VMEM((rows, LANES), F32),
            pltpu.VMEM((rows, LANES), F32),
            pltpu.VMEM((rows * 8, LANES), F32),
            pltpu.VMEM((width, mapped), F32),
            pltpu.VMEM((col_count, capacity, width), F32),
            dma((2,)),
            dma((MAX_SUB - 1,)),
            dma(()),
            dma(()),
            dma((sec_count,)),
        ],
        limit=24,
    )
    returned = lax.all_to_all(
        back.reshape(sec_count * col_count, capacity, width),
        ("sec", "col"),
        split_axis=0,
        concat_axis=0,
        tiled=True,
    )
    new_block, advanced, places = call(
        functools.partial(energy_kernel, segments=segments, padded=padded),
        "energy",
        [
            ("far", state),
            ("far", water),
            ("far", spill),
            ("far", flats),
            ("auto", base),
            ("auto", weights),
            ("near", received),
            ("auto", mixing),
            ("auto", homes),
        ],
        [
            ("far", state.shape, BF16),
            ("near", (count, width), F32),
            ("near", (count, LANES), F32),
        ],
        scratch=[
            pltpu.VMEM(state.shape, BF16),
            wide(),
            wide(MAX_SUB - 1),
            pltpu.VMEM((MAX_SUB + 3, rows, LANES), F32),
            pltpu.VMEM(state.shape, BF16),
            wide(),
            wide(),
            wide(),
            wide(),
            dma((fields,)),
            dma(()),
            dma((MAX_SUB - 1,)),
            dma(()),
            dma((fields,)),
        ],
        limit=32,
    )
    (new_columns,) = call(
        functools.partial(final_kernel, levels=levels, idle=col_count, padded=padded),
        "final",
        [("near", advanced), ("near", places), ("near", returned)],
        [("auto", (count, width), F32)],
        scratch=[pltpu.VMEM((clouds * padded, width), F32)],
    )
    return new_columns, new_block[None]


def solution(mesh):
    in_specs = (
        P("col", None),
        P(),
        P("col", None),
        P("col", None),
        P("col"),
        P("sec", None, None, None, "col"),
        P(),
        P(),
    )
    out_specs = (P("col", None), P("sec", None, None, None, "col"))
    return jax.shard_map(body, mesh=mesh, in_specs=in_specs, out_specs=out_specs, check_vma=False)
```

```python
import functools

import jax
import jax.numpy as jnp
from jax import lax
from jax.experimental import pallas as pl
from jax.experimental.pallas import tpu as pltpu
from jax.sharding import PartitionSpec as P

MAX_SUB = 4
RELAX = 0.25
HORIZ = 0.12
VERTIC = 0.1
LATENT = 2.5
VMIX = 0.2
HIGH = lax.Precision.HIGHEST
LANES = 128
F32 = jnp.float32
BF16 = jnp.bfloat16
STEP = 10
SHRINK = 1.0 / LATENT
I32 = jnp.int32


def iota(shape, dim):
    return lax.broadcasted_iota(I32, shape, dim)


def mm(a, b, contract, precision=HIGH):
    return lax.dot_general(
        a, b, (contract, ((), ())), precision=precision, preferred_element_type=F32
    )


NN = ((1,), (0,))
NT = ((1,), (1,))
TN = ((0,), (0,))


def divided(value, by):
    return jnp.floor((value.astype(F32) + 0.5) * (1.0 / by)).astype(I32)


def split(values):
    high = values.astype(BF16)
    rest = values - high.astype(F32)
    middle = rest.astype(BF16)
    low = (rest - middle.astype(F32)).astype(BF16)
    return low, middle, high


def select(picks, values, contract, swap=False):
    total = None
    for part in split(values):
        a, b = (part, picks) if swap else (picks, part)
        term = lax.dot_general(a, b, (contract, ((), ())), preferred_element_type=F32)
        total = term if total is None else total + term
    return total


def vertical_mix(values, levels):
    upper = jnp.concatenate([values[1:levels], values[levels - 1 : levels]], axis=0)
    lower = jnp.concatenate([values[0:1], values[0 : levels - 1]], axis=0)
    inner = values[0:levels]
    return inner + VERTIC * (upper + lower - 2.0 * inner)


def element_of_row(rows):
    elements = rows // 4
    hit = divided(iota((rows, elements), 0), 4) == iota((rows, elements), 1)
    return jnp.where(hit, 1.0, 0.0).astype(BF16)


def element_means(columns_ref):
    elements = columns_ref.shape[0] // 4
    total = columns_ref[pl.ds(0, elements, stride=4), :]
    for k in range(1, 4):
        total = total + columns_ref[pl.ds(k, elements, stride=4), :]
    return 0.25 * total


def own_part(values, means, mixing, levels):
    rows, width = values.shape
    lane = iota((rows, width), 1)
    level = lane - levels * divided(lane, levels)
    upper = jnp.where(level == levels - 1, values, pltpu.roll(values, width - 1, 1))
    lower = jnp.where(level == 0, values, pltpu.roll(values, 1, 1))
    mean = select(element_of_row(rows), means, NN)
    return values - (4.0 * mixing) * mean + VMIX * (upper + lower - 2.0 * values)


def slots_of(targets, col_count, padded, clouds):
    rows = targets.shape[1]
    onehot = jnp.where(iota((clouds, rows), 0) == targets, 1.0, 0.0)
    before = jnp.where(iota((rows, rows), 0) < iota((rows, rows), 1), 1.0, 0.0)
    running = mm(onehot.astype(BF16), before.astype(BF16), NN, None)
    ranks = jnp.sum(running * onehot, axis=0, keepdims=True).astype(I32)
    owner = divided(targets, col_count)
    return owner, (targets - owner * col_count) * padded + ranks


def blocked(ref, value, levels):
    ref[...] = jnp.zeros_like(ref)
    for f in range(ref.shape[0] // levels):
        ref[f * levels : f * levels + value.shape[0], f * levels : (f + 1) * levels] = value


def host_kernel(
    columns_ref,
    mixing_ref,
    neighbours_ref,
    targets_ref,
    substeps_ref,
    map_ref,
    out_ref,
    fold_ref,
    *,
    padded,
    clouds,
):
    rows, width = columns_ref.shape
    cloud_levels, levels = map_ref.shape
    col_count = out_ref.shape[0]
    block = col_count * padded
    means = element_means(columns_ref)
    for c in range(col_count):
        out_ref[c, padded:, :] = means
    blocked(fold_ref, RELAX * vertical_mix(map_ref[...], cloud_levels), levels)
    owner, slot = slots_of(targets_ref[...], col_count, padded, clouds)
    mine = jnp.where(owner + 1 == lax.axis_index("sec"), slot, -1)
    pack = jnp.where(iota((block, rows), 0) == mine, 1.0, 0.0).astype(BF16)
    base = own_part(columns_ref[...], means, mixing_ref[...], levels)
    count = neighbours_ref.shape[0]
    ids = select(element_of_row(rows), neighbours_ref[...].astype(F32), NT, swap=True)
    extras = jnp.concatenate(
        [
            jnp.zeros((cloud_levels, rows), F32),
            ids,
            jnp.zeros((levels - 1 - cloud_levels - count, rows), F32),
            substeps_ref[...].astype(F32),
            jnp.zeros((width - levels, rows), F32),
        ],
        axis=0,
    )
    sent = mm(select(pack, base, NN), fold_ref[...], NT) + select(pack, extras, NT)
    for c in range(col_count):
        out_ref[c, :padded, :] = sent[c * padded : (c + 1) * padded]


def aside_kernel(
    columns_ref,
    mixing_ref,
    neighbours_ref,
    targets_ref,
    map_ref,
    base_ref,
    weights_ref,
    homes_ref,
    fold_ref,
    unfold_ref,
    *,
    col_count,
    padded,
    clouds,
    half,
    held,
):
    rows, width = columns_ref.shape
    cloud_levels, levels = map_ref.shape
    elements = rows // 4
    position = lax.axis_index("col")
    base_ref[...] = own_part(
        columns_ref[...], element_means(columns_ref), mixing_ref[...], levels
    )
    near = neighbours_ref[...] - (position - 1) * elements
    near = jnp.where(near < 0, near + elements * col_count, near)
    near = jnp.where(near >= elements * col_count, near - elements * col_count, near)
    window = iota((3 * elements, elements), 0)
    picks = jnp.zeros((3 * elements, elements), F32)
    for k in range(near.shape[0]):
        picks = picks + jnp.where(window == near[k : k + 1, :], 1.0, 0.0)
    weights_ref[...] = mm(element_of_row(rows), picks.astype(BF16), NT, None).astype(BF16)
    owner, slot = slots_of(targets_ref[...], col_count, padded, clouds)
    place = divided(slot, padded)
    rank = slot - place * padded
    upper = jnp.where(rank >= half, 1, 0)
    parity = lax.axis_index("sec") % 2
    cloud = owner * col_count + place + jnp.where(upper == parity, 0, clouds)
    everywhere = (cloud * held + rank - half * upper).astype(F32)
    identity = jnp.where(iota((rows, rows), 0) == iota((rows, rows), 1), 1.0, 0.0)
    homes_ref[...] = select(
        identity.astype(BF16), jnp.broadcast_to(everywhere, (LANES, rows)), NT
    )
    blocked(fold_ref, RELAX * vertical_mix(map_ref[...], cloud_levels), levels)
    fold_ref[...] = fold_ref[...] * mixing_ref[...]
    blocked(unfold_ref, map_ref[...], levels)


class Segment:
    def __init__(self, lane0, width, levels, begin):
        self.lane0, self.width, self.begin, self.levels = lane0, width, begin, levels
        self.steps = -(-levels // (LANES // width))
        self.groups = -(-levels // self.steps)
        self.missing = self.groups * self.steps - levels
        self.blocks = -(-self.steps // STEP)
        self.rows = (begin + 1, begin + 1 + self.steps)

    def group_steps(self, g):
        return self.steps - (self.missing if g == self.groups - 1 else 0)


def segments_of(slots, levels):
    segments, begin = [], 0
    for lane0 in range(0, slots, LANES):
        segments.append(Segment(lane0, min(LANES, slots - lane0), levels, begin))
        begin += segments[-1].steps + 2
    rows = max([begin] + [s.begin + 2 + s.blocks * STEP for s in segments])
    return segments, rows, -(-rows // 8) * 8


def fill_spare(segments, load, store):
    def turned(value, shift):
        tall = jnp.broadcast_to(value, (8, LANES)) if value.shape[0] == 1 else value
        return pltpu.roll(tall, shift % LANES, 1)[: value.shape[0]]

    for s in segments:
        if s.missing:
            row = s.rows[1] - s.missing
            value = load(row - 1)
            lane = iota(value.shape, 1)
            store(row, jnp.where(lane >= (s.groups - 1) * s.width, value, load(row)))
        first, last = load(s.rows[0]), load(s.rows[1] - 1)
        before, after = first, last
        if s.groups > 1:
            lane = iota(first.shape, 1)
            before = jnp.where(lane < s.width, first, turned(last, s.width))
            after = jnp.where(lane < (s.groups - 1) * s.width, turned(first, -s.width), last)
        store(s.begin, before)
        store(s.rows[1], after)


def fill_wide(segments, ref):
    def store(row, value):
        ref[row] = value

    fill_spare(segments, lambda row: ref[row], store)


def fill_flat(segments, ref):
    def store(row, value):
        ref[row : row + 1, :] = value

    fill_spare(segments, lambda row: ref[row : row + 1, :], store)


def linear(below, here, above):
    east = [pltpu.roll(here[3], 1, 0), here[0], here[1], here[2]]
    west = [here[1], here[2], here[3], pltpu.roll(here[0], 7, 0)]
    keep = (1.0 - 2.0 * HORIZ - 2.0 * VERTIC) / VERTIC
    return [
        (below[j] + above[j]) + ((HORIZ / VERTIC) * (east[j] + west[j]) + keep * here[j])
        for j in range(4)
    ]


def groups(ref, index):
    return [ref[index + (pl.ds(8 * j, 8),)] for j in range(4)]


def strided(ref, row):
    return [ref[row, pl.ds(j, 8, stride=4), :] for j in range(4)]


def sweep(segment, load, work):
    def block(i, carry):
        row = segment.begin + i * STEP
        held = [load(row), load(row + 1)]
        for k in range(STEP):
            held.append(load(row + k + 2))
            work(row + k + 1, held[k], held[k + 1], held[k + 2])
        return carry

    lax.fori_loop(0, segment.blocks, block, 0)


def each(count, size, work):
    size = min(size, count)

    def run(first):
        for k in range(size):
            work(first + k)

    if count // size:
        lax.fori_loop(0, count // size, lambda i, c: (run(i * size), c)[1], 0)
    if count % size:
        run(count - size)


def widen(state_ref, natural_ref, segments, scale):
    levels, columns, _ = state_ref.shape
    for s in segments:
        at = slice(s.lane0, s.lane0 + s.width)

        def one(k):
            parts = []
            for g in range(s.groups):
                level = jnp.minimum(g * s.steps + k, levels - 1)
                parts.append(state_ref[level, :, at].astype(F32))
            spare = LANES - s.groups * s.width
            if spare:
                parts.append(jnp.zeros((columns, spare), F32))
            value = jnp.concatenate(parts, axis=1) if len(parts) > 1 else parts[0]
            natural_ref[s.begin + 1 + k] = scale * value if scale != 1.0 else value

        each(s.steps, STEP, one)


def folded_sums(sums_ref, columns):
    rows = sums_ref.shape[0] // 8
    total = sums_ref[pl.ds(0, rows, stride=8), :]
    for k in range(1, 8):
        total = total + sums_ref[pl.ds(k, rows, stride=8), :]
    return total * (1.0 / columns)


def slab(row):
    return pl.ds(pl.multiple_of(row * 8, 8), 8)


def spread_row(ref, row):
    return jnp.broadcast_to(ref[pl.ds(row, 1), :], (8, LANES))


def turn(value, shift):
    if not shift:
        return value
    height = value.shape[0]
    tall = -(-height // 8) * 8
    if tall != height:
        fill = jnp.zeros((tall - height, LANES), F32)
        value = jnp.concatenate([value, fill], axis=0)
    return pltpu.roll(value, shift % LANES, 1)[:height]


def each(count, size, work):
    size = min(size, count)

    def run(first):
        for k in range(size):
            work(first + k)

    if count // size:
        lax.fori_loop(0, count // size, lambda i, c: (run(i * size), c)[1], 0)
    if count % size:
        run(count - size)


def widen(state_ref, natural_ref, segments, scale):
    levels, columns, _ = state_ref.shape
    for s in segments:
        at = slice(s.lane0, s.lane0 + s.width)

        def one(k):
            parts = []
            for g in range(s.groups):
                level = jnp.minimum(g * s.steps + k, levels - 1)
                parts.append(state_ref[level, :, at].astype(F32))
            spare = LANES - s.groups * s.width
            if spare:
                parts.append(jnp.zeros((columns, spare), F32))
            value = jnp.concatenate(parts, axis=1) if len(parts) > 1 else parts[0]
            natural_ref[s.begin + 1 + k] = scale * value if scale != 1.0 else value

        each(s.steps, STEP, one)


def folded_sums(sums_ref, columns):
    rows = sums_ref.shape[0] // 8
    total = sums_ref[pl.ds(0, rows, stride=8), :]
    for k in range(1, 8):
        total = total + sums_ref[pl.ds(k, rows, stride=8), :]
    return total * (1.0 / columns)


def slab(row):
    return pl.ds(pl.multiple_of(row * 8, 8), 8)


def spread_row(ref, row):
    return jnp.broadcast_to(ref[pl.ds(row, 1), :], (8, LANES))


def lane_places(segments):
    return [(s, g) for s in segments for g in range(s.groups)]


def slot_map(segments, block, capacity, padded):
    tiles = []
    for s in segments:
        lane = iota((8, LANES), 1)
        slot = s.lane0 + lane
        row = slot + (padded - capacity) * divided(slot, capacity)
        row = jnp.where(lane < s.width, row, -1)[0:1]
        tiles.append(jnp.where(iota((block, LANES), 0) == row, 1.0, 0.0).astype(BF16))
    return jnp.concatenate(tiles, axis=1)


def prepare_kernel(
    state_ref,
    saturation_ref,
    moved_ref,
    means_ref,
    limits_ref,
    energy_far,
    state_buf,
    natural_ref,
    sums_ref,
    flat_ref,
    energy_buf,
    sems,
    out_sem,
    *,
    segments,
):
    fields, levels, columns, _ = state_ref.shape
    loads = [
        pltpu.make_async_copy(state_ref.at[f], state_buf.at[f], sems.at[f]) for f in range(fields)
    ]
    loads[1].start()
    loads[0].start()
    tall = flat_ref.shape[0]
    here = iota((tall, levels), 0) == iota((tall, levels), 1)
    diagonal = jnp.where(here, 0.5 * saturation_ref[...], 0.0)
    flat_ref[...] = select(jnp.ones((levels, LANES), BF16), diagonal, NN, swap=True)
    limits_ref[...] = jnp.zeros_like(limits_ref)
    for s in segments:
        lane = iota((s.steps, LANES), 1)
        value = flat_ref[0 : s.steps, :]
        for g in range(1, s.groups):
            other = flat_ref[g * s.steps : (g + 1) * s.steps, :]
            value = jnp.where(lane >= g * s.width, other, value)
        limits_ref[s.rows[0] : s.rows[1], :] = value
    sums_ref[...] = jnp.zeros_like(sums_ref)
    for f, scale, target in ((1, 1.0, moved_ref), (0, SHRINK, energy_buf)):
        loads[f].wait()
        widen(state_buf.at[f], natural_ref, segments, scale)
        fill_wide(segments, natural_ref)
        for s in segments:

            def work(row, below, here, above):
                out = linear(below, here, above)
                for j in range(4):
                    target[row, pl.ds(8 * j, 8), :] = out[j]
                sums_ref[slab(row), :] = (here[0] + here[1]) + (here[2] + here[3])

            sweep(s, lambda row: strided(natural_ref, row), work)
        means_ref[f] = folded_sums(sums_ref, columns) * (1.0 / scale)
    leave = pltpu.make_async_copy(energy_buf, energy_far, out_sem)
    leave.start()
    leave.wait()


def water_kernel(
    received_ref,
    moved_ref,
    means_ref,
    limits_ref,
    fold_far,
    unfold_far,
    water_far,
    spill_far,
    flats_far,
    back_far,
    fold_ref,
    unfold_ref,
    even_ref,
    odd_ref,
    spill_buf,
    flats_ref,
    goal_ref,
    mean_ref,
    shift_ref,
    limit_ref,
    sums_ref,
    change_ref,
    back_ref,
    in_sems,
    spill_sems,
    water_sem,
    flat_sem,
    back_sems,
    *,
    segments,
    capacity,
    padded,
    stride,
    levels,
    neighbours,
):
    rows = means_ref.shape[1]
    columns = even_ref.shape[1]
    loads = [
        pltpu.make_async_copy(fold_far, fold_ref, in_sems.at[0]),
        pltpu.make_async_copy(unfold_far, unfold_ref, in_sems.at[1]),
    ]
    for load in loads:
        load.start()
    hosts = received_ref.shape[0]
    block = hosts * padded
    places = slot_map(segments, block, capacity, padded)
    sent = jnp.concatenate([received_ref[j, :padded, :] for j in range(hosts)], axis=0)
    means = jnp.concatenate([received_ref[j, padded:, :] for j in range(hosts)], axis=0)
    element = iota((block, means.shape[0]), 1).astype(F32)
    taken = sent[:, stride - 1 : stride] > 0.0
    wanted = jnp.zeros(element.shape, F32)
    for k in range(neighbours):
        ids = jnp.where(taken, sent[:, levels + k : levels + k + 1], -1.0)
        wanted = wanted + jnp.where(element == ids, 1.0, 0.0)
    spread = select(wanted.astype(BF16), means, NN)
    loads[0].wait()
    sent = sent + mm(spread, fold_ref[...], NT)
    arrived = select(places, sent, TN, swap=True)
    goal_ref[...] = jnp.zeros_like(goal_ref)
    flats_ref[...] = jnp.zeros_like(flats_ref)
    sums_ref[...] = jnp.zeros_like(sums_ref)
    counts = flats_ref.at[MAX_SUB + 2]
    for t, s in enumerate(segments):
        lanes = slice(t * LANES, (t + 1) * LANES)
        count = None
        for g in range(s.groups):
            number = s.group_steps(g)
            at = slice(s.rows[0], s.rows[0] + number)
            for f in range(2):
                first = f * stride + g * s.steps
                part = turn(arrived[first : first + number, lanes], g * s.width)
                goal_ref[f, at, :] = goal_ref[f, at, :] + part if g else part
            part = turn(arrived[stride - 1 : stride, lanes], g * s.width)
            count = part if count is None else count + part
        counts[s.rows[0] : s.rows[1], :] = jnp.broadcast_to(count, (s.steps, LANES))
    for f in range(2):
        mean_ref[f] = means_ref[f]
    copies = []
    source, target = None, even_ref
    for n in range(MAX_SUB):
        scale = 10.0 ** (n + 1)
        last = n + 1 == MAX_SUB
        expected = []
        for f in range(2):
            fill_flat(segments, mean_ref.at[f])
            mean = mean_ref[f]
            mixed = mean + VERTIC * (
                pltpu.roll(mean, 1, 0) + pltpu.roll(mean, rows - 1, 0) - 2.0 * mean
            )
            offset = goal_ref[f] - RELAX * mixed
            expected.append(mixed + offset)
            if f == 1:
                shift_ref[...] = scale * offset
            else:
                flats_ref[n] = (scale * SHRINK) * offset
        limit_ref[...] = scale * limits_ref[...]
        if last:
            flats_ref[MAX_SUB] = shift_ref[...]
            flats_ref[MAX_SUB + 1] = limit_ref[...]
            copies.append(pltpu.make_async_copy(flats_ref, flats_far, flat_sem))
            copies[-1].start()
        for s in segments:
            active = spread_row(counts, s.rows[0]) > float(n)

            def finish(row, lin, old):
                shift = spread_row(shift_ref, row)
                limit = spread_row(limit_ref, row)
                total = None
                for j in range(4):
                    v = lin[j] + shift
                    c = jnp.maximum(0.5 * v - limit, 0.0)
                    total = c if total is None else total + c
                    if last:
                        continue
                    u = v - c
                    if old is not None:
                        u = jnp.where(active, u, old[j])
                    spill_buf[n, row, pl.ds(8 * j, 8), :] = c
                    target[row, pl.ds(8 * j, 8), :] = u
                sums_ref[slab(row), :] = total

            if n == 0:

                def block(i, carry):
                    for k in range(STEP):
                        row = s.begin + 1 + i * STEP + k
                        finish(row, groups(moved_ref, (row,)), None)
                    return carry

                lax.fori_loop(0, s.blocks, block, 0)
            else:

                def work(row, below, here, above):
                    finish(row, linear(below, here, above), here)

                sweep(s, lambda row: groups(source, (row,)), work)
        if not last:
            copies.append(
                pltpu.make_async_copy(spill_buf.at[n], spill_far.at[n], spill_sems.at[n])
            )
            copies[-1].start()
            fill_wide(segments, target)
            source, target = target, (odd_ref if target is even_ref else even_ref)
        if n + 2 == MAX_SUB:
            copies.append(pltpu.make_async_copy(source, water_far, water_sem))
            copies[-1].start()
        spilled = folded_sums(sums_ref, columns) * (1.0 / scale)
        step = [expected[0] + LATENT * spilled, expected[1] - spilled]
        keep = counts[...] > float(n)
        for f in range(2):
            mean_ref[f] = jnp.where(keep, step[f], mean_ref[f])
    change_ref[...] = jnp.zeros_like(change_ref)
    for f in range(2):
        change = mean_ref[f] - means_ref[f]
        for t, s in enumerate(segments):
            for g in range(s.groups):
                first, number = f * stride + g * s.steps, s.group_steps(g)
                part = turn(change[s.rows[0] : s.rows[0] + number], -g * s.width)
                change_ref[first : first + number, t * LANES : (t + 1) * LANES] = part
    spread = select(places, change_ref[...], NT)
    loads[1].wait()
    back = mm(spread, unfold_ref[...], NN)
    half = back_ref.shape[2]
    for h in range(2):
        for j in range(hosts):
            first = j * padded + h * half
            back_ref[h, j] = back[first : first + half]
    for i in range(back_far.shape[0]):
        copies.append(pltpu.make_async_copy(back_ref.at[i % 2], back_far.at[i], back_sems.at[i]))
        copies[-1].start()
    for copy in copies:
        copy.wait()


def energy_kernel(
    state_ref,
    energy_far,
    water_far,
    spill_far,
    flats_far,
    base_far,
    weights_far,
    mixing_far,
    homes_far,
    received_ref,
    out_ref,
    advanced_ref,
    places_ref,
    state_buf,
    energy_buf,
    water_buf,
    spill_buf,
    flats_ref,
    base_ref,
    weights_ref,
    mixing_ref,
    out_buf,
    even_ref,
    odd_ref,
    natural_ref,
    state_sems,
    in_sems,
    spill_sems,
    out_sems,
    *,
    segments,
    padded,
):
    fields, levels, columns, _ = state_ref.shape
    final = MAX_SUB - 1
    pairs = (
        (flats_far, flats_ref),
        (base_far, base_ref),
        (weights_far, weights_ref),
        (mixing_far, mixing_ref),
        (water_far, water_buf),
        (energy_far, energy_buf),
        (homes_far, places_ref),
    )
    loads = [pltpu.make_async_copy(x, y, in_sems.at[i]) for i, (x, y) in enumerate(pairs)]
    flats, bases, shares, mixings, waters, first, homes = loads
    states = [
        pltpu.make_async_copy(state_ref.at[f], state_buf.at[f], state_sems.at[f])
        for f in range(fields)
    ]
    spills = [
        pltpu.make_async_copy(spill_far.at[n], spill_buf.at[n], spill_sems.at[n])
        for n in range(final)
    ]
    for copy in loads[:5] + [states[1], first] + spills + [states[0], homes]:
        copy.start()
    cut = -(-levels // 2)
    spans = ((0, cut), (cut, levels - cut))

    def leave(f, part):
        at = pl.ds(*spans[part])
        return pltpu.make_async_copy(
            out_buf.at[f, at], out_ref.at[f, at], out_sems.at[2 * f + part]
        )

    counts = flats_ref.at[MAX_SUB + 2]

    def finish_field(f, found):
        for s in segments[::-1]:
            count = spread_row(counts, s.rows[0])
            back = jnp.zeros((8, LANES), F32)
            for n in range(1, MAX_SUB + 1):
                scale = 10.0**-n * (LATENT if f == 0 else 1.0)
                back = jnp.where(count == float(n), scale, back)
            at = slice(s.lane0, s.lane0 + s.width)
            held = jnp.broadcast_to(count[0:1, : s.width], (columns, s.width)) > 0.0

            def permute(k):
                row = s.begin + 1 + k
                value = groups(found, (row,))
                for j in range(4):
                    natural_ref[row, pl.ds(j, 8, stride=4), :] = value[j] * back

            def narrow(g, k):
                level = g * s.steps + k
                lanes = slice(g * s.width, (g + 1) * s.width)
                old = state_buf[f, level, :, at].astype(F32)
                value = jnp.where(held, natural_ref[s.begin + 1 + k, :, lanes], old)
                out_buf[f, level, :, at] = value.astype(BF16)

            each(s.steps, STEP, permute)
            if s is segments[0] and s.groups == 1:
                for part, (begin, number) in enumerate(spans):
                    each(number, STEP, lambda k: narrow(0, begin + k))
                    leave(f, part).start()
            else:
                for g in range(s.groups):
                    each(s.group_steps(g), STEP, lambda k: narrow(g, k))
        if segments[0].groups > 1:
            for part in range(2):
                leave(f, part).start()

    bases.wait()
    shares.wait()
    mixings.wait()
    hosts = received_ref.shape[0]
    position = lax.axis_index("col")
    around = [jnp.where(position == 0, hosts - 1, position - 1), position]
    around.append(jnp.where(position == hosts - 1, 0, position + 1))
    means = jnp.concatenate([received_ref[j, padded:, :] for j in around], axis=0)
    advanced_ref[...] = base_ref[...] + mixing_ref[...] * select(weights_ref[...], means, NN)
    flats.wait()
    waters.wait()
    for s in segments:
        active = spread_row(counts, s.rows[0]) > float(final)

        def last(row, below, here, above):
            water = linear(below, here, above)
            push = spread_row(flats_ref.at[MAX_SUB], row)
            limit = spread_row(flats_ref.at[MAX_SUB + 1], row)
            for j in range(4):
                v = water[j] + push
                c = jnp.maximum(0.5 * v - limit, 0.0)
                spill_buf[final, row, pl.ds(8 * j, 8), :] = c
                even_ref[row, pl.ds(8 * j, 8), :] = jnp.where(active, v - c, here[j])

        sweep(s, lambda row: groups(water_buf, (row,)), last)
    states[1].wait()
    finish_field(1, even_ref)
    first.wait()
    source, target = None, odd_ref
    for n in range(MAX_SUB):
        if n < final:
            spills[n].wait()
        for s in segments:
            active = spread_row(counts, s.rows[0]) > float(n)

            def start(i, carry):
                for k in range(STEP):
                    row = s.begin + 1 + i * STEP + k
                    shift = spread_row(flats_ref.at[n], row)
                    lin, spill = groups(energy_buf, (row,)), groups(spill_buf, (n, row))
                    for j in range(4):
                        target[row, pl.ds(8 * j, 8), :] = (lin[j] + shift) + spill[j]
                return carry

            def work(row, below, here, above):
                shift = spread_row(flats_ref.at[n], row)
                lin = linear(below, here, above)
                spill = groups(spill_buf, (n, row))
                for j in range(4):
                    u = (lin[j] + shift) + spill[j]
                    target[row, pl.ds(8 * j, 8), :] = jnp.where(active, u, here[j])

            if n == 0:
                lax.fori_loop(0, s.blocks, start, 0)
            else:
                sweep(s, lambda row: groups(source, (row,)), work)
        if n < final:
            fill_wide(segments, target)
        source, target = target, (odd_ref if target is even_ref else even_ref)
    states[0].wait()
    finish_field(0, source)
    homes.wait()
    for f in range(fields):
        for part in range(2):
            leave(f, part).wait()


def final_kernel(
    advanced_ref, places_ref, mine_ref, other_ref, out_ref, table_ref, *, levels, idle, held
):
    rows, width = advanced_ref.shape
    sources, half, _ = mine_ref.shape
    clouds = sources - idle
    if half != held:
        table_ref[...] = jnp.zeros_like(table_ref)
    for i, ref in enumerate((mine_ref, other_ref)):
        for j in range(clouds):
            first = (i * clouds + j) * held
            table_ref[first : first + half, :] = ref[idle + j]
    place = places_ref[:, :1].astype(I32)
    picks = jnp.where(iota((rows, table_ref.shape[0]), 1) == place, 1.0, 0.0)
    summed = advanced_ref[...] + select(picks.astype(BF16), table_ref[...], NN)
    water = divided(iota((rows, width), 1), levels) == 1
    out_ref[...] = jnp.where(water, jnp.maximum(summed, 0.0), summed)


SPACES = dict(
    auto=pl.BlockSpec(memory_space=pltpu.VMEM),
    near=pl.BlockSpec(memory_space=pltpu.VMEM),
    far=pl.BlockSpec(memory_space=pl.ANY),
    scalar=pl.BlockSpec(memory_space=pltpu.SMEM),
)


def call(kernel, name, inputs, outputs, scratch=(), limit=8):
    kept = dict(near=pltpu.VMEM, auto=pltpu.HBM, far=pltpu.HBM, scalar=pltpu.HBM)
    arrays = [pltpu.with_memory_space_constraint(x, kept[space]) for space, x in inputs]
    shapes = [kept[space](dims, dtype) for space, dims, dtype in outputs]
    return pl.pallas_call(
        kernel,
        out_shape=shapes,
        in_specs=[SPACES[space] for space, _ in inputs],
        out_specs=[SPACES[space] for space, _, _ in outputs],
        scratch_shapes=list(scratch),
        compiler_params=pltpu.CompilerParams(vmem_limit_bytes=limit << 20),
        name=name,
    )(*arrays)


def body(
    column_state, mixing_rate, neighbours, assignment, substeps, cloud_state, level_map, saturation
):
    col_count = lax.axis_size("col")
    sec_count = lax.axis_size("sec")
    count, width = column_state.shape
    cloud_levels, levels = level_map.shape
    _, fields, _, columns, slots = cloud_state.shape
    elements = count // 4
    capacity = slots // col_count
    padded = -(-capacity // 8) * 8
    half = -(-capacity // 2)
    held = -(-half // 8) * 8
    block = col_count * padded
    clouds = (sec_count - 1) * col_count
    segments, used, rows = segments_of(slots, cloud_levels)
    mapped = LANES * len(segments)
    mixing = mixing_rate.reshape(1, width)
    state = cloud_state[0]
    dma = pltpu.SemaphoreType.DMA

    def wide(*lead):
        return pltpu.VMEM((*lead, rows, columns, LANES), F32)

    hosts = dict(padded=padded, clouds=clouds)
    places_in = [
        ("auto", column_state),
        ("auto", mixing),
        ("auto", neighbours.T),
        ("auto", assignment.reshape(1, count)),
    ]
    outgoing, _ = call(
        functools.partial(host_kernel, **hosts),
        "host",
        places_in + [("auto", substeps.reshape(1, count)), ("auto", level_map)],
        [("auto", (col_count, padded + elements, width), F32), ("near", (width, width), F32)],
    )
    received = lax.all_to_all(outgoing, "col", split_axis=0, concat_axis=0, tiled=True)
    base, weights, homes, fold, unfold = call(
        functools.partial(aside_kernel, col_count=col_count, half=half, held=held, **hosts),
        "aside",
        places_in + [("auto", level_map)],
        [
            ("auto", (count, width), F32),
            ("auto", (count, 3 * elements), BF16),
            ("auto", (count, LANES), F32),
            ("auto", (width, width), F32),
            ("auto", (width, width), F32),
        ],
    )
    moved, cloud_means, limits, energy = call(
        functools.partial(prepare_kernel, segments=segments),
        "prepare",
        [("far", state), ("auto", saturation.reshape(1, cloud_levels))],
        [
            ("near", (used, columns, LANES), F32),
            ("near", (fields, rows, LANES), F32),
            ("near", (rows, LANES), F32),
            ("far", (used, columns, LANES), F32),
        ],
        scratch=[
            pltpu.VMEM(state.shape, BF16),
            wide(),
            pltpu.VMEM((rows * 8, LANES), F32),
            pltpu.VMEM((max(s.groups * s.steps for s in segments), LANES), F32),
            pltpu.VMEM((used, columns, LANES), F32),
            dma((fields,)),
            dma(()),
        ],
        limit=16,
    )
    water, spill, flats, back = call(
        functools.partial(
            water_kernel,
            segments=segments,
            capacity=capacity,
            padded=padded,
            stride=levels,
            levels=cloud_levels,
            neighbours=neighbours.shape[1],
        ),
        "water",
        [
            ("near", received),
            ("near", moved),
            ("near", cloud_means),
            ("near", limits),
            ("far", fold),
            ("far", unfold),
        ],
        [
            ("far", (rows, columns, LANES), F32),
            ("far", (MAX_SUB - 1, rows, columns, LANES), F32),
            ("far", (MAX_SUB + 3, rows, LANES), F32),
            ("far", (sec_count, col_count, half, width), F32),
        ],
        scratch=[
            pltpu.VMEM((width, width), F32),
            pltpu.VMEM((width, width), F32),
            wide(),
            wide(),
            wide(MAX_SUB - 1),
            pltpu.VMEM((MAX_SUB + 3, rows, LANES), F32),
            pltpu.VMEM((fields, rows, LANES), F32),
            pltpu.VMEM((fields, rows, LANES), F32),
            pltpu.VMEM((rows, LANES), F32),
            pltpu.VMEM((rows, LANES), F32),
            pltpu.VMEM((rows * 8, LANES), F32),
            pltpu.VMEM((width, mapped), F32),
            pltpu.VMEM((2, col_count, half, width), F32),
            dma((2,)),
            dma((MAX_SUB - 1,)),
            dma(()),
            dma(()),
            dma((sec_count,)),
        ],
        limit=24,
    )
    returned = lax.all_to_all(
        back.reshape(sec_count * col_count, half, width),
        ("sec", "col"),
        split_axis=0,
        concat_axis=0,
        tiled=True,
    )
    new_block, advanced, places = call(
        functools.partial(energy_kernel, segments=segments, padded=padded),
        "energy",
        [
            ("far", state),
            ("far", energy),
            ("far", water),
            ("far", spill),
            ("far", flats),
            ("far", base),
            ("far", weights),
            ("far", mixing),
            ("far", homes),
            ("near", received),
        ],
        [
            ("far", state.shape, BF16),
            ("near", (count, width), F32),
            ("near", (count, LANES), F32),
        ],
        scratch=[
            pltpu.VMEM(state.shape, BF16),
            pltpu.VMEM((used, columns, LANES), F32),
            wide(),
            wide(MAX_SUB),
            pltpu.VMEM((MAX_SUB + 3, rows, LANES), F32),
            pltpu.VMEM((count, width), F32),
            pltpu.VMEM((count, 3 * elements), BF16),
            pltpu.VMEM((1, width), F32),
            pltpu.VMEM(state.shape, BF16),
            wide(),
            wide(),
            wide(),
            dma((fields,)),
            dma((7,)),
            dma((MAX_SUB - 1,)),
            dma((2 * fields,)),
        ],
        limit=32,
    )
    returned, advanced = lax.optimization_barrier((returned, advanced))
    pairs = [(i, i ^ 1) for i in range(sec_count)]
    partner = lax.ppermute(returned, "sec", pairs)
    (new_columns,) = call(
        functools.partial(final_kernel, levels=levels, idle=col_count, held=held),
        "final",
        [("near", advanced), ("near", places), ("near", returned), ("near", partner)],
        [("auto", (count, width), F32)],
        scratch=[pltpu.VMEM((2 * clouds * held, width), F32)],
    )
    return new_columns, new_block[None]


def solution(mesh):
    in_specs = (
        P("col", None),
        P(),
        P("col", None),
        P("col", None),
        P("col"),
        P("sec", None, None, None, "col"),
        P(),
        P(),
    )
    out_specs = (P("col", None), P("sec", None, None, None, "col"))
    return jax.shard_map(body, mesh=mesh, in_specs=in_specs, out_specs=out_specs, check_vma=False)
```

```python
import functools

import jax
import jax.numpy as jnp
from jax import lax
from jax.experimental import pallas as pl
from jax.experimental.pallas import tpu as pltpu
from jax.sharding import PartitionSpec as P

MAX_SUB = 4
RELAX = 0.25
HORIZ = 0.12
VERTIC = 0.1
LATENT = 2.5
VMIX = 0.2
HIGH = lax.Precision.HIGHEST
LANES = 128
F32 = jnp.float32
BF16 = jnp.bfloat16
STEP = 10
SHRINK = 1.0 / LATENT
I32 = jnp.int32


def iota(shape, dim):
    return lax.broadcasted_iota(I32, shape, dim)


def mm(a, b, contract, precision=HIGH):
    return lax.dot_general(
        a, b, (contract, ((), ())), precision=precision, preferred_element_type=F32
    )


NN = ((1,), (0,))
NT = ((1,), (1,))
TN = ((0,), (0,))


def divided(value, by):
    return jnp.floor((value.astype(F32) + 0.5) * (1.0 / by)).astype(I32)


def split(values):
    high = values.astype(BF16)
    rest = values - high.astype(F32)
    middle = rest.astype(BF16)
    low = (rest - middle.astype(F32)).astype(BF16)
    return low, middle, high


def select(picks, values, contract, swap=False):
    total = None
    for part in split(values):
        a, b = (part, picks) if swap else (picks, part)
        term = lax.dot_general(a, b, (contract, ((), ())), preferred_element_type=F32)
        total = term if total is None else total + term
    return total


def product(a, b, contract):
    (al, am, ah), (bl, bm, bh) = split(a), split(b)
    total = None
    for x, y in ((al, bh), (ah, bl), (am, bm), (am, bh), (ah, bm), (ah, bh)):
        term = lax.dot_general(x, y, (contract, ((), ())), preferred_element_type=F32)
        total = term if total is None else total + term
    return total


def vertical_mix(values, levels):
    upper = jnp.concatenate([values[1:levels], values[levels - 1 : levels]], axis=0)
    lower = jnp.concatenate([values[0:1], values[0 : levels - 1]], axis=0)
    inner = values[0:levels]
    return inner + VERTIC * (upper + lower - 2.0 * inner)


def element_of_row(rows):
    elements = rows // 4
    hit = divided(iota((rows, elements), 0), 4) == iota((rows, elements), 1)
    return jnp.where(hit, 1.0, 0.0).astype(BF16)


def element_means(columns_ref):
    elements = columns_ref.shape[0] // 4
    total = columns_ref[pl.ds(0, elements, stride=4), :]
    for k in range(1, 4):
        total = total + columns_ref[pl.ds(k, elements, stride=4), :]
    return 0.25 * total


def own_part(values, means, mixing, levels):
    rows, width = values.shape
    lane = iota((rows, width), 1)
    level = lane - levels * divided(lane, levels)
    upper = jnp.where(level == levels - 1, values, pltpu.roll(values, width - 1, 1))
    lower = jnp.where(level == 0, values, pltpu.roll(values, 1, 1))
    mean = select(element_of_row(rows), means, NN)
    return values - (4.0 * mixing) * mean + VMIX * (upper + lower - 2.0 * values)


def joined_means(mine_ref, other_ref, share, order):
    first = lax.axis_index("sec") % 2 == 0
    parts = []
    for j in order:
        mine, other = mine_ref[j, :share, :], other_ref[j, :share, :]
        parts += [jnp.where(first, mine, other), jnp.where(first, other, mine)]
    return jnp.concatenate(parts, axis=0)


def slots_of(targets, col_count, padded, clouds):
    rows = targets.shape[1]
    onehot = jnp.where(iota((clouds, rows), 0) == targets, 1.0, 0.0)
    before = jnp.where(iota((rows, rows), 0) < iota((rows, rows), 1), 1.0, 0.0)
    running = mm(onehot.astype(BF16), before.astype(BF16), NN, None)
    ranks = jnp.sum(running * onehot, axis=0, keepdims=True).astype(I32)
    owner = divided(targets, col_count)
    return owner, (targets - owner * col_count) * padded + ranks


def blocked(ref, value, levels):
    ref[...] = jnp.zeros_like(ref)
    for f in range(ref.shape[0] // levels):
        ref[f * levels : f * levels + value.shape[0], f * levels : (f + 1) * levels] = value


def host_kernel(
    columns_ref,
    mixing_ref,
    neighbours_ref,
    targets_ref,
    substeps_ref,
    map_ref,
    out_ref,
    fold_ref,
    *,
    padded,
    clouds,
):
    rows, width = columns_ref.shape
    cloud_levels, levels = map_ref.shape
    col_count = out_ref.shape[0]
    block = col_count * padded
    means = element_means(columns_ref)
    share = means.shape[0] // 2
    section = lax.axis_index("sec")
    part = jnp.where(section % 2 == 0, means[:share], means[share:])
    for c in range(col_count):
        out_ref[c, :share, :] = part
    blocked(fold_ref, RELAX * vertical_mix(map_ref[...], cloud_levels), levels)
    owner, slot = slots_of(targets_ref[...], col_count, padded, clouds)
    mine = jnp.where(owner + 1 == section, slot, -1)
    pack = jnp.where(iota((block, rows), 0) == mine, 1.0, 0.0).astype(BF16)
    base = own_part(columns_ref[...], means, mixing_ref[...], levels)
    count = neighbours_ref.shape[0]
    ids = select(element_of_row(rows), neighbours_ref[...].astype(F32), NT, swap=True)
    extras = jnp.concatenate(
        [
            jnp.zeros((cloud_levels, rows), F32),
            ids,
            jnp.zeros((levels - 1 - cloud_levels - count, rows), F32),
            substeps_ref[...].astype(F32),
            jnp.zeros((width - levels, rows), F32),
        ],
        axis=0,
    )
    sent = product(select(pack, base, NN), fold_ref[...], NT) + select(pack, extras, NT)
    capacity = out_ref.shape[1] - share
    for c in range(col_count):
        out_ref[c, share:, :] = sent[c * padded : c * padded + capacity]


def aside(
    columns_ref,
    mixing_ref,
    neighbours_ref,
    targets_ref,
    map_ref,
    base_ref,
    weights_ref,
    homes_ref,
    fold_ref,
    unfold_ref,
    col_count,
    padded,
    clouds,
    half,
    held,
):
    rows, width = columns_ref.shape
    cloud_levels, levels = map_ref.shape
    elements = rows // 4
    position = lax.axis_index("col")
    base_ref[...] = own_part(
        columns_ref[...], element_means(columns_ref), mixing_ref[...], levels
    )
    near = neighbours_ref[...] - (position - 1) * elements
    near = jnp.where(near < 0, near + elements * col_count, near)
    near = jnp.where(near >= elements * col_count, near - elements * col_count, near)
    window = iota((3 * elements, elements), 0)
    picks = jnp.zeros((3 * elements, elements), F32)
    for k in range(near.shape[0]):
        picks = picks + jnp.where(window == near[k : k + 1, :], 1.0, 0.0)
    weights_ref[...] = mm(element_of_row(rows), picks.astype(BF16), NT, None).astype(BF16)
    owner, slot = slots_of(targets_ref[...], col_count, padded, clouds)
    place = divided(slot, padded)
    rank = slot - place * padded
    upper = jnp.where(rank >= half, 1, 0)
    parity = lax.axis_index("sec") % 2
    cloud = owner * col_count + place + jnp.where(upper == parity, 0, clouds)
    everywhere = (cloud * held + rank - half * upper).astype(F32)
    identity = jnp.where(iota((rows, rows), 0) == iota((rows, rows), 1), 1.0, 0.0)
    homes_ref[...] = select(
        identity.astype(BF16), jnp.broadcast_to(everywhere, (LANES, rows)), NT
    )
    blocked(fold_ref, RELAX * vertical_mix(map_ref[...], cloud_levels), levels)
    fold_ref[...] = fold_ref[...] * mixing_ref[...]
    blocked(unfold_ref, map_ref[...], levels)


class Segment:
    def __init__(self, lane0, width, levels, begin):
        self.lane0, self.width, self.begin, self.levels = lane0, width, begin, levels
        self.steps = -(-levels // (LANES // width))
        self.groups = -(-levels // self.steps)
        self.missing = self.groups * self.steps - levels
        self.blocks = -(-self.steps // STEP)
        self.rows = (begin + 1, begin + 1 + self.steps)

    def group_steps(self, g):
        return self.steps - (self.missing if g == self.groups - 1 else 0)


def segments_of(slots, levels):
    segments, begin = [], 0
    for lane0 in range(0, slots, LANES):
        segments.append(Segment(lane0, min(LANES, slots - lane0), levels, begin))
        begin += segments[-1].steps + 2
    rows = max([begin] + [s.begin + 2 + s.blocks * STEP for s in segments])
    return segments, rows, -(-rows // 8) * 8


def fill_spare(segments, load, store):
    def turned(value, shift):
        tall = jnp.broadcast_to(value, (8, LANES)) if value.shape[0] == 1 else value
        return pltpu.roll(tall, shift % LANES, 1)[: value.shape[0]]

    for s in segments:
        if s.missing:
            row = s.rows[1] - s.missing
            value = load(row - 1)
            lane = iota(value.shape, 1)
            store(row, jnp.where(lane >= (s.groups - 1) * s.width, value, load(row)))
        first, last = load(s.rows[0]), load(s.rows[1] - 1)
        before, after = first, last
        if s.groups > 1:
            lane = iota(first.shape, 1)
            before = jnp.where(lane < s.width, first, turned(last, s.width))
            after = jnp.where(lane < (s.groups - 1) * s.width, turned(first, -s.width), last)
        store(s.begin, before)
        store(s.rows[1], after)


def fill_wide(segments, ref):
    def store(row, value):
        ref[row] = value

    fill_spare(segments, lambda row: ref[row], store)


def fill_flat(segments, ref):
    def store(row, value):
        ref[row : row + 1, :] = value

    fill_spare(segments, lambda row: ref[row : row + 1, :], store)


def linear(below, here, above):
    east = [pltpu.roll(here[3], 1, 0), here[0], here[1], here[2]]
    west = [here[1], here[2], here[3], pltpu.roll(here[0], 7, 0)]
    keep = (1.0 - 2.0 * HORIZ - 2.0 * VERTIC) / VERTIC
    return [
        (below[j] + above[j]) + ((HORIZ / VERTIC) * (east[j] + west[j]) + keep * here[j])
        for j in range(4)
    ]


def groups(ref, index):
    return [ref[index + (pl.ds(8 * j, 8),)] for j in range(4)]


def strided(ref, row):
    return [ref[row, pl.ds(j, 8, stride=4), :] for j in range(4)]


def sweep(segment, load, work):
    def block(i, carry):
        row = segment.begin + i * STEP
        held = [load(row), load(row + 1)]
        for k in range(STEP):
            held.append(load(row + k + 2))
            work(row + k + 1, held[k], held[k + 1], held[k + 2])
        return carry

    lax.fori_loop(0, segment.blocks, block, 0)


def each(count, size, work):
    size = min(size, count)

    def run(first):
        for k in range(size):
            work(first + k)

    if count // size:
        lax.fori_loop(0, count // size, lambda i, c: (run(i * size), c)[1], 0)
    if count % size:
        run(count - size)


def widen(state_ref, natural_ref, segments, scale):
    levels, columns, _ = state_ref.shape
    for s in segments:
        at = slice(s.lane0, s.lane0 + s.width)

        def one(k):
            parts = []
            for g in range(s.groups):
                level = jnp.minimum(g * s.steps + k, levels - 1)
                parts.append(state_ref[level, :, at].astype(F32))
            spare = LANES - s.groups * s.width
            if spare:
                parts.append(jnp.zeros((columns, spare), F32))
            value = jnp.concatenate(parts, axis=1) if len(parts) > 1 else parts[0]
            natural_ref[s.begin + 1 + k] = scale * value if scale != 1.0 else value

        each(s.steps, STEP, one)


def folded_sums(sums_ref, columns):
    rows = sums_ref.shape[0] // 8
    total = sums_ref[pl.ds(0, rows, stride=8), :]
    for k in range(1, 8):
        total = total + sums_ref[pl.ds(k, rows, stride=8), :]
    return total * (1.0 / columns)


def slab(row):
    return pl.ds(pl.multiple_of(row * 8, 8), 8)


def spread_row(ref, row):
    return jnp.broadcast_to(ref[pl.ds(row, 1), :], (8, LANES))


def turn(value, shift):
    if not shift:
        return value
    height = value.shape[0]
    tall = -(-height // 8) * 8
    if tall != height:
        fill = jnp.zeros((tall - height, LANES), F32)
        value = jnp.concatenate([value, fill], axis=0)
    return pltpu.roll(value, shift % LANES, 1)[:height]


def each(count, size, work):
    size = min(size, count)

    def run(first):
        for k in range(size):
            work(first + k)

    if count // size:
        lax.fori_loop(0, count // size, lambda i, c: (run(i * size), c)[1], 0)
    if count % size:
        run(count - size)


def widen(state_ref, natural_ref, segments, scale):
    levels, columns, _ = state_ref.shape
    for s in segments:
        at = slice(s.lane0, s.lane0 + s.width)

        def one(k):
            parts = []
            for g in range(s.groups):
                level = jnp.minimum(g * s.steps + k, levels - 1)
                parts.append(state_ref[level, :, at].astype(F32))
            spare = LANES - s.groups * s.width
            if spare:
                parts.append(jnp.zeros((columns, spare), F32))
            value = jnp.concatenate(parts, axis=1) if len(parts) > 1 else parts[0]
            natural_ref[s.begin + 1 + k] = scale * value if scale != 1.0 else value

        each(s.steps, STEP, one)


def folded_sums(sums_ref, columns):
    rows = sums_ref.shape[0] // 8
    total = sums_ref[pl.ds(0, rows, stride=8), :]
    for k in range(1, 8):
        total = total + sums_ref[pl.ds(k, rows, stride=8), :]
    return total * (1.0 / columns)


def slab(row):
    return pl.ds(pl.multiple_of(row * 8, 8), 8)


def spread_row(ref, row):
    return jnp.broadcast_to(ref[pl.ds(row, 1), :], (8, LANES))


def lane_places(segments):
    return [(s, g) for s in segments for g in range(s.groups)]


def slot_map(segments, block, capacity, padded):
    tiles = []
    for s in segments:
        lane = iota((8, LANES), 1)
        slot = s.lane0 + lane
        row = slot + (padded - capacity) * divided(slot, capacity)
        row = jnp.where(lane < s.width, row, -1)[0:1]
        tiles.append(jnp.where(iota((block, LANES), 0) == row, 1.0, 0.0).astype(BF16))
    return jnp.concatenate(tiles, axis=1)


def prepare_kernel(
    state_ref,
    columns_far,
    mixing_far,
    neighbours_far,
    targets_far,
    map_far,
    saturation_far,
    moved_ref,
    means_ref,
    limits_ref,
    energy_far,
    base_far,
    weights_far,
    homes_far,
    fold_far,
    unfold_far,
    state_buf,
    natural_ref,
    sums_ref,
    flat_ref,
    energy_buf,
    columns_ref,
    mixing_ref,
    neighbours_ref,
    targets_ref,
    map_ref,
    saturation_ref,
    base_ref,
    weights_ref,
    homes_ref,
    fold_ref,
    unfold_ref,
    sems,
    in_sems,
    out_sems,
    *,
    segments,
    **host,
):
    fields, levels, columns, _ = state_ref.shape
    given = (
        (columns_far, columns_ref),
        (mixing_far, mixing_ref),
        (neighbours_far, neighbours_ref),
        (targets_far, targets_ref),
        (map_far, map_ref),
        (saturation_far, saturation_ref),
    )
    starts = [pltpu.make_async_copy(x, y, in_sems.at[i]) for i, (x, y) in enumerate(given)]
    loads = [
        pltpu.make_async_copy(state_ref.at[f], state_buf.at[f], sems.at[f]) for f in range(fields)
    ]
    for copy in starts + loads:
        copy.start()
    made = (
        (base_ref, base_far),
        (weights_ref, weights_far),
        (homes_ref, homes_far),
        (fold_ref, fold_far),
        (unfold_ref, unfold_far),
        (energy_buf, energy_far),
    )
    leaves = [pltpu.make_async_copy(x, y, out_sems.at[i]) for i, (x, y) in enumerate(made)]
    for copy in starts:
        copy.wait()
    tall = flat_ref.shape[0]
    here = iota((tall, levels), 0) == iota((tall, levels), 1)
    diagonal = jnp.where(here, 0.5 * saturation_ref[...], 0.0)
    flat_ref[...] = select(jnp.ones((levels, LANES), BF16), diagonal, NN, swap=True)
    limits_ref[...] = jnp.zeros_like(limits_ref)
    for s in segments:
        lane = iota((s.steps, LANES), 1)
        value = flat_ref[0 : s.steps, :]
        for g in range(1, s.groups):
            other = flat_ref[g * s.steps : (g + 1) * s.steps, :]
            value = jnp.where(lane >= g * s.width, other, value)
        limits_ref[s.rows[0] : s.rows[1], :] = value
    sums_ref[...] = jnp.zeros_like(sums_ref)
    aside(
        columns_ref,
        mixing_ref,
        neighbours_ref,
        targets_ref,
        map_ref,
        base_ref,
        weights_ref,
        homes_ref,
        fold_ref,
        unfold_ref,
        **host,
    )
    for copy in leaves[:5]:
        copy.start()
    for f, scale, target in ((0, SHRINK, energy_buf), (1, 1.0, moved_ref)):
        loads[f].wait()
        widen(state_buf.at[f], natural_ref, segments, scale)
        fill_wide(segments, natural_ref)
        for s in segments:

            def work(row, below, here, above):
                out = linear(below, here, above)
                for j in range(4):
                    target[row, pl.ds(8 * j, 8), :] = out[j]
                sums_ref[slab(row), :] = (here[0] + here[1]) + (here[2] + here[3])

            sweep(s, lambda row: strided(natural_ref, row), work)
        if f == 0:
            leaves[5].start()
        means_ref[f] = folded_sums(sums_ref, columns) * (1.0 / scale)
    for copy in leaves:
        copy.wait()


def water_kernel(
    received_ref,
    other_ref,
    moved_ref,
    means_ref,
    limits_ref,
    fold_far,
    unfold_far,
    water_far,
    spill_far,
    flats_far,
    back_far,
    fold_ref,
    unfold_ref,
    even_ref,
    odd_ref,
    spill_buf,
    flats_ref,
    goal_ref,
    mean_ref,
    shift_ref,
    limit_ref,
    sums_ref,
    change_ref,
    back_ref,
    in_sems,
    spill_sems,
    water_sem,
    flat_sem,
    back_sems,
    *,
    segments,
    capacity,
    padded,
    stride,
    levels,
    neighbours,
):
    rows = means_ref.shape[1]
    columns = even_ref.shape[1]
    loads = [
        pltpu.make_async_copy(fold_far, fold_ref, in_sems.at[0]),
        pltpu.make_async_copy(unfold_far, unfold_ref, in_sems.at[1]),
    ]
    for load in loads:
        load.start()
    hosts = received_ref.shape[0]
    block = hosts * padded
    places = slot_map(segments, block, capacity, padded)
    share = received_ref.shape[1] - capacity
    parts = []
    for j in range(hosts):
        parts.append(received_ref[j, share:, :])
        if padded != capacity:
            parts.append(jnp.zeros((padded - capacity, LANES), F32))
    sent = jnp.concatenate(parts, axis=0)
    means = joined_means(received_ref, other_ref, share, range(hosts))
    arrived = select(places, sent, TN, swap=True)
    loads[0].wait()
    folded = product(fold_ref[...], means, NT)
    taken = arrived[stride - 1 : stride] > 0.0
    ids = [
        jnp.where(taken, arrived[levels + k : levels + k + 1], -1.0) for k in range(neighbours)
    ]
    chunk = min(256, means.shape[0])
    for first in range(0, means.shape[0], chunk):
        element = (iota((chunk, arrived.shape[1]), 0) + first).astype(F32)
        wanted = jnp.where(element == ids[0], 1.0, 0.0)
        for k in range(1, neighbours):
            wanted = wanted + jnp.where(element == ids[k], 1.0, 0.0)
        part = folded[:, first : first + chunk]
        arrived = arrived + select(wanted.astype(BF16), part, NN, swap=True)
    goal_ref[...] = jnp.zeros_like(goal_ref)
    flats_ref[...] = jnp.zeros_like(flats_ref)
    sums_ref[...] = jnp.zeros_like(sums_ref)
    counts = flats_ref.at[MAX_SUB + 2]
    for t, s in enumerate(segments):
        lanes = slice(t * LANES, (t + 1) * LANES)
        count = None
        for g in range(s.groups):
            number = s.group_steps(g)
            at = slice(s.rows[0], s.rows[0] + number)
            for f in range(2):
                first = f * stride + g * s.steps
                part = turn(arrived[first : first + number, lanes], g * s.width)
                goal_ref[f, at, :] = goal_ref[f, at, :] + part if g else part
            part = turn(arrived[stride - 1 : stride, lanes], g * s.width)
            count = part if count is None else count + part
        counts[s.rows[0] : s.rows[1], :] = jnp.broadcast_to(count, (s.steps, LANES))
    for f in range(2):
        mean_ref[f] = means_ref[f]
    copies = []
    source, target = None, even_ref
    for n in range(MAX_SUB):
        scale = 10.0 ** (n + 1)
        last = n + 1 == MAX_SUB
        expected = []
        for f in range(2):
            fill_flat(segments, mean_ref.at[f])
            mean = mean_ref[f]
            mixed = mean + VERTIC * (
                pltpu.roll(mean, 1, 0) + pltpu.roll(mean, rows - 1, 0) - 2.0 * mean
            )
            offset = goal_ref[f] - RELAX * mixed
            expected.append(mixed + offset)
            if f == 1:
                shift_ref[...] = scale * offset
            else:
                flats_ref[n] = (scale * SHRINK) * offset
        limit_ref[...] = scale * limits_ref[...]
        if last:
            flats_ref[MAX_SUB] = shift_ref[...]
            flats_ref[MAX_SUB + 1] = limit_ref[...]
            copies.append(pltpu.make_async_copy(flats_ref, flats_far, flat_sem))
            copies[-1].start()
        for s in segments:
            active = spread_row(counts, s.rows[0]) > float(n)

            def finish(row, lin, old):
                shift = spread_row(shift_ref, row)
                limit = spread_row(limit_ref, row)
                total = None
                for j in range(4):
                    v = lin[j] + shift
                    c = jnp.maximum(0.5 * v - limit, 0.0)
                    total = c if total is None else total + c
                    if last:
                        continue
                    u = v - c
                    if old is not None:
                        u = jnp.where(active, u, old[j])
                    spill_buf[n, row, pl.ds(8 * j, 8), :] = c
                    target[row, pl.ds(8 * j, 8), :] = u
                sums_ref[slab(row), :] = total

            if n == 0:

                def block(i, carry):
                    for k in range(STEP):
                        row = s.begin + 1 + i * STEP + k
                        finish(row, groups(moved_ref, (row,)), None)
                    return carry

                lax.fori_loop(0, s.blocks, block, 0)
            else:

                def work(row, below, here, above):
                    finish(row, linear(below, here, above), here)

                sweep(s, lambda row: groups(source, (row,)), work)
        if not last:
            copies.append(
                pltpu.make_async_copy(spill_buf.at[n], spill_far.at[n], spill_sems.at[n])
            )
            copies[-1].start()
            fill_wide(segments, target)
            source, target = target, (odd_ref if target is even_ref else even_ref)
        if n + 2 == MAX_SUB:
            copies.append(pltpu.make_async_copy(source, water_far, water_sem))
            copies[-1].start()
        spilled = folded_sums(sums_ref, columns) * (1.0 / scale)
        step = [expected[0] + LATENT * spilled, expected[1] - spilled]
        keep = counts[...] > float(n)
        for f in range(2):
            mean_ref[f] = jnp.where(keep, step[f], mean_ref[f])
    change_ref[...] = jnp.zeros_like(change_ref)
    for f in range(2):
        change = mean_ref[f] - means_ref[f]
        for t, s in enumerate(segments):
            for g in range(s.groups):
                first, number = f * stride + g * s.steps, s.group_steps(g)
                part = turn(change[s.rows[0] : s.rows[0] + number], -g * s.width)
                change_ref[first : first + number, t * LANES : (t + 1) * LANES] = part
    spread = select(places, change_ref[...], NT)
    loads[1].wait()
    back = product(spread, unfold_ref[...], NN)
    half = back_ref.shape[2]
    for h in range(2):
        for j in range(hosts):
            first = j * padded + h * half
            back_ref[h, j] = back[first : first + half]
    for i in range(back_far.shape[0]):
        copies.append(pltpu.make_async_copy(back_ref.at[i % 2], back_far.at[i], back_sems.at[i]))
        copies[-1].start()
    for copy in copies:
        copy.wait()


def energy_kernel(
    state_ref,
    energy_far,
    water_far,
    spill_far,
    flats_far,
    base_far,
    weights_far,
    mixing_far,
    homes_far,
    received_ref,
    other_ref,
    out_ref,
    advanced_ref,
    places_ref,
    state_buf,
    energy_buf,
    water_buf,
    spill_buf,
    flats_ref,
    base_ref,
    weights_ref,
    mixing_ref,
    out_buf,
    even_ref,
    odd_ref,
    natural_ref,
    state_sems,
    in_sems,
    spill_sems,
    out_sems,
    *,
    segments,
    share,
):
    fields, levels, columns, _ = state_ref.shape
    final = MAX_SUB - 1
    pairs = (
        (flats_far, flats_ref),
        (base_far, base_ref),
        (weights_far, weights_ref),
        (mixing_far, mixing_ref),
        (water_far, water_buf),
        (energy_far, energy_buf),
        (homes_far, places_ref),
    )
    loads = [pltpu.make_async_copy(x, y, in_sems.at[i]) for i, (x, y) in enumerate(pairs)]
    flats, bases, shares, mixings, waters, first, homes = loads
    states = [
        pltpu.make_async_copy(state_ref.at[f], state_buf.at[f], state_sems.at[f])
        for f in range(fields)
    ]
    spills = [
        pltpu.make_async_copy(spill_far.at[n], spill_buf.at[n], spill_sems.at[n])
        for n in range(final)
    ]
    for copy in loads[:5] + [states[1], first] + spills + [states[0], homes]:
        copy.start()
    cut = -(-levels // 2)
    spans = ((0, cut), (cut, levels - cut))

    def leave(f, part):
        at = pl.ds(*spans[part])
        return pltpu.make_async_copy(
            out_buf.at[f, at], out_ref.at[f, at], out_sems.at[2 * f + part]
        )

    counts = flats_ref.at[MAX_SUB + 2]

    def finish_field(f, found):
        for s in segments[::-1]:
            count = spread_row(counts, s.rows[0])
            back = jnp.zeros((8, LANES), F32)
            for n in range(1, MAX_SUB + 1):
                scale = 10.0**-n * (LATENT if f == 0 else 1.0)
                back = jnp.where(count == float(n), scale, back)
            at = slice(s.lane0, s.lane0 + s.width)
            held = jnp.broadcast_to(count[0:1, : s.width], (columns, s.width)) > 0.0

            def permute(k):
                row = s.begin + 1 + k
                value = groups(found, (row,))
                for j in range(4):
                    natural_ref[row, pl.ds(j, 8, stride=4), :] = value[j] * back

            def narrow(g, k):
                level = g * s.steps + k
                lanes = slice(g * s.width, (g + 1) * s.width)
                old = state_buf[f, level, :, at].astype(F32)
                value = jnp.where(held, natural_ref[s.begin + 1 + k, :, lanes], old)
                out_buf[f, level, :, at] = value.astype(BF16)

            each(s.steps, STEP, permute)
            if s is segments[0] and s.groups == 1:
                for part, (begin, number) in enumerate(spans):
                    each(number, STEP, lambda k: narrow(0, begin + k))
                    leave(f, part).start()
            else:
                for g in range(s.groups):
                    each(s.group_steps(g), STEP, lambda k: narrow(g, k))
        if segments[0].groups > 1:
            for part in range(2):
                leave(f, part).start()

    bases.wait()
    shares.wait()
    mixings.wait()
    hosts = received_ref.shape[0]
    position = lax.axis_index("col")
    around = [jnp.where(position == 0, hosts - 1, position - 1), position]
    around.append(jnp.where(position == hosts - 1, 0, position + 1))
    means = joined_means(received_ref, other_ref, share, around)
    advanced_ref[...] = base_ref[...] + mixing_ref[...] * select(weights_ref[...], means, NN)
    flats.wait()
    waters.wait()
    for s in segments:
        active = spread_row(counts, s.rows[0]) > float(final)

        def last(row, below, here, above):
            water = linear(below, here, above)
            push = spread_row(flats_ref.at[MAX_SUB], row)
            limit = spread_row(flats_ref.at[MAX_SUB + 1], row)
            for j in range(4):
                v = water[j] + push
                c = jnp.maximum(0.5 * v - limit, 0.0)
                spill_buf[final, row, pl.ds(8 * j, 8), :] = c
                even_ref[row, pl.ds(8 * j, 8), :] = jnp.where(active, v - c, here[j])

        sweep(s, lambda row: groups(water_buf, (row,)), last)
    states[1].wait()
    finish_field(1, even_ref)
    first.wait()
    source, target = None, odd_ref
    for n in range(MAX_SUB):
        if n < final:
            spills[n].wait()
        for s in segments:
            active = spread_row(counts, s.rows[0]) > float(n)

            def start(i, carry):
                for k in range(STEP):
                    row = s.begin + 1 + i * STEP + k
                    shift = spread_row(flats_ref.at[n], row)
                    lin, spill = groups(energy_buf, (row,)), groups(spill_buf, (n, row))
                    for j in range(4):
                        target[row, pl.ds(8 * j, 8), :] = (lin[j] + shift) + spill[j]
                return carry

            def work(row, below, here, above):
                shift = spread_row(flats_ref.at[n], row)
                lin = linear(below, here, above)
                spill = groups(spill_buf, (n, row))
                for j in range(4):
                    u = (lin[j] + shift) + spill[j]
                    target[row, pl.ds(8 * j, 8), :] = jnp.where(active, u, here[j])

            if n == 0:
                lax.fori_loop(0, s.blocks, start, 0)
            else:
                sweep(s, lambda row: groups(source, (row,)), work)
        if n < final:
            fill_wide(segments, target)
        source, target = target, (odd_ref if target is even_ref else even_ref)
    states[0].wait()
    finish_field(0, source)
    homes.wait()
    for f in range(fields):
        for part in range(2):
            leave(f, part).wait()


def final_kernel(
    advanced_ref, places_ref, mine_ref, other_ref, out_ref, table_ref, *, levels, idle, held
):
    rows, width = advanced_ref.shape
    sources, half, _ = mine_ref.shape
    clouds = sources - idle
    if half != held:
        table_ref[...] = jnp.zeros_like(table_ref)
    for i, ref in enumerate((mine_ref, other_ref)):
        for j in range(clouds):
            first = (i * clouds + j) * held
            table_ref[first : first + half, :] = ref[idle + j]
    place = places_ref[:, :1].astype(I32)
    picks = jnp.where(iota((rows, table_ref.shape[0]), 1) == place, 1.0, 0.0)
    summed = advanced_ref[...] + select(picks.astype(BF16), table_ref[...], NN)
    water = divided(iota((rows, width), 1), levels) == 1
    out_ref[...] = jnp.where(water, jnp.maximum(summed, 0.0), summed)


SPACES = dict(
    auto=pl.BlockSpec(memory_space=pltpu.VMEM),
    near=pl.BlockSpec(memory_space=pltpu.VMEM),
    far=pl.BlockSpec(memory_space=pl.ANY),
    scalar=pl.BlockSpec(memory_space=pltpu.SMEM),
)


def call(kernel, name, inputs, outputs, scratch=(), limit=8):
    kept = dict(near=pltpu.VMEM, auto=pltpu.HBM, far=pltpu.HBM, scalar=pltpu.HBM)
    arrays = [pltpu.with_memory_space_constraint(x, kept[space]) for space, x in inputs]
    shapes = [kept[space](dims, dtype) for space, dims, dtype in outputs]
    return pl.pallas_call(
        kernel,
        out_shape=shapes,
        in_specs=[SPACES[space] for space, _ in inputs],
        out_specs=[SPACES[space] for space, _, _ in outputs],
        scratch_shapes=list(scratch),
        compiler_params=pltpu.CompilerParams(vmem_limit_bytes=limit << 20),
        name=name,
    )(*arrays)


def body(
    column_state, mixing_rate, neighbours, assignment, substeps, cloud_state, level_map, saturation
):
    col_count = lax.axis_size("col")
    sec_count = lax.axis_size("sec")
    count, width = column_state.shape
    cloud_levels, levels = level_map.shape
    _, fields, _, columns, slots = cloud_state.shape
    elements = count // 4
    capacity = slots // col_count
    padded = -(-capacity // 8) * 8
    half = -(-capacity // 2)
    held = -(-half // 8) * 8
    block = col_count * padded
    clouds = (sec_count - 1) * col_count
    segments, used, rows = segments_of(slots, cloud_levels)
    mapped = LANES * len(segments)
    mixing = mixing_rate.reshape(1, width)
    state = cloud_state[0]
    dma = pltpu.SemaphoreType.DMA

    def wide(*lead):
        return pltpu.VMEM((*lead, rows, columns, LANES), F32)

    hosts = dict(padded=padded, clouds=clouds)
    places_in = [
        ("auto", column_state),
        ("auto", mixing),
        ("auto", neighbours.T),
        ("auto", assignment.reshape(1, count)),
    ]
    outgoing, _ = call(
        functools.partial(host_kernel, **hosts),
        "host",
        places_in + [("auto", substeps.reshape(1, count)), ("auto", level_map)],
        [("auto", (col_count, elements // 2 + capacity, width), F32), ("near", (width, width), F32)],
    )
    received = lax.all_to_all(outgoing, "col", split_axis=0, concat_axis=0, tiled=True)
    moved, cloud_means, limits, energy, base, weights, homes, fold, unfold = call(
        functools.partial(
            prepare_kernel,
            segments=segments,
            col_count=col_count,
            half=half,
            held=held,
            **hosts,
        ),
        "prepare",
        [("far", state)]
        + [("far", x) for _, x in places_in]
        + [("far", level_map), ("far", saturation.reshape(1, cloud_levels))],
        [
            ("near", (used, columns, LANES), F32),
            ("near", (fields, rows, LANES), F32),
            ("near", (rows, LANES), F32),
            ("far", (used, columns, LANES), F32),
            ("far", (count, width), F32),
            ("far", (count, 3 * elements), BF16),
            ("far", (count, LANES), F32),
            ("far", (width, width), F32),
            ("far", (width, width), F32),
        ],
        scratch=[
            pltpu.VMEM(state.shape, BF16),
            wide(),
            pltpu.VMEM((rows * 8, LANES), F32),
            pltpu.VMEM((max(s.groups * s.steps for s in segments), LANES), F32),
            pltpu.VMEM((used, columns, LANES), F32),
            pltpu.VMEM((count, width), F32),
            pltpu.VMEM((1, width), F32),
            pltpu.VMEM((neighbours.shape[1], elements), I32),
            pltpu.VMEM((1, count), I32),
            pltpu.VMEM((cloud_levels, levels), F32),
            pltpu.VMEM((1, cloud_levels), F32),
            pltpu.VMEM((count, width), F32),
            pltpu.VMEM((count, 3 * elements), BF16),
            pltpu.VMEM((count, LANES), F32),
            pltpu.VMEM((width, width), F32),
            pltpu.VMEM((width, width), F32),
            dma((fields,)),
            dma((6,)),
            dma((6,)),
        ],
        limit=16,
    )
    received, moved, base = lax.optimization_barrier((received, moved, base))
    pairs = [(i, i ^ 1) for i in range(sec_count)]
    other = lax.ppermute(received, "sec", pairs)
    water, spill, flats, back = call(
        functools.partial(
            water_kernel,
            segments=segments,
            capacity=capacity,
            padded=padded,
            stride=levels,
            levels=cloud_levels,
            neighbours=neighbours.shape[1],
        ),
        "water",
        [
            ("near", received),
            ("near", other),
            ("near", moved),
            ("near", cloud_means),
            ("near", limits),
            ("far", fold),
            ("far", unfold),
        ],
        [
            ("far", (rows, columns, LANES), F32),
            ("far", (MAX_SUB - 1, rows, columns, LANES), F32),
            ("far", (MAX_SUB + 3, rows, LANES), F32),
            ("far", (sec_count, col_count, half, width), F32),
        ],
        scratch=[
            pltpu.VMEM((width, width), F32),
            pltpu.VMEM((width, width), F32),
            wide(),
            wide(),
            wide(MAX_SUB - 1),
            pltpu.VMEM((MAX_SUB + 3, rows, LANES), F32),
            pltpu.VMEM((fields, rows, LANES), F32),
            pltpu.VMEM((fields, rows, LANES), F32),
            pltpu.VMEM((rows, LANES), F32),
            pltpu.VMEM((rows, LANES), F32),
            pltpu.VMEM((rows * 8, LANES), F32),
            pltpu.VMEM((width, mapped), F32),
            pltpu.VMEM((2, col_count, half, width), F32),
            dma((2,)),
            dma((MAX_SUB - 1,)),
            dma(()),
            dma(()),
            dma((sec_count,)),
        ],
        limit=24,
    )
    returned = lax.all_to_all(
        back.reshape(sec_count * col_count, half, width),
        ("sec", "col"),
        split_axis=0,
        concat_axis=0,
        tiled=True,
    )
    new_block, advanced, places = call(
        functools.partial(energy_kernel, segments=segments, share=elements // 2),
        "energy",
        [
            ("far", state),
            ("far", energy),
            ("far", water),
            ("far", spill),
            ("far", flats),
            ("far", base),
            ("far", weights),
            ("far", mixing),
            ("far", homes),
            ("near", received),
            ("near", other),
        ],
        [
            ("far", state.shape, BF16),
            ("near", (count, width), F32),
            ("near", (count, LANES), F32),
        ],
        scratch=[
            pltpu.VMEM(state.shape, BF16),
            pltpu.VMEM((used, columns, LANES), F32),
            wide(),
            wide(MAX_SUB),
            pltpu.VMEM((MAX_SUB + 3, rows, LANES), F32),
            pltpu.VMEM((count, width), F32),
            pltpu.VMEM((count, 3 * elements), BF16),
            pltpu.VMEM((1, width), F32),
            pltpu.VMEM(state.shape, BF16),
            wide(),
            wide(),
            wide(),
            dma((fields,)),
            dma((7,)),
            dma((MAX_SUB - 1,)),
            dma((2 * fields,)),
        ],
        limit=32,
    )
    returned, advanced = lax.optimization_barrier((returned, advanced))
    partner = lax.ppermute(returned, "sec", pairs)
    (new_columns,) = call(
        functools.partial(final_kernel, levels=levels, idle=col_count, held=held),
        "final",
        [("near", advanced), ("near", places), ("near", returned), ("near", partner)],
        [("auto", (count, width), F32)],
        scratch=[pltpu.VMEM((2 * clouds * held, width), F32)],
    )
    return new_columns, new_block[None]


def solution(mesh):
    in_specs = (
        P("col", None),
        P(),
        P("col", None),
        P("col", None),
        P("col"),
        P("sec", None, None, None, "col"),
        P(),
        P(),
    )
    out_specs = (P("col", None), P("sec", None, None, None, "col"))
    return jax.shard_map(body, mesh=mesh, in_specs=in_specs, out_specs=out_specs, check_vma=False)
```

```python
import functools

import jax
import jax.numpy as jnp
from jax import lax
from jax.experimental import pallas as pl
from jax.experimental.pallas import tpu as pltpu
from jax.sharding import PartitionSpec as P

MAX_SUB = 4
RELAX = 0.25
HORIZ = 0.12
VERTIC = 0.1
LATENT = 2.5
VMIX = 0.2
HIGH = lax.Precision.HIGHEST
LANES = 128
F32 = jnp.float32
BF16 = jnp.bfloat16
STEP = 10
SHRINK = 1.0 / LATENT
I32 = jnp.int32


def iota(shape, dim):
    return lax.broadcasted_iota(I32, shape, dim)


def mm(a, b, contract, precision=HIGH):
    return lax.dot_general(
        a, b, (contract, ((), ())), precision=precision, preferred_element_type=F32
    )


NN = ((1,), (0,))
NT = ((1,), (1,))
TN = ((0,), (0,))


def divided(value, by):
    return jnp.floor((value.astype(F32) + 0.5) * (1.0 / by)).astype(I32)


def split(values):
    high = values.astype(BF16)
    rest = values - high.astype(F32)
    middle = rest.astype(BF16)
    low = (rest - middle.astype(F32)).astype(BF16)
    return low, middle, high


def select(picks, values, contract, swap=False):
    total = None
    for part in split(values):
        a, b = (part, picks) if swap else (picks, part)
        term = lax.dot_general(a, b, (contract, ((), ())), preferred_element_type=F32)
        total = term if total is None else total + term
    return total


def product(a, b, contract):
    (al, am, ah), (bl, bm, bh) = split(a), split(b)
    total = None
    for x, y in ((al, bh), (ah, bl), (am, bm), (am, bh), (ah, bm), (ah, bh)):
        term = lax.dot_general(x, y, (contract, ((), ())), preferred_element_type=F32)
        total = term if total is None else total + term
    return total


def vertical_mix(values, levels):
    upper = jnp.concatenate([values[1:levels], values[levels - 1 : levels]], axis=0)
    lower = jnp.concatenate([values[0:1], values[0 : levels - 1]], axis=0)
    inner = values[0:levels]
    return inner + VERTIC * (upper + lower - 2.0 * inner)


def element_of_row(rows):
    elements = rows // 4
    hit = divided(iota((rows, elements), 0), 4) == iota((rows, elements), 1)
    return jnp.where(hit, 1.0, 0.0).astype(BF16)


def element_means(columns_ref):
    elements = columns_ref.shape[0] // 4
    total = columns_ref[pl.ds(0, elements, stride=4), :]
    for k in range(1, 4):
        total = total + columns_ref[pl.ds(k, elements, stride=4), :]
    return 0.25 * total


def own_part(values, means, mixing, levels):
    rows, width = values.shape
    lane = iota((rows, width), 1)
    level = lane - levels * divided(lane, levels)
    upper = jnp.where(level == levels - 1, values, pltpu.roll(values, width - 1, 1))
    lower = jnp.where(level == 0, values, pltpu.roll(values, 1, 1))
    mean = select(element_of_row(rows), means, NN)
    return values - (4.0 * mixing) * mean + VMIX * (upper + lower - 2.0 * values)


def joined_means(mine_ref, other_ref, share, order):
    first = lax.axis_index("sec") % 2 == 0
    parts = []
    for j in order:
        mine, other = mine_ref[j, :share, :], other_ref[j, :share, :]
        parts += [jnp.where(first, mine, other), jnp.where(first, other, mine)]
    return jnp.concatenate(parts, axis=0)


def slots_of(targets, col_count, padded, clouds):
    rows = targets.shape[1]
    onehot = jnp.where(iota((clouds, rows), 0) == targets, 1.0, 0.0)
    before = jnp.where(iota((rows, rows), 0) < iota((rows, rows), 1), 1.0, 0.0)
    running = mm(onehot.astype(BF16), before.astype(BF16), NN, None)
    ranks = jnp.sum(running * onehot, axis=0, keepdims=True).astype(I32)
    owner = divided(targets, col_count)
    return owner, (targets - owner * col_count) * padded + ranks


def blocked(ref, value, levels):
    ref[...] = jnp.zeros_like(ref)
    for f in range(ref.shape[0] // levels):
        ref[f * levels : f * levels + value.shape[0], f * levels : (f + 1) * levels] = value


def host_kernel(
    columns_ref,
    mixing_ref,
    neighbours_ref,
    targets_ref,
    substeps_ref,
    map_ref,
    out_ref,
    fold_ref,
    *,
    padded,
    clouds,
):
    rows, width = columns_ref.shape
    cloud_levels, levels = map_ref.shape
    col_count = out_ref.shape[0]
    block = col_count * padded
    means = element_means(columns_ref)
    share = means.shape[0] // 2
    section = lax.axis_index("sec")
    part = jnp.where(section % 2 == 0, means[:share], means[share:])
    for c in range(col_count):
        out_ref[c, :share, :] = part
    blocked(fold_ref, RELAX * vertical_mix(map_ref[...], cloud_levels), levels)
    owner, slot = slots_of(targets_ref[...], col_count, padded, clouds)
    mine = jnp.where(owner + 1 == section, slot, -1)
    pack = jnp.where(iota((block, rows), 0) == mine, 1.0, 0.0).astype(BF16)
    base = own_part(columns_ref[...], means, mixing_ref[...], levels)
    count = neighbours_ref.shape[0]
    ids = select(element_of_row(rows), neighbours_ref[...].astype(F32), NT, swap=True)
    extras = jnp.concatenate(
        [
            jnp.zeros((cloud_levels, rows), F32),
            ids,
            jnp.zeros((levels - 1 - cloud_levels - count, rows), F32),
            substeps_ref[...].astype(F32),
            jnp.zeros((width - levels, rows), F32),
        ],
        axis=0,
    )
    folded = product(base, fold_ref[...], NT)
    sent = select(pack, folded, NN) + select(pack, extras, NT)
    capacity = out_ref.shape[1] - share
    for c in range(col_count):
        out_ref[c, share:, :] = sent[c * padded : c * padded + capacity]


def aside(
    columns_ref,
    mixing_ref,
    neighbours_ref,
    targets_ref,
    map_ref,
    base_ref,
    weights_ref,
    homes_ref,
    fold_ref,
    unfold_ref,
    col_count,
    padded,
    clouds,
    half,
    held,
):
    rows, width = columns_ref.shape
    cloud_levels, levels = map_ref.shape
    elements = rows // 4
    position = lax.axis_index("col")
    base_ref[...] = own_part(
        columns_ref[...], element_means(columns_ref), mixing_ref[...], levels
    )
    near = neighbours_ref[...] - (position - 1) * elements
    near = jnp.where(near < 0, near + elements * col_count, near)
    near = jnp.where(near >= elements * col_count, near - elements * col_count, near)
    window = iota((3 * elements, elements), 0)
    picks = jnp.zeros((3 * elements, elements), F32)
    for k in range(near.shape[0]):
        picks = picks + jnp.where(window == near[k : k + 1, :], 1.0, 0.0)
    weights_ref[...] = mm(element_of_row(rows), picks.astype(BF16), NT, None).astype(BF16)
    owner, slot = slots_of(targets_ref[...], col_count, padded, clouds)
    place = divided(slot, padded)
    rank = slot - place * padded
    upper = jnp.where(rank >= half, 1, 0)
    parity = lax.axis_index("sec") % 2
    cloud = owner * col_count + place + jnp.where(upper == parity, 0, clouds)
    everywhere = (cloud * held + rank - half * upper).astype(F32)
    identity = jnp.where(iota((rows, rows), 0) == iota((rows, rows), 1), 1.0, 0.0)
    homes_ref[...] = select(
        identity.astype(BF16), jnp.broadcast_to(everywhere, (LANES, rows)), NT
    )
    blocked(fold_ref, RELAX * vertical_mix(map_ref[...], cloud_levels), levels)
    fold_ref[...] = fold_ref[...] * mixing_ref[...]
    blocked(unfold_ref, map_ref[...], levels)


class Segment:
    def __init__(self, lane0, width, levels, begin):
        self.lane0, self.width, self.begin, self.levels = lane0, width, begin, levels
        self.steps = -(-levels // (LANES // width))
        self.groups = -(-levels // self.steps)
        self.missing = self.groups * self.steps - levels
        self.blocks = -(-self.steps // STEP)
        self.rows = (begin + 1, begin + 1 + self.steps)

    def group_steps(self, g):
        return self.steps - (self.missing if g == self.groups - 1 else 0)


def segments_of(slots, levels):
    segments, begin = [], 0
    for lane0 in range(0, slots, LANES):
        segments.append(Segment(lane0, min(LANES, slots - lane0), levels, begin))
        begin += segments[-1].steps + 2
    rows = max([begin] + [s.begin + 2 + s.blocks * STEP for s in segments])
    return segments, rows, -(-rows // 8) * 8


def fill_spare(segments, load, store):
    def turned(value, shift):
        tall = jnp.broadcast_to(value, (8, LANES)) if value.shape[0] == 1 else value
        return pltpu.roll(tall, shift % LANES, 1)[: value.shape[0]]

    for s in segments:
        if s.missing:
            row = s.rows[1] - s.missing
            value = load(row - 1)
            lane = iota(value.shape, 1)
            store(row, jnp.where(lane >= (s.groups - 1) * s.width, value, load(row)))
        first, last = load(s.rows[0]), load(s.rows[1] - 1)
        before, after = first, last
        if s.groups > 1:
            lane = iota(first.shape, 1)
            before = jnp.where(lane < s.width, first, turned(last, s.width))
            after = jnp.where(lane < (s.groups - 1) * s.width, turned(first, -s.width), last)
        store(s.begin, before)
        store(s.rows[1], after)


def fill_wide(segments, ref):
    def store(row, value):
        ref[row] = value

    fill_spare(segments, lambda row: ref[row], store)


def fill_flat(segments, ref):
    def store(row, value):
        ref[row : row + 1, :] = value

    fill_spare(segments, lambda row: ref[row : row + 1, :], store)


def linear(below, here, above):
    east = [pltpu.roll(here[3], 1, 0), here[0], here[1], here[2]]
    west = [here[1], here[2], here[3], pltpu.roll(here[0], 7, 0)]
    keep = (1.0 - 2.0 * HORIZ - 2.0 * VERTIC) / VERTIC
    return [
        (below[j] + above[j]) + ((HORIZ / VERTIC) * (east[j] + west[j]) + keep * here[j])
        for j in range(4)
    ]


def groups(ref, index):
    return [ref[index + (pl.ds(8 * j, 8),)] for j in range(4)]


def strided(ref, row):
    return [ref[row, pl.ds(j, 8, stride=4), :] for j in range(4)]


def sweep(segment, load, work):
    def block(i, carry):
        row = segment.begin + i * STEP
        held = [load(row), load(row + 1)]
        for k in range(STEP):
            held.append(load(row + k + 2))
            work(row + k + 1, held[k], held[k + 1], held[k + 2])
        return carry

    lax.fori_loop(0, segment.blocks, block, 0)


def each(count, size, work):
    size = min(size, count)

    def run(first):
        for k in range(size):
            work(first + k)

    if count // size:
        lax.fori_loop(0, count // size, lambda i, c: (run(i * size), c)[1], 0)
    if count % size:
        run(count - size)


def widen(state_ref, natural_ref, segments, scale):
    levels, columns, _ = state_ref.shape
    for s in segments:
        at = slice(s.lane0, s.lane0 + s.width)

        def one(k):
            parts = []
            for g in range(s.groups):
                level = jnp.minimum(g * s.steps + k, levels - 1)
                parts.append(state_ref[level, :, at].astype(F32))
            spare = LANES - s.groups * s.width
            if spare:
                parts.append(jnp.zeros((columns, spare), F32))
            value = jnp.concatenate(parts, axis=1) if len(parts) > 1 else parts[0]
            natural_ref[s.begin + 1 + k] = scale * value if scale != 1.0 else value

        each(s.steps, STEP, one)


def folded_sums(sums_ref, columns):
    rows = sums_ref.shape[0] // 8
    total = sums_ref[pl.ds(0, rows, stride=8), :]
    for k in range(1, 8):
        total = total + sums_ref[pl.ds(k, rows, stride=8), :]
    return total * (1.0 / columns)


def slab(row):
    return pl.ds(pl.multiple_of(row * 8, 8), 8)


def spread_row(ref, row):
    return jnp.broadcast_to(ref[pl.ds(row, 1), :], (8, LANES))


def turn(value, shift):
    if not shift:
        return value
    height = value.shape[0]
    tall = -(-height // 8) * 8
    if tall != height:
        fill = jnp.zeros((tall - height, LANES), F32)
        value = jnp.concatenate([value, fill], axis=0)
    return pltpu.roll(value, shift % LANES, 1)[:height]


def each(count, size, work):
    size = min(size, count)

    def run(first):
        for k in range(size):
            work(first + k)

    if count // size:
        lax.fori_loop(0, count // size, lambda i, c: (run(i * size), c)[1], 0)
    if count % size:
        run(count - size)


def widen(state_ref, natural_ref, segments, scale):
    levels, columns, _ = state_ref.shape
    for s in segments:
        at = slice(s.lane0, s.lane0 + s.width)

        def one(k):
            parts = []
            for g in range(s.groups):
                level = jnp.minimum(g * s.steps + k, levels - 1)
                parts.append(state_ref[level, :, at].astype(F32))
            spare = LANES - s.groups * s.width
            if spare:
                parts.append(jnp.zeros((columns, spare), F32))
            value = jnp.concatenate(parts, axis=1) if len(parts) > 1 else parts[0]
            natural_ref[s.begin + 1 + k] = scale * value if scale != 1.0 else value

        each(s.steps, STEP, one)


def folded_sums(sums_ref, columns):
    rows = sums_ref.shape[0] // 8
    total = sums_ref[pl.ds(0, rows, stride=8), :]
    for k in range(1, 8):
        total = total + sums_ref[pl.ds(k, rows, stride=8), :]
    return total * (1.0 / columns)


def slab(row):
    return pl.ds(pl.multiple_of(row * 8, 8), 8)


def spread_row(ref, row):
    return jnp.broadcast_to(ref[pl.ds(row, 1), :], (8, LANES))


def lane_places(segments):
    return [(s, g) for s in segments for g in range(s.groups)]


def slot_map(segments, block, capacity, padded):
    tiles = []
    for s in segments:
        lane = iota((8, LANES), 1)
        slot = s.lane0 + lane
        row = slot + (padded - capacity) * divided(slot, capacity)
        row = jnp.where(lane < s.width, row, -1)[0:1]
        tiles.append(jnp.where(iota((block, LANES), 0) == row, 1.0, 0.0).astype(BF16))
    return jnp.concatenate(tiles, axis=1)


def prepare_kernel(
    state_ref,
    columns_far,
    mixing_far,
    neighbours_far,
    targets_far,
    map_far,
    saturation_far,
    moved_ref,
    means_ref,
    limits_ref,
    energy_far,
    base_far,
    weights_far,
    homes_far,
    fold_ref,
    unfold_far,
    state_buf,
    natural_ref,
    sums_ref,
    flat_ref,
    energy_buf,
    columns_ref,
    mixing_ref,
    neighbours_ref,
    targets_ref,
    map_ref,
    saturation_ref,
    base_ref,
    weights_ref,
    homes_ref,
    unfold_ref,
    sems,
    in_sems,
    out_sems,
    *,
    segments,
    **host,
):
    fields, levels, columns, _ = state_ref.shape
    given = (
        (columns_far, columns_ref),
        (mixing_far, mixing_ref),
        (neighbours_far, neighbours_ref),
        (targets_far, targets_ref),
        (map_far, map_ref),
        (saturation_far, saturation_ref),
    )
    starts = [pltpu.make_async_copy(x, y, in_sems.at[i]) for i, (x, y) in enumerate(given)]
    loads = [
        pltpu.make_async_copy(state_ref.at[f], state_buf.at[f], sems.at[f]) for f in range(fields)
    ]
    for copy in starts + loads:
        copy.start()
    made = (
        (base_ref, base_far),
        (weights_ref, weights_far),
        (homes_ref, homes_far),
        (unfold_ref, unfold_far),
        (energy_buf, energy_far),
    )
    leaves = [pltpu.make_async_copy(x, y, out_sems.at[i]) for i, (x, y) in enumerate(made)]
    for copy in starts:
        copy.wait()
    tall = flat_ref.shape[0]
    here = iota((tall, levels), 0) == iota((tall, levels), 1)
    diagonal = jnp.where(here, 0.5 * saturation_ref[...], 0.0)
    flat_ref[...] = select(jnp.ones((levels, LANES), BF16), diagonal, NN, swap=True)
    limits_ref[...] = jnp.zeros_like(limits_ref)
    for s in segments:
        lane = iota((s.steps, LANES), 1)
        value = flat_ref[0 : s.steps, :]
        for g in range(1, s.groups):
            other = flat_ref[g * s.steps : (g + 1) * s.steps, :]
            value = jnp.where(lane >= g * s.width, other, value)
        limits_ref[s.rows[0] : s.rows[1], :] = value
    sums_ref[...] = jnp.zeros_like(sums_ref)
    aside(
        columns_ref,
        mixing_ref,
        neighbours_ref,
        targets_ref,
        map_ref,
        base_ref,
        weights_ref,
        homes_ref,
        fold_ref,
        unfold_ref,
        **host,
    )
    for copy in leaves[:4]:
        copy.start()
    for f, scale, target in ((0, SHRINK, energy_buf), (1, 1.0, moved_ref)):
        loads[f].wait()
        widen(state_buf.at[f], natural_ref, segments, scale)
        fill_wide(segments, natural_ref)
        for s in segments:

            def work(row, below, here, above):
                out = linear(below, here, above)
                for j in range(4):
                    target[row, pl.ds(8 * j, 8), :] = out[j]
                sums_ref[slab(row), :] = (here[0] + here[1]) + (here[2] + here[3])

            sweep(s, lambda row: strided(natural_ref, row), work)
        if f == 0:
            leaves[4].start()
        means_ref[f] = folded_sums(sums_ref, columns) * (1.0 / scale)
    for copy in leaves:
        copy.wait()


def neighbour_part(arrived, means, fold, share, parity, levels, stride, neighbours):
    folded = product(fold, means, NT)
    taken = arrived[stride - 1 : stride] > 0.0
    ids = [
        jnp.where(taken, arrived[levels + k : levels + k + 1], -1.0) for k in range(neighbours)
    ]
    total = None
    chunk = min(256, means.shape[0])
    for first in range(0, means.shape[0], chunk):
        row = iota((chunk, arrived.shape[1]), 0) + first
        element = (row + share * divided(row, share) + share * parity).astype(F32)
        wanted = jnp.where(element == ids[0], 1.0, 0.0)
        for k in range(1, neighbours):
            wanted = wanted + jnp.where(element == ids[k], 1.0, 0.0)
        part = folded[:, first : first + chunk]
        term = select(wanted.astype(BF16), part, NN, swap=True)
        total = term if total is None else total + term
    return total


def halves(ref, share):
    return jnp.concatenate([ref[j, :share, :] for j in range(ref.shape[0])], axis=0)


def arrive_kernel(
    received_ref, fold_ref, arrived_ref, places_ref, *, segments, capacity, padded, **sizes
):
    hosts = received_ref.shape[0]
    share = received_ref.shape[1] - capacity
    places = slot_map(segments, hosts * padded, capacity, padded)
    places_ref[...] = places
    parts = []
    for j in range(hosts):
        parts.append(received_ref[j, share:, :])
        if padded != capacity:
            parts.append(jnp.zeros((padded - capacity, LANES), F32))
    arrived = select(places, jnp.concatenate(parts, axis=0), TN, swap=True)
    parity = lax.axis_index("sec") % 2
    arrived_ref[...] = arrived + neighbour_part(
        arrived, halves(received_ref, share), fold_ref[...], share, parity, **sizes
    )


def water_kernel(
    arrived_ref,
    places_ref,
    other_ref,
    moved_ref,
    means_ref,
    limits_ref,
    fold_ref,
    unfold_far,
    water_far,
    spill_far,
    flats_far,
    back_far,
    unfold_ref,
    even_ref,
    odd_ref,
    spill_buf,
    flats_ref,
    goal_ref,
    mean_ref,
    shift_ref,
    limit_ref,
    sums_ref,
    change_ref,
    back_ref,
    in_sem,
    spill_sems,
    water_sem,
    flat_sem,
    back_sems,
    *,
    segments,
    share,
    padded,
    stride,
    levels,
    neighbours,
):
    rows = means_ref.shape[1]
    columns = even_ref.shape[1]
    load = pltpu.make_async_copy(unfold_far, unfold_ref, in_sem)
    load.start()
    hosts = other_ref.shape[0]
    parity = 1 - lax.axis_index("sec") % 2
    arrived = arrived_ref[...]
    arrived = arrived + neighbour_part(
        arrived,
        halves(other_ref, share),
        fold_ref[...],
        share,
        parity,
        levels,
        stride,
        neighbours,
    )
    goal_ref[...] = jnp.zeros_like(goal_ref)
    flats_ref[...] = jnp.zeros_like(flats_ref)
    sums_ref[...] = jnp.zeros_like(sums_ref)
    counts = flats_ref.at[MAX_SUB + 2]
    for t, s in enumerate(segments):
        lanes = slice(t * LANES, (t + 1) * LANES)
        count = None
        for g in range(s.groups):
            number = s.group_steps(g)
            at = slice(s.rows[0], s.rows[0] + number)
            for f in range(2):
                first = f * stride + g * s.steps
                part = turn(arrived[first : first + number, lanes], g * s.width)
                goal_ref[f, at, :] = goal_ref[f, at, :] + part if g else part
            part = turn(arrived[stride - 1 : stride, lanes], g * s.width)
            count = part if count is None else count + part
        counts[s.rows[0] : s.rows[1], :] = jnp.broadcast_to(count, (s.steps, LANES))
    for f in range(2):
        mean_ref[f] = means_ref[f]
    copies = []
    source, target = None, even_ref
    for n in range(MAX_SUB):
        scale = 10.0 ** (n + 1)
        last = n + 1 == MAX_SUB
        expected = []
        for f in range(2):
            fill_flat(segments, mean_ref.at[f])
            mean = mean_ref[f]
            mixed = mean + VERTIC * (
                pltpu.roll(mean, 1, 0) + pltpu.roll(mean, rows - 1, 0) - 2.0 * mean
            )
            offset = goal_ref[f] - RELAX * mixed
            expected.append(mixed + offset)
            if f == 1:
                shift_ref[...] = scale * offset
            else:
                flats_ref[n] = (scale * SHRINK) * offset
        limit_ref[...] = scale * limits_ref[...]
        if last:
            flats_ref[MAX_SUB] = shift_ref[...]
            flats_ref[MAX_SUB + 1] = limit_ref[...]
            copies.append(pltpu.make_async_copy(flats_ref, flats_far, flat_sem))
            copies[-1].start()
        for s in segments:
            active = spread_row(counts, s.rows[0]) > float(n)

            def finish(row, lin, old):
                shift = spread_row(shift_ref, row)
                limit = spread_row(limit_ref, row)
                total = None
                for j in range(4):
                    v = lin[j] + shift
                    c = jnp.maximum(0.5 * v - limit, 0.0)
                    total = c if total is None else total + c
                    if last:
                        continue
                    u = v - c
                    if old is not None:
                        u = jnp.where(active, u, old[j])
                    spill_buf[n, row, pl.ds(8 * j, 8), :] = c
                    target[row, pl.ds(8 * j, 8), :] = u
                sums_ref[slab(row), :] = total

            if n == 0:

                def block(i, carry):
                    for k in range(STEP):
                        row = s.begin + 1 + i * STEP + k
                        finish(row, groups(moved_ref, (row,)), None)
                    return carry

                lax.fori_loop(0, s.blocks, block, 0)
            else:

                def work(row, below, here, above):
                    finish(row, linear(below, here, above), here)

                sweep(s, lambda row: groups(source, (row,)), work)
        if not last:
            copies.append(
                pltpu.make_async_copy(spill_buf.at[n], spill_far.at[n], spill_sems.at[n])
            )
            copies[-1].start()
            fill_wide(segments, target)
            source, target = target, (odd_ref if target is even_ref else even_ref)
        if n + 2 == MAX_SUB:
            copies.append(pltpu.make_async_copy(source, water_far, water_sem))
            copies[-1].start()
        spilled = folded_sums(sums_ref, columns) * (1.0 / scale)
        step = [expected[0] + LATENT * spilled, expected[1] - spilled]
        keep = counts[...] > float(n)
        for f in range(2):
            mean_ref[f] = jnp.where(keep, step[f], mean_ref[f])
    change_ref[...] = jnp.zeros_like(change_ref)
    for f in range(2):
        change = mean_ref[f] - means_ref[f]
        for t, s in enumerate(segments):
            for g in range(s.groups):
                first, number = f * stride + g * s.steps, s.group_steps(g)
                part = turn(change[s.rows[0] : s.rows[0] + number], -g * s.width)
                change_ref[first : first + number, t * LANES : (t + 1) * LANES] = part
    spread = select(places_ref[...], change_ref[...], NT)
    load.wait()
    back = product(spread, unfold_ref[...], NN)
    half = back_ref.shape[2]
    for h in range(2):
        for j in range(hosts):
            first = j * padded + h * half
            back_ref[h, j] = back[first : first + half]
    for i in range(back_far.shape[0]):
        copies.append(pltpu.make_async_copy(back_ref.at[i % 2], back_far.at[i], back_sems.at[i]))
        copies[-1].start()
    for copy in copies:
        copy.wait()


def energy_kernel(
    state_ref,
    energy_far,
    water_far,
    spill_far,
    flats_far,
    base_far,
    weights_far,
    mixing_far,
    homes_far,
    received_ref,
    other_ref,
    out_ref,
    advanced_ref,
    picks_ref,
    state_buf,
    energy_buf,
    water_buf,
    spill_buf,
    flats_ref,
    base_ref,
    weights_ref,
    mixing_ref,
    homes_ref,
    out_buf,
    even_ref,
    odd_ref,
    natural_ref,
    state_sems,
    in_sems,
    spill_sems,
    out_sems,
    *,
    segments,
    share,
):
    fields, levels, columns, _ = state_ref.shape
    final = MAX_SUB - 1
    pairs = (
        (flats_far, flats_ref),
        (base_far, base_ref),
        (weights_far, weights_ref),
        (mixing_far, mixing_ref),
        (water_far, water_buf),
        (energy_far, energy_buf),
        (homes_far, homes_ref),
    )
    loads = [pltpu.make_async_copy(x, y, in_sems.at[i]) for i, (x, y) in enumerate(pairs)]
    flats, bases, shares, mixings, waters, first, homes = loads
    states = [
        pltpu.make_async_copy(state_ref.at[f], state_buf.at[f], state_sems.at[f])
        for f in range(fields)
    ]
    spills = [
        pltpu.make_async_copy(spill_far.at[n], spill_buf.at[n], spill_sems.at[n])
        for n in range(final)
    ]
    for copy in loads[:5] + [states[1], first] + spills + [states[0], homes]:
        copy.start()
    cut = -(-levels // 2)
    spans = ((0, cut), (cut, levels - cut))

    def leave(f, part):
        at = pl.ds(*spans[part])
        return pltpu.make_async_copy(
            out_buf.at[f, at], out_ref.at[f, at], out_sems.at[2 * f + part]
        )

    counts = flats_ref.at[MAX_SUB + 2]

    def finish_field(f, found):
        for s in segments[::-1]:
            count = spread_row(counts, s.rows[0])
            back = jnp.zeros((8, LANES), F32)
            for n in range(1, MAX_SUB + 1):
                scale = 10.0**-n * (LATENT if f == 0 else 1.0)
                back = jnp.where(count == float(n), scale, back)
            at = slice(s.lane0, s.lane0 + s.width)
            held = jnp.broadcast_to(count[0:1, : s.width], (columns, s.width)) > 0.0

            def permute(k):
                row = s.begin + 1 + k
                value = groups(found, (row,))
                for j in range(4):
                    natural_ref[row, pl.ds(j, 8, stride=4), :] = value[j] * back

            def narrow(g, k):
                level = g * s.steps + k
                lanes = slice(g * s.width, (g + 1) * s.width)
                old = state_buf[f, level, :, at].astype(F32)
                value = jnp.where(held, natural_ref[s.begin + 1 + k, :, lanes], old)
                out_buf[f, level, :, at] = value.astype(BF16)

            each(s.steps, STEP, permute)
            if s is segments[0] and s.groups == 1:
                for part, (begin, number) in enumerate(spans):
                    each(number, STEP, lambda k: narrow(0, begin + k))
                    leave(f, part).start()
            else:
                for g in range(s.groups):
                    each(s.group_steps(g), STEP, lambda k: narrow(g, k))
        if segments[0].groups > 1:
            for part in range(2):
                leave(f, part).start()

    bases.wait()
    shares.wait()
    mixings.wait()
    hosts = received_ref.shape[0]
    position = lax.axis_index("col")
    around = [jnp.where(position == 0, hosts - 1, position - 1), position]
    around.append(jnp.where(position == hosts - 1, 0, position + 1))
    means = joined_means(received_ref, other_ref, share, around)
    advanced_ref[...] = base_ref[...] + mixing_ref[...] * select(weights_ref[...], means, NN)
    flats.wait()
    waters.wait()
    for s in segments:
        active = spread_row(counts, s.rows[0]) > float(final)

        def last(row, below, here, above):
            water = linear(below, here, above)
            push = spread_row(flats_ref.at[MAX_SUB], row)
            limit = spread_row(flats_ref.at[MAX_SUB + 1], row)
            for j in range(4):
                v = water[j] + push
                c = jnp.maximum(0.5 * v - limit, 0.0)
                spill_buf[final, row, pl.ds(8 * j, 8), :] = c
                even_ref[row, pl.ds(8 * j, 8), :] = jnp.where(active, v - c, here[j])

        sweep(s, lambda row: groups(water_buf, (row,)), last)
    states[1].wait()
    finish_field(1, even_ref)
    first.wait()
    source, target = None, odd_ref
    for n in range(MAX_SUB):
        if n < final:
            spills[n].wait()
        for s in segments:
            active = spread_row(counts, s.rows[0]) > float(n)

            def start(i, carry):
                for k in range(STEP):
                    row = s.begin + 1 + i * STEP + k
                    shift = spread_row(flats_ref.at[n], row)
                    lin, spill = groups(energy_buf, (row,)), groups(spill_buf, (n, row))
                    for j in range(4):
                        target[row, pl.ds(8 * j, 8), :] = (lin[j] + shift) + spill[j]
                return carry

            def work(row, below, here, above):
                shift = spread_row(flats_ref.at[n], row)
                lin = linear(below, here, above)
                spill = groups(spill_buf, (n, row))
                for j in range(4):
                    u = (lin[j] + shift) + spill[j]
                    target[row, pl.ds(8 * j, 8), :] = jnp.where(active, u, here[j])

            if n == 0:
                lax.fori_loop(0, s.blocks, start, 0)
            else:
                sweep(s, lambda row: groups(source, (row,)), work)
        if n < final:
            fill_wide(segments, target)
        source, target = target, (odd_ref if target is even_ref else even_ref)
    states[0].wait()
    finish_field(0, source)
    homes.wait()
    place = homes_ref[:, :1].astype(I32)
    picks_ref[...] = jnp.where(iota(picks_ref.shape, 1) == place, 1.0, 0.0).astype(BF16)
    for f in range(fields):
        for part in range(2):
            leave(f, part).wait()


def final_kernel(
    advanced_ref, picks_ref, mine_ref, other_ref, out_ref, table_ref, *, levels, idle, held
):
    rows, width = advanced_ref.shape
    sources, half, _ = mine_ref.shape
    clouds = sources - idle
    if half != held:
        table_ref[...] = jnp.zeros_like(table_ref)
    for i, ref in enumerate((mine_ref, other_ref)):
        for j in range(clouds):
            first = (i * clouds + j) * held
            table_ref[first : first + half, :] = ref[idle + j]
    summed = advanced_ref[...] + select(picks_ref[...], table_ref[...], NN)
    water = divided(iota((rows, width), 1), levels) == 1
    out_ref[...] = jnp.where(water, jnp.maximum(summed, 0.0), summed)


SPACES = dict(
    auto=pl.BlockSpec(memory_space=pltpu.VMEM),
    near=pl.BlockSpec(memory_space=pltpu.VMEM),
    far=pl.BlockSpec(memory_space=pl.ANY),
    scalar=pl.BlockSpec(memory_space=pltpu.SMEM),
)


def call(kernel, name, inputs, outputs, scratch=(), limit=8):
    kept = dict(near=pltpu.VMEM, auto=pltpu.HBM, far=pltpu.HBM, scalar=pltpu.HBM)
    arrays = [pltpu.with_memory_space_constraint(x, kept[space]) for space, x in inputs]
    shapes = [kept[space](dims, dtype) for space, dims, dtype in outputs]
    return pl.pallas_call(
        kernel,
        out_shape=shapes,
        in_specs=[SPACES[space] for space, _ in inputs],
        out_specs=[SPACES[space] for space, _, _ in outputs],
        scratch_shapes=list(scratch),
        compiler_params=pltpu.CompilerParams(vmem_limit_bytes=limit << 20),
        name=name,
    )(*arrays)


def body(
    column_state, mixing_rate, neighbours, assignment, substeps, cloud_state, level_map, saturation
):
    col_count = lax.axis_size("col")
    sec_count = lax.axis_size("sec")
    count, width = column_state.shape
    cloud_levels, levels = level_map.shape
    _, fields, _, columns, slots = cloud_state.shape
    elements = count // 4
    capacity = slots // col_count
    padded = -(-capacity // 8) * 8
    half = -(-capacity // 2)
    held = -(-half // 8) * 8
    block = col_count * padded
    clouds = (sec_count - 1) * col_count
    segments, used, rows = segments_of(slots, cloud_levels)
    mapped = LANES * len(segments)
    mixing = mixing_rate.reshape(1, width)
    state = cloud_state[0]
    dma = pltpu.SemaphoreType.DMA

    def wide(*lead):
        return pltpu.VMEM((*lead, rows, columns, LANES), F32)

    hosts = dict(padded=padded, clouds=clouds)
    places_in = [
        ("auto", column_state),
        ("auto", mixing),
        ("auto", neighbours.T),
        ("auto", assignment.reshape(1, count)),
    ]
    outgoing, _ = call(
        functools.partial(host_kernel, **hosts),
        "host",
        places_in + [("auto", substeps.reshape(1, count)), ("auto", level_map)],
        [("auto", (col_count, elements // 2 + capacity, width), F32), ("near", (width, width), F32)],
    )
    received = lax.all_to_all(outgoing, "col", split_axis=0, concat_axis=0, tiled=True)
    moved, cloud_means, limits, energy, base, weights, homes, fold, unfold = call(
        functools.partial(
            prepare_kernel,
            segments=segments,
            col_count=col_count,
            half=half,
            held=held,
            **hosts,
        ),
        "prepare",
        [("far", state)]
        + [("far", x) for _, x in places_in]
        + [("far", level_map), ("far", saturation.reshape(1, cloud_levels))],
        [
            ("near", (used, columns, LANES), F32),
            ("near", (fields, rows, LANES), F32),
            ("near", (rows, LANES), F32),
            ("far", (used, columns, LANES), F32),
            ("far", (count, width), F32),
            ("far", (count, 3 * elements), BF16),
            ("far", (count, LANES), F32),
            ("near", (width, width), F32),
            ("far", (width, width), F32),
        ],
        scratch=[
            pltpu.VMEM(state.shape, BF16),
            wide(),
            pltpu.VMEM((rows * 8, LANES), F32),
            pltpu.VMEM((max(s.groups * s.steps for s in segments), LANES), F32),
            pltpu.VMEM((used, columns, LANES), F32),
            pltpu.VMEM((count, width), F32),
            pltpu.VMEM((1, width), F32),
            pltpu.VMEM((neighbours.shape[1], elements), I32),
            pltpu.VMEM((1, count), I32),
            pltpu.VMEM((cloud_levels, levels), F32),
            pltpu.VMEM((1, cloud_levels), F32),
            pltpu.VMEM((count, width), F32),
            pltpu.VMEM((count, 3 * elements), BF16),
            pltpu.VMEM((count, LANES), F32),
            pltpu.VMEM((width, width), F32),
            dma((fields,)),
            dma((6,)),
            dma((5,)),
        ],
        limit=16,
    )
    received, moved, base = lax.optimization_barrier((received, moved, base))
    pairs = [(i, i ^ 1) for i in range(sec_count)]
    other = lax.ppermute(received, "sec", pairs)
    sizes = dict(stride=levels, levels=cloud_levels, neighbours=neighbours.shape[1])
    arrived, places = call(
        functools.partial(
            arrive_kernel, segments=segments, capacity=capacity, padded=padded, **sizes
        ),
        "arrive",
        [("near", received), ("near", fold)],
        [("near", (width, mapped), F32), ("near", (block, mapped), BF16)],
    )
    water, spill, flats, back = call(
        functools.partial(
            water_kernel, segments=segments, share=elements // 2, padded=padded, **sizes
        ),
        "water",
        [
            ("near", arrived),
            ("near", places),
            ("near", other),
            ("near", moved),
            ("near", cloud_means),
            ("near", limits),
            ("near", fold),
            ("far", unfold),
        ],
        [
            ("far", (rows, columns, LANES), F32),
            ("far", (MAX_SUB - 1, rows, columns, LANES), F32),
            ("far", (MAX_SUB + 3, rows, LANES), F32),
            ("far", (sec_count, col_count, half, width), F32),
        ],
        scratch=[
            pltpu.VMEM((width, width), F32),
            wide(),
            wide(),
            wide(MAX_SUB - 1),
            pltpu.VMEM((MAX_SUB + 3, rows, LANES), F32),
            pltpu.VMEM((fields, rows, LANES), F32),
            pltpu.VMEM((fields, rows, LANES), F32),
            pltpu.VMEM((rows, LANES), F32),
            pltpu.VMEM((rows, LANES), F32),
            pltpu.VMEM((rows * 8, LANES), F32),
            pltpu.VMEM((width, mapped), F32),
            pltpu.VMEM((2, col_count, half, width), F32),
            dma(()),
            dma((MAX_SUB - 1,)),
            dma(()),
            dma(()),
            dma((sec_count,)),
        ],
        limit=24,
    )
    returned = lax.all_to_all(
        back.reshape(sec_count * col_count, half, width),
        ("sec", "col"),
        split_axis=0,
        concat_axis=0,
        tiled=True,
    )
    new_block, advanced, picks = call(
        functools.partial(energy_kernel, segments=segments, share=elements // 2),
        "energy",
        [
            ("far", state),
            ("far", energy),
            ("far", water),
            ("far", spill),
            ("far", flats),
            ("far", base),
            ("far", weights),
            ("far", mixing),
            ("far", homes),
            ("near", received),
            ("near", other),
        ],
        [
            ("far", state.shape, BF16),
            ("near", (count, width), F32),
            ("near", (count, 2 * clouds * held), BF16),
        ],
        scratch=[
            pltpu.VMEM(state.shape, BF16),
            pltpu.VMEM((used, columns, LANES), F32),
            wide(),
            wide(MAX_SUB),
            pltpu.VMEM((MAX_SUB + 3, rows, LANES), F32),
            pltpu.VMEM((count, width), F32),
            pltpu.VMEM((count, 3 * elements), BF16),
            pltpu.VMEM((1, width), F32),
            pltpu.VMEM((count, LANES), F32),
            pltpu.VMEM(state.shape, BF16),
            wide(),
            wide(),
            wide(),
            dma((fields,)),
            dma((7,)),
            dma((MAX_SUB - 1,)),
            dma((2 * fields,)),
        ],
        limit=32,
    )
    returned, advanced = lax.optimization_barrier((returned, advanced))
    partner = lax.ppermute(returned, "sec", pairs)
    (new_columns,) = call(
        functools.partial(final_kernel, levels=levels, idle=col_count, held=held),
        "final",
        [("near", advanced), ("near", picks), ("near", returned), ("near", partner)],
        [("auto", (count, width), F32)],
        scratch=[pltpu.VMEM((2 * clouds * held, width), F32)],
    )
    return new_columns, new_block[None]


def solution(mesh):
    in_specs = (
        P("col", None),
        P(),
        P("col", None),
        P("col", None),
        P("col"),
        P("sec", None, None, None, "col"),
        P(),
        P(),
    )
    out_specs = (P("col", None), P("sec", None, None, None, "col"))
    return jax.shard_map(body, mesh=mesh, in_specs=in_specs, out_specs=out_specs, check_vma=False)
```

```python
import functools

import jax
import jax.numpy as jnp
from jax import lax
from jax.experimental import pallas as pl
from jax.experimental.pallas import tpu as pltpu
from jax.sharding import PartitionSpec as P

MAX_SUB = 4
RELAX = 0.25
HORIZ = 0.12
VERTIC = 0.1
LATENT = 2.5
GROW = 20.0
VMIX = 0.2
HIGH = lax.Precision.HIGHEST
LANES = 128
F32 = jnp.float32
BF16 = jnp.bfloat16
STEP = 10
SHRINK = 1.0 / LATENT
I32 = jnp.int32


def iota(shape, dim):
    return lax.broadcasted_iota(I32, shape, dim)


def mm(a, b, contract, precision=HIGH):
    return lax.dot_general(
        a, b, (contract, ((), ())), precision=precision, preferred_element_type=F32
    )


NN = ((1,), (0,))
NT = ((1,), (1,))
TN = ((0,), (0,))


def divided(value, by):
    return jnp.floor((value.astype(F32) + 0.5) * (1.0 / by)).astype(I32)


def split(values):
    high = values.astype(BF16)
    rest = values - high.astype(F32)
    middle = rest.astype(BF16)
    low = (rest - middle.astype(F32)).astype(BF16)
    return low, middle, high


def select(picks, values, contract, swap=False):
    total = None
    for part in split(values):
        a, b = (part, picks) if swap else (picks, part)
        term = lax.dot_general(a, b, (contract, ((), ())), preferred_element_type=F32)
        total = term if total is None else total + term
    return total


def product(a, b, contract):
    (al, am, ah), (bl, bm, bh) = split(a), split(b)
    total = None
    for x, y in ((al, bh), (ah, bl), (am, bm), (am, bh), (ah, bm), (ah, bh)):
        term = lax.dot_general(x, y, (contract, ((), ())), preferred_element_type=F32)
        total = term if total is None else total + term
    return total


def vertical_mix(values, levels):
    upper = jnp.concatenate([values[1:levels], values[levels - 1 : levels]], axis=0)
    lower = jnp.concatenate([values[0:1], values[0 : levels - 1]], axis=0)
    inner = values[0:levels]
    return inner + VERTIC * (upper + lower - 2.0 * inner)


def element_of_row(rows):
    elements = rows // 4
    hit = divided(iota((rows, elements), 0), 4) == iota((rows, elements), 1)
    return jnp.where(hit, 1.0, 0.0).astype(BF16)


def element_means(columns_ref):
    elements = columns_ref.shape[0] // 4
    total = columns_ref[pl.ds(0, elements, stride=4), :]
    for k in range(1, 4):
        total = total + columns_ref[pl.ds(k, elements, stride=4), :]
    return 0.25 * total


def own_part(values, means, mixing, levels):
    rows, width = values.shape
    lane = iota((rows, width), 1)
    level = lane - levels * divided(lane, levels)
    upper = jnp.where(level == levels - 1, values, pltpu.roll(values, width - 1, 1))
    lower = jnp.where(level == 0, values, pltpu.roll(values, 1, 1))
    mean = select(element_of_row(rows), means, NN)
    return values - (4.0 * mixing) * mean + VMIX * (upper + lower - 2.0 * values)


def joined_means(mine_ref, other_ref, share, order):
    first = lax.axis_index("sec") % 2 == 0
    parts = []
    for j in order:
        mine, other = mine_ref[j, :share, :], other_ref[j, :share, :]
        parts += [jnp.where(first, mine, other), jnp.where(first, other, mine)]
    return jnp.concatenate(parts, axis=0)


def slots_of(targets, col_count, padded, clouds):
    rows = targets.shape[1]
    onehot = jnp.where(iota((clouds, rows), 0) == targets, 1.0, 0.0)
    before = jnp.where(iota((rows, rows), 0) < iota((rows, rows), 1), 1.0, 0.0)
    running = mm(onehot.astype(BF16), before.astype(BF16), NN, None)
    ranks = jnp.sum(running * onehot, axis=0, keepdims=True).astype(I32)
    owner = divided(targets, col_count)
    return owner, (targets - owner * col_count) * padded + ranks


def blocked(ref, value, levels):
    ref[...] = jnp.zeros_like(ref)
    for f in range(ref.shape[0] // levels):
        ref[f * levels : f * levels + value.shape[0], f * levels : (f + 1) * levels] = value


def host_kernel(
    columns_ref,
    mixing_ref,
    neighbours_ref,
    targets_ref,
    substeps_ref,
    map_ref,
    out_ref,
    fold_ref,
    *,
    padded,
    clouds,
):
    rows, width = columns_ref.shape
    cloud_levels, levels = map_ref.shape
    col_count = out_ref.shape[0]
    block = col_count * padded
    means = element_means(columns_ref)
    share = means.shape[0] // 2
    section = lax.axis_index("sec")
    part = jnp.where(section % 2 == 0, means[:share], means[share:])
    for c in range(col_count):
        out_ref[c, :share, :] = part
    blocked(fold_ref, RELAX * vertical_mix(map_ref[...], cloud_levels), levels)
    owner, slot = slots_of(targets_ref[...], col_count, padded, clouds)
    mine = jnp.where(owner + 1 == section, slot, -1)
    pack = jnp.where(iota((block, rows), 0) == mine, 1.0, 0.0).astype(BF16)
    base = own_part(columns_ref[...], means, mixing_ref[...], levels)
    count = neighbours_ref.shape[0]
    ids = select(element_of_row(rows), neighbours_ref[...].astype(F32), NT, swap=True)
    extras = jnp.concatenate(
        [
            jnp.zeros((cloud_levels, rows), F32),
            ids,
            jnp.zeros((levels - 1 - cloud_levels - count, rows), F32),
            substeps_ref[...].astype(F32),
            jnp.zeros((width - levels, rows), F32),
        ],
        axis=0,
    )
    sent = product(select(pack, base, NN), fold_ref[...], NT) + select(pack, extras, NT)
    capacity = out_ref.shape[1] - share
    for c in range(col_count):
        out_ref[c, share:, :] = sent[c * padded : c * padded + capacity]


def aside(
    columns_ref,
    mixing_ref,
    neighbours_ref,
    targets_ref,
    map_ref,
    base_ref,
    weights_ref,
    homes_ref,
    fold_ref,
    unfold_ref,
    col_count,
    padded,
    clouds,
    half,
    held,
):
    rows, width = columns_ref.shape
    cloud_levels, levels = map_ref.shape
    elements = rows // 4
    position = lax.axis_index("col")
    base_ref[...] = own_part(
        columns_ref[...], element_means(columns_ref), mixing_ref[...], levels
    )
    near = neighbours_ref[...] - (position - 1) * elements
    near = jnp.where(near < 0, near + elements * col_count, near)
    near = jnp.where(near >= elements * col_count, near - elements * col_count, near)
    window = iota((3 * elements, elements), 0)
    picks = jnp.zeros((3 * elements, elements), F32)
    for k in range(near.shape[0]):
        picks = picks + jnp.where(window == near[k : k + 1, :], 1.0, 0.0)
    weights_ref[...] = mm(element_of_row(rows), picks.astype(BF16), NT, None).astype(BF16)
    owner, slot = slots_of(targets_ref[...], col_count, padded, clouds)
    place = divided(slot, padded)
    rank = slot - place * padded
    upper = jnp.where(rank >= half, 1, 0)
    parity = lax.axis_index("sec") % 2
    cloud = owner * col_count + place + jnp.where(upper == parity, 0, clouds)
    everywhere = (cloud * held + rank - half * upper).astype(F32)
    identity = jnp.where(iota((rows, rows), 0) == iota((rows, rows), 1), 1.0, 0.0)
    homes_ref[...] = select(
        identity.astype(BF16), jnp.broadcast_to(everywhere, (LANES, rows)), NT
    )
    blocked(fold_ref, RELAX * vertical_mix(map_ref[...], cloud_levels), levels)
    fold_ref[...] = fold_ref[...] * mixing_ref[...]
    blocked(unfold_ref, map_ref[...], levels)


class Segment:
    def __init__(self, lane0, width, levels, begin):
        self.lane0, self.width, self.begin, self.levels = lane0, width, begin, levels
        self.steps = -(-levels // (LANES // width))
        self.groups = -(-levels // self.steps)
        self.missing = self.groups * self.steps - levels
        self.blocks = -(-self.steps // STEP)
        self.rows = (begin + 1, begin + 1 + self.steps)

    def group_steps(self, g):
        return self.steps - (self.missing if g == self.groups - 1 else 0)


def segments_of(slots, levels):
    segments, begin = [], 0
    for lane0 in range(0, slots, LANES):
        segments.append(Segment(lane0, min(LANES, slots - lane0), levels, begin))
        begin += segments[-1].steps + 2
    rows = max([begin] + [s.begin + 2 + s.blocks * STEP for s in segments])
    return segments, rows, -(-rows // 8) * 8


def fill_spare(segments, load, store):
    def turned(value, shift):
        tall = jnp.broadcast_to(value, (8, LANES)) if value.shape[0] == 1 else value
        return pltpu.roll(tall, shift % LANES, 1)[: value.shape[0]]

    for s in segments:
        if s.missing:
            row = s.rows[1] - s.missing
            value = load(row - 1)
            lane = iota(value.shape, 1)
            store(row, jnp.where(lane >= (s.groups - 1) * s.width, value, load(row)))
        first, last = load(s.rows[0]), load(s.rows[1] - 1)
        before, after = first, last
        if s.groups > 1:
            lane = iota(first.shape, 1)
            before = jnp.where(lane < s.width, first, turned(last, s.width))
            after = jnp.where(lane < (s.groups - 1) * s.width, turned(first, -s.width), last)
        store(s.begin, before)
        store(s.rows[1], after)


def fill_wide(segments, ref):
    def store(row, value):
        ref[row] = value

    fill_spare(segments, lambda row: ref[row], store)


def fill_flat(segments, ref):
    def store(row, value):
        ref[row : row + 1, :] = value

    fill_spare(segments, lambda row: ref[row : row + 1, :], store)


def linear(below, here, above):
    east = [pltpu.roll(here[3], 1, 0), here[0], here[1], here[2]]
    west = [here[1], here[2], here[3], pltpu.roll(here[0], 7, 0)]
    keep = (1.0 - 2.0 * HORIZ - 2.0 * VERTIC) / VERTIC
    return [
        (below[j] + above[j]) + ((HORIZ / VERTIC) * (east[j] + west[j]) + keep * here[j])
        for j in range(4)
    ]


def groups(ref, index):
    return [ref[index + (pl.ds(8 * j, 8),)] for j in range(4)]


def strided(ref, row):
    return [ref[row, pl.ds(j, 8, stride=4), :] for j in range(4)]


def sweep(segment, load, work):
    def block(i, carry):
        row = segment.begin + i * STEP
        held = [load(row), load(row + 1)]
        for k in range(STEP):
            held.append(load(row + k + 2))
            work(row + k + 1, held[k], held[k + 1], held[k + 2])
        return carry

    lax.fori_loop(0, segment.blocks, block, 0)


def each(count, size, work):
    size = min(size, count)

    def run(first):
        for k in range(size):
            work(first + k)

    if count // size:
        lax.fori_loop(0, count // size, lambda i, c: (run(i * size), c)[1], 0)
    if count % size:
        run(count - size)


def widen(state_ref, natural_ref, segments, scale):
    levels, columns, _ = state_ref.shape
    for s in segments:
        at = slice(s.lane0, s.lane0 + s.width)

        def one(k):
            parts = []
            for g in range(s.groups):
                level = jnp.minimum(g * s.steps + k, levels - 1)
                parts.append(state_ref[level, :, at].astype(F32))
            spare = LANES - s.groups * s.width
            if spare:
                parts.append(jnp.zeros((columns, spare), F32))
            value = jnp.concatenate(parts, axis=1) if len(parts) > 1 else parts[0]
            natural_ref[s.begin + 1 + k] = scale * value if scale != 1.0 else value

        each(s.steps, STEP, one)


def folded_sums(sums_ref, columns):
    rows = sums_ref.shape[0] // 8
    total = sums_ref[pl.ds(0, rows, stride=8), :]
    for k in range(1, 8):
        total = total + sums_ref[pl.ds(k, rows, stride=8), :]
    return total * (1.0 / columns)


def slab(row):
    return pl.ds(pl.multiple_of(row * 8, 8), 8)


def spread_row(ref, row):
    return jnp.broadcast_to(ref[pl.ds(row, 1), :], (8, LANES))


def turn(value, shift):
    if not shift:
        return value
    height = value.shape[0]
    tall = -(-height // 8) * 8
    if tall != height:
        fill = jnp.zeros((tall - height, LANES), F32)
        value = jnp.concatenate([value, fill], axis=0)
    return pltpu.roll(value, shift % LANES, 1)[:height]


def each(count, size, work):
    size = min(size, count)

    def run(first):
        for k in range(size):
            work(first + k)

    if count // size:
        lax.fori_loop(0, count // size, lambda i, c: (run(i * size), c)[1], 0)
    if count % size:
        run(count - size)


def widen(state_ref, natural_ref, segments, scale):
    levels, columns, _ = state_ref.shape
    for s in segments:
        at = slice(s.lane0, s.lane0 + s.width)

        def one(k):
            parts = []
            for g in range(s.groups):
                level = jnp.minimum(g * s.steps + k, levels - 1)
                parts.append(state_ref[level, :, at].astype(F32))
            spare = LANES - s.groups * s.width
            if spare:
                parts.append(jnp.zeros((columns, spare), F32))
            value = jnp.concatenate(parts, axis=1) if len(parts) > 1 else parts[0]
            natural_ref[s.begin + 1 + k] = scale * value if scale != 1.0 else value

        each(s.steps, STEP, one)


def folded_sums(sums_ref, columns):
    rows = sums_ref.shape[0] // 8
    total = sums_ref[pl.ds(0, rows, stride=8), :]
    for k in range(1, 8):
        total = total + sums_ref[pl.ds(k, rows, stride=8), :]
    return total * (1.0 / columns)


def slab(row):
    return pl.ds(pl.multiple_of(row * 8, 8), 8)


def spread_row(ref, row):
    return jnp.broadcast_to(ref[pl.ds(row, 1), :], (8, LANES))


def lane_places(segments):
    return [(s, g) for s in segments for g in range(s.groups)]


def slot_map(segments, block, capacity, padded):
    tiles = []
    for s in segments:
        lane = iota((8, LANES), 1)
        slot = s.lane0 + lane
        row = slot + (padded - capacity) * divided(slot, capacity)
        row = jnp.where(lane < s.width, row, -1)[0:1]
        tiles.append(jnp.where(iota((block, LANES), 0) == row, 1.0, 0.0).astype(BF16))
    return jnp.concatenate(tiles, axis=1)


def prepare_kernel(
    state_ref,
    columns_far,
    mixing_far,
    neighbours_far,
    targets_far,
    map_far,
    saturation_far,
    moved_ref,
    means_ref,
    limits_ref,
    energy_far,
    base_far,
    weights_far,
    homes_far,
    fold_ref,
    unfold_far,
    state_buf,
    natural_ref,
    sums_ref,
    flat_ref,
    energy_buf,
    columns_ref,
    mixing_ref,
    neighbours_ref,
    targets_ref,
    map_ref,
    saturation_ref,
    base_ref,
    weights_ref,
    homes_ref,
    unfold_ref,
    sems,
    in_sems,
    out_sems,
    *,
    segments,
    **host,
):
    fields, levels, columns, _ = state_ref.shape
    given = (
        (columns_far, columns_ref),
        (mixing_far, mixing_ref),
        (neighbours_far, neighbours_ref),
        (targets_far, targets_ref),
        (map_far, map_ref),
        (saturation_far, saturation_ref),
    )
    starts = [pltpu.make_async_copy(x, y, in_sems.at[i]) for i, (x, y) in enumerate(given)]
    loads = [
        pltpu.make_async_copy(state_ref.at[f], state_buf.at[f], sems.at[f]) for f in range(fields)
    ]
    for copy in starts + loads:
        copy.start()
    made = (
        (base_ref, base_far),
        (weights_ref, weights_far),
        (homes_ref, homes_far),
        (unfold_ref, unfold_far),
        (energy_buf, energy_far),
    )
    leaves = [pltpu.make_async_copy(x, y, out_sems.at[i]) for i, (x, y) in enumerate(made)]
    for copy in starts:
        copy.wait()
    tall = flat_ref.shape[0]
    here = iota((tall, levels), 0) == iota((tall, levels), 1)
    diagonal = jnp.where(here, saturation_ref[...], 0.0)
    flat_ref[...] = select(jnp.ones((levels, LANES), BF16), diagonal, NN, swap=True)
    limits_ref[...] = jnp.zeros_like(limits_ref)
    for s in segments:
        lane = iota((s.steps, LANES), 1)
        value = flat_ref[0 : s.steps, :]
        for g in range(1, s.groups):
            other = flat_ref[g * s.steps : (g + 1) * s.steps, :]
            value = jnp.where(lane >= g * s.width, other, value)
        limits_ref[s.rows[0] : s.rows[1], :] = value
    sums_ref[...] = jnp.zeros_like(sums_ref)
    aside(
        columns_ref,
        mixing_ref,
        neighbours_ref,
        targets_ref,
        map_ref,
        base_ref,
        weights_ref,
        homes_ref,
        fold_ref,
        unfold_ref,
        **host,
    )
    for copy in leaves[:4]:
        copy.start()
    for f, scale, target in ((0, SHRINK, energy_buf), (1, 1.0, moved_ref)):
        loads[f].wait()
        widen(state_buf.at[f], natural_ref, segments, scale)
        fill_wide(segments, natural_ref)
        for s in segments:

            def work(row, below, here, above):
                out = linear(below, here, above)
                for j in range(4):
                    target[row, pl.ds(8 * j, 8), :] = out[j]
                sums_ref[slab(row), :] = (here[0] + here[1]) + (here[2] + here[3])

            sweep(s, lambda row: strided(natural_ref, row), work)
        if f == 0:
            leaves[4].start()
        means_ref[f] = folded_sums(sums_ref, columns) * (1.0 / scale)
    for copy in leaves:
        copy.wait()


def neighbour_part(arrived, means, fold, share, parity, levels, stride, neighbours):
    folded = product(fold, means, NT)
    taken = arrived[stride - 1 : stride] > 0.0
    ids = [
        jnp.where(taken, arrived[levels + k : levels + k + 1], -1.0) for k in range(neighbours)
    ]
    total = None
    chunk = min(256, means.shape[0])
    for first in range(0, means.shape[0], chunk):
        row = iota((chunk, arrived.shape[1]), 0) + first
        element = (row + share * divided(row, share) + share * parity).astype(F32)
        wanted = jnp.where(element == ids[0], 1.0, 0.0)
        for k in range(1, neighbours):
            wanted = wanted + jnp.where(element == ids[k], 1.0, 0.0)
        part = folded[:, first : first + chunk]
        term = select(wanted.astype(BF16), part, NN, swap=True)
        total = term if total is None else total + term
    return total


def halves(ref, share):
    return jnp.concatenate([ref[j, :share, :] for j in range(ref.shape[0])], axis=0)


def arrive_kernel(
    received_ref, fold_ref, arrived_ref, places_ref, *, segments, capacity, padded, **sizes
):
    hosts = received_ref.shape[0]
    share = received_ref.shape[1] - capacity
    places = slot_map(segments, hosts * padded, capacity, padded)
    places_ref[...] = places
    parts = []
    for j in range(hosts):
        parts.append(received_ref[j, share:, :])
        if padded != capacity:
            parts.append(jnp.zeros((padded - capacity, LANES), F32))
    arrived = select(places, jnp.concatenate(parts, axis=0), TN, swap=True)
    parity = lax.axis_index("sec") % 2
    arrived_ref[...] = arrived + neighbour_part(
        arrived, halves(received_ref, share), fold_ref[...], share, parity, **sizes
    )


def water_kernel(
    arrived_ref,
    places_ref,
    other_ref,
    moved_ref,
    means_ref,
    limits_ref,
    fold_ref,
    unfold_far,
    water_far,
    spill_far,
    flats_far,
    back_far,
    unfold_ref,
    even_ref,
    odd_ref,
    spill_buf,
    flats_ref,
    goal_ref,
    mean_ref,
    shift_ref,
    limit_ref,
    sums_ref,
    change_ref,
    back_ref,
    in_sem,
    spill_sems,
    water_sem,
    flat_sem,
    back_sems,
    *,
    segments,
    share,
    padded,
    stride,
    levels,
    neighbours,
):
    rows = means_ref.shape[1]
    columns = even_ref.shape[1]
    load = pltpu.make_async_copy(unfold_far, unfold_ref, in_sem)
    load.start()
    hosts = other_ref.shape[0]
    parity = 1 - lax.axis_index("sec") % 2
    arrived = arrived_ref[...]
    arrived = arrived + neighbour_part(
        arrived,
        halves(other_ref, share),
        fold_ref[...],
        share,
        parity,
        levels,
        stride,
        neighbours,
    )
    goal_ref[...] = jnp.zeros_like(goal_ref)
    flats_ref[...] = jnp.zeros_like(flats_ref)
    sums_ref[...] = jnp.zeros_like(sums_ref)
    counts = flats_ref.at[MAX_SUB + 2]
    for t, s in enumerate(segments):
        lanes = slice(t * LANES, (t + 1) * LANES)
        count = None
        for g in range(s.groups):
            number = s.group_steps(g)
            at = slice(s.rows[0], s.rows[0] + number)
            for f in range(2):
                first = f * stride + g * s.steps
                part = turn(arrived[first : first + number, lanes], g * s.width)
                goal_ref[f, at, :] = goal_ref[f, at, :] + part if g else part
            part = turn(arrived[stride - 1 : stride, lanes], g * s.width)
            count = part if count is None else count + part
        counts[s.rows[0] : s.rows[1], :] = jnp.broadcast_to(count, (s.steps, LANES))
    for f in range(2):
        mean_ref[f] = means_ref[f]
    copies = []
    source, target = None, even_ref
    for n in range(MAX_SUB):
        scale = 0.5 * GROW ** (n + 1)
        last = n + 1 == MAX_SUB
        expected = []
        for f in range(2):
            fill_flat(segments, mean_ref.at[f])
            mean = mean_ref[f]
            mixed = mean + VERTIC * (
                pltpu.roll(mean, 1, 0) + pltpu.roll(mean, rows - 1, 0) - 2.0 * mean
            )
            offset = goal_ref[f] - RELAX * mixed
            expected.append(mixed + offset)
            if f == 1:
                shift_ref[...] = scale * offset
            else:
                flats_ref[n] = (scale * SHRINK) * offset
        limit_ref[...] = scale * limits_ref[...]
        if last:
            flats_ref[MAX_SUB] = shift_ref[...]
            flats_ref[MAX_SUB + 1] = limit_ref[...]
            copies.append(pltpu.make_async_copy(flats_ref, flats_far, flat_sem))
            copies[-1].start()
        for s in segments:
            active = spread_row(counts, s.rows[0]) > float(n)

            def finish(row, lin, old):
                shift = spread_row(shift_ref, row)
                limit = spread_row(limit_ref, row)
                total = None
                for j in range(4):
                    v = lin[j] + shift
                    low = jnp.minimum(v, limit)
                    total = low if total is None else total + low
                    if last:
                        continue
                    u = v + low
                    if old is not None:
                        u = jnp.where(active, u, old[j])
                    spill_buf[n, row, pl.ds(8 * j, 8), :] = v - low
                    target[row, pl.ds(8 * j, 8), :] = u
                sums_ref[slab(row), :] = total

            if n == 0:

                def block(i, carry):
                    for k in range(STEP):
                        row = s.begin + 1 + i * STEP + k
                        finish(row, groups(moved_ref, (row,)), None)
                    return carry

                lax.fori_loop(0, s.blocks, block, 0)
            else:

                def work(row, below, here, above):
                    finish(row, linear(below, here, above), here)

                sweep(s, lambda row: groups(source, (row,)), work)
        if not last:
            copies.append(
                pltpu.make_async_copy(spill_buf.at[n], spill_far.at[n], spill_sems.at[n])
            )
            copies[-1].start()
            fill_wide(segments, target)
            source, target = target, (odd_ref if target is even_ref else even_ref)
        if n + 2 == MAX_SUB:
            copies.append(pltpu.make_async_copy(source, water_far, water_sem))
            copies[-1].start()
        spilled = 0.5 * (expected[1] - folded_sums(sums_ref, columns) * (1.0 / scale))
        step = [expected[0] + LATENT * spilled, expected[1] - spilled]
        keep = counts[...] > float(n)
        for f in range(2):
            mean_ref[f] = jnp.where(keep, step[f], mean_ref[f])
    change_ref[...] = jnp.zeros_like(change_ref)
    for f in range(2):
        change = mean_ref[f] - means_ref[f]
        for t, s in enumerate(segments):
            for g in range(s.groups):
                first, number = f * stride + g * s.steps, s.group_steps(g)
                part = turn(change[s.rows[0] : s.rows[0] + number], -g * s.width)
                change_ref[first : first + number, t * LANES : (t + 1) * LANES] = part
    spread = select(places_ref[...], change_ref[...], NT)
    load.wait()
    back = product(spread, unfold_ref[...], NN)
    half = back_ref.shape[2]
    for h in range(2):
        for j in range(hosts):
            first = j * padded + h * half
            back_ref[h, j] = back[first : first + half]
    for i in range(back_far.shape[0]):
        copies.append(pltpu.make_async_copy(back_ref.at[i % 2], back_far.at[i], back_sems.at[i]))
        copies[-1].start()
    for copy in copies:
        copy.wait()


def energy_kernel(
    state_ref,
    energy_far,
    water_far,
    spill_far,
    flats_far,
    base_far,
    weights_far,
    mixing_far,
    homes_far,
    received_ref,
    other_ref,
    out_ref,
    advanced_ref,
    picks_ref,
    state_buf,
    energy_buf,
    water_buf,
    spill_buf,
    flats_ref,
    base_ref,
    weights_ref,
    mixing_ref,
    homes_ref,
    out_buf,
    even_ref,
    odd_ref,
    natural_ref,
    state_sems,
    in_sems,
    spill_sems,
    out_sems,
    *,
    segments,
    share,
):
    fields, levels, columns, _ = state_ref.shape
    final = MAX_SUB - 1
    pairs = (
        (flats_far, flats_ref),
        (base_far, base_ref),
        (weights_far, weights_ref),
        (mixing_far, mixing_ref),
        (water_far, water_buf),
        (energy_far, energy_buf),
        (homes_far, homes_ref),
    )
    loads = [pltpu.make_async_copy(x, y, in_sems.at[i]) for i, (x, y) in enumerate(pairs)]
    flats, bases, shares, mixings, waters, first, homes = loads
    states = [
        pltpu.make_async_copy(state_ref.at[f], state_buf.at[f], state_sems.at[f])
        for f in range(fields)
    ]
    spills = [
        pltpu.make_async_copy(spill_far.at[n], spill_buf.at[n], spill_sems.at[n])
        for n in range(final)
    ]
    for copy in loads[:5] + [states[1], first] + spills + [states[0], homes]:
        copy.start()
    cut = -(-levels // 2)
    spans = ((0, cut), (cut, levels - cut))

    def leave(f, part):
        at = pl.ds(*spans[part])
        return pltpu.make_async_copy(
            out_buf.at[f, at], out_ref.at[f, at], out_sems.at[2 * f + part]
        )

    counts = flats_ref.at[MAX_SUB + 2]

    def finish_field(f, found):
        for s in segments[::-1]:
            count = spread_row(counts, s.rows[0])
            back = jnp.zeros((8, LANES), F32)
            for n in range(1, MAX_SUB + 1):
                scale = GROW**-n * (LATENT if f == 0 else 1.0)
                back = jnp.where(count == float(n), scale, back)
            at = slice(s.lane0, s.lane0 + s.width)
            held = jnp.broadcast_to(count[0:1, : s.width], (columns, s.width)) > 0.0

            def permute(k):
                row = s.begin + 1 + k
                value = groups(found, (row,))
                for j in range(4):
                    natural_ref[row, pl.ds(j, 8, stride=4), :] = value[j] * back

            def narrow(g, k):
                level = g * s.steps + k
                lanes = slice(g * s.width, (g + 1) * s.width)
                old = state_buf[f, level, :, at].astype(F32)
                value = jnp.where(held, natural_ref[s.begin + 1 + k, :, lanes], old)
                out_buf[f, level, :, at] = value.astype(BF16)

            each(s.steps, STEP, permute)
            if s is segments[0] and s.groups == 1:
                for part, (begin, number) in enumerate(spans):
                    each(number, STEP, lambda k: narrow(0, begin + k))
                    leave(f, part).start()
            else:
                for g in range(s.groups):
                    each(s.group_steps(g), STEP, lambda k: narrow(g, k))
        if segments[0].groups > 1:
            for part in range(2):
                leave(f, part).start()

    bases.wait()
    shares.wait()
    mixings.wait()
    hosts = received_ref.shape[0]
    position = lax.axis_index("col")
    around = [jnp.where(position == 0, hosts - 1, position - 1), position]
    around.append(jnp.where(position == hosts - 1, 0, position + 1))
    means = joined_means(received_ref, other_ref, share, around)
    advanced_ref[...] = base_ref[...] + mixing_ref[...] * select(weights_ref[...], means, NN)
    flats.wait()
    waters.wait()
    for s in segments:
        active = spread_row(counts, s.rows[0]) > float(final)

        def last(row, below, here, above):
            water = linear(below, here, above)
            push = spread_row(flats_ref.at[MAX_SUB], row)
            limit = spread_row(flats_ref.at[MAX_SUB + 1], row)
            for j in range(4):
                v = water[j] + push
                low = jnp.minimum(v, limit)
                spill_buf[final, row, pl.ds(8 * j, 8), :] = v - low
                even_ref[row, pl.ds(8 * j, 8), :] = jnp.where(active, v + low, here[j])

        sweep(s, lambda row: groups(water_buf, (row,)), last)
    states[1].wait()
    finish_field(1, even_ref)
    first.wait()
    source, target = None, odd_ref
    for n in range(MAX_SUB):
        if n < final:
            spills[n].wait()
        for s in segments:
            active = spread_row(counts, s.rows[0]) > float(n)

            def start(i, carry):
                for k in range(STEP):
                    row = s.begin + 1 + i * STEP + k
                    shift = spread_row(flats_ref.at[n], row)
                    lin, spill = groups(energy_buf, (row,)), groups(spill_buf, (n, row))
                    for j in range(4):
                        target[row, pl.ds(8 * j, 8), :] = 2.0 * (lin[j] + shift) + spill[j]
                return carry

            def work(row, below, here, above):
                shift = spread_row(flats_ref.at[n], row)
                lin = linear(below, here, above)
                spill = groups(spill_buf, (n, row))
                for j in range(4):
                    u = 2.0 * (lin[j] + shift) + spill[j]
                    target[row, pl.ds(8 * j, 8), :] = jnp.where(active, u, here[j])

            if n == 0:
                lax.fori_loop(0, s.blocks, start, 0)
            else:
                sweep(s, lambda row: groups(source, (row,)), work)
        if n < final:
            fill_wide(segments, target)
        source, target = target, (odd_ref if target is even_ref else even_ref)
    states[0].wait()
    finish_field(0, source)
    homes.wait()
    place = homes_ref[:, :1].astype(I32)
    picks_ref[...] = jnp.where(iota(picks_ref.shape, 1) == place, 1.0, 0.0).astype(BF16)
    for f in range(fields):
        for part in range(2):
            leave(f, part).wait()


def gather_half(picks_ref, half_ref, table_ref, idle, part):
    sources, half, _ = half_ref.shape
    height = table_ref.shape[0]
    held = height // (sources - idle)
    if half != held:
        table_ref[...] = jnp.zeros_like(table_ref)
    for j in range(sources - idle):
        table_ref[j * held : j * held + half, :] = half_ref[idle + j]
    picks = picks_ref[:, part * height : (part + 1) * height]
    return select(picks, table_ref[...], NN)


def nearly_kernel(advanced_ref, picks_ref, mine_ref, out_ref, table_ref, *, idle):
    out_ref[...] = advanced_ref[...] + gather_half(picks_ref, mine_ref, table_ref, idle, 0)


def final_kernel(nearly_ref, picks_ref, other_ref, out_ref, table_ref, *, levels, idle):
    summed = nearly_ref[...] + gather_half(picks_ref, other_ref, table_ref, idle, 1)
    water = divided(iota(summed.shape, 1), levels) == 1
    out_ref[...] = jnp.where(water, jnp.maximum(summed, 0.0), summed)


SPACES = dict(
    auto=pl.BlockSpec(memory_space=pltpu.VMEM),
    near=pl.BlockSpec(memory_space=pltpu.VMEM),
    far=pl.BlockSpec(memory_space=pl.ANY),
    scalar=pl.BlockSpec(memory_space=pltpu.SMEM),
)


def call(kernel, name, inputs, outputs, scratch=(), limit=8):
    kept = dict(near=pltpu.VMEM, auto=pltpu.HBM, far=pltpu.HBM, scalar=pltpu.HBM)
    arrays = [pltpu.with_memory_space_constraint(x, kept[space]) for space, x in inputs]
    shapes = [kept[space](dims, dtype) for space, dims, dtype in outputs]
    return pl.pallas_call(
        kernel,
        out_shape=shapes,
        in_specs=[SPACES[space] for space, _ in inputs],
        out_specs=[SPACES[space] for space, _, _ in outputs],
        scratch_shapes=list(scratch),
        compiler_params=pltpu.CompilerParams(vmem_limit_bytes=limit << 20),
        name=name,
    )(*arrays)


def body(
    column_state, mixing_rate, neighbours, assignment, substeps, cloud_state, level_map, saturation
):
    col_count = lax.axis_size("col")
    sec_count = lax.axis_size("sec")
    count, width = column_state.shape
    cloud_levels, levels = level_map.shape
    _, fields, _, columns, slots = cloud_state.shape
    elements = count // 4
    capacity = slots // col_count
    padded = -(-capacity // 8) * 8
    half = -(-capacity // 2)
    held = -(-half // 8) * 8
    block = col_count * padded
    clouds = (sec_count - 1) * col_count
    segments, used, rows = segments_of(slots, cloud_levels)
    mapped = LANES * len(segments)
    mixing = mixing_rate.reshape(1, width)
    state = cloud_state[0]
    dma = pltpu.SemaphoreType.DMA

    def wide(*lead):
        return pltpu.VMEM((*lead, rows, columns, LANES), F32)

    hosts = dict(padded=padded, clouds=clouds)
    places_in = [
        ("auto", column_state),
        ("auto", mixing),
        ("auto", neighbours.T),
        ("auto", assignment.reshape(1, count)),
    ]
    outgoing, _ = call(
        functools.partial(host_kernel, **hosts),
        "host",
        places_in + [("auto", substeps.reshape(1, count)), ("auto", level_map)],
        [("auto", (col_count, elements // 2 + capacity, width), F32), ("near", (width, width), F32)],
    )
    received = lax.all_to_all(outgoing, "col", split_axis=0, concat_axis=0, tiled=True)
    moved, cloud_means, limits, energy, base, weights, homes, fold, unfold = call(
        functools.partial(
            prepare_kernel,
            segments=segments,
            col_count=col_count,
            half=half,
            held=held,
            **hosts,
        ),
        "prepare",
        [("far", state)]
        + [("far", x) for _, x in places_in]
        + [("far", level_map), ("far", saturation.reshape(1, cloud_levels))],
        [
            ("near", (used, columns, LANES), F32),
            ("near", (fields, rows, LANES), F32),
            ("near", (rows, LANES), F32),
            ("far", (used, columns, LANES), F32),
            ("far", (count, width), F32),
            ("far", (count, 3 * elements), BF16),
            ("far", (count, LANES), F32),
            ("near", (width, width), F32),
            ("far", (width, width), F32),
        ],
        scratch=[
            pltpu.VMEM(state.shape, BF16),
            wide(),
            pltpu.VMEM((rows * 8, LANES), F32),
            pltpu.VMEM((max(s.groups * s.steps for s in segments), LANES), F32),
            pltpu.VMEM((used, columns, LANES), F32),
            pltpu.VMEM((count, width), F32),
            pltpu.VMEM((1, width), F32),
            pltpu.VMEM((neighbours.shape[1], elements), I32),
            pltpu.VMEM((1, count), I32),
            pltpu.VMEM((cloud_levels, levels), F32),
            pltpu.VMEM((1, cloud_levels), F32),
            pltpu.VMEM((count, width), F32),
            pltpu.VMEM((count, 3 * elements), BF16),
            pltpu.VMEM((count, LANES), F32),
            pltpu.VMEM((width, width), F32),
            dma((fields,)),
            dma((6,)),
            dma((5,)),
        ],
        limit=16,
    )
    received, moved, base = lax.optimization_barrier((received, moved, base))
    pairs = [(i, i ^ 1) for i in range(sec_count)]
    other = lax.ppermute(received, "sec", pairs)
    sizes = dict(stride=levels, levels=cloud_levels, neighbours=neighbours.shape[1])
    arrived, places = call(
        functools.partial(
            arrive_kernel, segments=segments, capacity=capacity, padded=padded, **sizes
        ),
        "arrive",
        [("near", received), ("near", fold)],
        [("near", (width, mapped), F32), ("near", (block, mapped), BF16)],
    )
    water, spill, flats, back = call(
        functools.partial(
            water_kernel, segments=segments, share=elements // 2, padded=padded, **sizes
        ),
        "water",
        [
            ("near", arrived),
            ("near", places),
            ("near", other),
            ("near", moved),
            ("near", cloud_means),
            ("near", limits),
            ("near", fold),
            ("far", unfold),
        ],
        [
            ("far", (rows, columns, LANES), F32),
            ("far", (MAX_SUB - 1, rows, columns, LANES), F32),
            ("far", (MAX_SUB + 3, rows, LANES), F32),
            ("far", (sec_count, col_count, half, width), F32),
        ],
        scratch=[
            pltpu.VMEM((width, width), F32),
            wide(),
            wide(),
            wide(MAX_SUB - 1),
            pltpu.VMEM((MAX_SUB + 3, rows, LANES), F32),
            pltpu.VMEM((fields, rows, LANES), F32),
            pltpu.VMEM((fields, rows, LANES), F32),
            pltpu.VMEM((rows, LANES), F32),
            pltpu.VMEM((rows, LANES), F32),
            pltpu.VMEM((rows * 8, LANES), F32),
            pltpu.VMEM((width, mapped), F32),
            pltpu.VMEM((2, col_count, half, width), F32),
            dma(()),
            dma((MAX_SUB - 1,)),
            dma(()),
            dma(()),
            dma((sec_count,)),
        ],
        limit=24,
    )
    returned = lax.all_to_all(
        back.reshape(sec_count * col_count, half, width),
        ("sec", "col"),
        split_axis=0,
        concat_axis=0,
        tiled=True,
    )
    new_block, advanced, picks = call(
        functools.partial(energy_kernel, segments=segments, share=elements // 2),
        "energy",
        [
            ("far", state),
            ("far", energy),
            ("far", water),
            ("far", spill),
            ("far", flats),
            ("far", base),
            ("far", weights),
            ("far", mixing),
            ("far", homes),
            ("near", received),
            ("near", other),
        ],
        [
            ("far", state.shape, BF16),
            ("near", (count, width), F32),
            ("near", (count, 2 * clouds * held), BF16),
        ],
        scratch=[
            pltpu.VMEM(state.shape, BF16),
            pltpu.VMEM((used, columns, LANES), F32),
            wide(),
            wide(MAX_SUB),
            pltpu.VMEM((MAX_SUB + 3, rows, LANES), F32),
            pltpu.VMEM((count, width), F32),
            pltpu.VMEM((count, 3 * elements), BF16),
            pltpu.VMEM((1, width), F32),
            pltpu.VMEM((count, LANES), F32),
            pltpu.VMEM(state.shape, BF16),
            wide(),
            wide(),
            wide(),
            dma((fields,)),
            dma((7,)),
            dma((MAX_SUB - 1,)),
            dma((2 * fields,)),
        ],
        limit=32,
    )
    returned, advanced = lax.optimization_barrier((returned, advanced))
    partner = lax.ppermute(returned, "sec", pairs)
    table = pltpu.VMEM((clouds * held, width), F32)
    (nearly,) = call(
        functools.partial(nearly_kernel, idle=col_count),
        "nearly",
        [("near", advanced), ("near", picks), ("near", returned)],
        [("near", (count, width), F32)],
        scratch=[table],
    )
    (new_columns,) = call(
        functools.partial(final_kernel, levels=levels, idle=col_count),
        "final",
        [("near", nearly), ("near", picks), ("near", partner)],
        [("auto", (count, width), F32)],
        scratch=[table],
    )
    return new_columns, new_block[None]


def solution(mesh):
    in_specs = (
        P("col", None),
        P(),
        P("col", None),
        P("col", None),
        P("col"),
        P("sec", None, None, None, "col"),
        P(),
        P(),
    )
    out_specs = (P("col", None), P("sec", None, None, None, "col"))
    return jax.shard_map(body, mesh=mesh, in_specs=in_specs, out_specs=out_specs, check_vma=False)
```

```python
import functools

import jax
import jax.numpy as jnp
from jax import lax
from jax.experimental import pallas as pl
from jax.experimental.pallas import tpu as pltpu
from jax.sharding import PartitionSpec as P

MAX_SUB = 4
RELAX = 0.25
HORIZ = 0.12
VERTIC = 0.1
LATENT = 2.5
GROW = 20.0
VMIX = 0.2
HIGH = lax.Precision.HIGHEST
LANES = 128
F32 = jnp.float32
BF16 = jnp.bfloat16
STEP = 10
QUAD = 4
SHRINK = 1.0 / LATENT
I32 = jnp.int32


def iota(shape, dim):
    return lax.broadcasted_iota(I32, shape, dim)


def mm(a, b, contract, precision=HIGH):
    return lax.dot_general(
        a, b, (contract, ((), ())), precision=precision, preferred_element_type=F32
    )


NN = ((1,), (0,))
NT = ((1,), (1,))
TN = ((0,), (0,))


def divided(value, by):
    return jnp.floor((value.astype(F32) + 0.5) * (1.0 / by)).astype(I32)


def split(values):
    high = values.astype(BF16)
    rest = values - high.astype(F32)
    middle = rest.astype(BF16)
    low = (rest - middle.astype(F32)).astype(BF16)
    return low, middle, high


def select(picks, values, contract, swap=False):
    total = None
    for part in split(values):
        a, b = (part, picks) if swap else (picks, part)
        term = lax.dot_general(a, b, (contract, ((), ())), preferred_element_type=F32)
        total = term if total is None else total + term
    return total


def product(a, b, contract):
    (al, am, ah), (bl, bm, bh) = split(a), split(b)
    total = None
    for x, y in ((al, bh), (ah, bl), (am, bm), (am, bh), (ah, bm), (ah, bh)):
        term = lax.dot_general(x, y, (contract, ((), ())), preferred_element_type=F32)
        total = term if total is None else total + term
    return total


def vertical_mix(values, levels):
    upper = jnp.concatenate([values[1:levels], values[levels - 1 : levels]], axis=0)
    lower = jnp.concatenate([values[0:1], values[0 : levels - 1]], axis=0)
    inner = values[0:levels]
    return inner + VERTIC * (upper + lower - 2.0 * inner)


def element_of_row(rows):
    elements = rows // 4
    hit = divided(iota((rows, elements), 0), 4) == iota((rows, elements), 1)
    return jnp.where(hit, 1.0, 0.0).astype(BF16)


def element_means(columns_ref):
    elements = columns_ref.shape[0] // 4
    total = columns_ref[pl.ds(0, elements, stride=4), :]
    for k in range(1, 4):
        total = total + columns_ref[pl.ds(k, elements, stride=4), :]
    return 0.25 * total


def own_part(values, means, mixing, levels):
    rows, width = values.shape
    lane = iota((rows, width), 1)
    level = lane - levels * divided(lane, levels)
    upper = jnp.where(level == levels - 1, values, pltpu.roll(values, width - 1, 1))
    lower = jnp.where(level == 0, values, pltpu.roll(values, 1, 1))
    mean = select(element_of_row(rows), means, NN)
    return values - (4.0 * mixing) * mean + VMIX * (upper + lower - 2.0 * values)


def joined_means(mine_ref, other_ref, share, order):
    first = lax.axis_index("sec") % 2 == 0
    parts = []
    for j in order:
        mine, other = mine_ref[j, :share, :], other_ref[j, :share, :]
        parts += [jnp.where(first, mine, other), jnp.where(first, other, mine)]
    return jnp.concatenate(parts, axis=0)


def slots_of(targets, col_count, padded, clouds):
    rows = targets.shape[1]
    onehot = jnp.where(iota((clouds, rows), 0) == targets, 1.0, 0.0)
    before = jnp.where(iota((rows, rows), 0) < iota((rows, rows), 1), 1.0, 0.0)
    running = mm(onehot.astype(BF16), before.astype(BF16), NN, None)
    ranks = jnp.sum(running * onehot, axis=0, keepdims=True).astype(I32)
    owner = divided(targets, col_count)
    return owner, (targets - owner * col_count) * padded + ranks


def blocked(ref, value, levels):
    ref[...] = jnp.zeros_like(ref)
    for f in range(ref.shape[0] // levels):
        ref[f * levels : f * levels + value.shape[0], f * levels : (f + 1) * levels] = value


def host_kernel(
    columns_ref,
    mixing_ref,
    neighbours_ref,
    targets_ref,
    substeps_ref,
    map_ref,
    out_ref,
    fold_ref,
    *,
    padded,
    clouds,
):
    rows, width = columns_ref.shape
    cloud_levels, levels = map_ref.shape
    col_count = out_ref.shape[0]
    block = col_count * padded
    means = element_means(columns_ref)
    share = means.shape[0] // 2
    section = lax.axis_index("sec")
    part = jnp.where(section % 2 == 0, means[:share], means[share:])
    for c in range(col_count):
        out_ref[c, :share, :] = part
    blocked(fold_ref, RELAX * vertical_mix(map_ref[...], cloud_levels), levels)
    owner, slot = slots_of(targets_ref[...], col_count, padded, clouds)
    mine = jnp.where(owner + 1 == section, slot, -1)
    pack = jnp.where(iota((block, rows), 0) == mine, 1.0, 0.0).astype(BF16)
    base = own_part(columns_ref[...], means, mixing_ref[...], levels)
    count = neighbours_ref.shape[0]
    ids = select(element_of_row(rows), neighbours_ref[...].astype(F32), NT, swap=True)
    extras = jnp.concatenate(
        [
            jnp.zeros((cloud_levels, rows), F32),
            ids,
            jnp.zeros((levels - 1 - cloud_levels - count, rows), F32),
            substeps_ref[...].astype(F32),
            jnp.zeros((width - levels, rows), F32),
        ],
        axis=0,
    )
    sent = product(select(pack, base, NN), fold_ref[...], NT) + select(pack, extras, NT)
    capacity = out_ref.shape[1] - share
    for c in range(col_count):
        out_ref[c, share:, :] = sent[c * padded : c * padded + capacity]


def aside(
    columns_ref,
    mixing_ref,
    neighbours_ref,
    targets_ref,
    map_ref,
    base_ref,
    weights_ref,
    homes_ref,
    fold_ref,
    unfold_ref,
    col_count,
    padded,
    clouds,
    half,
    held,
):
    rows, width = columns_ref.shape
    cloud_levels, levels = map_ref.shape
    elements = rows // 4
    position = lax.axis_index("col")
    base_ref[...] = own_part(
        columns_ref[...], element_means(columns_ref), mixing_ref[...], levels
    )
    near = neighbours_ref[...] - (position - 1) * elements
    near = jnp.where(near < 0, near + elements * col_count, near)
    near = jnp.where(near >= elements * col_count, near - elements * col_count, near)
    window = iota((3 * elements, elements), 0)
    picks = jnp.zeros((3 * elements, elements), F32)
    for k in range(near.shape[0]):
        picks = picks + jnp.where(window == near[k : k + 1, :], 1.0, 0.0)
    weights_ref[...] = mm(element_of_row(rows), picks.astype(BF16), NT, None).astype(BF16)
    owner, slot = slots_of(targets_ref[...], col_count, padded, clouds)
    place = divided(slot, padded)
    rank = slot - place * padded
    upper = jnp.where(rank >= half, 1, 0)
    parity = lax.axis_index("sec") % 2
    cloud = owner * col_count + place + jnp.where(upper == parity, 0, clouds)
    everywhere = (cloud * held + rank - half * upper).astype(F32)
    identity = jnp.where(iota((rows, rows), 0) == iota((rows, rows), 1), 1.0, 0.0)
    homes_ref[...] = select(
        identity.astype(BF16), jnp.broadcast_to(everywhere, (LANES, rows)), NT
    )
    blocked(fold_ref, RELAX * vertical_mix(map_ref[...], cloud_levels), levels)
    fold_ref[...] = fold_ref[...] * mixing_ref[...]
    blocked(unfold_ref, map_ref[...], levels)


class Segment:
    def __init__(self, lane0, width, levels, begin):
        self.lane0, self.width, self.begin, self.levels = lane0, width, begin, levels
        self.steps = -(-levels // (LANES // width))
        self.groups = -(-levels // self.steps)
        self.missing = self.groups * self.steps - levels
        self.blocks = -(-self.steps // STEP)
        self.rows = (begin + 1, begin + 1 + self.steps)

    def group_steps(self, g):
        return self.steps - (self.missing if g == self.groups - 1 else 0)


def segments_of(slots, levels):
    segments, begin = [], 0
    for lane0 in range(0, slots, LANES):
        segments.append(Segment(lane0, min(LANES, slots - lane0), levels, begin))
        begin += segments[-1].steps + 2
    rows = max([begin] + [s.begin + 2 + s.blocks * STEP for s in segments])
    return segments, rows, -(-rows // 8) * 8


def fill_spare(segments, load, store):
    def turned(value, shift):
        tall = jnp.broadcast_to(value, (8, LANES)) if value.shape[0] == 1 else value
        return pltpu.roll(tall, shift % LANES, 1)[: value.shape[0]]

    for s in segments:
        if s.missing:
            row = s.rows[1] - s.missing
            value = load(row - 1)
            lane = iota(value.shape, 1)
            store(row, jnp.where(lane >= (s.groups - 1) * s.width, value, load(row)))
        first, last = load(s.rows[0]), load(s.rows[1] - 1)
        before, after = first, last
        if s.groups > 1:
            lane = iota(first.shape, 1)
            before = jnp.where(lane < s.width, first, turned(last, s.width))
            after = jnp.where(lane < (s.groups - 1) * s.width, turned(first, -s.width), last)
        store(s.begin, before)
        store(s.rows[1], after)


def fill_wide(segments, ref):
    def store(row, value):
        ref[row] = value

    fill_spare(segments, lambda row: ref[row], store)


def fill_flat(segments, ref):
    def store(row, value):
        ref[row : row + 1, :] = value

    fill_spare(segments, lambda row: ref[row : row + 1, :], store)


def linear(below, here, above):
    east = [pltpu.roll(here[3], 1, 0), here[0], here[1], here[2]]
    west = [here[1], here[2], here[3], pltpu.roll(here[0], 7, 0)]
    keep = (1.0 - 2.0 * HORIZ - 2.0 * VERTIC) / VERTIC
    return [
        (below[j] + above[j]) + ((HORIZ / VERTIC) * (east[j] + west[j]) + keep * here[j])
        for j in range(4)
    ]


def groups(ref, index):
    return [ref[index + (pl.ds(8 * j, 8),)] for j in range(4)]


def strided(ref, row):
    return [ref[row, pl.ds(j, 8, stride=4), :] for j in range(4)]


def sweep(segment, load, work):
    def block(i, carry):
        row = segment.begin + i * STEP
        held = [load(row), load(row + 1)]
        for k in range(STEP):
            held.append(load(row + k + 2))
            work(row + k + 1, held[k], held[k + 1], held[k + 2])
        return carry

    lax.fori_loop(0, segment.blocks, block, 0)


def each(count, size, work):
    size = min(size, count)

    def run(first):
        for k in range(size):
            work(first + k)

    if count // size:
        lax.fori_loop(0, count // size, lambda i, c: (run(i * size), c)[1], 0)
    if count % size:
        run(count - size)


def widen(state_ref, natural_ref, segments, scale):
    levels, columns, _ = state_ref.shape
    for s in segments:
        at = slice(s.lane0, s.lane0 + s.width)

        def one(k):
            parts = []
            for g in range(s.groups):
                level = jnp.minimum(g * s.steps + k, levels - 1)
                parts.append(state_ref[level, :, at].astype(F32))
            spare = LANES - s.groups * s.width
            if spare:
                parts.append(jnp.zeros((columns, spare), F32))
            value = jnp.concatenate(parts, axis=1) if len(parts) > 1 else parts[0]
            natural_ref[s.begin + 1 + k] = scale * value if scale != 1.0 else value

        each(s.steps, STEP, one)


def folded_sums(sums_ref, columns):
    rows = sums_ref.shape[0] // 8
    total = sums_ref[pl.ds(0, rows, stride=8), :]
    for k in range(1, 8):
        total = total + sums_ref[pl.ds(k, rows, stride=8), :]
    return total * (1.0 / columns)


def slab(row):
    return pl.ds(pl.multiple_of(row * 8, 8), 8)


def spread_row(ref, row):
    return jnp.broadcast_to(ref[pl.ds(row, 1), :], (8, LANES))


def turn(value, shift):
    if not shift:
        return value
    height = value.shape[0]
    tall = -(-height // 8) * 8
    if tall != height:
        fill = jnp.zeros((tall - height, LANES), F32)
        value = jnp.concatenate([value, fill], axis=0)
    return pltpu.roll(value, shift % LANES, 1)[:height]


def each(count, size, work):
    size = min(size, count)

    def run(first):
        for k in range(size):
            work(first + k)

    if count // size:
        lax.fori_loop(0, count // size, lambda i, c: (run(i * size), c)[1], 0)
    if count % size:
        run(count - size)


def widen(state_ref, natural_ref, segments, scale):
    levels, columns, _ = state_ref.shape
    for s in segments:
        at = slice(s.lane0, s.lane0 + s.width)

        def one(k):
            parts = []
            for g in range(s.groups):
                level = jnp.minimum(g * s.steps + k, levels - 1)
                parts.append(state_ref[level, :, at].astype(F32))
            spare = LANES - s.groups * s.width
            if spare:
                parts.append(jnp.zeros((columns, spare), F32))
            value = jnp.concatenate(parts, axis=1) if len(parts) > 1 else parts[0]
            natural_ref[s.begin + 1 + k] = scale * value if scale != 1.0 else value

        each(s.steps, STEP, one)


def folded_sums(sums_ref, columns):
    rows = sums_ref.shape[0] // 8
    total = sums_ref[pl.ds(0, rows, stride=8), :]
    for k in range(1, 8):
        total = total + sums_ref[pl.ds(k, rows, stride=8), :]
    return total * (1.0 / columns)


def slab(row):
    return pl.ds(pl.multiple_of(row * 8, 8), 8)


def spread_row(ref, row):
    return jnp.broadcast_to(ref[pl.ds(row, 1), :], (8, LANES))


def lane_places(segments):
    return [(s, g) for s in segments for g in range(s.groups)]


def slot_map(segments, block, capacity, padded):
    tiles = []
    for s in segments:
        lane = iota((8, LANES), 1)
        slot = s.lane0 + lane
        row = slot + (padded - capacity) * divided(slot, capacity)
        row = jnp.where(lane < s.width, row, -1)[0:1]
        tiles.append(jnp.where(iota((block, LANES), 0) == row, 1.0, 0.0).astype(BF16))
    return jnp.concatenate(tiles, axis=1)


def prepare_kernel(
    state_ref,
    columns_far,
    mixing_far,
    neighbours_far,
    targets_far,
    map_far,
    saturation_far,
    moved_ref,
    means_ref,
    limits_ref,
    energy_far,
    base_far,
    weights_far,
    homes_far,
    fold_ref,
    unfold_far,
    state_buf,
    natural_ref,
    sums_ref,
    flat_ref,
    energy_buf,
    columns_ref,
    mixing_ref,
    neighbours_ref,
    targets_ref,
    map_ref,
    saturation_ref,
    base_ref,
    weights_ref,
    homes_ref,
    unfold_ref,
    sems,
    in_sems,
    out_sems,
    *,
    segments,
    **host,
):
    fields, levels, columns, _ = state_ref.shape
    given = (
        (columns_far, columns_ref),
        (mixing_far, mixing_ref),
        (neighbours_far, neighbours_ref),
        (targets_far, targets_ref),
        (map_far, map_ref),
        (saturation_far, saturation_ref),
    )
    starts = [pltpu.make_async_copy(x, y, in_sems.at[i]) for i, (x, y) in enumerate(given)]
    loads = [
        pltpu.make_async_copy(state_ref.at[f], state_buf.at[f], sems.at[f]) for f in range(fields)
    ]
    for copy in starts + loads:
        copy.start()
    made = (
        (base_ref, base_far),
        (weights_ref, weights_far),
        (homes_ref, homes_far),
        (unfold_ref, unfold_far),
        (energy_buf, energy_far),
    )
    leaves = [pltpu.make_async_copy(x, y, out_sems.at[i]) for i, (x, y) in enumerate(made)]
    for copy in starts:
        copy.wait()
    tall = flat_ref.shape[0]
    here = iota((tall, levels), 0) == iota((tall, levels), 1)
    diagonal = jnp.where(here, saturation_ref[...], 0.0)
    flat_ref[...] = select(jnp.ones((levels, LANES), BF16), diagonal, NN, swap=True)
    limits_ref[...] = jnp.zeros_like(limits_ref)
    for s in segments:
        lane = iota((s.steps, LANES), 1)
        value = flat_ref[0 : s.steps, :]
        for g in range(1, s.groups):
            other = flat_ref[g * s.steps : (g + 1) * s.steps, :]
            value = jnp.where(lane >= g * s.width, other, value)
        limits_ref[s.rows[0] : s.rows[1], :] = value
    sums_ref[...] = jnp.zeros_like(sums_ref)
    aside(
        columns_ref,
        mixing_ref,
        neighbours_ref,
        targets_ref,
        map_ref,
        base_ref,
        weights_ref,
        homes_ref,
        fold_ref,
        unfold_ref,
        **host,
    )
    for copy in leaves[:4]:
        copy.start()
    for f, scale, target in ((0, SHRINK, energy_buf), (1, 1.0, moved_ref)):
        loads[f].wait()
        widen(state_buf.at[f], natural_ref, segments, scale)
        fill_wide(segments, natural_ref)
        for s in segments:

            def work(row, below, here, above):
                out = linear(below, here, above)
                for j in range(4):
                    target[row, pl.ds(8 * j, 8), :] = out[j]
                sums_ref[slab(row), :] = (here[0] + here[1]) + (here[2] + here[3])

            sweep(s, lambda row: strided(natural_ref, row), work)
        if f == 0:
            leaves[4].start()
        means_ref[f] = folded_sums(sums_ref, columns) * (1.0 / scale)
    for copy in leaves:
        copy.wait()


def neighbour_part(arrived, means, fold, share, parity, levels, stride, neighbours):
    folded = product(fold, means, NT)
    taken = arrived[stride - 1 : stride] > 0.0
    ids = [
        jnp.where(taken, arrived[levels + k : levels + k + 1], -1.0) for k in range(neighbours)
    ]
    total = None
    chunk = min(256, means.shape[0])
    for first in range(0, means.shape[0], chunk):
        row = iota((chunk, arrived.shape[1]), 0) + first
        element = (row + share * divided(row, share) + share * parity).astype(F32)
        wanted = jnp.where(element == ids[0], 1.0, 0.0)
        for k in range(1, neighbours):
            wanted = wanted + jnp.where(element == ids[k], 1.0, 0.0)
        part = folded[:, first : first + chunk]
        term = select(wanted.astype(BF16), part, NN, swap=True)
        total = term if total is None else total + term
    return total


def halves(ref, share):
    return jnp.concatenate([ref[j, :share, :] for j in range(ref.shape[0])], axis=0)


def arrive_kernel(
    received_ref, fold_ref, arrived_ref, places_ref, *, segments, capacity, padded, **sizes
):
    hosts = received_ref.shape[0]
    share = received_ref.shape[1] - capacity
    places = slot_map(segments, hosts * padded, capacity, padded)
    places_ref[...] = places
    parts = []
    for j in range(hosts):
        parts.append(received_ref[j, share:, :])
        if padded != capacity:
            parts.append(jnp.zeros((padded - capacity, LANES), F32))
    arrived = select(places, jnp.concatenate(parts, axis=0), TN, swap=True)
    parity = lax.axis_index("sec") % 2
    arrived_ref[...] = arrived + neighbour_part(
        arrived, halves(received_ref, share), fold_ref[...], share, parity, **sizes
    )


def water_kernel(
    arrived_ref,
    places_ref,
    other_ref,
    moved_ref,
    means_ref,
    limits_ref,
    fold_ref,
    unfold_far,
    water_far,
    spill_far,
    flats_far,
    back_far,
    unfold_ref,
    even_ref,
    odd_ref,
    spill_buf,
    flats_ref,
    goal_ref,
    mean_ref,
    shift_ref,
    limit_ref,
    sums_ref,
    change_ref,
    back_ref,
    in_sem,
    spill_sems,
    water_sem,
    flat_sem,
    back_sems,
    *,
    segments,
    share,
    padded,
    stride,
    levels,
    neighbours,
):
    rows = means_ref.shape[1]
    columns = even_ref.shape[1]
    load = pltpu.make_async_copy(unfold_far, unfold_ref, in_sem)
    load.start()
    hosts = other_ref.shape[0]
    parity = 1 - lax.axis_index("sec") % 2
    arrived = arrived_ref[...]
    arrived = arrived + neighbour_part(
        arrived,
        halves(other_ref, share),
        fold_ref[...],
        share,
        parity,
        levels,
        stride,
        neighbours,
    )
    goal_ref[...] = jnp.zeros_like(goal_ref)
    flats_ref[...] = jnp.zeros_like(flats_ref)
    sums_ref[...] = jnp.zeros_like(sums_ref)
    counts = flats_ref.at[MAX_SUB + 2]
    for t, s in enumerate(segments):
        lanes = slice(t * LANES, (t + 1) * LANES)
        count = None
        for g in range(s.groups):
            number = s.group_steps(g)
            at = slice(s.rows[0], s.rows[0] + number)
            for f in range(2):
                first = f * stride + g * s.steps
                part = turn(arrived[first : first + number, lanes], g * s.width)
                goal_ref[f, at, :] = goal_ref[f, at, :] + part if g else part
            part = turn(arrived[stride - 1 : stride, lanes], g * s.width)
            count = part if count is None else count + part
        counts[s.rows[0] : s.rows[1], :] = jnp.broadcast_to(count, (s.steps, LANES))
    for f in range(2):
        mean_ref[f] = means_ref[f]
    copies = []
    source, target = None, even_ref
    for n in range(MAX_SUB):
        scale = 0.5 * GROW ** (n + 1)
        last = n + 1 == MAX_SUB
        expected = []
        for f in range(2):
            fill_flat(segments, mean_ref.at[f])
            mean = mean_ref[f]
            mixed = mean + VERTIC * (
                pltpu.roll(mean, 1, 0) + pltpu.roll(mean, rows - 1, 0) - 2.0 * mean
            )
            offset = goal_ref[f] - RELAX * mixed
            expected.append(mixed + offset)
            if f == 1:
                shift_ref[...] = scale * offset
            else:
                flats_ref[n] = (scale * SHRINK) * offset
        limit_ref[...] = scale * limits_ref[...]
        if last:
            flats_ref[MAX_SUB] = shift_ref[...]
            flats_ref[MAX_SUB + 1] = limit_ref[...]
            copies.append(pltpu.make_async_copy(flats_ref, flats_far, flat_sem))
            copies[-1].start()
        for s in segments:
            active = spread_row(counts, s.rows[0]) > float(n)

            def finish(row, lin, old):
                shift = spread_row(shift_ref, row)
                limit = spread_row(limit_ref, row)
                total = None
                for j in range(4):
                    v = lin[j] + shift
                    low = jnp.minimum(v, limit)
                    total = low if total is None else total + low
                    if last:
                        continue
                    u = v + low
                    if old is not None:
                        u = jnp.where(active, u, old[j])
                    spill_buf[n, row, pl.ds(8 * j, 8), :] = v - low
                    target[row, pl.ds(8 * j, 8), :] = u
                sums_ref[slab(row), :] = total

            if n == 0:

                def block(i, carry):
                    for k in range(STEP):
                        row = s.begin + 1 + i * STEP + k
                        finish(row, groups(moved_ref, (row,)), None)
                    return carry

                lax.fori_loop(0, s.blocks, block, 0)
            else:

                def work(row, below, here, above):
                    finish(row, linear(below, here, above), here)

                sweep(s, lambda row: groups(source, (row,)), work)
        if not last:
            copies.append(
                pltpu.make_async_copy(spill_buf.at[n], spill_far.at[n], spill_sems.at[n])
            )
            copies[-1].start()
            fill_wide(segments, target)
            source, target = target, (odd_ref if target is even_ref else even_ref)
        if n + 2 == MAX_SUB:
            copies.append(pltpu.make_async_copy(source, water_far, water_sem))
            copies[-1].start()
        spilled = 0.5 * (expected[1] - folded_sums(sums_ref, columns) * (1.0 / scale))
        step = [expected[0] + LATENT * spilled, expected[1] - spilled]
        keep = counts[...] > float(n)
        for f in range(2):
            mean_ref[f] = jnp.where(keep, step[f], mean_ref[f])
    change_ref[...] = jnp.zeros_like(change_ref)
    for f in range(2):
        change = mean_ref[f] - means_ref[f]
        for t, s in enumerate(segments):
            for g in range(s.groups):
                first, number = f * stride + g * s.steps, s.group_steps(g)
                part = turn(change[s.rows[0] : s.rows[0] + number], -g * s.width)
                change_ref[first : first + number, t * LANES : (t + 1) * LANES] = part
    spread = select(places_ref[...], change_ref[...], NT)
    load.wait()
    back = product(spread, unfold_ref[...], NN)
    quads = back_ref.shape[2]
    for h in range(2):
        for j in range(hosts):
            for q in range(quads):
                first = j * padded + (h * quads + q) * QUAD
                back_ref[h, j, q] = back[first : first + QUAD]
    for i in range(back_far.shape[0]):
        copies.append(pltpu.make_async_copy(back_ref.at[i % 2], back_far.at[i], back_sems.at[i]))
        copies[-1].start()
    for copy in copies:
        copy.wait()


def energy_kernel(
    state_ref,
    energy_far,
    water_far,
    spill_far,
    flats_far,
    base_far,
    weights_far,
    mixing_far,
    homes_far,
    received_ref,
    other_ref,
    out_ref,
    advanced_ref,
    picks_ref,
    state_buf,
    energy_buf,
    water_buf,
    spill_buf,
    flats_ref,
    base_ref,
    weights_ref,
    mixing_ref,
    homes_ref,
    out_buf,
    even_ref,
    odd_ref,
    natural_ref,
    state_sems,
    in_sems,
    spill_sems,
    out_sems,
    *,
    segments,
    share,
):
    fields, levels, columns, _ = state_ref.shape
    final = MAX_SUB - 1
    pairs = (
        (flats_far, flats_ref),
        (base_far, base_ref),
        (weights_far, weights_ref),
        (mixing_far, mixing_ref),
        (water_far, water_buf),
        (energy_far, energy_buf),
        (homes_far, homes_ref),
    )
    loads = [pltpu.make_async_copy(x, y, in_sems.at[i]) for i, (x, y) in enumerate(pairs)]
    flats, bases, shares, mixings, waters, first, homes = loads
    states = [
        pltpu.make_async_copy(state_ref.at[f], state_buf.at[f], state_sems.at[f])
        for f in range(fields)
    ]
    spills = [
        pltpu.make_async_copy(spill_far.at[n], spill_buf.at[n], spill_sems.at[n])
        for n in range(final)
    ]
    for copy in loads[:5] + [states[1], first] + spills + [states[0], homes]:
        copy.start()
    cut = -(-levels // 2)
    spans = ((0, cut), (cut, levels - cut))

    def leave(f, part):
        at = pl.ds(*spans[part])
        return pltpu.make_async_copy(
            out_buf.at[f, at], out_ref.at[f, at], out_sems.at[2 * f + part]
        )

    counts = flats_ref.at[MAX_SUB + 2]

    def finish_field(f, found):
        for s in segments[::-1]:
            count = spread_row(counts, s.rows[0])
            back = jnp.zeros((8, LANES), F32)
            for n in range(1, MAX_SUB + 1):
                scale = GROW**-n * (LATENT if f == 0 else 1.0)
                back = jnp.where(count == float(n), scale, back)
            at = slice(s.lane0, s.lane0 + s.width)
            held = jnp.broadcast_to(count[0:1, : s.width], (columns, s.width)) > 0.0

            def permute(k):
                row = s.begin + 1 + k
                value = groups(found, (row,))
                for j in range(4):
                    natural_ref[row, pl.ds(j, 8, stride=4), :] = value[j] * back

            def narrow(g, k):
                level = g * s.steps + k
                lanes = slice(g * s.width, (g + 1) * s.width)
                old = state_buf[f, level, :, at].astype(F32)
                value = jnp.where(held, natural_ref[s.begin + 1 + k, :, lanes], old)
                out_buf[f, level, :, at] = value.astype(BF16)

            each(s.steps, STEP, permute)
            if s is segments[0] and s.groups == 1:
                for part, (begin, number) in enumerate(spans):
                    each(number, STEP, lambda k: narrow(0, begin + k))
                    leave(f, part).start()
            else:
                for g in range(s.groups):
                    each(s.group_steps(g), STEP, lambda k: narrow(g, k))
        if segments[0].groups > 1:
            for part in range(2):
                leave(f, part).start()

    bases.wait()
    shares.wait()
    mixings.wait()
    hosts = received_ref.shape[0]
    position = lax.axis_index("col")
    around = [jnp.where(position == 0, hosts - 1, position - 1), position]
    around.append(jnp.where(position == hosts - 1, 0, position + 1))
    means = joined_means(received_ref, other_ref, share, around)
    advanced_ref[...] = base_ref[...] + mixing_ref[...] * select(weights_ref[...], means, NN)
    flats.wait()
    waters.wait()
    for s in segments:
        active = spread_row(counts, s.rows[0]) > float(final)

        def last(row, below, here, above):
            water = linear(below, here, above)
            push = spread_row(flats_ref.at[MAX_SUB], row)
            limit = spread_row(flats_ref.at[MAX_SUB + 1], row)
            for j in range(4):
                v = water[j] + push
                low = jnp.minimum(v, limit)
                spill_buf[final, row, pl.ds(8 * j, 8), :] = v - low
                even_ref[row, pl.ds(8 * j, 8), :] = jnp.where(active, v + low, here[j])

        sweep(s, lambda row: groups(water_buf, (row,)), last)
    states[1].wait()
    finish_field(1, even_ref)
    first.wait()
    source, target = None, odd_ref
    for n in range(MAX_SUB):
        if n < final:
            spills[n].wait()
        for s in segments:
            active = spread_row(counts, s.rows[0]) > float(n)

            def start(i, carry):
                for k in range(STEP):
                    row = s.begin + 1 + i * STEP + k
                    shift = spread_row(flats_ref.at[n], row)
                    lin, spill = groups(energy_buf, (row,)), groups(spill_buf, (n, row))
                    for j in range(4):
                        target[row, pl.ds(8 * j, 8), :] = 2.0 * (lin[j] + shift) + spill[j]
                return carry

            def work(row, below, here, above):
                shift = spread_row(flats_ref.at[n], row)
                lin = linear(below, here, above)
                spill = groups(spill_buf, (n, row))
                for j in range(4):
                    u = 2.0 * (lin[j] + shift) + spill[j]
                    target[row, pl.ds(8 * j, 8), :] = jnp.where(active, u, here[j])

            if n == 0:
                lax.fori_loop(0, s.blocks, start, 0)
            else:
                sweep(s, lambda row: groups(source, (row,)), work)
        if n < final:
            fill_wide(segments, target)
        source, target = target, (odd_ref if target is even_ref else even_ref)
    states[0].wait()
    finish_field(0, source)
    homes.wait()
    place = homes_ref[:, :1].astype(I32)
    picks_ref[...] = jnp.where(iota(picks_ref.shape, 1) == place, 1.0, 0.0).astype(BF16)
    for f in range(fields):
        for part in range(2):
            leave(f, part).wait()


def gather_half(picks_ref, half_ref, table_ref, idle, part):
    sources, quads, _, _ = half_ref.shape
    height = table_ref.shape[0]
    held = height // (sources - idle)
    if quads * QUAD != held:
        table_ref[...] = jnp.zeros_like(table_ref)
    for j in range(sources - idle):
        for q in range(quads):
            first = j * held + q * QUAD
            table_ref[first : first + QUAD, :] = half_ref[idle + j, q]
    picks = picks_ref[:, part * height : (part + 1) * height]
    return select(picks, table_ref[...], NN)


def nearly_kernel(advanced_ref, picks_ref, mine_ref, out_ref, table_ref, *, idle):
    out_ref[...] = advanced_ref[...] + gather_half(picks_ref, mine_ref, table_ref, idle, 0)


def final_kernel(nearly_ref, picks_ref, other_ref, out_ref, table_ref, *, levels, idle):
    summed = nearly_ref[...] + gather_half(picks_ref, other_ref, table_ref, idle, 1)
    water = divided(iota(summed.shape, 1), levels) == 1
    out_ref[...] = jnp.where(water, jnp.maximum(summed, 0.0), summed)


SPACES = dict(
    auto=pl.BlockSpec(memory_space=pltpu.VMEM),
    near=pl.BlockSpec(memory_space=pltpu.VMEM),
    far=pl.BlockSpec(memory_space=pl.ANY),
    scalar=pl.BlockSpec(memory_space=pltpu.SMEM),
)


def call(kernel, name, inputs, outputs, scratch=(), limit=8):
    kept = dict(near=pltpu.VMEM, auto=pltpu.HBM, far=pltpu.HBM, scalar=pltpu.HBM)
    arrays = [pltpu.with_memory_space_constraint(x, kept[space]) for space, x in inputs]
    shapes = [kept[space](dims, dtype) for space, dims, dtype in outputs]
    return pl.pallas_call(
        kernel,
        out_shape=shapes,
        in_specs=[SPACES[space] for space, _ in inputs],
        out_specs=[SPACES[space] for space, _, _ in outputs],
        scratch_shapes=list(scratch),
        compiler_params=pltpu.CompilerParams(vmem_limit_bytes=limit << 20),
        name=name,
    )(*arrays)


def body(
    column_state, mixing_rate, neighbours, assignment, substeps, cloud_state, level_map, saturation
):
    col_count = lax.axis_size("col")
    sec_count = lax.axis_size("sec")
    count, width = column_state.shape
    cloud_levels, levels = level_map.shape
    _, fields, _, columns, slots = cloud_state.shape
    elements = count // 4
    capacity = slots // col_count
    half = -(-capacity // (2 * QUAD)) * QUAD
    held = -(-half // 8) * 8
    padded = -(-max(capacity, 2 * half) // 8) * 8
    block = col_count * padded
    clouds = (sec_count - 1) * col_count
    segments, used, rows = segments_of(slots, cloud_levels)
    mapped = LANES * len(segments)
    mixing = mixing_rate.reshape(1, width)
    state = cloud_state[0]
    dma = pltpu.SemaphoreType.DMA

    def wide(*lead):
        return pltpu.VMEM((*lead, rows, columns, LANES), F32)

    hosts = dict(padded=padded, clouds=clouds)
    places_in = [
        ("auto", column_state),
        ("auto", mixing),
        ("auto", neighbours.T),
        ("auto", assignment.reshape(1, count)),
    ]
    outgoing, _ = call(
        functools.partial(host_kernel, **hosts),
        "host",
        places_in + [("auto", substeps.reshape(1, count)), ("auto", level_map)],
        [("auto", (col_count, elements // 2 + capacity, width), F32), ("near", (width, width), F32)],
    )
    received = lax.all_to_all(outgoing, "col", split_axis=0, concat_axis=0, tiled=True)
    moved, cloud_means, limits, energy, base, weights, homes, fold, unfold = call(
        functools.partial(
            prepare_kernel,
            segments=segments,
            col_count=col_count,
            half=half,
            held=held,
            **hosts,
        ),
        "prepare",
        [("far", state)]
        + [("far", x) for _, x in places_in]
        + [("far", level_map), ("far", saturation.reshape(1, cloud_levels))],
        [
            ("near", (used, columns, LANES), F32),
            ("near", (fields, rows, LANES), F32),
            ("near", (rows, LANES), F32),
            ("far", (used, columns, LANES), F32),
            ("far", (count, width), F32),
            ("far", (count, 3 * elements), BF16),
            ("far", (count, LANES), F32),
            ("near", (width, width), F32),
            ("far", (width, width), F32),
        ],
        scratch=[
            pltpu.VMEM(state.shape, BF16),
            wide(),
            pltpu.VMEM((rows * 8, LANES), F32),
            pltpu.VMEM((max(s.groups * s.steps for s in segments), LANES), F32),
            pltpu.VMEM((used, columns, LANES), F32),
            pltpu.VMEM((count, width), F32),
            pltpu.VMEM((1, width), F32),
            pltpu.VMEM((neighbours.shape[1], elements), I32),
            pltpu.VMEM((1, count), I32),
            pltpu.VMEM((cloud_levels, levels), F32),
            pltpu.VMEM((1, cloud_levels), F32),
            pltpu.VMEM((count, width), F32),
            pltpu.VMEM((count, 3 * elements), BF16),
            pltpu.VMEM((count, LANES), F32),
            pltpu.VMEM((width, width), F32),
            dma((fields,)),
            dma((6,)),
            dma((5,)),
        ],
        limit=16,
    )
    received, moved, base = lax.optimization_barrier((received, moved, base))
    pairs = [(i, i ^ 1) for i in range(sec_count)]
    other = lax.ppermute(received, "sec", pairs)
    sizes = dict(stride=levels, levels=cloud_levels, neighbours=neighbours.shape[1])
    arrived, places = call(
        functools.partial(
            arrive_kernel, segments=segments, capacity=capacity, padded=padded, **sizes
        ),
        "arrive",
        [("near", received), ("near", fold)],
        [("near", (width, mapped), F32), ("near", (block, mapped), BF16)],
    )
    water, spill, flats, back = call(
        functools.partial(
            water_kernel, segments=segments, share=elements // 2, padded=padded, **sizes
        ),
        "water",
        [
            ("near", arrived),
            ("near", places),
            ("near", other),
            ("near", moved),
            ("near", cloud_means),
            ("near", limits),
            ("near", fold),
            ("far", unfold),
        ],
        [
            ("far", (rows, columns, LANES), F32),
            ("far", (MAX_SUB - 1, rows, columns, LANES), F32),
            ("far", (MAX_SUB + 3, rows, LANES), F32),
            ("far", (sec_count, col_count, half // QUAD, QUAD, width), F32),
        ],
        scratch=[
            pltpu.VMEM((width, width), F32),
            wide(),
            wide(),
            wide(MAX_SUB - 1),
            pltpu.VMEM((MAX_SUB + 3, rows, LANES), F32),
            pltpu.VMEM((fields, rows, LANES), F32),
            pltpu.VMEM((fields, rows, LANES), F32),
            pltpu.VMEM((rows, LANES), F32),
            pltpu.VMEM((rows, LANES), F32),
            pltpu.VMEM((rows * 8, LANES), F32),
            pltpu.VMEM((width, mapped), F32),
            pltpu.VMEM((2, col_count, half // QUAD, QUAD, width), F32),
            dma(()),
            dma((MAX_SUB - 1,)),
            dma(()),
            dma(()),
            dma((sec_count,)),
        ],
        limit=24,
    )
    returned = lax.all_to_all(
        back.reshape(sec_count * col_count, half // QUAD, QUAD, width),
        ("sec", "col"),
        split_axis=0,
        concat_axis=0,
        tiled=True,
    )
    new_block, advanced, picks = call(
        functools.partial(energy_kernel, segments=segments, share=elements // 2),
        "energy",
        [
            ("far", state),
            ("far", energy),
            ("far", water),
            ("far", spill),
            ("far", flats),
            ("far", base),
            ("far", weights),
            ("far", mixing),
            ("far", homes),
            ("near", received),
            ("near", other),
        ],
        [
            ("far", state.shape, BF16),
            ("near", (count, width), F32),
            ("near", (count, 2 * clouds * held), BF16),
        ],
        scratch=[
            pltpu.VMEM(state.shape, BF16),
            pltpu.VMEM((used, columns, LANES), F32),
            wide(),
            wide(MAX_SUB),
            pltpu.VMEM((MAX_SUB + 3, rows, LANES), F32),
            pltpu.VMEM((count, width), F32),
            pltpu.VMEM((count, 3 * elements), BF16),
            pltpu.VMEM((1, width), F32),
            pltpu.VMEM((count, LANES), F32),
            pltpu.VMEM(state.shape, BF16),
            wide(),
            wide(),
            wide(),
            dma((fields,)),
            dma((7,)),
            dma((MAX_SUB - 1,)),
            dma((2 * fields,)),
        ],
        limit=32,
    )
    returned, advanced = lax.optimization_barrier((returned, advanced))
    partner = lax.ppermute(returned, "sec", pairs)
    table = pltpu.VMEM((clouds * held, width), F32)
    (nearly,) = call(
        functools.partial(nearly_kernel, idle=col_count),
        "nearly",
        [("near", advanced), ("near", picks), ("near", returned)],
        [("near", (count, width), F32)],
        scratch=[table],
    )
    (new_columns,) = call(
        functools.partial(final_kernel, levels=levels, idle=col_count),
        "final",
        [("near", nearly), ("near", picks), ("near", partner)],
        [("auto", (count, width), F32)],
        scratch=[table],
    )
    return new_columns, new_block[None]


def solution(mesh):
    in_specs = (
        P("col", None),
        P(),
        P("col", None),
        P("col", None),
        P("col"),
        P("sec", None, None, None, "col"),
        P(),
        P(),
    )
    out_specs = (P("col", None), P("sec", None, None, None, "col"))
    return jax.shard_map(body, mesh=mesh, in_specs=in_specs, out_specs=out_specs, check_vma=False)
```

```python
import functools

import jax
import jax.numpy as jnp
from jax import lax
from jax.experimental import pallas as pl
from jax.experimental.pallas import tpu as pltpu
from jax.sharding import PartitionSpec as P

MAX_SUB = 4
RELAX = 0.25
HORIZ = 0.12
VERTIC = 0.1
LATENT = 2.5
GROW = 20.0
VMIX = 0.2
HIGH = lax.Precision.HIGHEST
LANES = 128
F32 = jnp.float32
BF16 = jnp.bfloat16
STEP = 10
QUAD = 4
SHRINK = 1.0 / LATENT
I32 = jnp.int32


def iota(shape, dim):
    return lax.broadcasted_iota(I32, shape, dim)


def mm(a, b, contract, precision=HIGH):
    return lax.dot_general(
        a, b, (contract, ((), ())), precision=precision, preferred_element_type=F32
    )


NN = ((1,), (0,))
NT = ((1,), (1,))
TN = ((0,), (0,))


def divided(value, by):
    return jnp.floor((value.astype(F32) + 0.5) * (1.0 / by)).astype(I32)


def split(values, count=3):
    parts, rest = [], values
    for _ in range(count - 1):
        parts.append(rest.astype(BF16))
        rest = rest - parts[-1].astype(F32)
    return [rest.astype(BF16)] + parts[::-1]


def select(picks, values, contract, swap=False):
    total = None
    for part in split(values):
        a, b = (part, picks) if swap else (picks, part)
        term = lax.dot_general(a, b, (contract, ((), ())), preferred_element_type=F32)
        total = term if total is None else total + term
    return total


def product(a, b, contract):
    (am, ah), (bm, bh) = split(a, 2), split(b, 2)
    total = None
    for x, y in ((am, bh), (ah, bm), (ah, bh)):
        term = lax.dot_general(x, y, (contract, ((), ())), preferred_element_type=F32)
        total = term if total is None else total + term
    return total


def vertical_mix(values, levels):
    upper = jnp.concatenate([values[1:levels], values[levels - 1 : levels]], axis=0)
    lower = jnp.concatenate([values[0:1], values[0 : levels - 1]], axis=0)
    inner = values[0:levels]
    return inner + VERTIC * (upper + lower - 2.0 * inner)


def element_of_row(rows):
    elements = rows // 4
    hit = divided(iota((rows, elements), 0), 4) == iota((rows, elements), 1)
    return jnp.where(hit, 1.0, 0.0).astype(BF16)


def element_means(columns_ref):
    elements = columns_ref.shape[0] // 4
    total = columns_ref[pl.ds(0, elements, stride=4), :]
    for k in range(1, 4):
        total = total + columns_ref[pl.ds(k, elements, stride=4), :]
    return 0.25 * total


def own_part(values, means, mixing, levels):
    rows, width = values.shape
    lane = iota((rows, width), 1)
    level = lane - levels * divided(lane, levels)
    upper = jnp.where(level == levels - 1, values, pltpu.roll(values, width - 1, 1))
    lower = jnp.where(level == 0, values, pltpu.roll(values, 1, 1))
    mean = select(element_of_row(rows), means, NN)
    return values - (4.0 * mixing) * mean + VMIX * (upper + lower - 2.0 * values)


def joined_means(mine_ref, other_ref, share, order):
    first = lax.axis_index("sec") % 2 == 0
    parts = []
    for j in order:
        mine, other = mine_ref[j, :share, :], other_ref[j, :share, :]
        parts += [jnp.where(first, mine, other), jnp.where(first, other, mine)]
    return jnp.concatenate(parts, axis=0)


def slots_of(targets, col_count, padded, clouds):
    rows = targets.shape[1]
    onehot = jnp.where(iota((clouds, rows), 0) == targets, 1.0, 0.0)
    before = jnp.where(iota((rows, rows), 0) < iota((rows, rows), 1), 1.0, 0.0)
    running = mm(onehot.astype(BF16), before.astype(BF16), NN, None)
    ranks = jnp.sum(running * onehot, axis=0, keepdims=True).astype(I32)
    owner = divided(targets, col_count)
    return owner, (targets - owner * col_count) * padded + ranks


def blocked(ref, value, levels):
    ref[...] = jnp.zeros_like(ref)
    for f in range(ref.shape[0] // levels):
        ref[f * levels : f * levels + value.shape[0], f * levels : (f + 1) * levels] = value


def host_kernel(
    columns_ref,
    mixing_ref,
    neighbours_ref,
    targets_ref,
    substeps_ref,
    map_ref,
    out_ref,
    fold_ref,
    *,
    padded,
    clouds,
):
    rows, width = columns_ref.shape
    cloud_levels, levels = map_ref.shape
    col_count = out_ref.shape[0]
    block = col_count * padded
    means = element_means(columns_ref)
    share = means.shape[0] // 2
    section = lax.axis_index("sec")
    part = jnp.where(section % 2 == 0, means[:share], means[share:])
    for c in range(col_count):
        out_ref[c, :share, :] = part
    blocked(fold_ref, RELAX * vertical_mix(map_ref[...], cloud_levels), levels)
    owner, slot = slots_of(targets_ref[...], col_count, padded, clouds)
    mine = jnp.where(owner + 1 == section, slot, -1)
    pack = jnp.where(iota((block, rows), 0) == mine, 1.0, 0.0).astype(BF16)
    base = own_part(columns_ref[...], means, mixing_ref[...], levels)
    count = neighbours_ref.shape[0]
    ids = select(element_of_row(rows), neighbours_ref[...].astype(F32), NT, swap=True)
    extras = jnp.concatenate(
        [
            jnp.zeros((cloud_levels, rows), F32),
            ids,
            jnp.zeros((levels - 1 - cloud_levels - count, rows), F32),
            substeps_ref[...].astype(F32),
            jnp.zeros((width - levels, rows), F32),
        ],
        axis=0,
    )
    sent = product(select(pack, base, NN), fold_ref[...], NT) + select(pack, extras, NT)
    capacity = out_ref.shape[1] - share
    for c in range(col_count):
        out_ref[c, share:, :] = sent[c * padded : c * padded + capacity]


def aside(
    columns_ref,
    mixing_ref,
    neighbours_ref,
    targets_ref,
    map_ref,
    base_ref,
    weights_ref,
    homes_ref,
    fold_ref,
    unfold_ref,
    col_count,
    padded,
    clouds,
    half,
    held,
):
    rows, width = columns_ref.shape
    cloud_levels, levels = map_ref.shape
    elements = rows // 4
    position = lax.axis_index("col")
    base_ref[...] = own_part(
        columns_ref[...], element_means(columns_ref), mixing_ref[...], levels
    )
    near = neighbours_ref[...] - (position - 1) * elements
    near = jnp.where(near < 0, near + elements * col_count, near)
    near = jnp.where(near >= elements * col_count, near - elements * col_count, near)
    window = iota((3 * elements, elements), 0)
    picks = jnp.zeros((3 * elements, elements), F32)
    for k in range(near.shape[0]):
        picks = picks + jnp.where(window == near[k : k + 1, :], 1.0, 0.0)
    weights_ref[...] = mm(element_of_row(rows), picks.astype(BF16), NT, None).astype(BF16)
    owner, slot = slots_of(targets_ref[...], col_count, padded, clouds)
    place = divided(slot, padded)
    rank = slot - place * padded
    upper = jnp.where(rank >= half, 1, 0)
    parity = lax.axis_index("sec") % 2
    cloud = owner * col_count + place
    row = jnp.where(upper == parity, cloud * held + rank - half * upper, -1)
    everywhere = row.astype(F32)
    identity = jnp.where(iota((rows, rows), 0) == iota((rows, rows), 1), 1.0, 0.0)
    homes_ref[...] = select(
        identity.astype(BF16), jnp.broadcast_to(everywhere, (LANES, rows)), NT
    )
    blocked(fold_ref, RELAX * vertical_mix(map_ref[...], cloud_levels), levels)
    fold_ref[...] = fold_ref[...] * mixing_ref[...]
    blocked(unfold_ref, map_ref[...], levels)


class Segment:
    def __init__(self, lane0, width, levels, begin):
        self.lane0, self.width, self.begin, self.levels = lane0, width, begin, levels
        self.steps = -(-levels // (LANES // width))
        self.groups = -(-levels // self.steps)
        self.missing = self.groups * self.steps - levels
        self.blocks = -(-self.steps // STEP)
        self.rows = (begin + 1, begin + 1 + self.steps)

    def group_steps(self, g):
        return self.steps - (self.missing if g == self.groups - 1 else 0)


def segments_of(slots, levels):
    segments, begin = [], 0
    for lane0 in range(0, slots, LANES):
        segments.append(Segment(lane0, min(LANES, slots - lane0), levels, begin))
        begin += segments[-1].steps + 2
    rows = max([begin] + [s.begin + 2 + s.blocks * STEP for s in segments])
    return segments, rows, -(-rows // 8) * 8


def fill_spare(segments, load, store):
    def turned(value, shift):
        tall = jnp.broadcast_to(value, (8, LANES)) if value.shape[0] == 1 else value
        return pltpu.roll(tall, shift % LANES, 1)[: value.shape[0]]

    for s in segments:
        if s.missing:
            row = s.rows[1] - s.missing
            value = load(row - 1)
            lane = iota(value.shape, 1)
            store(row, jnp.where(lane >= (s.groups - 1) * s.width, value, load(row)))
        first, last = load(s.rows[0]), load(s.rows[1] - 1)
        before, after = first, last
        if s.groups > 1:
            lane = iota(first.shape, 1)
            before = jnp.where(lane < s.width, first, turned(last, s.width))
            after = jnp.where(lane < (s.groups - 1) * s.width, turned(first, -s.width), last)
        store(s.begin, before)
        store(s.rows[1], after)


def fill_wide(segments, ref):
    def store(row, value):
        ref[row] = value

    fill_spare(segments, lambda row: ref[row], store)


def fill_flat(segments, ref):
    def store(row, value):
        ref[row : row + 1, :] = value

    fill_spare(segments, lambda row: ref[row : row + 1, :], store)


def linear(below, here, above):
    east = [pltpu.roll(here[3], 1, 0), here[0], here[1], here[2]]
    west = [here[1], here[2], here[3], pltpu.roll(here[0], 7, 0)]
    keep = (1.0 - 2.0 * HORIZ - 2.0 * VERTIC) / VERTIC
    return [
        (below[j] + above[j]) + ((HORIZ / VERTIC) * (east[j] + west[j]) + keep * here[j])
        for j in range(4)
    ]


def groups(ref, index):
    return [ref[index + (pl.ds(8 * j, 8),)] for j in range(4)]


def strided(ref, row):
    return [ref[row, pl.ds(j, 8, stride=4), :] for j in range(4)]


def sweep(segment, load, work):
    def block(i, carry):
        row = segment.begin + i * STEP
        held = [load(row), load(row + 1)]
        for k in range(STEP):
            held.append(load(row + k + 2))
            work(row + k + 1, held[k], held[k + 1], held[k + 2])
        return carry

    lax.fori_loop(0, segment.blocks, block, 0)


def each(count, size, work):
    size = min(size, count)

    def run(first):
        for k in range(size):
            work(first + k)

    if count // size:
        lax.fori_loop(0, count // size, lambda i, c: (run(i * size), c)[1], 0)
    if count % size:
        run(count - size)


def widen(state_ref, natural_ref, segments, scale):
    levels, columns, _ = state_ref.shape
    for s in segments:
        at = slice(s.lane0, s.lane0 + s.width)

        def one(k):
            parts = []
            for g in range(s.groups):
                level = jnp.minimum(g * s.steps + k, levels - 1)
                parts.append(state_ref[level, :, at].astype(F32))
            spare = LANES - s.groups * s.width
            if spare:
                parts.append(jnp.zeros((columns, spare), F32))
            value = jnp.concatenate(parts, axis=1) if len(parts) > 1 else parts[0]
            natural_ref[s.begin + 1 + k] = scale * value if scale != 1.0 else value

        each(s.steps, STEP, one)


def folded_sums(sums_ref, columns):
    rows = sums_ref.shape[0] // 8
    total = sums_ref[pl.ds(0, rows, stride=8), :]
    for k in range(1, 8):
        total = total + sums_ref[pl.ds(k, rows, stride=8), :]
    return total * (1.0 / columns)


def slab(row):
    return pl.ds(pl.multiple_of(row * 8, 8), 8)


def spread_row(ref, row):
    return jnp.broadcast_to(ref[pl.ds(row, 1), :], (8, LANES))


def turn(value, shift):
    if not shift:
        return value
    height = value.shape[0]
    tall = -(-height // 8) * 8
    if tall != height:
        fill = jnp.zeros((tall - height, LANES), F32)
        value = jnp.concatenate([value, fill], axis=0)
    return pltpu.roll(value, shift % LANES, 1)[:height]


def each(count, size, work):
    size = min(size, count)

    def run(first):
        for k in range(size):
            work(first + k)

    if count // size:
        lax.fori_loop(0, count // size, lambda i, c: (run(i * size), c)[1], 0)
    if count % size:
        run(count - size)


def widen(state_ref, natural_ref, segments, scale):
    levels, columns, _ = state_ref.shape
    for s in segments:
        at = slice(s.lane0, s.lane0 + s.width)

        def one(k):
            parts = []
            for g in range(s.groups):
                level = jnp.minimum(g * s.steps + k, levels - 1)
                parts.append(state_ref[level, :, at].astype(F32))
            spare = LANES - s.groups * s.width
            if spare:
                parts.append(jnp.zeros((columns, spare), F32))
            value = jnp.concatenate(parts, axis=1) if len(parts) > 1 else parts[0]
            natural_ref[s.begin + 1 + k] = scale * value if scale != 1.0 else value

        each(s.steps, STEP, one)


def folded_sums(sums_ref, columns):
    rows = sums_ref.shape[0] // 8
    total = sums_ref[pl.ds(0, rows, stride=8), :]
    for k in range(1, 8):
        total = total + sums_ref[pl.ds(k, rows, stride=8), :]
    return total * (1.0 / columns)


def slab(row):
    return pl.ds(pl.multiple_of(row * 8, 8), 8)


def spread_row(ref, row):
    return jnp.broadcast_to(ref[pl.ds(row, 1), :], (8, LANES))


def lane_places(segments):
    return [(s, g) for s in segments for g in range(s.groups)]


def slot_map(segments, block, capacity, padded):
    tiles = []
    for s in segments:
        lane = iota((8, LANES), 1)
        slot = s.lane0 + lane
        row = slot + (padded - capacity) * divided(slot, capacity)
        row = jnp.where(lane < s.width, row, -1)[0:1]
        tiles.append(jnp.where(iota((block, LANES), 0) == row, 1.0, 0.0).astype(BF16))
    return jnp.concatenate(tiles, axis=1)


def prepare_kernel(
    state_ref,
    columns_far,
    mixing_far,
    neighbours_far,
    targets_far,
    map_far,
    saturation_far,
    moved_ref,
    means_ref,
    limits_ref,
    energy_far,
    base_far,
    weights_far,
    homes_far,
    fold_ref,
    unfold_far,
    state_buf,
    natural_ref,
    sums_ref,
    flat_ref,
    energy_buf,
    columns_ref,
    mixing_ref,
    neighbours_ref,
    targets_ref,
    map_ref,
    saturation_ref,
    base_ref,
    weights_ref,
    homes_ref,
    unfold_ref,
    sems,
    in_sems,
    out_sems,
    *,
    segments,
    **host,
):
    fields, levels, columns, _ = state_ref.shape
    given = (
        (columns_far, columns_ref),
        (mixing_far, mixing_ref),
        (neighbours_far, neighbours_ref),
        (targets_far, targets_ref),
        (map_far, map_ref),
        (saturation_far, saturation_ref),
    )
    starts = [pltpu.make_async_copy(x, y, in_sems.at[i]) for i, (x, y) in enumerate(given)]
    loads = [
        pltpu.make_async_copy(state_ref.at[f], state_buf.at[f], sems.at[f]) for f in range(fields)
    ]
    for copy in starts + loads:
        copy.start()
    made = (
        (base_ref, base_far),
        (weights_ref, weights_far),
        (homes_ref, homes_far),
        (unfold_ref, unfold_far),
        (energy_buf, energy_far),
    )
    leaves = [pltpu.make_async_copy(x, y, out_sems.at[i]) for i, (x, y) in enumerate(made)]
    for copy in starts:
        copy.wait()
    tall = flat_ref.shape[0]
    here = iota((tall, levels), 0) == iota((tall, levels), 1)
    diagonal = jnp.where(here, saturation_ref[...], 0.0)
    flat_ref[...] = select(jnp.ones((levels, LANES), BF16), diagonal, NN, swap=True)
    limits_ref[...] = jnp.zeros_like(limits_ref)
    for s in segments:
        lane = iota((s.steps, LANES), 1)
        value = flat_ref[0 : s.steps, :]
        for g in range(1, s.groups):
            other = flat_ref[g * s.steps : (g + 1) * s.steps, :]
            value = jnp.where(lane >= g * s.width, other, value)
        limits_ref[s.rows[0] : s.rows[1], :] = value
    sums_ref[...] = jnp.zeros_like(sums_ref)
    aside(
        columns_ref,
        mixing_ref,
        neighbours_ref,
        targets_ref,
        map_ref,
        base_ref,
        weights_ref,
        homes_ref,
        fold_ref,
        unfold_ref,
        **host,
    )
    for copy in leaves[:4]:
        copy.start()
    for f, scale, target in ((0, SHRINK, energy_buf), (1, 1.0, moved_ref)):
        loads[f].wait()
        widen(state_buf.at[f], natural_ref, segments, scale)
        fill_wide(segments, natural_ref)
        for s in segments:

            def work(row, below, here, above):
                out = linear(below, here, above)
                for j in range(4):
                    target[row, pl.ds(8 * j, 8), :] = out[j]
                sums_ref[slab(row), :] = (here[0] + here[1]) + (here[2] + here[3])

            sweep(s, lambda row: strided(natural_ref, row), work)
        if f == 0:
            leaves[4].start()
        means_ref[f] = folded_sums(sums_ref, columns) * (1.0 / scale)
    for copy in leaves:
        copy.wait()


def neighbour_part(arrived, means, fold, share, parity, levels, stride, neighbours):
    folded = product(fold, means, NT)
    taken = arrived[stride - 1 : stride] > 0.0
    ids = [
        jnp.where(taken, arrived[levels + k : levels + k + 1], -1.0) for k in range(neighbours)
    ]
    total = None
    chunk = min(256, means.shape[0])
    for first in range(0, means.shape[0], chunk):
        row = iota((chunk, arrived.shape[1]), 0) + first
        element = (row + share * divided(row, share) + share * parity).astype(F32)
        wanted = jnp.where(element == ids[0], 1.0, 0.0)
        for k in range(1, neighbours):
            wanted = wanted + jnp.where(element == ids[k], 1.0, 0.0)
        part = folded[:, first : first + chunk]
        term = select(wanted.astype(BF16), part, NN, swap=True)
        total = term if total is None else total + term
    return total


def halves(ref, share):
    return jnp.concatenate([ref[j, :share, :] for j in range(ref.shape[0])], axis=0)


def arrive_kernel(
    received_ref, fold_ref, arrived_ref, places_ref, *, segments, capacity, padded, **sizes
):
    hosts = received_ref.shape[0]
    share = received_ref.shape[1] - capacity
    places = slot_map(segments, hosts * padded, capacity, padded)
    places_ref[...] = places
    parts = []
    for j in range(hosts):
        parts.append(received_ref[j, share:, :])
        if padded != capacity:
            parts.append(jnp.zeros((padded - capacity, LANES), F32))
    arrived = select(places, jnp.concatenate(parts, axis=0), TN, swap=True)
    parity = lax.axis_index("sec") % 2
    arrived_ref[...] = arrived + neighbour_part(
        arrived, halves(received_ref, share), fold_ref[...], share, parity, **sizes
    )


def water_kernel(
    arrived_ref,
    places_ref,
    other_ref,
    moved_ref,
    means_ref,
    limits_ref,
    fold_ref,
    unfold_far,
    water_far,
    spill_far,
    flats_far,
    back_far,
    unfold_ref,
    even_ref,
    odd_ref,
    spill_buf,
    flats_ref,
    goal_ref,
    mean_ref,
    shift_ref,
    limit_ref,
    sums_ref,
    change_ref,
    back_ref,
    in_sem,
    spill_sems,
    water_sem,
    flat_sem,
    back_sems,
    *,
    segments,
    share,
    padded,
    stride,
    levels,
    neighbours,
):
    rows = means_ref.shape[1]
    columns = even_ref.shape[1]
    load = pltpu.make_async_copy(unfold_far, unfold_ref, in_sem)
    load.start()
    hosts = other_ref.shape[0]
    parity = 1 - lax.axis_index("sec") % 2
    arrived = arrived_ref[...]
    arrived = arrived + neighbour_part(
        arrived,
        halves(other_ref, share),
        fold_ref[...],
        share,
        parity,
        levels,
        stride,
        neighbours,
    )
    goal_ref[...] = jnp.zeros_like(goal_ref)
    flats_ref[...] = jnp.zeros_like(flats_ref)
    sums_ref[...] = jnp.zeros_like(sums_ref)
    counts = flats_ref.at[MAX_SUB + 2]
    for t, s in enumerate(segments):
        lanes = slice(t * LANES, (t + 1) * LANES)
        count = None
        for g in range(s.groups):
            number = s.group_steps(g)
            at = slice(s.rows[0], s.rows[0] + number)
            for f in range(2):
                first = f * stride + g * s.steps
                part = turn(arrived[first : first + number, lanes], g * s.width)
                goal_ref[f, at, :] = goal_ref[f, at, :] + part if g else part
            part = turn(arrived[stride - 1 : stride, lanes], g * s.width)
            count = part if count is None else count + part
        counts[s.rows[0] : s.rows[1], :] = jnp.broadcast_to(count, (s.steps, LANES))
    for f in range(2):
        mean_ref[f] = means_ref[f]
    copies = []
    source, target = None, even_ref
    for n in range(MAX_SUB):
        scale = 0.5 * GROW ** (n + 1)
        last = n + 1 == MAX_SUB
        expected = []
        for f in range(2):
            fill_flat(segments, mean_ref.at[f])
            mean = mean_ref[f]
            mixed = mean + VERTIC * (
                pltpu.roll(mean, 1, 0) + pltpu.roll(mean, rows - 1, 0) - 2.0 * mean
            )
            offset = goal_ref[f] - RELAX * mixed
            expected.append(mixed + offset)
            if f == 1:
                shift_ref[...] = scale * offset
            else:
                flats_ref[n] = (scale * SHRINK) * offset
        limit_ref[...] = scale * limits_ref[...]
        if last:
            flats_ref[MAX_SUB] = shift_ref[...]
            flats_ref[MAX_SUB + 1] = limit_ref[...]
            copies.append(pltpu.make_async_copy(flats_ref, flats_far, flat_sem))
            copies[-1].start()
        for s in segments:
            active = spread_row(counts, s.rows[0]) > float(n)

            def finish(row, lin, old):
                shift = spread_row(shift_ref, row)
                limit = spread_row(limit_ref, row)
                total = None
                for j in range(4):
                    v = lin[j] + shift
                    low = jnp.minimum(v, limit)
                    total = low if total is None else total + low
                    if last:
                        continue
                    u = v + low
                    if old is not None:
                        u = jnp.where(active, u, old[j])
                    spill_buf[n, row, pl.ds(8 * j, 8), :] = v - low
                    target[row, pl.ds(8 * j, 8), :] = u
                sums_ref[slab(row), :] = total

            if n == 0:

                def block(i, carry):
                    for k in range(STEP):
                        row = s.begin + 1 + i * STEP + k
                        finish(row, groups(moved_ref, (row,)), None)
                    return carry

                lax.fori_loop(0, s.blocks, block, 0)
            else:

                def work(row, below, here, above):
                    finish(row, linear(below, here, above), here)

                sweep(s, lambda row: groups(source, (row,)), work)
        if not last:
            copies.append(
                pltpu.make_async_copy(spill_buf.at[n], spill_far.at[n], spill_sems.at[n])
            )
            copies[-1].start()
            fill_wide(segments, target)
            source, target = target, (odd_ref if target is even_ref else even_ref)
        if n + 2 == MAX_SUB:
            copies.append(pltpu.make_async_copy(source, water_far, water_sem))
            copies[-1].start()
        spilled = 0.5 * (expected[1] - folded_sums(sums_ref, columns) * (1.0 / scale))
        step = [expected[0] + LATENT * spilled, expected[1] - spilled]
        keep = counts[...] > float(n)
        for f in range(2):
            mean_ref[f] = jnp.where(keep, step[f], mean_ref[f])
    change_ref[...] = jnp.zeros_like(change_ref)
    for f in range(2):
        change = mean_ref[f] - means_ref[f]
        for t, s in enumerate(segments):
            for g in range(s.groups):
                first, number = f * stride + g * s.steps, s.group_steps(g)
                part = turn(change[s.rows[0] : s.rows[0] + number], -g * s.width)
                change_ref[first : first + number, t * LANES : (t + 1) * LANES] = part
    spread = select(places_ref[...], change_ref[...], NT)
    load.wait()
    back = product(spread, unfold_ref[...], NN)
    quads = back_ref.shape[2]
    for h in range(2):
        for j in range(hosts):
            for q in range(quads):
                first = j * padded + (h * quads + q) * QUAD
                back_ref[h, j, q] = back[first : first + QUAD]
    for i in range(back_far.shape[0]):
        copies.append(pltpu.make_async_copy(back_ref.at[i % 2], back_far.at[i], back_sems.at[i]))
        copies[-1].start()
    for copy in copies:
        copy.wait()


def energy_kernel(
    state_ref,
    energy_far,
    water_far,
    spill_far,
    flats_far,
    base_far,
    weights_far,
    mixing_far,
    homes_far,
    received_ref,
    other_ref,
    out_ref,
    advanced_ref,
    picks_ref,
    state_buf,
    energy_buf,
    water_buf,
    spill_buf,
    flats_ref,
    base_ref,
    weights_ref,
    mixing_ref,
    homes_ref,
    out_buf,
    even_ref,
    odd_ref,
    natural_ref,
    state_sems,
    in_sems,
    spill_sems,
    out_sems,
    *,
    segments,
    share,
):
    fields, levels, columns, _ = state_ref.shape
    final = MAX_SUB - 1
    pairs = (
        (flats_far, flats_ref),
        (base_far, base_ref),
        (weights_far, weights_ref),
        (mixing_far, mixing_ref),
        (water_far, water_buf),
        (energy_far, energy_buf),
        (homes_far, homes_ref),
    )
    loads = [pltpu.make_async_copy(x, y, in_sems.at[i]) for i, (x, y) in enumerate(pairs)]
    flats, bases, shares, mixings, waters, first, homes = loads
    states = [
        pltpu.make_async_copy(state_ref.at[f], state_buf.at[f], state_sems.at[f])
        for f in range(fields)
    ]
    spills = [
        pltpu.make_async_copy(spill_far.at[n], spill_buf.at[n], spill_sems.at[n])
        for n in range(final)
    ]
    for copy in loads[:5] + [states[1], first] + spills + [states[0], homes]:
        copy.start()
    cut = -(-levels // 2)
    spans = ((0, cut), (cut, levels - cut))

    def leave(f, part):
        at = pl.ds(*spans[part])
        return pltpu.make_async_copy(
            out_buf.at[f, at], out_ref.at[f, at], out_sems.at[2 * f + part]
        )

    counts = flats_ref.at[MAX_SUB + 2]

    def finish_field(f, found):
        for s in segments[::-1]:
            count = spread_row(counts, s.rows[0])
            back = jnp.zeros((8, LANES), F32)
            for n in range(1, MAX_SUB + 1):
                scale = GROW**-n * (LATENT if f == 0 else 1.0)
                back = jnp.where(count == float(n), scale, back)
            at = slice(s.lane0, s.lane0 + s.width)
            held = jnp.broadcast_to(count[0:1, : s.width], (columns, s.width)) > 0.0

            def permute(k):
                row = s.begin + 1 + k
                value = groups(found, (row,))
                for j in range(4):
                    natural_ref[row, pl.ds(j, 8, stride=4), :] = value[j] * back

            def narrow(g, k):
                level = g * s.steps + k
                lanes = slice(g * s.width, (g + 1) * s.width)
                old = state_buf[f, level, :, at].astype(F32)
                value = jnp.where(held, natural_ref[s.begin + 1 + k, :, lanes], old)
                out_buf[f, level, :, at] = value.astype(BF16)

            each(s.steps, STEP, permute)
            if s is segments[0] and s.groups == 1:
                for part, (begin, number) in enumerate(spans):
                    each(number, STEP, lambda k: narrow(0, begin + k))
                    leave(f, part).start()
            else:
                for g in range(s.groups):
                    each(s.group_steps(g), STEP, lambda k: narrow(g, k))
        if segments[0].groups > 1:
            for part in range(2):
                leave(f, part).start()

    bases.wait()
    shares.wait()
    mixings.wait()
    hosts = received_ref.shape[0]
    position = lax.axis_index("col")
    around = [jnp.where(position == 0, hosts - 1, position - 1), position]
    around.append(jnp.where(position == hosts - 1, 0, position + 1))
    means = joined_means(received_ref, other_ref, share, around)
    advanced_ref[...] = base_ref[...] + mixing_ref[...] * select(weights_ref[...], means, NN)
    flats.wait()
    waters.wait()
    for s in segments:
        active = spread_row(counts, s.rows[0]) > float(final)

        def last(row, below, here, above):
            water = linear(below, here, above)
            push = spread_row(flats_ref.at[MAX_SUB], row)
            limit = spread_row(flats_ref.at[MAX_SUB + 1], row)
            for j in range(4):
                v = water[j] + push
                low = jnp.minimum(v, limit)
                spill_buf[final, row, pl.ds(8 * j, 8), :] = v - low
                even_ref[row, pl.ds(8 * j, 8), :] = jnp.where(active, v + low, here[j])

        sweep(s, lambda row: groups(water_buf, (row,)), last)
    states[1].wait()
    finish_field(1, even_ref)
    first.wait()
    source, target = None, odd_ref
    for n in range(MAX_SUB):
        if n < final:
            spills[n].wait()
        for s in segments:
            active = spread_row(counts, s.rows[0]) > float(n)

            def start(i, carry):
                for k in range(STEP):
                    row = s.begin + 1 + i * STEP + k
                    shift = spread_row(flats_ref.at[n], row)
                    lin, spill = groups(energy_buf, (row,)), groups(spill_buf, (n, row))
                    for j in range(4):
                        target[row, pl.ds(8 * j, 8), :] = 2.0 * (lin[j] + shift) + spill[j]
                return carry

            def work(row, below, here, above):
                shift = spread_row(flats_ref.at[n], row)
                lin = linear(below, here, above)
                spill = groups(spill_buf, (n, row))
                for j in range(4):
                    u = 2.0 * (lin[j] + shift) + spill[j]
                    target[row, pl.ds(8 * j, 8), :] = jnp.where(active, u, here[j])

            if n == 0:
                lax.fori_loop(0, s.blocks, start, 0)
            else:
                sweep(s, lambda row: groups(source, (row,)), work)
        if n < final:
            fill_wide(segments, target)
        source, target = target, (odd_ref if target is even_ref else even_ref)
    states[0].wait()
    finish_field(0, source)
    homes.wait()
    place = homes_ref[:, :1].astype(I32)
    picks_ref[...] = jnp.where(iota(picks_ref.shape, 1) == place, 1.0, 0.0).astype(BF16)
    for f in range(fields):
        for part in range(2):
            leave(f, part).wait()


def nearly_kernel(picks_ref, mine_ref, out_ref, table_ref, *, idle):
    sources, quads, _, _ = mine_ref.shape
    held = table_ref.shape[0] // (sources - idle)
    if quads * QUAD != held:
        table_ref[...] = jnp.zeros_like(table_ref)
    for j in range(sources - idle):
        for q in range(quads):
            first = j * held + q * QUAD
            table_ref[first : first + QUAD, :] = mine_ref[idle + j, q]
    out_ref[...] = select(picks_ref[...], table_ref[...], NN)


def final_kernel(advanced_ref, mine_ref, other_ref, out_ref, *, levels):
    summed = advanced_ref[...] + (mine_ref[...] + other_ref[...])
    water = divided(iota(summed.shape, 1), levels) == 1
    out_ref[...] = jnp.where(water, jnp.maximum(summed, 0.0), summed)


SPACES = dict(
    auto=pl.BlockSpec(memory_space=pltpu.VMEM),
    near=pl.BlockSpec(memory_space=pltpu.VMEM),
    far=pl.BlockSpec(memory_space=pl.ANY),
    scalar=pl.BlockSpec(memory_space=pltpu.SMEM),
)


def call(kernel, name, inputs, outputs, scratch=(), limit=8):
    kept = dict(near=pltpu.VMEM, auto=pltpu.HBM, far=pltpu.HBM, scalar=pltpu.HBM)
    arrays = [pltpu.with_memory_space_constraint(x, kept[space]) for space, x in inputs]
    shapes = [kept[space](dims, dtype) for space, dims, dtype in outputs]
    return pl.pallas_call(
        kernel,
        out_shape=shapes,
        in_specs=[SPACES[space] for space, _ in inputs],
        out_specs=[SPACES[space] for space, _, _ in outputs],
        scratch_shapes=list(scratch),
        compiler_params=pltpu.CompilerParams(vmem_limit_bytes=limit << 20),
        name=name,
    )(*arrays)


def body(
    column_state, mixing_rate, neighbours, assignment, substeps, cloud_state, level_map, saturation
):
    col_count = lax.axis_size("col")
    sec_count = lax.axis_size("sec")
    count, width = column_state.shape
    cloud_levels, levels = level_map.shape
    _, fields, _, columns, slots = cloud_state.shape
    elements = count // 4
    capacity = slots // col_count
    half = -(-capacity // (2 * QUAD)) * QUAD
    held = -(-half // 8) * 8
    padded = -(-max(capacity, 2 * half) // 8) * 8
    block = col_count * padded
    clouds = (sec_count - 1) * col_count
    segments, used, rows = segments_of(slots, cloud_levels)
    mapped = LANES * len(segments)
    mixing = mixing_rate.reshape(1, width)
    state = cloud_state[0]
    dma = pltpu.SemaphoreType.DMA

    def wide(*lead):
        return pltpu.VMEM((*lead, rows, columns, LANES), F32)

    hosts = dict(padded=padded, clouds=clouds)
    places_in = [
        ("auto", column_state),
        ("auto", mixing),
        ("auto", neighbours.T),
        ("auto", assignment.reshape(1, count)),
    ]
    outgoing, _ = call(
        functools.partial(host_kernel, **hosts),
        "host",
        places_in + [("auto", substeps.reshape(1, count)), ("auto", level_map)],
        [("auto", (col_count, elements // 2 + capacity, width), F32), ("near", (width, width), F32)],
    )
    received = lax.all_to_all(outgoing, "col", split_axis=0, concat_axis=0, tiled=True)
    moved, cloud_means, limits, energy, base, weights, homes, fold, unfold = call(
        functools.partial(
            prepare_kernel,
            segments=segments,
            col_count=col_count,
            half=half,
            held=held,
            **hosts,
        ),
        "prepare",
        [("far", state)]
        + [("far", x) for _, x in places_in]
        + [("far", level_map), ("far", saturation.reshape(1, cloud_levels))],
        [
            ("near", (used, columns, LANES), F32),
            ("near", (fields, rows, LANES), F32),
            ("near", (rows, LANES), F32),
            ("far", (used, columns, LANES), F32),
            ("far", (count, width), F32),
            ("far", (count, 3 * elements), BF16),
            ("far", (count, LANES), F32),
            ("near", (width, width), F32),
            ("far", (width, width), F32),
        ],
        scratch=[
            pltpu.VMEM(state.shape, BF16),
            wide(),
            pltpu.VMEM((rows * 8, LANES), F32),
            pltpu.VMEM((max(s.groups * s.steps for s in segments), LANES), F32),
            pltpu.VMEM((used, columns, LANES), F32),
            pltpu.VMEM((count, width), F32),
            pltpu.VMEM((1, width), F32),
            pltpu.VMEM((neighbours.shape[1], elements), I32),
            pltpu.VMEM((1, count), I32),
            pltpu.VMEM((cloud_levels, levels), F32),
            pltpu.VMEM((1, cloud_levels), F32),
            pltpu.VMEM((count, width), F32),
            pltpu.VMEM((count, 3 * elements), BF16),
            pltpu.VMEM((count, LANES), F32),
            pltpu.VMEM((width, width), F32),
            dma((fields,)),
            dma((6,)),
            dma((5,)),
        ],
        limit=16,
    )
    received, moved, base = lax.optimization_barrier((received, moved, base))
    pairs = [(i, i ^ 1) for i in range(sec_count)]
    other = lax.ppermute(received, "sec", pairs)
    sizes = dict(stride=levels, levels=cloud_levels, neighbours=neighbours.shape[1])
    arrived, places = call(
        functools.partial(
            arrive_kernel, segments=segments, capacity=capacity, padded=padded, **sizes
        ),
        "arrive",
        [("near", received), ("near", fold)],
        [("near", (width, mapped), F32), ("near", (block, mapped), BF16)],
    )
    water, spill, flats, back = call(
        functools.partial(
            water_kernel, segments=segments, share=elements // 2, padded=padded, **sizes
        ),
        "water",
        [
            ("near", arrived),
            ("near", places),
            ("near", other),
            ("near", moved),
            ("near", cloud_means),
            ("near", limits),
            ("near", fold),
            ("far", unfold),
        ],
        [
            ("far", (rows, columns, LANES), F32),
            ("far", (MAX_SUB - 1, rows, columns, LANES), F32),
            ("far", (MAX_SUB + 3, rows, LANES), F32),
            ("far", (sec_count, col_count, half // QUAD, QUAD, width), F32),
        ],
        scratch=[
            pltpu.VMEM((width, width), F32),
            wide(),
            wide(),
            wide(MAX_SUB - 1),
            pltpu.VMEM((MAX_SUB + 3, rows, LANES), F32),
            pltpu.VMEM((fields, rows, LANES), F32),
            pltpu.VMEM((fields, rows, LANES), F32),
            pltpu.VMEM((rows, LANES), F32),
            pltpu.VMEM((rows, LANES), F32),
            pltpu.VMEM((rows * 8, LANES), F32),
            pltpu.VMEM((width, mapped), F32),
            pltpu.VMEM((2, col_count, half // QUAD, QUAD, width), F32),
            dma(()),
            dma((MAX_SUB - 1,)),
            dma(()),
            dma(()),
            dma((sec_count,)),
        ],
        limit=24,
    )
    returned = lax.all_to_all(
        back.reshape(sec_count * col_count, half // QUAD, QUAD, width),
        ("sec", "col"),
        split_axis=0,
        concat_axis=0,
        tiled=True,
    )
    new_block, advanced, picks = call(
        functools.partial(energy_kernel, segments=segments, share=elements // 2),
        "energy",
        [
            ("far", state),
            ("far", energy),
            ("far", water),
            ("far", spill),
            ("far", flats),
            ("far", base),
            ("far", weights),
            ("far", mixing),
            ("far", homes),
            ("near", received),
            ("near", other),
        ],
        [
            ("far", state.shape, BF16),
            ("near", (count, width), F32),
            ("near", (count, clouds * held), BF16),
        ],
        scratch=[
            pltpu.VMEM(state.shape, BF16),
            pltpu.VMEM((used, columns, LANES), F32),
            wide(),
            wide(MAX_SUB),
            pltpu.VMEM((MAX_SUB + 3, rows, LANES), F32),
            pltpu.VMEM((count, width), F32),
            pltpu.VMEM((count, 3 * elements), BF16),
            pltpu.VMEM((1, width), F32),
            pltpu.VMEM((count, LANES), F32),
            pltpu.VMEM(state.shape, BF16),
            wide(),
            wide(),
            wide(),
            dma((fields,)),
            dma((7,)),
            dma((MAX_SUB - 1,)),
            dma((2 * fields,)),
        ],
        limit=32,
    )
    returned, advanced = lax.optimization_barrier((returned, advanced))
    (mine,) = call(
        functools.partial(nearly_kernel, idle=col_count),
        "nearly",
        [("near", picks), ("near", returned)],
        [("near", (count, width), F32)],
        scratch=[pltpu.VMEM((clouds * held, width), F32)],
    )
    partner = lax.ppermute(mine, "sec", pairs)
    (new_columns,) = call(
        functools.partial(final_kernel, levels=levels),
        "final",
        [("near", advanced), ("near", mine), ("near", partner)],
        [("auto", (count, width), F32)],
    )
    return new_columns, new_block[None]


def solution(mesh):
    in_specs = (
        P("col", None),
        P(),
        P("col", None),
        P("col", None),
        P("col"),
        P("sec", None, None, None, "col"),
        P(),
        P(),
    )
    out_specs = (P("col", None), P("sec", None, None, None, "col"))
    return jax.shard_map(body, mesh=mesh, in_specs=in_specs, out_specs=out_specs, check_vma=False)
```

```python
import functools

import jax
import jax.numpy as jnp
from jax import lax
from jax.experimental import pallas as pl
from jax.experimental.pallas import tpu as pltpu
from jax.sharding import PartitionSpec as P

MAX_SUB = 4
RELAX = 0.25
HORIZ = 0.12
VERTIC = 0.1
LATENT = 2.5
GROW = 20.0
VMIX = 0.2
HIGH = lax.Precision.HIGHEST
LANES = 128
F32 = jnp.float32
BF16 = jnp.bfloat16
STEP = 20
QUAD = 4
SHRINK = 1.0 / LATENT
I32 = jnp.int32


def iota(shape, dim):
    return lax.broadcasted_iota(I32, shape, dim)


def mm(a, b, contract, precision=HIGH):
    return lax.dot_general(
        a, b, (contract, ((), ())), precision=precision, preferred_element_type=F32
    )


NN = ((1,), (0,))
NT = ((1,), (1,))
TN = ((0,), (0,))


def divided(value, by):
    return jnp.floor((value.astype(F32) + 0.5) * (1.0 / by)).astype(I32)


def split(values, count=3):
    parts, rest = [], values
    for _ in range(count - 1):
        parts.append(rest.astype(BF16))
        rest = rest - parts[-1].astype(F32)
    return [rest.astype(BF16)] + parts[::-1]


def select(picks, values, contract, swap=False):
    total = None
    for part in split(values):
        a, b = (part, picks) if swap else (picks, part)
        term = lax.dot_general(a, b, (contract, ((), ())), preferred_element_type=F32)
        total = term if total is None else total + term
    return total


def product(a, b, contract):
    (am, ah), (bm, bh) = split(a, 2), split(b, 2)
    total = None
    for x, y in ((am, bh), (ah, bm), (ah, bh)):
        term = lax.dot_general(x, y, (contract, ((), ())), preferred_element_type=F32)
        total = term if total is None else total + term
    return total


def vertical_mix(values, levels):
    upper = jnp.concatenate([values[1:levels], values[levels - 1 : levels]], axis=0)
    lower = jnp.concatenate([values[0:1], values[0 : levels - 1]], axis=0)
    inner = values[0:levels]
    return inner + VERTIC * (upper + lower - 2.0 * inner)


def element_of_row(rows):
    elements = rows // 4
    hit = divided(iota((rows, elements), 0), 4) == iota((rows, elements), 1)
    return jnp.where(hit, 1.0, 0.0).astype(BF16)


def element_means(columns_ref):
    elements = columns_ref.shape[0] // 4
    total = columns_ref[pl.ds(0, elements, stride=4), :]
    for k in range(1, 4):
        total = total + columns_ref[pl.ds(k, elements, stride=4), :]
    return 0.25 * total


def own_part(values, means, mixing, levels):
    rows, width = values.shape
    lane = iota((rows, width), 1)
    level = lane - levels * divided(lane, levels)
    upper = jnp.where(level == levels - 1, values, pltpu.roll(values, width - 1, 1))
    lower = jnp.where(level == 0, values, pltpu.roll(values, 1, 1))
    mean = select(element_of_row(rows), means, NN)
    return values - (4.0 * mixing) * mean + VMIX * (upper + lower - 2.0 * values)


def joined_means(mine_ref, other_ref, share, order):
    first = lax.axis_index("sec") % 2 == 0
    parts = []
    for j in order:
        mine, other = mine_ref[j, :share, :], other_ref[j, :share, :]
        parts += [jnp.where(first, mine, other), jnp.where(first, other, mine)]
    return jnp.concatenate(parts, axis=0)


def slots_of(targets, col_count, padded, clouds):
    rows = targets.shape[1]
    onehot = jnp.where(iota((clouds, rows), 0) == targets, 1.0, 0.0)
    before = jnp.where(iota((rows, rows), 0) < iota((rows, rows), 1), 1.0, 0.0)
    running = mm(onehot.astype(BF16), before.astype(BF16), NN, None)
    ranks = jnp.sum(running * onehot, axis=0, keepdims=True).astype(I32)
    owner = divided(targets, col_count)
    return owner, (targets - owner * col_count) * padded + ranks


def blocked(ref, value, levels):
    ref[...] = jnp.zeros_like(ref)
    for f in range(ref.shape[0] // levels):
        ref[f * levels : f * levels + value.shape[0], f * levels : (f + 1) * levels] = value


def host_kernel(
    columns_ref,
    mixing_ref,
    neighbours_ref,
    targets_ref,
    substeps_ref,
    map_ref,
    out_ref,
    fold_ref,
    *,
    padded,
    clouds,
):
    rows, width = columns_ref.shape
    cloud_levels, levels = map_ref.shape
    col_count = out_ref.shape[0]
    block = col_count * padded
    means = element_means(columns_ref)
    share = means.shape[0] // 2
    section = lax.axis_index("sec")
    part = jnp.where(section % 2 == 0, means[:share], means[share:])
    for c in range(col_count):
        out_ref[c, :share, :] = part
    blocked(fold_ref, RELAX * vertical_mix(map_ref[...], cloud_levels), levels)
    owner, slot = slots_of(targets_ref[...], col_count, padded, clouds)
    mine = jnp.where(owner + 1 == section, slot, -1)
    pack = jnp.where(iota((block, rows), 0) == mine, 1.0, 0.0).astype(BF16)
    base = own_part(columns_ref[...], means, mixing_ref[...], levels)
    count = neighbours_ref.shape[0]
    ids = select(element_of_row(rows), neighbours_ref[...].astype(F32), NT, swap=True)
    extras = jnp.concatenate(
        [
            jnp.zeros((cloud_levels, rows), F32),
            ids,
            jnp.zeros((levels - 1 - cloud_levels - count, rows), F32),
            substeps_ref[...].astype(F32),
            jnp.zeros((width - levels, rows), F32),
        ],
        axis=0,
    )
    sent = product(select(pack, base, NN), fold_ref[...], NT) + select(pack, extras, NT)
    capacity = out_ref.shape[1] - share
    for c in range(col_count):
        out_ref[c, share:, :] = sent[c * padded : c * padded + capacity]


def aside(
    columns_ref,
    mixing_ref,
    neighbours_ref,
    targets_ref,
    map_ref,
    base_ref,
    weights_ref,
    homes_ref,
    fold_ref,
    unfold_ref,
    col_count,
    padded,
    clouds,
    half,
    held,
):
    rows, width = columns_ref.shape
    cloud_levels, levels = map_ref.shape
    elements = rows // 4
    position = lax.axis_index("col")
    base_ref[...] = own_part(
        columns_ref[...], element_means(columns_ref), mixing_ref[...], levels
    )
    near = neighbours_ref[...] - (position - 1) * elements
    near = jnp.where(near < 0, near + elements * col_count, near)
    near = jnp.where(near >= elements * col_count, near - elements * col_count, near)
    window = iota((3 * elements, elements), 0)
    picks = jnp.zeros((3 * elements, elements), F32)
    for k in range(near.shape[0]):
        picks = picks + jnp.where(window == near[k : k + 1, :], 1.0, 0.0)
    weights_ref[...] = mm(element_of_row(rows), picks.astype(BF16), NT, None).astype(BF16)
    owner, slot = slots_of(targets_ref[...], col_count, padded, clouds)
    place = divided(slot, padded)
    rank = slot - place * padded
    upper = jnp.where(rank >= half, 1, 0)
    parity = lax.axis_index("sec") % 2
    cloud = owner * col_count + place
    row = jnp.where(upper == parity, cloud * held + rank - half * upper, -1)
    everywhere = row.astype(F32)
    identity = jnp.where(iota((rows, rows), 0) == iota((rows, rows), 1), 1.0, 0.0)
    homes_ref[...] = select(
        identity.astype(BF16), jnp.broadcast_to(everywhere, (LANES, rows)), NT
    )
    blocked(fold_ref, RELAX * vertical_mix(map_ref[...], cloud_levels), levels)
    fold_ref[...] = fold_ref[...] * mixing_ref[...]
    blocked(unfold_ref, map_ref[...], levels)


class Segment:
    def __init__(self, lane0, width, levels, begin):
        self.lane0, self.width, self.begin, self.levels = lane0, width, begin, levels
        self.steps = -(-levels // (LANES // width))
        self.groups = -(-levels // self.steps)
        self.missing = self.groups * self.steps - levels
        self.blocks = -(-self.steps // STEP)
        self.rows = (begin + 1, begin + 1 + self.steps)

    def group_steps(self, g):
        return self.steps - (self.missing if g == self.groups - 1 else 0)


def segments_of(slots, levels):
    segments, begin = [], 0
    for lane0 in range(0, slots, LANES):
        segments.append(Segment(lane0, min(LANES, slots - lane0), levels, begin))
        begin += segments[-1].steps + 2
    rows = max([begin] + [s.begin + 2 + s.blocks * STEP for s in segments])
    return segments, rows, -(-rows // 8) * 8


def fill_spare(segments, load, store):
    def turned(value, shift):
        tall = jnp.broadcast_to(value, (8, LANES)) if value.shape[0] == 1 else value
        return pltpu.roll(tall, shift % LANES, 1)[: value.shape[0]]

    for s in segments:
        if s.missing:
            row = s.rows[1] - s.missing
            value = load(row - 1)
            lane = iota(value.shape, 1)
            store(row, jnp.where(lane >= (s.groups - 1) * s.width, value, load(row)))
        first, last = load(s.rows[0]), load(s.rows[1] - 1)
        before, after = first, last
        if s.groups > 1:
            lane = iota(first.shape, 1)
            before = jnp.where(lane < s.width, first, turned(last, s.width))
            after = jnp.where(lane < (s.groups - 1) * s.width, turned(first, -s.width), last)
        store(s.begin, before)
        store(s.rows[1], after)


def fill_wide(segments, ref):
    def store(row, value):
        ref[row] = value

    fill_spare(segments, lambda row: ref[row], store)


def fill_flat(segments, ref):
    def store(row, value):
        ref[row : row + 1, :] = value

    fill_spare(segments, lambda row: ref[row : row + 1, :], store)


def linear(below, here, above):
    east = [pltpu.roll(here[3], 1, 0), here[0], here[1], here[2]]
    west = [here[1], here[2], here[3], pltpu.roll(here[0], 7, 0)]
    keep = (1.0 - 2.0 * HORIZ - 2.0 * VERTIC) / VERTIC
    return [
        (below[j] + above[j]) + ((HORIZ / VERTIC) * (east[j] + west[j]) + keep * here[j])
        for j in range(4)
    ]


def groups(ref, index):
    return [ref[index + (pl.ds(8 * j, 8),)] for j in range(4)]


def strided(ref, row):
    return [ref[row, pl.ds(j, 8, stride=4), :] for j in range(4)]


def sweep(segment, load, work):
    def block(i, carry):
        row = segment.begin + i * STEP
        held = [load(row), load(row + 1)]
        for k in range(STEP):
            held.append(load(row + k + 2))
            work(row + k + 1, held[k], held[k + 1], held[k + 2])
        return carry

    lax.fori_loop(0, segment.blocks, block, 0)


def each(count, size, work):
    size = min(size, count)

    def run(first):
        for k in range(size):
            work(first + k)

    if count // size:
        lax.fori_loop(0, count // size, lambda i, c: (run(i * size), c)[1], 0)
    if count % size:
        run(count - size)


def widen(state_ref, natural_ref, segments, scale):
    levels, columns, _ = state_ref.shape
    for s in segments:
        at = slice(s.lane0, s.lane0 + s.width)

        def one(k):
            parts = []
            for g in range(s.groups):
                level = jnp.minimum(g * s.steps + k, levels - 1)
                parts.append(state_ref[level, :, at].astype(F32))
            spare = LANES - s.groups * s.width
            if spare:
                parts.append(jnp.zeros((columns, spare), F32))
            value = jnp.concatenate(parts, axis=1) if len(parts) > 1 else parts[0]
            natural_ref[s.begin + 1 + k] = scale * value if scale != 1.0 else value

        each(s.steps, STEP, one)


def folded_sums(sums_ref, columns):
    rows = sums_ref.shape[0] // 8
    total = sums_ref[pl.ds(0, rows, stride=8), :]
    for k in range(1, 8):
        total = total + sums_ref[pl.ds(k, rows, stride=8), :]
    return total * (1.0 / columns)


def slab(row):
    return pl.ds(pl.multiple_of(row * 8, 8), 8)


def spread_row(ref, row):
    return jnp.broadcast_to(ref[pl.ds(row, 1), :], (8, LANES))


def turn(value, shift):
    if not shift:
        return value
    height = value.shape[0]
    tall = -(-height // 8) * 8
    if tall != height:
        fill = jnp.zeros((tall - height, LANES), F32)
        value = jnp.concatenate([value, fill], axis=0)
    return pltpu.roll(value, shift % LANES, 1)[:height]


def each(count, size, work):
    size = min(size, count)

    def run(first):
        for k in range(size):
            work(first + k)

    if count // size:
        lax.fori_loop(0, count // size, lambda i, c: (run(i * size), c)[1], 0)
    if count % size:
        run(count - size)


def widen(state_ref, natural_ref, segments, scale):
    levels, columns, _ = state_ref.shape
    for s in segments:
        at = slice(s.lane0, s.lane0 + s.width)

        def one(k):
            parts = []
            for g in range(s.groups):
                level = jnp.minimum(g * s.steps + k, levels - 1)
                parts.append(state_ref[level, :, at].astype(F32))
            spare = LANES - s.groups * s.width
            if spare:
                parts.append(jnp.zeros((columns, spare), F32))
            value = jnp.concatenate(parts, axis=1) if len(parts) > 1 else parts[0]
            natural_ref[s.begin + 1 + k] = scale * value if scale != 1.0 else value

        each(s.steps, STEP, one)


def folded_sums(sums_ref, columns):
    rows = sums_ref.shape[0] // 8
    total = sums_ref[pl.ds(0, rows, stride=8), :]
    for k in range(1, 8):
        total = total + sums_ref[pl.ds(k, rows, stride=8), :]
    return total * (1.0 / columns)


def slab(row):
    return pl.ds(pl.multiple_of(row * 8, 8), 8)


def spread_row(ref, row):
    return jnp.broadcast_to(ref[pl.ds(row, 1), :], (8, LANES))


def lane_places(segments):
    return [(s, g) for s in segments for g in range(s.groups)]


def slot_map(segments, block, capacity, padded):
    tiles = []
    for s in segments:
        lane = iota((8, LANES), 1)
        slot = s.lane0 + lane
        row = slot + (padded - capacity) * divided(slot, capacity)
        row = jnp.where(lane < s.width, row, -1)[0:1]
        tiles.append(jnp.where(iota((block, LANES), 0) == row, 1.0, 0.0).astype(BF16))
    return jnp.concatenate(tiles, axis=1)


def prepare_kernel(
    state_ref,
    columns_far,
    mixing_far,
    neighbours_far,
    targets_far,
    map_far,
    saturation_far,
    moved_ref,
    means_ref,
    limits_ref,
    energy_far,
    base_far,
    weights_far,
    homes_far,
    fold_ref,
    unfold_far,
    state_buf,
    natural_ref,
    sums_ref,
    flat_ref,
    energy_buf,
    columns_ref,
    mixing_ref,
    neighbours_ref,
    targets_ref,
    map_ref,
    saturation_ref,
    base_ref,
    weights_ref,
    homes_ref,
    unfold_ref,
    sems,
    in_sems,
    out_sems,
    *,
    segments,
    **host,
):
    fields, levels, columns, _ = state_ref.shape
    given = (
        (columns_far, columns_ref),
        (mixing_far, mixing_ref),
        (neighbours_far, neighbours_ref),
        (targets_far, targets_ref),
        (map_far, map_ref),
        (saturation_far, saturation_ref),
    )
    starts = [pltpu.make_async_copy(x, y, in_sems.at[i]) for i, (x, y) in enumerate(given)]
    loads = [
        pltpu.make_async_copy(state_ref.at[f], state_buf.at[f], sems.at[f]) for f in range(fields)
    ]
    for copy in starts + loads:
        copy.start()
    made = (
        (base_ref, base_far),
        (weights_ref, weights_far),
        (homes_ref, homes_far),
        (unfold_ref, unfold_far),
        (energy_buf, energy_far),
    )
    leaves = [pltpu.make_async_copy(x, y, out_sems.at[i]) for i, (x, y) in enumerate(made)]
    for copy in starts:
        copy.wait()
    tall = flat_ref.shape[0]
    here = iota((tall, levels), 0) == iota((tall, levels), 1)
    diagonal = jnp.where(here, saturation_ref[...], 0.0)
    flat_ref[...] = select(jnp.ones((levels, LANES), BF16), diagonal, NN, swap=True)
    limits_ref[...] = jnp.zeros_like(limits_ref)
    for s in segments:
        lane = iota((s.steps, LANES), 1)
        value = flat_ref[0 : s.steps, :]
        for g in range(1, s.groups):
            other = flat_ref[g * s.steps : (g + 1) * s.steps, :]
            value = jnp.where(lane >= g * s.width, other, value)
        limits_ref[s.rows[0] : s.rows[1], :] = value
    sums_ref[...] = jnp.zeros_like(sums_ref)
    aside(
        columns_ref,
        mixing_ref,
        neighbours_ref,
        targets_ref,
        map_ref,
        base_ref,
        weights_ref,
        homes_ref,
        fold_ref,
        unfold_ref,
        **host,
    )
    for copy in leaves[:4]:
        copy.start()
    for f, scale, target in ((0, SHRINK, energy_buf), (1, 1.0, moved_ref)):
        loads[f].wait()
        widen(state_buf.at[f], natural_ref, segments, scale)
        fill_wide(segments, natural_ref)
        for s in segments:

            def work(row, below, here, above):
                out = linear(below, here, above)
                for j in range(4):
                    target[row, pl.ds(8 * j, 8), :] = out[j]
                sums_ref[slab(row), :] = (here[0] + here[1]) + (here[2] + here[3])

            sweep(s, lambda row: strided(natural_ref, row), work)
        if f == 0:
            leaves[4].start()
        means_ref[f] = folded_sums(sums_ref, columns) * (1.0 / scale)
    for copy in leaves:
        copy.wait()


def neighbour_part(arrived, means, fold, share, parity, levels, stride, neighbours):
    folded = product(fold, means, NT)
    taken = arrived[stride - 1 : stride] > 0.0
    ids = [
        jnp.where(taken, arrived[levels + k : levels + k + 1], -1.0) for k in range(neighbours)
    ]
    total = None
    chunk = min(256, means.shape[0])
    for first in range(0, means.shape[0], chunk):
        row = iota((chunk, arrived.shape[1]), 0) + first
        element = (row + share * divided(row, share) + share * parity).astype(F32)
        wanted = jnp.where(element == ids[0], 1.0, 0.0)
        for k in range(1, neighbours):
            wanted = wanted + jnp.where(element == ids[k], 1.0, 0.0)
        part = folded[:, first : first + chunk]
        term = select(wanted.astype(BF16), part, NN, swap=True)
        total = term if total is None else total + term
    return total


def halves(ref, share):
    return jnp.concatenate([ref[j, :share, :] for j in range(ref.shape[0])], axis=0)


def arrive_kernel(
    received_ref, fold_ref, arrived_ref, places_ref, *, segments, capacity, padded, **sizes
):
    hosts = received_ref.shape[0]
    share = received_ref.shape[1] - capacity
    places = slot_map(segments, hosts * padded, capacity, padded)
    places_ref[...] = places
    parts = []
    for j in range(hosts):
        parts.append(received_ref[j, share:, :])
        if padded != capacity:
            parts.append(jnp.zeros((padded - capacity, LANES), F32))
    arrived = select(places, jnp.concatenate(parts, axis=0), TN, swap=True)
    parity = lax.axis_index("sec") % 2
    arrived_ref[...] = arrived + neighbour_part(
        arrived, halves(received_ref, share), fold_ref[...], share, parity, **sizes
    )


def water_kernel(
    arrived_ref,
    places_ref,
    other_ref,
    moved_ref,
    means_ref,
    limits_ref,
    fold_ref,
    unfold_far,
    water_far,
    spill_far,
    flats_far,
    back_far,
    unfold_ref,
    even_ref,
    odd_ref,
    spill_buf,
    flats_ref,
    goal_ref,
    mean_ref,
    shift_ref,
    limit_ref,
    sums_ref,
    change_ref,
    back_ref,
    in_sem,
    spill_sems,
    water_sem,
    flat_sem,
    back_sems,
    *,
    segments,
    share,
    padded,
    stride,
    levels,
    neighbours,
):
    rows = means_ref.shape[1]
    columns = even_ref.shape[1]
    load = pltpu.make_async_copy(unfold_far, unfold_ref, in_sem)
    load.start()
    hosts = other_ref.shape[0]
    parity = 1 - lax.axis_index("sec") % 2
    arrived = arrived_ref[...]
    arrived = arrived + neighbour_part(
        arrived,
        halves(other_ref, share),
        fold_ref[...],
        share,
        parity,
        levels,
        stride,
        neighbours,
    )
    goal_ref[...] = jnp.zeros_like(goal_ref)
    flats_ref[...] = jnp.zeros_like(flats_ref)
    sums_ref[...] = jnp.zeros_like(sums_ref)
    counts = flats_ref.at[MAX_SUB + 2]
    for t, s in enumerate(segments):
        lanes = slice(t * LANES, (t + 1) * LANES)
        count = None
        for g in range(s.groups):
            number = s.group_steps(g)
            at = slice(s.rows[0], s.rows[0] + number)
            for f in range(2):
                first = f * stride + g * s.steps
                part = turn(arrived[first : first + number, lanes], g * s.width)
                goal_ref[f, at, :] = goal_ref[f, at, :] + part if g else part
            part = turn(arrived[stride - 1 : stride, lanes], g * s.width)
            count = part if count is None else count + part
        counts[s.rows[0] : s.rows[1], :] = jnp.broadcast_to(count, (s.steps, LANES))
    for f in range(2):
        mean_ref[f] = means_ref[f]
    copies = []
    source, target = None, even_ref
    for n in range(MAX_SUB):
        scale = 0.5 * GROW ** (n + 1)
        last = n + 1 == MAX_SUB
        expected = []
        for f in range(2):
            fill_flat(segments, mean_ref.at[f])
            mean = mean_ref[f]
            mixed = mean + VERTIC * (
                pltpu.roll(mean, 1, 0) + pltpu.roll(mean, rows - 1, 0) - 2.0 * mean
            )
            offset = goal_ref[f] - RELAX * mixed
            expected.append(mixed + offset)
            if f == 1:
                shift_ref[...] = scale * offset
            else:
                flats_ref[n] = (scale * SHRINK) * offset
        limit_ref[...] = scale * limits_ref[...]
        if last:
            flats_ref[MAX_SUB] = shift_ref[...]
            flats_ref[MAX_SUB + 1] = limit_ref[...]
            copies.append(pltpu.make_async_copy(flats_ref, flats_far, flat_sem))
            copies[-1].start()
        for s in segments:
            active = spread_row(counts, s.rows[0]) > float(n)

            def finish(row, lin, old):
                shift = spread_row(shift_ref, row)
                limit = spread_row(limit_ref, row)
                total = None
                for j in range(4):
                    v = lin[j] + shift
                    low = jnp.minimum(v, limit)
                    total = low if total is None else total + low
                    if last:
                        continue
                    u = v + low
                    if old is not None:
                        u = jnp.where(active, u, old[j])
                    spill_buf[n, row, pl.ds(8 * j, 8), :] = v - low
                    target[row, pl.ds(8 * j, 8), :] = u
                sums_ref[slab(row), :] = total

            if n == 0:

                def block(i, carry):
                    for k in range(STEP):
                        row = s.begin + 1 + i * STEP + k
                        finish(row, groups(moved_ref, (row,)), None)
                    return carry

                lax.fori_loop(0, s.blocks, block, 0)
            else:

                def work(row, below, here, above):
                    finish(row, linear(below, here, above), here)

                sweep(s, lambda row: groups(source, (row,)), work)
        if not last:
            copies.append(
                pltpu.make_async_copy(spill_buf.at[n], spill_far.at[n], spill_sems.at[n])
            )
            copies[-1].start()
            fill_wide(segments, target)
            source, target = target, (odd_ref if target is even_ref else even_ref)
        if n + 2 == MAX_SUB:
            copies.append(pltpu.make_async_copy(source, water_far, water_sem))
            copies[-1].start()
        spilled = 0.5 * (expected[1] - folded_sums(sums_ref, columns) * (1.0 / scale))
        step = [expected[0] + LATENT * spilled, expected[1] - spilled]
        keep = counts[...] > float(n)
        for f in range(2):
            mean_ref[f] = jnp.where(keep, step[f], mean_ref[f])
    change_ref[...] = jnp.zeros_like(change_ref)
    for f in range(2):
        change = mean_ref[f] - means_ref[f]
        for t, s in enumerate(segments):
            for g in range(s.groups):
                first, number = f * stride + g * s.steps, s.group_steps(g)
                part = turn(change[s.rows[0] : s.rows[0] + number], -g * s.width)
                change_ref[first : first + number, t * LANES : (t + 1) * LANES] = part
    spread = select(places_ref[...], change_ref[...], NT)
    load.wait()
    back = product(spread, unfold_ref[...], NN)
    quads = back_ref.shape[2]
    for h in range(2):
        for j in range(hosts):
            for q in range(quads):
                first = j * padded + (h * quads + q) * QUAD
                back_ref[h, j, q] = back[first : first + QUAD]
    for i in range(back_far.shape[0]):
        copies.append(pltpu.make_async_copy(back_ref.at[i % 2], back_far.at[i], back_sems.at[i]))
        copies[-1].start()
    for copy in copies:
        copy.wait()


def energy_kernel(
    state_ref,
    energy_far,
    water_far,
    spill_far,
    flats_far,
    base_far,
    weights_far,
    mixing_far,
    homes_far,
    received_ref,
    other_ref,
    out_ref,
    advanced_ref,
    picks_ref,
    state_buf,
    energy_buf,
    water_buf,
    spill_buf,
    flats_ref,
    base_ref,
    weights_ref,
    mixing_ref,
    homes_ref,
    out_buf,
    even_ref,
    odd_ref,
    natural_ref,
    state_sems,
    in_sems,
    spill_sems,
    out_sems,
    *,
    segments,
    share,
):
    fields, levels, columns, _ = state_ref.shape
    final = MAX_SUB - 1
    pairs = (
        (flats_far, flats_ref),
        (base_far, base_ref),
        (weights_far, weights_ref),
        (mixing_far, mixing_ref),
        (water_far, water_buf),
        (energy_far, energy_buf),
        (homes_far, homes_ref),
    )
    loads = [pltpu.make_async_copy(x, y, in_sems.at[i]) for i, (x, y) in enumerate(pairs)]
    flats, bases, shares, mixings, waters, first, homes = loads
    states = [
        pltpu.make_async_copy(state_ref.at[f], state_buf.at[f], state_sems.at[f])
        for f in range(fields)
    ]
    spills = [
        pltpu.make_async_copy(spill_far.at[n], spill_buf.at[n], spill_sems.at[n])
        for n in range(final)
    ]
    for copy in loads[:5] + [states[1], first] + spills + [states[0], homes]:
        copy.start()
    cut = -(-levels // 2)
    spans = ((0, cut), (cut, levels - cut))

    def leave(f, part):
        at = pl.ds(*spans[part])
        return pltpu.make_async_copy(
            out_buf.at[f, at], out_ref.at[f, at], out_sems.at[2 * f + part]
        )

    counts = flats_ref.at[MAX_SUB + 2]

    def finish_field(f, found):
        for s in segments[::-1]:
            count = spread_row(counts, s.rows[0])
            back = jnp.zeros((8, LANES), F32)
            for n in range(1, MAX_SUB + 1):
                scale = GROW**-n * (LATENT if f == 0 else 1.0)
                back = jnp.where(count == float(n), scale, back)
            at = slice(s.lane0, s.lane0 + s.width)
            held = jnp.broadcast_to(count[0:1, : s.width], (columns, s.width)) > 0.0

            def permute(k):
                row = s.begin + 1 + k
                value = groups(found, (row,))
                for j in range(4):
                    natural_ref[row, pl.ds(j, 8, stride=4), :] = value[j] * back

            def narrow(g, k):
                level = g * s.steps + k
                lanes = slice(g * s.width, (g + 1) * s.width)
                old = state_buf[f, level, :, at].astype(F32)
                value = jnp.where(held, natural_ref[s.begin + 1 + k, :, lanes], old)
                out_buf[f, level, :, at] = value.astype(BF16)

            each(s.steps, STEP, permute)
            if s is segments[0] and s.groups == 1:
                for part, (begin, number) in enumerate(spans):
                    each(number, STEP, lambda k: narrow(0, begin + k))
                    leave(f, part).start()
            else:
                for g in range(s.groups):
                    each(s.group_steps(g), STEP, lambda k: narrow(g, k))
        if segments[0].groups > 1:
            for part in range(2):
                leave(f, part).start()

    bases.wait()
    shares.wait()
    mixings.wait()
    hosts = received_ref.shape[0]
    position = lax.axis_index("col")
    around = [jnp.where(position == 0, hosts - 1, position - 1), position]
    around.append(jnp.where(position == hosts - 1, 0, position + 1))
    means = joined_means(received_ref, other_ref, share, around)
    advanced_ref[...] = base_ref[...] + mixing_ref[...] * select(weights_ref[...], means, NN)
    flats.wait()
    waters.wait()
    for s in segments:
        active = spread_row(counts, s.rows[0]) > float(final)

        def last(row, below, here, above):
            water = linear(below, here, above)
            push = spread_row(flats_ref.at[MAX_SUB], row)
            limit = spread_row(flats_ref.at[MAX_SUB + 1], row)
            for j in range(4):
                v = water[j] + push
                low = jnp.minimum(v, limit)
                spill_buf[final, row, pl.ds(8 * j, 8), :] = v - low
                even_ref[row, pl.ds(8 * j, 8), :] = jnp.where(active, v + low, here[j])

        sweep(s, lambda row: groups(water_buf, (row,)), last)
    states[1].wait()
    finish_field(1, even_ref)
    first.wait()
    source, target = None, odd_ref
    for n in range(MAX_SUB):
        if n < final:
            spills[n].wait()
        for s in segments:
            active = spread_row(counts, s.rows[0]) > float(n)

            def start(i, carry):
                for k in range(STEP):
                    row = s.begin + 1 + i * STEP + k
                    shift = spread_row(flats_ref.at[n], row)
                    lin, spill = groups(energy_buf, (row,)), groups(spill_buf, (n, row))
                    for j in range(4):
                        target[row, pl.ds(8 * j, 8), :] = 2.0 * (lin[j] + shift) + spill[j]
                return carry

            def work(row, below, here, above):
                shift = spread_row(flats_ref.at[n], row)
                lin = linear(below, here, above)
                spill = groups(spill_buf, (n, row))
                for j in range(4):
                    u = 2.0 * (lin[j] + shift) + spill[j]
                    target[row, pl.ds(8 * j, 8), :] = jnp.where(active, u, here[j])

            if n == 0:
                lax.fori_loop(0, s.blocks, start, 0)
            else:
                sweep(s, lambda row: groups(source, (row,)), work)
        if n < final:
            fill_wide(segments, target)
        source, target = target, (odd_ref if target is even_ref else even_ref)
    states[0].wait()
    finish_field(0, source)
    homes.wait()
    place = homes_ref[:, :1].astype(I32)
    picks_ref[...] = jnp.where(iota(picks_ref.shape, 1) == place, 1.0, 0.0).astype(BF16)
    for f in range(fields):
        for part in range(2):
            leave(f, part).wait()


def nearly_kernel(picks_ref, mine_ref, out_ref, table_ref, *, idle):
    sources, quads, _, _ = mine_ref.shape
    held = table_ref.shape[0] // (sources - idle)
    if quads * QUAD != held:
        table_ref[...] = jnp.zeros_like(table_ref)
    for j in range(sources - idle):
        for q in range(quads):
            first = j * held + q * QUAD
            table_ref[first : first + QUAD, :] = mine_ref[idle + j, q]
    out_ref[...] = select(picks_ref[...], table_ref[...], NN)


def final_kernel(advanced_ref, mine_ref, other_ref, out_ref, *, levels):
    summed = advanced_ref[...] + (mine_ref[...] + other_ref[...])
    water = divided(iota(summed.shape, 1), levels) == 1
    out_ref[...] = jnp.where(water, jnp.maximum(summed, 0.0), summed)


SPACES = dict(
    auto=pl.BlockSpec(memory_space=pltpu.VMEM),
    near=pl.BlockSpec(memory_space=pltpu.VMEM),
    far=pl.BlockSpec(memory_space=pl.ANY),
    scalar=pl.BlockSpec(memory_space=pltpu.SMEM),
)


def call(kernel, name, inputs, outputs, scratch=(), limit=8):
    kept = dict(near=pltpu.VMEM, auto=pltpu.HBM, far=pltpu.HBM, scalar=pltpu.HBM)
    arrays = [pltpu.with_memory_space_constraint(x, kept[space]) for space, x in inputs]
    shapes = [kept[space](dims, dtype) for space, dims, dtype in outputs]
    return pl.pallas_call(
        kernel,
        out_shape=shapes,
        in_specs=[SPACES[space] for space, _ in inputs],
        out_specs=[SPACES[space] for space, _, _ in outputs],
        scratch_shapes=list(scratch),
        compiler_params=pltpu.CompilerParams(vmem_limit_bytes=limit << 20),
        name=name,
    )(*arrays)


def body(
    column_state, mixing_rate, neighbours, assignment, substeps, cloud_state, level_map, saturation
):
    col_count = lax.axis_size("col")
    sec_count = lax.axis_size("sec")
    count, width = column_state.shape
    cloud_levels, levels = level_map.shape
    _, fields, _, columns, slots = cloud_state.shape
    elements = count // 4
    capacity = slots // col_count
    half = -(-capacity // (2 * QUAD)) * QUAD
    held = -(-half // 8) * 8
    padded = -(-max(capacity, 2 * half) // 8) * 8
    block = col_count * padded
    clouds = (sec_count - 1) * col_count
    segments, used, rows = segments_of(slots, cloud_levels)
    mapped = LANES * len(segments)
    mixing = mixing_rate.reshape(1, width)
    state = cloud_state[0]
    dma = pltpu.SemaphoreType.DMA

    def wide(*lead):
        return pltpu.VMEM((*lead, rows, columns, LANES), F32)

    hosts = dict(padded=padded, clouds=clouds)
    places_in = [
        ("auto", column_state),
        ("auto", mixing),
        ("auto", neighbours.T),
        ("auto", assignment.reshape(1, count)),
    ]
    outgoing, _ = call(
        functools.partial(host_kernel, **hosts),
        "host",
        places_in + [("auto", substeps.reshape(1, count)), ("auto", level_map)],
        [("auto", (col_count, elements // 2 + capacity, width), F32), ("near", (width, width), F32)],
    )
    received = lax.all_to_all(outgoing, "col", split_axis=0, concat_axis=0, tiled=True)
    moved, cloud_means, limits, energy, base, weights, homes, fold, unfold = call(
        functools.partial(
            prepare_kernel,
            segments=segments,
            col_count=col_count,
            half=half,
            held=held,
            **hosts,
        ),
        "prepare",
        [("far", state)]
        + [("far", x) for _, x in places_in]
        + [("far", level_map), ("far", saturation.reshape(1, cloud_levels))],
        [
            ("near", (used, columns, LANES), F32),
            ("near", (fields, rows, LANES), F32),
            ("near", (rows, LANES), F32),
            ("far", (used, columns, LANES), F32),
            ("far", (count, width), F32),
            ("far", (count, 3 * elements), BF16),
            ("far", (count, LANES), F32),
            ("near", (width, width), F32),
            ("far", (width, width), F32),
        ],
        scratch=[
            pltpu.VMEM(state.shape, BF16),
            wide(),
            pltpu.VMEM((rows * 8, LANES), F32),
            pltpu.VMEM((max(s.groups * s.steps for s in segments), LANES), F32),
            pltpu.VMEM((used, columns, LANES), F32),
            pltpu.VMEM((count, width), F32),
            pltpu.VMEM((1, width), F32),
            pltpu.VMEM((neighbours.shape[1], elements), I32),
            pltpu.VMEM((1, count), I32),
            pltpu.VMEM((cloud_levels, levels), F32),
            pltpu.VMEM((1, cloud_levels), F32),
            pltpu.VMEM((count, width), F32),
            pltpu.VMEM((count, 3 * elements), BF16),
            pltpu.VMEM((count, LANES), F32),
            pltpu.VMEM((width, width), F32),
            dma((fields,)),
            dma((6,)),
            dma((5,)),
        ],
        limit=16,
    )
    received, moved, base = lax.optimization_barrier((received, moved, base))
    pairs = [(i, i ^ 1) for i in range(sec_count)]
    other = lax.ppermute(received, "sec", pairs)
    sizes = dict(stride=levels, levels=cloud_levels, neighbours=neighbours.shape[1])
    arrived, places = call(
        functools.partial(
            arrive_kernel, segments=segments, capacity=capacity, padded=padded, **sizes
        ),
        "arrive",
        [("near", received), ("near", fold)],
        [("near", (width, mapped), F32), ("near", (block, mapped), BF16)],
    )
    water, spill, flats, back = call(
        functools.partial(
            water_kernel, segments=segments, share=elements // 2, padded=padded, **sizes
        ),
        "water",
        [
            ("near", arrived),
            ("near", places),
            ("near", other),
            ("near", moved),
            ("near", cloud_means),
            ("near", limits),
            ("near", fold),
            ("far", unfold),
        ],
        [
            ("far", (rows, columns, LANES), F32),
            ("far", (MAX_SUB - 1, rows, columns, LANES), F32),
            ("far", (MAX_SUB + 3, rows, LANES), F32),
            ("far", (sec_count, col_count, half // QUAD, QUAD, width), F32),
        ],
        scratch=[
            pltpu.VMEM((width, width), F32),
            wide(),
            wide(),
            wide(MAX_SUB - 1),
            pltpu.VMEM((MAX_SUB + 3, rows, LANES), F32),
            pltpu.VMEM((fields, rows, LANES), F32),
            pltpu.VMEM((fields, rows, LANES), F32),
            pltpu.VMEM((rows, LANES), F32),
            pltpu.VMEM((rows, LANES), F32),
            pltpu.VMEM((rows * 8, LANES), F32),
            pltpu.VMEM((width, mapped), F32),
            pltpu.VMEM((2, col_count, half // QUAD, QUAD, width), F32),
            dma(()),
            dma((MAX_SUB - 1,)),
            dma(()),
            dma(()),
            dma((sec_count,)),
        ],
        limit=24,
    )
    returned = lax.all_to_all(
        back.reshape(sec_count * col_count, half // QUAD, QUAD, width),
        ("sec", "col"),
        split_axis=0,
        concat_axis=0,
        tiled=True,
    )
    new_block, advanced, picks = call(
        functools.partial(energy_kernel, segments=segments, share=elements // 2),
        "energy",
        [
            ("far", state),
            ("far", energy),
            ("far", water),
            ("far", spill),
            ("far", flats),
            ("far", base),
            ("far", weights),
            ("far", mixing),
            ("far", homes),
            ("near", received),
            ("near", other),
        ],
        [
            ("far", state.shape, BF16),
            ("near", (count, width), F32),
            ("near", (count, clouds * held), BF16),
        ],
        scratch=[
            pltpu.VMEM(state.shape, BF16),
            pltpu.VMEM((used, columns, LANES), F32),
            wide(),
            wide(MAX_SUB),
            pltpu.VMEM((MAX_SUB + 3, rows, LANES), F32),
            pltpu.VMEM((count, width), F32),
            pltpu.VMEM((count, 3 * elements), BF16),
            pltpu.VMEM((1, width), F32),
            pltpu.VMEM((count, LANES), F32),
            pltpu.VMEM(state.shape, BF16),
            wide(),
            wide(),
            wide(),
            dma((fields,)),
            dma((7,)),
            dma((MAX_SUB - 1,)),
            dma((2 * fields,)),
        ],
        limit=32,
    )
    returned, advanced = lax.optimization_barrier((returned, advanced))
    (mine,) = call(
        functools.partial(nearly_kernel, idle=col_count),
        "nearly",
        [("near", picks), ("near", returned)],
        [("near", (count, width), F32)],
        scratch=[pltpu.VMEM((clouds * held, width), F32)],
    )
    partner = lax.ppermute(mine, "sec", pairs)
    (new_columns,) = call(
        functools.partial(final_kernel, levels=levels),
        "final",
        [("near", advanced), ("near", mine), ("near", partner)],
        [("auto", (count, width), F32)],
    )
    return new_columns, new_block[None]


def solution(mesh):
    in_specs = (
        P("col", None),
        P(),
        P("col", None),
        P("col", None),
        P("col"),
        P("sec", None, None, None, "col"),
        P(),
        P(),
    )
    out_specs = (P("col", None), P("sec", None, None, None, "col"))
    return jax.shard_map(body, mesh=mesh, in_specs=in_specs, out_specs=out_specs, check_vma=False)
```

```python
import functools

import jax
import jax.numpy as jnp
from jax import lax
from jax.experimental import pallas as pl
from jax.experimental.pallas import tpu as pltpu
from jax.sharding import PartitionSpec as P

MAX_SUB = 4
RELAX = 0.25
HORIZ = 0.12
VERTIC = 0.1
LATENT = 2.5
GROW = 20.0
VMIX = 0.2
HIGH = lax.Precision.HIGHEST
LANES = 128
F32 = jnp.float32
BF16 = jnp.bfloat16
STEP = 20
QUAD = 4
SHRINK = 1.0 / LATENT
I32 = jnp.int32


def iota(shape, dim):
    return lax.broadcasted_iota(I32, shape, dim)


def mm(a, b, contract, precision=HIGH):
    return lax.dot_general(
        a, b, (contract, ((), ())), precision=precision, preferred_element_type=F32
    )


NN = ((1,), (0,))
NT = ((1,), (1,))
TN = ((0,), (0,))


def divided(value, by):
    return jnp.floor((value.astype(F32) + 0.5) * (1.0 / by)).astype(I32)


def split(values, count=3):
    parts, rest = [], values
    for _ in range(count - 1):
        parts.append(rest.astype(BF16))
        rest = rest - parts[-1].astype(F32)
    return [rest.astype(BF16)] + parts[::-1]


def select(picks, values, contract, swap=False, count=3):
    total = None
    for part in split(values, count):
        a, b = (part, picks) if swap else (picks, part)
        term = lax.dot_general(a, b, (contract, ((), ())), preferred_element_type=F32)
        total = term if total is None else total + term
    return total


def product(a, b, contract):
    (am, ah), (bm, bh) = split(a, 2), split(b, 2)
    total = None
    for x, y in ((am, bh), (ah, bm), (ah, bh)):
        term = lax.dot_general(x, y, (contract, ((), ())), preferred_element_type=F32)
        total = term if total is None else total + term
    return total


def vertical_mix(values, levels):
    upper = jnp.concatenate([values[1:levels], values[levels - 1 : levels]], axis=0)
    lower = jnp.concatenate([values[0:1], values[0 : levels - 1]], axis=0)
    inner = values[0:levels]
    return inner + VERTIC * (upper + lower - 2.0 * inner)


def element_of_row(rows):
    elements = rows // 4
    hit = divided(iota((rows, elements), 0), 4) == iota((rows, elements), 1)
    return jnp.where(hit, 1.0, 0.0).astype(BF16)


def element_means(columns_ref):
    elements = columns_ref.shape[0] // 4
    total = columns_ref[pl.ds(0, elements, stride=4), :]
    for k in range(1, 4):
        total = total + columns_ref[pl.ds(k, elements, stride=4), :]
    return 0.25 * total


def own_part(values, means, mixing, levels):
    rows, width = values.shape
    lane = iota((rows, width), 1)
    level = lane - levels * divided(lane, levels)
    upper = jnp.where(level == levels - 1, values, pltpu.roll(values, width - 1, 1))
    lower = jnp.where(level == 0, values, pltpu.roll(values, 1, 1))
    mean = select(element_of_row(rows), means, NN)
    return values - (4.0 * mixing) * mean + VMIX * (upper + lower - 2.0 * values)


def joined_means(mine_ref, other_ref, share, order):
    first = lax.axis_index("sec") % 2 == 0
    parts = []
    for j in order:
        mine, other = mine_ref[j, :share, :], other_ref[j, :share, :]
        parts += [jnp.where(first, mine, other), jnp.where(first, other, mine)]
    return jnp.concatenate(parts, axis=0)


def slots_of(targets, col_count, padded, clouds):
    rows = targets.shape[1]
    onehot = jnp.where(iota((clouds, rows), 0) == targets, 1.0, 0.0)
    before = jnp.where(iota((rows, rows), 0) < iota((rows, rows), 1), 1.0, 0.0)
    running = mm(onehot.astype(BF16), before.astype(BF16), NN, None)
    ranks = jnp.sum(running * onehot, axis=0, keepdims=True).astype(I32)
    owner = divided(targets, col_count)
    return owner, (targets - owner * col_count) * padded + ranks


def blocked(ref, value, levels):
    ref[...] = jnp.zeros_like(ref)
    for f in range(ref.shape[0] // levels):
        ref[f * levels : f * levels + value.shape[0], f * levels : (f + 1) * levels] = value


def host_kernel(
    columns_ref,
    mixing_ref,
    neighbours_ref,
    targets_ref,
    substeps_ref,
    map_ref,
    out_ref,
    fold_ref,
    *,
    padded,
    clouds,
):
    rows, width = columns_ref.shape
    cloud_levels, levels = map_ref.shape
    col_count = out_ref.shape[0]
    block = col_count * padded
    means = element_means(columns_ref)
    share = means.shape[0] // 2
    section = lax.axis_index("sec")
    part = jnp.where(section % 2 == 0, means[:share], means[share:])
    for c in range(col_count):
        out_ref[c, :share, :] = part
    blocked(fold_ref, RELAX * vertical_mix(map_ref[...], cloud_levels), levels)
    owner, slot = slots_of(targets_ref[...], col_count, padded, clouds)
    mine = jnp.where(owner + 1 == section, slot, -1)
    pack = jnp.where(iota((block, rows), 0) == mine, 1.0, 0.0).astype(BF16)
    base = own_part(columns_ref[...], means, mixing_ref[...], levels)
    count = neighbours_ref.shape[0]
    ids = select(element_of_row(rows), neighbours_ref[...].astype(F32), NT, swap=True, count=2)
    extras = jnp.concatenate(
        [
            jnp.zeros((cloud_levels, rows), F32),
            ids,
            jnp.zeros((levels - 1 - cloud_levels - count, rows), F32),
            substeps_ref[...].astype(F32),
            jnp.zeros((width - levels, rows), F32),
        ],
        axis=0,
    )
    sent = product(select(pack, base, NN, count=2), fold_ref[...], NT) + select(pack, extras, NT, count=2)
    capacity = out_ref.shape[1] - share
    for c in range(col_count):
        out_ref[c, share:, :] = sent[c * padded : c * padded + capacity]


def aside(
    columns_ref,
    mixing_ref,
    neighbours_ref,
    targets_ref,
    map_ref,
    base_ref,
    weights_ref,
    homes_ref,
    fold_ref,
    unfold_ref,
    col_count,
    padded,
    clouds,
    half,
    held,
):
    rows, width = columns_ref.shape
    cloud_levels, levels = map_ref.shape
    elements = rows // 4
    position = lax.axis_index("col")
    base_ref[...] = own_part(
        columns_ref[...], element_means(columns_ref), mixing_ref[...], levels
    )
    near = neighbours_ref[...] - (position - 1) * elements
    near = jnp.where(near < 0, near + elements * col_count, near)
    near = jnp.where(near >= elements * col_count, near - elements * col_count, near)
    window = iota((3 * elements, elements), 0)
    picks = jnp.zeros((3 * elements, elements), F32)
    for k in range(near.shape[0]):
        picks = picks + jnp.where(window == near[k : k + 1, :], 1.0, 0.0)
    weights_ref[...] = mm(element_of_row(rows), picks.astype(BF16), NT, None).astype(BF16)
    owner, slot = slots_of(targets_ref[...], col_count, padded, clouds)
    place = divided(slot, padded)
    rank = slot - place * padded
    upper = jnp.where(rank >= half, 1, 0)
    parity = lax.axis_index("sec") % 2
    cloud = owner * col_count + place
    row = jnp.where(upper == parity, cloud * held + rank - half * upper, -1)
    everywhere = row.astype(F32)
    identity = jnp.where(iota((rows, rows), 0) == iota((rows, rows), 1), 1.0, 0.0)
    homes_ref[...] = select(
        identity.astype(BF16), jnp.broadcast_to(everywhere, (LANES, rows)), NT
    )
    blocked(fold_ref, RELAX * vertical_mix(map_ref[...], cloud_levels), levels)
    fold_ref[...] = fold_ref[...] * mixing_ref[...]
    blocked(unfold_ref, map_ref[...], levels)


class Segment:
    def __init__(self, lane0, width, levels, begin):
        self.lane0, self.width, self.begin, self.levels = lane0, width, begin, levels
        self.steps = -(-levels // (LANES // width))
        self.groups = -(-levels // self.steps)
        self.missing = self.groups * self.steps - levels
        self.blocks = -(-self.steps // STEP)
        self.rows = (begin + 1, begin + 1 + self.steps)

    def group_steps(self, g):
        return self.steps - (self.missing if g == self.groups - 1 else 0)


def segments_of(slots, levels):
    segments, begin = [], 0
    for lane0 in range(0, slots, LANES):
        segments.append(Segment(lane0, min(LANES, slots - lane0), levels, begin))
        begin += segments[-1].steps + 2
    rows = max([begin] + [s.begin + 2 + s.blocks * STEP for s in segments])
    return segments, rows, -(-rows // 8) * 8


def fill_spare(segments, load, store):
    def turned(value, shift):
        tall = jnp.broadcast_to(value, (8, LANES)) if value.shape[0] == 1 else value
        return pltpu.roll(tall, shift % LANES, 1)[: value.shape[0]]

    for s in segments:
        if s.missing:
            row = s.rows[1] - s.missing
            value = load(row - 1)
            lane = iota(value.shape, 1)
            store(row, jnp.where(lane >= (s.groups - 1) * s.width, value, load(row)))
        first, last = load(s.rows[0]), load(s.rows[1] - 1)
        before, after = first, last
        if s.groups > 1:
            lane = iota(first.shape, 1)
            before = jnp.where(lane < s.width, first, turned(last, s.width))
            after = jnp.where(lane < (s.groups - 1) * s.width, turned(first, -s.width), last)
        store(s.begin, before)
        store(s.rows[1], after)


def fill_wide(segments, ref):
    def store(row, value):
        ref[row] = value

    fill_spare(segments, lambda row: ref[row], store)


def fill_flat(segments, ref):
    def store(row, value):
        ref[row : row + 1, :] = value

    fill_spare(segments, lambda row: ref[row : row + 1, :], store)


def linear(below, here, above):
    east = [pltpu.roll(here[3], 1, 0), here[0], here[1], here[2]]
    west = [here[1], here[2], here[3], pltpu.roll(here[0], 7, 0)]
    keep = (1.0 - 2.0 * HORIZ - 2.0 * VERTIC) / VERTIC
    return [
        (below[j] + above[j]) + ((HORIZ / VERTIC) * (east[j] + west[j]) + keep * here[j])
        for j in range(4)
    ]


def groups(ref, index):
    return [ref[index + (pl.ds(8 * j, 8),)] for j in range(4)]


def strided(ref, row):
    return [ref[row, pl.ds(j, 8, stride=4), :] for j in range(4)]


def sweep(segment, load, work):
    def block(i, carry):
        row = segment.begin + i * STEP
        held = [load(row), load(row + 1)]
        for k in range(STEP):
            held.append(load(row + k + 2))
            work(row + k + 1, held[k], held[k + 1], held[k + 2])
        return carry

    lax.fori_loop(0, segment.blocks, block, 0)


def each(count, size, work):
    size = min(size, count)

    def run(first):
        for k in range(size):
            work(first + k)

    if count // size:
        lax.fori_loop(0, count // size, lambda i, c: (run(i * size), c)[1], 0)
    if count % size:
        run(count - size)


def widen(state_ref, natural_ref, segments, scale):
    levels, columns, _ = state_ref.shape
    for s in segments:
        at = slice(s.lane0, s.lane0 + s.width)

        def one(k):
            parts = []
            for g in range(s.groups):
                level = jnp.minimum(g * s.steps + k, levels - 1)
                parts.append(state_ref[level, :, at].astype(F32))
            spare = LANES - s.groups * s.width
            if spare:
                parts.append(jnp.zeros((columns, spare), F32))
            value = jnp.concatenate(parts, axis=1) if len(parts) > 1 else parts[0]
            natural_ref[s.begin + 1 + k] = scale * value if scale != 1.0 else value

        each(s.steps, STEP, one)


def folded_sums(sums_ref, columns):
    rows = sums_ref.shape[0] // 8
    total = sums_ref[pl.ds(0, rows, stride=8), :]
    for k in range(1, 8):
        total = total + sums_ref[pl.ds(k, rows, stride=8), :]
    return total * (1.0 / columns)


def slab(row):
    return pl.ds(pl.multiple_of(row * 8, 8), 8)


def spread_row(ref, row):
    return jnp.broadcast_to(ref[pl.ds(row, 1), :], (8, LANES))


def turn(value, shift):
    if not shift:
        return value
    height = value.shape[0]
    tall = -(-height // 8) * 8
    if tall != height:
        fill = jnp.zeros((tall - height, LANES), F32)
        value = jnp.concatenate([value, fill], axis=0)
    return pltpu.roll(value, shift % LANES, 1)[:height]


def each(count, size, work):
    size = min(size, count)

    def run(first):
        for k in range(size):
            work(first + k)

    if count // size:
        lax.fori_loop(0, count // size, lambda i, c: (run(i * size), c)[1], 0)
    if count % size:
        run(count - size)


def widen(state_ref, natural_ref, segments, scale):
    levels, columns, _ = state_ref.shape
    for s in segments:
        at = slice(s.lane0, s.lane0 + s.width)

        def one(k):
            parts = []
            for g in range(s.groups):
                level = jnp.minimum(g * s.steps + k, levels - 1)
                parts.append(state_ref[level, :, at].astype(F32))
            spare = LANES - s.groups * s.width
            if spare:
                parts.append(jnp.zeros((columns, spare), F32))
            value = jnp.concatenate(parts, axis=1) if len(parts) > 1 else parts[0]
            natural_ref[s.begin + 1 + k] = scale * value if scale != 1.0 else value

        each(s.steps, STEP, one)


def folded_sums(sums_ref, columns):
    rows = sums_ref.shape[0] // 8
    total = sums_ref[pl.ds(0, rows, stride=8), :]
    for k in range(1, 8):
        total = total + sums_ref[pl.ds(k, rows, stride=8), :]
    return total * (1.0 / columns)


def slab(row):
    return pl.ds(pl.multiple_of(row * 8, 8), 8)


def spread_row(ref, row):
    return jnp.broadcast_to(ref[pl.ds(row, 1), :], (8, LANES))


def lane_places(segments):
    return [(s, g) for s in segments for g in range(s.groups)]


def slot_map(segments, block, capacity, padded):
    tiles = []
    for s in segments:
        lane = iota((8, LANES), 1)
        slot = s.lane0 + lane
        row = slot + (padded - capacity) * divided(slot, capacity)
        row = jnp.where(lane < s.width, row, -1)[0:1]
        tiles.append(jnp.where(iota((block, LANES), 0) == row, 1.0, 0.0).astype(BF16))
    return jnp.concatenate(tiles, axis=1)


def prepare_kernel(
    state_ref,
    columns_far,
    mixing_far,
    neighbours_far,
    targets_far,
    map_far,
    saturation_far,
    moved_ref,
    means_ref,
    limits_ref,
    energy_far,
    base_far,
    weights_far,
    homes_far,
    fold_ref,
    unfold_far,
    state_buf,
    natural_ref,
    sums_ref,
    flat_ref,
    energy_buf,
    columns_ref,
    mixing_ref,
    neighbours_ref,
    targets_ref,
    map_ref,
    saturation_ref,
    base_ref,
    weights_ref,
    homes_ref,
    unfold_ref,
    sems,
    in_sems,
    out_sems,
    *,
    segments,
    **host,
):
    fields, levels, columns, _ = state_ref.shape
    given = (
        (columns_far, columns_ref),
        (mixing_far, mixing_ref),
        (neighbours_far, neighbours_ref),
        (targets_far, targets_ref),
        (map_far, map_ref),
        (saturation_far, saturation_ref),
    )
    starts = [pltpu.make_async_copy(x, y, in_sems.at[i]) for i, (x, y) in enumerate(given)]
    loads = [
        pltpu.make_async_copy(state_ref.at[f], state_buf.at[f], sems.at[f]) for f in range(fields)
    ]
    for copy in starts + loads:
        copy.start()
    made = (
        (base_ref, base_far),
        (weights_ref, weights_far),
        (homes_ref, homes_far),
        (unfold_ref, unfold_far),
        (energy_buf, energy_far),
    )
    leaves = [pltpu.make_async_copy(x, y, out_sems.at[i]) for i, (x, y) in enumerate(made)]
    for copy in starts:
        copy.wait()
    tall = flat_ref.shape[0]
    here = iota((tall, levels), 0) == iota((tall, levels), 1)
    diagonal = jnp.where(here, saturation_ref[...], 0.0)
    flat_ref[...] = select(jnp.ones((levels, LANES), BF16), diagonal, NN, swap=True)
    limits_ref[...] = jnp.zeros_like(limits_ref)
    for s in segments:
        lane = iota((s.steps, LANES), 1)
        value = flat_ref[0 : s.steps, :]
        for g in range(1, s.groups):
            other = flat_ref[g * s.steps : (g + 1) * s.steps, :]
            value = jnp.where(lane >= g * s.width, other, value)
        limits_ref[s.rows[0] : s.rows[1], :] = value
    sums_ref[...] = jnp.zeros_like(sums_ref)
    aside(
        columns_ref,
        mixing_ref,
        neighbours_ref,
        targets_ref,
        map_ref,
        base_ref,
        weights_ref,
        homes_ref,
        fold_ref,
        unfold_ref,
        **host,
    )
    for copy in leaves[:4]:
        copy.start()
    for f, scale, target in ((0, SHRINK, energy_buf), (1, 1.0, moved_ref)):
        loads[f].wait()
        widen(state_buf.at[f], natural_ref, segments, scale)
        fill_wide(segments, natural_ref)
        for s in segments:

            def work(row, below, here, above):
                out = linear(below, here, above)
                for j in range(4):
                    target[row, pl.ds(8 * j, 8), :] = out[j]
                sums_ref[slab(row), :] = (here[0] + here[1]) + (here[2] + here[3])

            sweep(s, lambda row: strided(natural_ref, row), work)
        if f == 0:
            leaves[4].start()
        means_ref[f] = folded_sums(sums_ref, columns) * (1.0 / scale)
    for copy in leaves:
        copy.wait()


def neighbour_part(arrived, means, fold, share, parity, levels, stride, neighbours):
    folded = product(fold, means, NT)
    taken = arrived[stride - 1 : stride] > 0.0
    ids = [
        jnp.where(taken, arrived[levels + k : levels + k + 1], -1.0) for k in range(neighbours)
    ]
    total = None
    chunk = min(256, means.shape[0])
    for first in range(0, means.shape[0], chunk):
        row = iota((chunk, arrived.shape[1]), 0) + first
        element = (row + share * divided(row, share) + share * parity).astype(F32)
        wanted = jnp.where(element == ids[0], 1.0, 0.0)
        for k in range(1, neighbours):
            wanted = wanted + jnp.where(element == ids[k], 1.0, 0.0)
        part = folded[:, first : first + chunk]
        term = select(wanted.astype(BF16), part, NN, swap=True, count=2)
        total = term if total is None else total + term
    return total


def halves(ref, share):
    return jnp.concatenate([ref[j, :share, :] for j in range(ref.shape[0])], axis=0)


def arrive_kernel(
    received_ref, fold_ref, arrived_ref, places_ref, *, segments, capacity, padded, **sizes
):
    hosts = received_ref.shape[0]
    share = received_ref.shape[1] - capacity
    places = slot_map(segments, hosts * padded, capacity, padded)
    places_ref[...] = places
    parts = []
    for j in range(hosts):
        parts.append(received_ref[j, share:, :])
        if padded != capacity:
            parts.append(jnp.zeros((padded - capacity, LANES), F32))
    arrived = select(places, jnp.concatenate(parts, axis=0), TN, swap=True)
    parity = lax.axis_index("sec") % 2
    arrived_ref[...] = arrived + neighbour_part(
        arrived, halves(received_ref, share), fold_ref[...], share, parity, **sizes
    )


def water_kernel(
    arrived_ref,
    places_ref,
    other_ref,
    moved_ref,
    means_ref,
    limits_ref,
    fold_ref,
    unfold_far,
    water_far,
    spill_far,
    flats_far,
    back_far,
    unfold_ref,
    even_ref,
    odd_ref,
    spill_buf,
    flats_ref,
    goal_ref,
    mean_ref,
    shift_ref,
    limit_ref,
    sums_ref,
    change_ref,
    back_ref,
    in_sem,
    spill_sems,
    water_sem,
    flat_sem,
    back_sems,
    *,
    segments,
    share,
    padded,
    stride,
    levels,
    neighbours,
):
    rows = means_ref.shape[1]
    columns = even_ref.shape[1]
    load = pltpu.make_async_copy(unfold_far, unfold_ref, in_sem)
    load.start()
    hosts = other_ref.shape[0]
    parity = 1 - lax.axis_index("sec") % 2
    arrived = arrived_ref[...]
    arrived = arrived + neighbour_part(
        arrived,
        halves(other_ref, share),
        fold_ref[...],
        share,
        parity,
        levels,
        stride,
        neighbours,
    )
    goal_ref[...] = jnp.zeros_like(goal_ref)
    flats_ref[...] = jnp.zeros_like(flats_ref)
    sums_ref[...] = jnp.zeros_like(sums_ref)
    counts = flats_ref.at[MAX_SUB + 2]
    for t, s in enumerate(segments):
        lanes = slice(t * LANES, (t + 1) * LANES)
        count = None
        for g in range(s.groups):
            number = s.group_steps(g)
            at = slice(s.rows[0], s.rows[0] + number)
            for f in range(2):
                first = f * stride + g * s.steps
                part = turn(arrived[first : first + number, lanes], g * s.width)
                goal_ref[f, at, :] = goal_ref[f, at, :] + part if g else part
            part = turn(arrived[stride - 1 : stride, lanes], g * s.width)
            count = part if count is None else count + part
        counts[s.rows[0] : s.rows[1], :] = jnp.broadcast_to(count, (s.steps, LANES))
    for f in range(2):
        mean_ref[f] = means_ref[f]
    copies = []
    source, target = None, even_ref
    for n in range(MAX_SUB):
        scale = 0.5 * GROW ** (n + 1)
        last = n + 1 == MAX_SUB
        expected = []
        for f in range(2):
            fill_flat(segments, mean_ref.at[f])
            mean = mean_ref[f]
            mixed = mean + VERTIC * (
                pltpu.roll(mean, 1, 0) + pltpu.roll(mean, rows - 1, 0) - 2.0 * mean
            )
            offset = goal_ref[f] - RELAX * mixed
            expected.append(mixed + offset)
            if f == 1:
                shift_ref[...] = scale * offset
            else:
                flats_ref[n] = (scale * SHRINK) * offset
        limit_ref[...] = scale * limits_ref[...]
        if last:
            flats_ref[MAX_SUB] = shift_ref[...]
            flats_ref[MAX_SUB + 1] = limit_ref[...]
            copies.append(pltpu.make_async_copy(flats_ref, flats_far, flat_sem))
            copies[-1].start()
        for s in segments:
            active = spread_row(counts, s.rows[0]) > float(n)

            def finish(row, lin, old):
                shift = spread_row(shift_ref, row)
                limit = spread_row(limit_ref, row)
                total = None
                for j in range(4):
                    v = lin[j] + shift
                    low = jnp.minimum(v, limit)
                    total = low if total is None else total + low
                    if last:
                        continue
                    u = v + low
                    if old is not None:
                        u = jnp.where(active, u, old[j])
                    spill_buf[n, row, pl.ds(8 * j, 8), :] = v - low
                    target[row, pl.ds(8 * j, 8), :] = u
                sums_ref[slab(row), :] = total

            if n == 0:

                def block(i, carry):
                    for k in range(STEP):
                        row = s.begin + 1 + i * STEP + k
                        finish(row, groups(moved_ref, (row,)), None)
                    return carry

                lax.fori_loop(0, s.blocks, block, 0)
            else:

                def work(row, below, here, above):
                    finish(row, linear(below, here, above), here)

                sweep(s, lambda row: groups(source, (row,)), work)
        if not last:
            copies.append(
                pltpu.make_async_copy(spill_buf.at[n], spill_far.at[n], spill_sems.at[n])
            )
            copies[-1].start()
            fill_wide(segments, target)
            source, target = target, (odd_ref if target is even_ref else even_ref)
        if n + 2 == MAX_SUB:
            copies.append(pltpu.make_async_copy(source, water_far, water_sem))
            copies[-1].start()
        spilled = 0.5 * (expected[1] - folded_sums(sums_ref, columns) * (1.0 / scale))
        step = [expected[0] + LATENT * spilled, expected[1] - spilled]
        keep = counts[...] > float(n)
        for f in range(2):
            mean_ref[f] = jnp.where(keep, step[f], mean_ref[f])
    change_ref[...] = jnp.zeros_like(change_ref)
    for f in range(2):
        change = mean_ref[f] - means_ref[f]
        for t, s in enumerate(segments):
            for g in range(s.groups):
                first, number = f * stride + g * s.steps, s.group_steps(g)
                part = turn(change[s.rows[0] : s.rows[0] + number], -g * s.width)
                change_ref[first : first + number, t * LANES : (t + 1) * LANES] = part
    spread = select(places_ref[...], change_ref[...], NT, count=2)
    load.wait()
    back = product(spread, unfold_ref[...], NN)
    quads = back_ref.shape[2]
    for h in range(2):
        for j in range(hosts):
            for q in range(quads):
                first = j * padded + (h * quads + q) * QUAD
                back_ref[h, j, q] = back[first : first + QUAD]
    for i in range(back_far.shape[0]):
        copies.append(pltpu.make_async_copy(back_ref.at[i % 2], back_far.at[i], back_sems.at[i]))
        copies[-1].start()
    for copy in copies:
        copy.wait()


def energy_kernel(
    state_ref,
    energy_far,
    water_far,
    spill_far,
    flats_far,
    base_far,
    weights_far,
    mixing_far,
    homes_far,
    received_ref,
    other_ref,
    out_ref,
    advanced_ref,
    picks_ref,
    state_buf,
    energy_buf,
    water_buf,
    spill_buf,
    flats_ref,
    base_ref,
    weights_ref,
    mixing_ref,
    homes_ref,
    out_buf,
    even_ref,
    odd_ref,
    natural_ref,
    state_sems,
    in_sems,
    spill_sems,
    out_sems,
    *,
    segments,
    share,
):
    fields, levels, columns, _ = state_ref.shape
    final = MAX_SUB - 1
    pairs = (
        (flats_far, flats_ref),
        (base_far, base_ref),
        (weights_far, weights_ref),
        (mixing_far, mixing_ref),
        (water_far, water_buf),
        (energy_far, energy_buf),
        (homes_far, homes_ref),
    )
    loads = [pltpu.make_async_copy(x, y, in_sems.at[i]) for i, (x, y) in enumerate(pairs)]
    flats, bases, shares, mixings, waters, first, homes = loads
    states = [
        pltpu.make_async_copy(state_ref.at[f], state_buf.at[f], state_sems.at[f])
        for f in range(fields)
    ]
    spills = [
        pltpu.make_async_copy(spill_far.at[n], spill_buf.at[n], spill_sems.at[n])
        for n in range(final)
    ]
    for copy in loads[:5] + [states[1], first] + spills + [states[0], homes]:
        copy.start()
    cut = -(-levels // 2)
    spans = ((0, cut), (cut, levels - cut))

    def leave(f, part):
        at = pl.ds(*spans[part])
        return pltpu.make_async_copy(
            out_buf.at[f, at], out_ref.at[f, at], out_sems.at[2 * f + part]
        )

    counts = flats_ref.at[MAX_SUB + 2]

    def finish_field(f, found):
        for s in segments[::-1]:
            count = spread_row(counts, s.rows[0])
            back = jnp.zeros((8, LANES), F32)
            for n in range(1, MAX_SUB + 1):
                scale = GROW**-n * (LATENT if f == 0 else 1.0)
                back = jnp.where(count == float(n), scale, back)
            at = slice(s.lane0, s.lane0 + s.width)
            held = jnp.broadcast_to(count[0:1, : s.width], (columns, s.width)) > 0.0

            def permute(k):
                row = s.begin + 1 + k
                value = groups(found, (row,))
                for j in range(4):
                    natural_ref[row, pl.ds(j, 8, stride=4), :] = value[j] * back

            def narrow(g, k):
                level = g * s.steps + k
                lanes = slice(g * s.width, (g + 1) * s.width)
                old = state_buf[f, level, :, at].astype(F32)
                value = jnp.where(held, natural_ref[s.begin + 1 + k, :, lanes], old)
                out_buf[f, level, :, at] = value.astype(BF16)

            each(s.steps, STEP, permute)
            if s is segments[0] and s.groups == 1:
                for part, (begin, number) in enumerate(spans):
                    each(number, STEP, lambda k: narrow(0, begin + k))
                    leave(f, part).start()
            else:
                for g in range(s.groups):
                    each(s.group_steps(g), STEP, lambda k: narrow(g, k))
        if segments[0].groups > 1:
            for part in range(2):
                leave(f, part).start()

    bases.wait()
    shares.wait()
    mixings.wait()
    hosts = received_ref.shape[0]
    position = lax.axis_index("col")
    around = [jnp.where(position == 0, hosts - 1, position - 1), position]
    around.append(jnp.where(position == hosts - 1, 0, position + 1))
    means = joined_means(received_ref, other_ref, share, around)
    advanced_ref[...] = base_ref[...] + mixing_ref[...] * select(weights_ref[...], means, NN)
    flats.wait()
    waters.wait()
    for s in segments:
        active = spread_row(counts, s.rows[0]) > float(final)

        def last(row, below, here, above):
            water = linear(below, here, above)
            push = spread_row(flats_ref.at[MAX_SUB], row)
            limit = spread_row(flats_ref.at[MAX_SUB + 1], row)
            for j in range(4):
                v = water[j] + push
                low = jnp.minimum(v, limit)
                spill_buf[final, row, pl.ds(8 * j, 8), :] = v - low
                even_ref[row, pl.ds(8 * j, 8), :] = jnp.where(active, v + low, here[j])

        sweep(s, lambda row: groups(water_buf, (row,)), last)
    states[1].wait()
    finish_field(1, even_ref)
    first.wait()
    source, target = None, odd_ref
    for n in range(MAX_SUB):
        if n < final:
            spills[n].wait()
        for s in segments:
            active = spread_row(counts, s.rows[0]) > float(n)

            def start(i, carry):
                for k in range(STEP):
                    row = s.begin + 1 + i * STEP + k
                    shift = spread_row(flats_ref.at[n], row)
                    lin, spill = groups(energy_buf, (row,)), groups(spill_buf, (n, row))
                    for j in range(4):
                        target[row, pl.ds(8 * j, 8), :] = 2.0 * (lin[j] + shift) + spill[j]
                return carry

            def work(row, below, here, above):
                shift = spread_row(flats_ref.at[n], row)
                lin = linear(below, here, above)
                spill = groups(spill_buf, (n, row))
                for j in range(4):
                    u = 2.0 * (lin[j] + shift) + spill[j]
                    target[row, pl.ds(8 * j, 8), :] = jnp.where(active, u, here[j])

            if n == 0:
                lax.fori_loop(0, s.blocks, start, 0)
            else:
                sweep(s, lambda row: groups(source, (row,)), work)
        if n < final:
            fill_wide(segments, target)
        source, target = target, (odd_ref if target is even_ref else even_ref)
    states[0].wait()
    finish_field(0, source)
    homes.wait()
    place = homes_ref[:, :1].astype(I32)
    picks_ref[...] = jnp.where(iota(picks_ref.shape, 1) == place, 1.0, 0.0).astype(BF16)
    for f in range(fields):
        for part in range(2):
            leave(f, part).wait()


def nearly_kernel(picks_ref, mine_ref, out_ref, table_ref, *, idle):
    sources, quads, _, _ = mine_ref.shape
    held = table_ref.shape[0] // (sources - idle)
    if quads * QUAD != held:
        table_ref[...] = jnp.zeros_like(table_ref)
    for j in range(sources - idle):
        for q in range(quads):
            first = j * held + q * QUAD
            table_ref[first : first + QUAD, :] = mine_ref[idle + j, q]
    out_ref[...] = select(picks_ref[...], table_ref[...], NN)


def final_kernel(advanced_ref, mine_ref, other_ref, out_ref, *, levels):
    summed = advanced_ref[...] + (mine_ref[...] + other_ref[...])
    water = divided(iota(summed.shape, 1), levels) == 1
    out_ref[...] = jnp.where(water, jnp.maximum(summed, 0.0), summed)


SPACES = dict(
    auto=pl.BlockSpec(memory_space=pltpu.VMEM),
    near=pl.BlockSpec(memory_space=pltpu.VMEM),
    far=pl.BlockSpec(memory_space=pl.ANY),
    scalar=pl.BlockSpec(memory_space=pltpu.SMEM),
)


def call(kernel, name, inputs, outputs, scratch=(), limit=8):
    kept = dict(near=pltpu.VMEM, auto=pltpu.HBM, far=pltpu.HBM, scalar=pltpu.HBM)
    arrays = [pltpu.with_memory_space_constraint(x, kept[space]) for space, x in inputs]
    shapes = [kept[space](dims, dtype) for space, dims, dtype in outputs]
    return pl.pallas_call(
        kernel,
        out_shape=shapes,
        in_specs=[SPACES[space] for space, _ in inputs],
        out_specs=[SPACES[space] for space, _, _ in outputs],
        scratch_shapes=list(scratch),
        compiler_params=pltpu.CompilerParams(vmem_limit_bytes=limit << 20),
        name=name,
    )(*arrays)


def body(
    column_state, mixing_rate, neighbours, assignment, substeps, cloud_state, level_map, saturation
):
    col_count = lax.axis_size("col")
    sec_count = lax.axis_size("sec")
    count, width = column_state.shape
    cloud_levels, levels = level_map.shape
    _, fields, _, columns, slots = cloud_state.shape
    elements = count // 4
    capacity = slots // col_count
    half = -(-capacity // (2 * QUAD)) * QUAD
    held = -(-half // 8) * 8
    padded = -(-max(capacity, 2 * half) // 8) * 8
    block = col_count * padded
    clouds = (sec_count - 1) * col_count
    segments, used, rows = segments_of(slots, cloud_levels)
    mapped = LANES * len(segments)
    mixing = mixing_rate.reshape(1, width)
    state = cloud_state[0]
    dma = pltpu.SemaphoreType.DMA

    def wide(*lead):
        return pltpu.VMEM((*lead, rows, columns, LANES), F32)

    hosts = dict(padded=padded, clouds=clouds)
    places_in = [
        ("auto", column_state),
        ("auto", mixing),
        ("auto", neighbours.T),
        ("auto", assignment.reshape(1, count)),
    ]
    outgoing, _ = call(
        functools.partial(host_kernel, **hosts),
        "host",
        places_in + [("auto", substeps.reshape(1, count)), ("auto", level_map)],
        [("auto", (col_count, elements // 2 + capacity, width), F32), ("near", (width, width), F32)],
    )
    received = lax.all_to_all(outgoing, "col", split_axis=0, concat_axis=0, tiled=True)
    moved, cloud_means, limits, energy, base, weights, homes, fold, unfold = call(
        functools.partial(
            prepare_kernel,
            segments=segments,
            col_count=col_count,
            half=half,
            held=held,
            **hosts,
        ),
        "prepare",
        [("far", state)]
        + [("far", x) for _, x in places_in]
        + [("far", level_map), ("far", saturation.reshape(1, cloud_levels))],
        [
            ("near", (used, columns, LANES), F32),
            ("near", (fields, rows, LANES), F32),
            ("near", (rows, LANES), F32),
            ("far", (used, columns, LANES), F32),
            ("far", (count, width), F32),
            ("far", (count, 3 * elements), BF16),
            ("far", (count, LANES), F32),
            ("near", (width, width), F32),
            ("far", (width, width), F32),
        ],
        scratch=[
            pltpu.VMEM(state.shape, BF16),
            wide(),
            pltpu.VMEM((rows * 8, LANES), F32),
            pltpu.VMEM((max(s.groups * s.steps for s in segments), LANES), F32),
            pltpu.VMEM((used, columns, LANES), F32),
            pltpu.VMEM((count, width), F32),
            pltpu.VMEM((1, width), F32),
            pltpu.VMEM((neighbours.shape[1], elements), I32),
            pltpu.VMEM((1, count), I32),
            pltpu.VMEM((cloud_levels, levels), F32),
            pltpu.VMEM((1, cloud_levels), F32),
            pltpu.VMEM((count, width), F32),
            pltpu.VMEM((count, 3 * elements), BF16),
            pltpu.VMEM((count, LANES), F32),
            pltpu.VMEM((width, width), F32),
            dma((fields,)),
            dma((6,)),
            dma((5,)),
        ],
        limit=16,
    )
    received, moved, base = lax.optimization_barrier((received, moved, base))
    pairs = [(i, i ^ 1) for i in range(sec_count)]
    other = lax.ppermute(received, "sec", pairs)
    sizes = dict(stride=levels, levels=cloud_levels, neighbours=neighbours.shape[1])
    arrived, places = call(
        functools.partial(
            arrive_kernel, segments=segments, capacity=capacity, padded=padded, **sizes
        ),
        "arrive",
        [("near", received), ("near", fold)],
        [("near", (width, mapped), F32), ("near", (block, mapped), BF16)],
    )
    water, spill, flats, back = call(
        functools.partial(
            water_kernel, segments=segments, share=elements // 2, padded=padded, **sizes
        ),
        "water",
        [
            ("near", arrived),
            ("near", places),
            ("near", other),
            ("near", moved),
            ("near", cloud_means),
            ("near", limits),
            ("near", fold),
            ("far", unfold),
        ],
        [
            ("far", (rows, columns, LANES), F32),
            ("far", (MAX_SUB - 1, rows, columns, LANES), F32),
            ("far", (MAX_SUB + 3, rows, LANES), F32),
            ("far", (sec_count, col_count, half // QUAD, QUAD, width), F32),
        ],
        scratch=[
            pltpu.VMEM((width, width), F32),
            wide(),
            wide(),
            wide(MAX_SUB - 1),
            pltpu.VMEM((MAX_SUB + 3, rows, LANES), F32),
            pltpu.VMEM((fields, rows, LANES), F32),
            pltpu.VMEM((fields, rows, LANES), F32),
            pltpu.VMEM((rows, LANES), F32),
            pltpu.VMEM((rows, LANES), F32),
            pltpu.VMEM((rows * 8, LANES), F32),
            pltpu.VMEM((width, mapped), F32),
            pltpu.VMEM((2, col_count, half // QUAD, QUAD, width), F32),
            dma(()),
            dma((MAX_SUB - 1,)),
            dma(()),
            dma(()),
            dma((sec_count,)),
        ],
        limit=24,
    )
    returned = lax.all_to_all(
        back.reshape(sec_count * col_count, half // QUAD, QUAD, width),
        ("sec", "col"),
        split_axis=0,
        concat_axis=0,
        tiled=True,
    )
    new_block, advanced, picks = call(
        functools.partial(energy_kernel, segments=segments, share=elements // 2),
        "energy",
        [
            ("far", state),
            ("far", energy),
            ("far", water),
            ("far", spill),
            ("far", flats),
            ("far", base),
            ("far", weights),
            ("far", mixing),
            ("far", homes),
            ("near", received),
            ("near", other),
        ],
        [
            ("far", state.shape, BF16),
            ("near", (count, width), F32),
            ("near", (count, clouds * held), BF16),
        ],
        scratch=[
            pltpu.VMEM(state.shape, BF16),
            pltpu.VMEM((used, columns, LANES), F32),
            wide(),
            wide(MAX_SUB),
            pltpu.VMEM((MAX_SUB + 3, rows, LANES), F32),
            pltpu.VMEM((count, width), F32),
            pltpu.VMEM((count, 3 * elements), BF16),
            pltpu.VMEM((1, width), F32),
            pltpu.VMEM((count, LANES), F32),
            pltpu.VMEM(state.shape, BF16),
            wide(),
            wide(),
            wide(),
            dma((fields,)),
            dma((7,)),
            dma((MAX_SUB - 1,)),
            dma((2 * fields,)),
        ],
        limit=32,
    )
    returned, advanced = lax.optimization_barrier((returned, advanced))
    (mine,) = call(
        functools.partial(nearly_kernel, idle=col_count),
        "nearly",
        [("near", picks), ("near", returned)],
        [("near", (count, width), F32)],
        scratch=[pltpu.VMEM((clouds * held, width), F32)],
    )
    partner = lax.ppermute(mine, "sec", pairs)
    (new_columns,) = call(
        functools.partial(final_kernel, levels=levels),
        "final",
        [("near", advanced), ("near", mine), ("near", partner)],
        [("auto", (count, width), F32)],
    )
    return new_columns, new_block[None]


def solution(mesh):
    in_specs = (
        P("col", None),
        P(),
        P("col", None),
        P("col", None),
        P("col"),
        P("sec", None, None, None, "col"),
        P(),
        P(),
    )
    out_specs = (P("col", None), P("sec", None, None, None, "col"))
    return jax.shard_map(body, mesh=mesh, in_specs=in_specs, out_specs=out_specs, check_vma=False)
```
